32 devices in a mesh: dp: 8 (over z, y), tensor: 4 (over x, core).
Axes of the slice: x: 2, y: 2, z: 4, core: 2. Of those that a mesh axis runs over, the one named last changes fastest.
Arguments:
- tokens: int32 [16384], P('dp'), may hold values from 0 to 8190
- lengths: int32 [16, 4], P('dp'), may hold values from 1 to 512, 1024 in all within a row
- timesteps: int32 [16], P('dp'), may hold values from 1 to 1000, as said below
- masks: int32 [16384], P('dp'), may hold values from 0 to 1, as said below
- step_count: int32 [1], replicated, may hold values from 2 to 20
- table: float32 [8192, 768], P('tensor', 'dp'), may hold values from -0.4375 to 0.4375
- joint_weight: float32 [768, 2304], P('dp', 'tensor'), may hold values from -0.21875 to 0.21875
- output_weight: float32 [768, 768], P('tensor', 'dp'), may hold values from -1.75 to 1.75
- upward_weight: float32 [768, 3072], P('dp', 'tensor'), may hold values from -0.21875 to 0.21875
- downward_weight: float32 [3072, 768], P('tensor', 'dp'), may hold values from -0.21875 to 0.21875
- gains: float32 [3, 768], P(None, 'dp'), may hold values from 0.5 to 1.5
- momentum_table: float32 [8192, 768], P('tensor', 'dp'), may hold values from -3.8146973e-06 to 3.8146973e-06
- momentum_joint: float32 [768, 2304], P('dp', 'tensor'), may hold values from -3.8146973e-06 to 3.8146973e-06
- momentum_output: float32 [768, 768], P('tensor', 'dp'), may hold values from -3.8146973e-06 to 3.8146973e-06
- momentum_upward: float32 [768, 3072], P('dp', 'tensor'), may hold values from -3.8146973e-06 to 3.8146973e-06
- momentum_downward: float32 [3072, 768], P('tensor', 'dp'), may hold values from -3.8146973e-06 to 3.8146973e-06
- momentum_gains: float32 [3, 768], P(None, 'dp'), may hold values from -1.9073486e-05 to 1.9073486e-05
- variance_table: float32 [8192, 768], P('tensor', 'dp'), may hold values from 2.9919196e-14 to 1.1967678e-13
- variance_joint: float32 [768, 2304], P('dp', 'tensor'), may hold values from 2.9919196e-14 to 1.1967678e-13
- variance_output: float32 [768, 768], P('tensor', 'dp'), may hold values from 2.9919196e-14 to 1.1967678e-13
- variance_upward: float32 [768, 3072], P('dp', 'tensor'), may hold values from 2.9919196e-14 to 1.1967678e-13
- variance_downward: float32 [3072, 768], P('tensor', 'dp'), may hold values from 2.9919196e-14 to 1.1967678e-13
- variance_gains: float32 [3, 768], P(None, 'dp'), may hold values from 7.4797986e-13 to 2.9919194e-12
Outputs:
- loss: float32 [], replicated
- grad_norm: float32 [], replicated
- new_momentum_table: float32 [8192, 768], P('tensor', 'dp')
- new_variance_table: float32 [8192, 768], P('tensor', 'dp')
- new_table: float32 [8192, 768], P('tensor', 'dp')
- new_momentum_joint: float32 [768, 2304], P('dp', 'tensor')
- new_variance_joint: float32 [768, 2304], P('dp', 'tensor')
- new_joint: float32 [768, 2304], P('dp', 'tensor')
- new_momentum_output: float32 [768, 768], P('tensor', 'dp')
- new_variance_output: float32 [768, 768], P('tensor', 'dp')
- new_output: float32 [768, 768], P('tensor', 'dp')
- new_momentum_upward: float32 [768, 3072], P('dp', 'tensor')
- new_variance_upward: float32 [768, 3072], P('dp', 'tensor')
- new_upward: float32 [768, 3072], P('dp', 'tensor')
- new_momentum_downward: float32 [3072, 768], P('tensor', 'dp')
- new_variance_downward: float32 [3072, 768], P('tensor', 'dp')
- new_downward: float32 [3072, 768], P('tensor', 'dp')
- new_momentum_gains: float32 [3, 768], P(None, 'dp')
- new_variance_gains: float32 [3, 768], P(None, 'dp')
- new_gains: float32 [3, 768], P(None, 'dp')
The draws below stay inside these ranges and needn't reach their ends.
Inputs may be any that keep to these rules, and one draw needn't show every extreme that they name: `timesteps`: a sequence's timestep is drawn uniformly; some sequence has timestep 1 and some has 1000. `masks`: each position of sequence s is masked independently with probability timesteps[s] / 1000.
All inputs are finite; a program needn't handle non-finite values.
Results may differ from the reference program's by a relative error of at most 0.0082.
Values may be sent and summed in bfloat16 or wider, within the bound.
A program may use at most 192 MiB of HBM per device.

```python
import math
import jax
import jax.numpy as jnp
import numpy as np
from jax import lax

D = 768
HEADS = 12
HEAD_DIM = 64
FF = 3072
VOCAB = 8192
SEQ_LEN = 1024
DOCS = 4
T_DIFF = 1000
SEQS = 16
TOKENS = 16384


def corruption(key):
    base = jax.random.fold_in(key, 17)
    step_draw = jax.random.randint(jax.random.fold_in(base, 1), (SEQS,), 1, T_DIFF + 1)
    first_spot = jax.random.randint(jax.random.fold_in(base, 2), (), 0, SEQS)
    second_spot = (first_spot + 1 + jax.random.randint(jax.random.fold_in(base, 3), (), 0, SEQS - 1)) % SEQS
    places = jnp.arange(SEQS)
    step_draw = jnp.where(places == first_spot, T_DIFF, step_draw)
    step_draw = jnp.where(places == second_spot, 1, step_draw)
    chance = jax.random.randint(jax.random.fold_in(base, 4), (SEQS, SEQ_LEN), 0, T_DIFF)
    absorbed = (chance < step_draw[:, None]).astype(jnp.int32).reshape(TOKENS)
    return (step_draw.astype(jnp.int32), absorbed)


def draw_timesteps(key, part):
    return corruption(key)[0]


def draw_masks(key, part):
    return corruption(key)[1]


def place_ends(values, stream_key, low, largest):
    place = [jax.random.randint(jax.random.fold_in(stream_key, axis), (), 0, length) for axis, length in enumerate(values.shape)]
    widest = values.shape.index(max(values.shape))
    beside = place[:widest] + [(place[widest] + 1) % values.shape[widest]] + place[widest + 1:]
    return values.at[tuple(place)].set(low).at[tuple(beside)].set(largest)


def steps_of(own_key, shape, split, low, top_value):
    loudness, own = 1.0, jax.random.fold_in(own_key, 6)
    for axis_at, blocks in split:
        steps = jnp.exp(jax.random.uniform(jax.random.fold_in(own, axis_at), (blocks,), jnp.float32, low / len(split), top_value / len(split)))
        loudness = loudness * jnp.repeat(steps, shape[axis_at] // blocks).reshape([-1 if axis == axis_at else 1 for axis in range(len(shape))])
    return loudness


def cumulative_ranks(number_of, skew):
    portions = [(1 << 20) // math.isqrt(rank ** skew) + 1 for rank in range(1, number_of + 1)]
    scale = 1 + sum(portions) // (1 << 30)
    return np.cumsum(np.array([max(1, weight // scale) for weight in portions]))


def ranked_ids(stream_key, extent, count, lean):
    table = cumulative_ranks(count, lean)
    lot = jax.random.randint(jax.random.fold_in(stream_key, 1), extent, 0, int(table[count - 1]))
    grade = jnp.searchsorted(jnp.asarray(table, jnp.int32), lot, side="right")
    return jax.random.permutation(jax.random.fold_in(stream_key, 2), count)[grade].astype(jnp.int32)


def length_profile(number_of, total, reach, lean):
    portions = [(1 << 20) // math.isqrt(rank ** lean) + 1 for rank in range(2, number_of + 1)]
    surplus, given = total - reach - (number_of - 1), [1] * (number_of - 1)
    while surplus > 0:
        free = [i for i in range(number_of - 1) if given[i] < reach]
        pool, left = sum([portions[i] for i in free]), surplus
        for i in free:
            more = min(reach - given[i], max(1, left * portions[i] // pool), surplus)
            given[i] = given[i] + more
            surplus = surplus - more
    return np.array([reach] + given)


def ragged(key, amount, total, limit, skew):
    if amount == 2:
        one = jax.random.randint(key, (), max(1, total - limit), min(limit, total - 1) + 1)
        return jnp.stack([one, total - one])
    sizes = jnp.asarray(length_profile(amount, total, limit, skew), jnp.int32)
    couples = (amount - 1) // 2
    donor, sink = sizes[1:1 + 2 * couples:2], sizes[2:2 + 2 * couples:2]
    margin = jnp.minimum(donor - 1, limit - sink)
    passed = jax.random.randint(jax.random.fold_in(key, 1), (couples,), 0, 1 << 20) % (margin + 1)
    sizes = sizes.at[1:1 + 2 * couples:2].set(donor - passed).at[2:2 + 2 * couples:2].set(sink + passed)
    return sizes[jax.random.permutation(jax.random.fold_in(key, 2), amount)]


def normal_values(own_key, extent, scale, limit, split=(), kind=jnp.bfloat16):
    array = jax.random.normal(own_key, extent, jnp.float32) * scale
    if len(split) > 0:
        array = steps_of(own_key, extent, split, -0.22, 0.18) * array
    return jnp.clip(array, min=-limit, max=limit).astype(kind)


def setup_inputs(seed: int = 0) -> dict:
    splits = jax.random.split(jax.random.key(seed), 24)
    return {
        "tokens": place_ends(ranked_ids(splits[0], (TOKENS,), VOCAB - 1, 2), jax.random.fold_in(splits[0], 3), 0, (VOCAB - 1) - 1).astype(jnp.int32),
        "lengths": jax.vmap(lambda own: ragged(own, DOCS, SEQ_LEN, SEQ_LEN // 2, 2))(jax.random.split(splits[1], SEQS)).reshape((SEQS, DOCS)).astype(jnp.int32),
        "timesteps": draw_timesteps(jax.random.fold_in(splits[23], 71), 0),
        "masks": draw_masks(jax.random.fold_in(splits[23], 71), 0),
        "step_count": jax.random.randint(splits[4], (1,), 2, 21).astype(jnp.int32),
        "table": normal_values(splits[5], (VOCAB, D), (D // 4) ** -0.5, 0.4375, ((0, 4), (1, 8)), jnp.float32),
        "joint_weight": normal_values(splits[6], (D, 3 * D), D ** -0.5, 0.21875, ((0, 8), (1, 4)), jnp.float32),
        "output_weight": normal_values(splits[7], (D, D), (D // 64) ** -0.5, 1.75, ((0, 4), (1, 8)), jnp.float32),
        "upward_weight": normal_values(splits[8], (D, FF), D ** -0.5, 0.21875, ((0, 8), (1, 4)), jnp.float32),
        "downward_weight": normal_values(splits[9], (FF, D), (FF // 4) ** -0.5, 0.21875, ((0, 4), (1, 8)), jnp.float32),
        "gains": jnp.clip(1.0 + 0.1 * jax.random.normal(splits[10], (3, D), jnp.float32), 0.5, 1.5),
        "momentum_table": normal_values(splits[11], (VOCAB, D), (0.0022 / (VOCAB * D + 4 * D * D + 2 * D * FF) ** 0.5), 3.814697265625e-06, ((0, 4), (1, 8)), jnp.float32),
        "momentum_joint": normal_values(splits[12], (D, 3 * D), (0.0022 / (VOCAB * D + 4 * D * D + 2 * D * FF) ** 0.5), 3.814697265625e-06, ((0, 8), (1, 4)), jnp.float32),
        "momentum_output": normal_values(splits[13], (D, D), (0.0022 / (VOCAB * D + 4 * D * D + 2 * D * FF) ** 0.5), 3.814697265625e-06, ((0, 4), (1, 8)), jnp.float32),
        "momentum_upward": normal_values(splits[14], (D, FF), (0.0022 / (VOCAB * D + 4 * D * D + 2 * D * FF) ** 0.5), 3.814697265625e-06, ((0, 8), (1, 4)), jnp.float32),
        "momentum_downward": normal_values(splits[15], (FF, D), (0.0022 / (VOCAB * D + 4 * D * D + 2 * D * FF) ** 0.5), 3.814697265625e-06, ((0, 4), (1, 8)), jnp.float32),
        "momentum_gains": normal_values(splits[16], (3, D), (0.011 / (VOCAB * D + 4 * D * D + 2 * D * FF) ** 0.5), 1.9073486328125e-05, ((1, 8),), jnp.float32),
        "variance_table": jnp.clip(jnp.exp(math.log(1.1967678367405532e-13) - 1.3862944 * jax.random.uniform(splits[17], (VOCAB, D), jnp.float32) ** steps_of(splits[17], (VOCAB, D), ((0, 4), (1, 8)), -0.2, 0.2)), 2.991919591851383e-14, 1.1967678367405532e-13),
        "variance_joint": jnp.clip(jnp.exp(math.log(1.1967678367405532e-13) - 1.3862944 * jax.random.uniform(splits[18], (D, 3 * D), jnp.float32) ** steps_of(splits[18], (D, 3 * D), ((0, 8), (1, 4)), -0.2, 0.2)), 2.991919591851383e-14, 1.1967678367405532e-13),
        "variance_output": jnp.clip(jnp.exp(math.log(1.1967678367405532e-13) - 1.3862944 * jax.random.uniform(splits[19], (D, D), jnp.float32) ** steps_of(splits[19], (D, D), ((0, 4), (1, 8)), -0.2, 0.2)), 2.991919591851383e-14, 1.1967678367405532e-13),
        "variance_upward": jnp.clip(jnp.exp(math.log(1.1967678367405532e-13) - 1.3862944 * jax.random.uniform(splits[20], (D, FF), jnp.float32) ** steps_of(splits[20], (D, FF), ((0, 8), (1, 4)), -0.2, 0.2)), 2.991919591851383e-14, 1.1967678367405532e-13),
        "variance_downward": jnp.clip(jnp.exp(math.log(1.1967678367405532e-13) - 1.3862944 * jax.random.uniform(splits[21], (FF, D), jnp.float32) ** steps_of(splits[21], (FF, D), ((0, 4), (1, 8)), -0.2, 0.2)), 2.991919591851383e-14, 1.1967678367405532e-13),
        "variance_gains": jnp.clip(jnp.exp(math.log(2.991919429221057e-12) - 1.3862944 * jax.random.uniform(splits[22], (3, D), jnp.float32) ** steps_of(splits[22], (3, D), ((1, 8),), -0.2, 0.2)), 7.479798573052643e-13, 2.991919429221057e-12),
    }


@jax.custom_vjp
def low(v):
    return lax.optimization_barrier(v.astype(jnp.bfloat16)).astype(jnp.float32)

@jax.custom_vjp
def low_back(v):
    return v

def low_keep(v):
    return (low(v), None)

def low_pass(kept, grad):
    return (grad,)

def back_keep(v):
    return (v, None)

def back_low(kept, grad):
    return (low(grad),)
low.defvjp(low_keep, low_pass)
low_back.defvjp(back_keep, back_low)
highest = lax.Precision.HIGHEST
eps_norm = 1e-06
neg_fill = -1000000000.0
beta_one = 0.9
beta_two = 0.999
adam_eps = 1e-08
clip_at = 0.02
rates = (0.05, 0.03, 0.25, 0.03, 0.03, 0.3)
decays = (0.1, 0.1, 0.1, 0.1, 0.1, 0.0)

def product(left, right):
    return jnp.dot(left, right, precision=highest, preferred_element_type=jnp.float32)

def rms_norm(values, gain):
    inverse = lax.rsqrt(lax.optimization_barrier(jnp.mean(values * values, axis=-1, keepdims=True)) + eps_norm)
    return values * inverse * gain

def rotate(values, cosine, sine):
    middle = values.shape[-1] // 2
    front_part = values[..., :middle]
    back_part = values[..., middle:]
    return jnp.concatenate([front_part * cosine - back_part * sine, back_part * cosine + front_part * sine], axis=-1)

def packing(lengths, tokens, masks, timesteps):
    seq_count = lengths.shape[0]
    position = jnp.arange(SEQ_LEN, dtype=jnp.int32)
    doc_ends = jnp.cumsum(lengths, axis=1)
    doc_starts = doc_ends - lengths
    segment = lax.optimization_barrier(jnp.sum((position[None, :, None] >= doc_ends[:, None, :]).astype(jnp.int32), axis=2))
    chosen = segment[:, :, None] == jnp.arange(DOCS, dtype=jnp.int32)[None, None, :]
    offset = position[None, :] - lax.optimization_barrier(jnp.sum(jnp.where(chosen, doc_starts[:, None, :], 0), axis=2))
    is_real = segment < DOCS - 1
    targets = tokens.reshape(seq_count, SEQ_LEN)
    corrupt = masks.reshape(seq_count, SEQ_LEN) == 1
    inputs = jnp.where(corrupt, VOCAB - 1, targets)
    factor = jnp.where(timesteps == 1, 1.0, T_DIFF / timesteps.astype(jnp.float32))
    weights = jnp.where(corrupt & is_real, factor[:, None], 0.0).astype(jnp.float32)
    inverse_freq = 10000.0 ** (-jnp.arange(HEAD_DIM // 2, dtype=jnp.float32) / (HEAD_DIM // 2))
    angles = offset.astype(jnp.float32)[:, :, None] * inverse_freq
    return (inputs, targets, weights, segment, is_real, jnp.cos(angles), jnp.sin(angles))

def group_loss(params, batch):
    table, joint_weight, output_weight, upward_weight, downward_weight, gains = params
    inputs, targets, weights, segment, cosine, sine = batch
    group_seqs = inputs.shape[0]
    rounded_table = low(table)
    gain_rows = low(gains)
    hidden_in = jnp.take(rounded_table, inputs, axis=0) * D ** 0.5
    normed_one = low(rms_norm(hidden_in, gain_rows[0]))
    projected = low_back(product(normed_one, low(joint_weight))).reshape(group_seqs, SEQ_LEN, HEADS, 3, HEAD_DIM)
    rot_cos = cosine[:, :, None, :]
    rot_sin = sine[:, :, None, :]
    query = low(rotate(projected[:, :, :, 0], rot_cos, rot_sin))
    key_rows = low(rotate(projected[:, :, :, 1], rot_cos, rot_sin))
    value_rows = low(projected[:, :, :, 2])
    scores = low_back(jnp.einsum('gqhe,gkhe->ghqk', query, key_rows, precision=highest) * HEAD_DIM ** (-0.5))
    same_doc = segment[:, None, :, None] == segment[:, None, None, :]
    scores = jnp.where(same_doc, scores, neg_fill)
    probs = low(jax.nn.softmax(scores, axis=-1))
    attended = low(low_back(jnp.einsum('ghqk,gkhe->gqhe', probs, value_rows, precision=highest)))
    after_attn = hidden_in + low_back(product(attended.reshape(group_seqs, SEQ_LEN, D), low(output_weight)))
    normed_two = low(rms_norm(after_attn, gain_rows[1]))
    activated = low(jax.nn.gelu(low_back(product(normed_two, low(upward_weight))), approximate=False))
    after_mlp = after_attn + low_back(product(activated, low(downward_weight)))
    normed_out = low(rms_norm(after_mlp, gain_rows[2]))
    logits = low_back(jnp.einsum('gld,vd->glv', normed_out, rounded_table, precision=highest))
    row_lse = jax.nn.logsumexp(logits, axis=-1)
    picked = jnp.take_along_axis(logits, targets[..., None], axis=-1)[..., 0]
    return jnp.sum(weights * (row_lse - picked))

def reference(tokens, lengths, timesteps, masks, step_count, table, joint_weight, output_weight, upward_weight, downward_weight, gains, momentum_table, momentum_joint, momentum_output, momentum_upward, momentum_downward, momentum_gains, variance_table, variance_joint, variance_output, variance_upward, variance_downward, variance_gains):
    inputs, targets, weights, segment, is_real, cosine, sine = packing(lengths, tokens, masks, timesteps)
    count = jnp.sum(is_real.astype(jnp.float32))
    batch = tuple((item.reshape((SEQS // 2, 2) + item.shape[1:]) for item in (inputs, targets, weights, segment, cosine, sine)))
    params = (table, joint_weight, output_weight, upward_weight, downward_weight, gains)

    def total(weights_all):

        def one_group(carry, piece):
            return (carry + jax.checkpoint(group_loss)(weights_all, piece), None)
        summed, unused = lax.scan(one_group, jnp.zeros((), jnp.float32), batch)
        return summed
    raw_loss, pull = jax.vjp(total, params)
    raw_grads = pull(jnp.ones((), jnp.float32))[0]
    grads = [grad_item / count for grad_item in raw_grads]
    loss = raw_loss / count
    square_total = jnp.zeros((), jnp.float32)
    for grad_item in grads:
        square_total = square_total + jnp.sum(grad_item * grad_item)
    grad_norm = jnp.sqrt(square_total)
    clip_scale = jnp.minimum(1.0, clip_at / grad_norm)
    step_float = step_count[0].astype(jnp.float32)
    fix_one = 1.0 - jnp.power(beta_one, step_float)
    fix_two = 1.0 - jnp.power(beta_two, step_float)
    moments_one = (momentum_table, momentum_joint, momentum_output, momentum_upward, momentum_downward, momentum_gains)
    moments_two = (variance_table, variance_joint, variance_output, variance_upward, variance_downward, variance_gains)
    updated = []
    for index in range(6):
        clipped = grads[index] * clip_scale
        moment_one = beta_one * moments_one[index] + (1.0 - beta_one) * clipped
        moment_two = beta_two * moments_two[index] + (1.0 - beta_two) * clipped * clipped
        stepped = moment_one / fix_one / (jnp.sqrt(moment_two / fix_two) + adam_eps)
        master = params[index]
        updated.extend([moment_one, moment_two, master - rates[index] * (stepped + decays[index] * master)])
    return (loss, grad_norm, updated[0], updated[1], updated[2], updated[3], updated[4], updated[5], updated[6], updated[7], updated[8], updated[9], updated[10], updated[11], updated[12], updated[13], updated[14], updated[15], updated[16], updated[17])
```

```python
import jax
import jax.numpy as jnp
from jax import lax
from jax.sharding import PartitionSpec as P

D = 768
HEAD_DIM = 64
VOCAB = 8192
SEQ_LEN = 1024
DOCS = 4
T_DIFF = 1000


eps_norm = 1e-06
neg_fill = -1000000000.0
beta_one = 0.9
beta_two = 0.999
adam_eps = 1e-08
clip_at = 0.02
rates = (0.05, 0.03, 0.25, 0.03, 0.03, 0.3)
decays = (0.1, 0.1, 0.1, 0.1, 0.1, 0.0)


def norm_apply(values, gain):
    inverse = lax.rsqrt(jnp.mean(values * values, axis=-1, keepdims=True) + eps_norm)
    return values * inverse * gain


def norm_back(values, gain, upstream):
    inverse = lax.rsqrt(jnp.mean(values * values, axis=-1, keepdims=True) + eps_norm)
    gain_grad = jnp.sum(upstream * values * inverse, axis=0)
    scaled = upstream * gain
    inner = jnp.mean(scaled * values, axis=-1, keepdims=True)
    return (inverse * (scaled - values * inverse * inverse * inner), gain_grad)


def rotate(values, cosine, sine):
    middle = values.shape[-1] // 2
    front_part = values[..., :middle]
    back_part = values[..., middle:]
    return jnp.concatenate(
        [front_part * cosine - back_part * sine, back_part * cosine + front_part * sine], axis=-1
    )


def groups_of(count):
    groups, bit, width = [], 1, 1
    while bit < count:
        masks = [bit]
        if width == 2 and bit * 2 < count:
            masks = [bit, 2 * bit, 3 * bit]
            bit = bit * 2
        groups.append(masks)
        bit, width = bit * 2, 2
    return groups


def swap(value, axis, mask):
    size = lax.axis_size(axis)
    return lax.ppermute(value, axis, [(place, place ^ mask) for place in range(size)])


def spread(value, masks):
    return jnp.concatenate([value] + [swap(value, "dp", mask) for mask in masks], axis=0)


def gather_all(value, x_last):
    groups = groups_of(lax.axis_size("dp"))
    for masks in groups[:0:-1]:
        value = spread(value, masks)
    if x_last:
        value = spread(value, groups[0])
        other = swap(value, "tensor", 2)
    else:
        other = swap(value, "tensor", 2)
        value = spread(value, groups[0])
        other = spread(other, groups[0])
    return [value, other, swap(value, "tensor", 1), swap(other, "tensor", 1)]


def wide(value):
    return value.astype(jnp.float32)


def narrow(value):
    return value.astype(jnp.bfloat16)


def fold(value, masks, last):
    rows = value.shape[0] // (len(masks) + 1)
    total = wide(value[:rows])
    for place, mask in enumerate(masks):
        total = total + wide(swap(value[(place + 1) * rows : (place + 2) * rows], "dp", mask))
    return total if last else narrow(total)


def reduce_all(quarters, x_first):
    groups = groups_of(lax.axis_size("dp"))
    own = narrow(wide(quarters[0]) + wide(swap(quarters[2], "tensor", 1)))
    other = narrow(wide(quarters[1]) + wide(swap(quarters[3], "tensor", 1)))
    if x_first:
        own = narrow(wide(own) + wide(swap(other, "tensor", 2)))
        own = fold(own, groups[0], len(groups) == 1)
    else:
        own = fold(own, groups[0], False)
        other = fold(other, groups[0], False)
        own = narrow(wide(own) + wide(swap(other, "tensor", 2)))
    for place in range(1, len(groups)):
        own = fold(own, groups[place], place == len(groups) - 1)
    return wide(own)


def everyone_sum(value):
    for masks in groups_of(lax.axis_size("dp")):
        value = sum([swap(value, "dp", mask) for mask in masks], value)
    for mask in (1, 2):
        value = value + swap(value, "tensor", mask)
    return value


def mm(left, right):
    return jnp.dot(left, right, preferred_element_type=jnp.float32)


def mm_nt(left, right):
    return lax.dot_general(left, right, (((1,), (1,)), ((), ())), preferred_element_type=jnp.float32)


def mm_tn(left, right):
    return lax.dot_general(left, right, (((0,), (0,)), ((), ())), preferred_element_type=jnp.float32)


def gelu_exact(values):
    return jax.nn.gelu(values, approximate=False)


def rotate_heads(values, cosine, sine):
    return rotate(values, cosine[:, None, :], sine[:, None, :])


def scores_of(query, key_rows, same_doc):
    scores = jnp.einsum(
        "qhe,khe->hqk", query, key_rows, preferred_element_type=jnp.float32
    ) * HEAD_DIM ** (-0.5)
    return jnp.where(same_doc[None], scores, neg_fill)


def split_heads(packed):
    packed = packed.reshape(packed.shape[0], -1, 3, HEAD_DIM)
    return packed[:, :, 0], packed[:, :, 1], packed[:, :, 2]


def attend(packed, same_doc):
    query, key_rows, value_rows = split_heads(packed)
    scores = scores_of(query, key_rows, same_doc)
    row_max = jnp.max(scores, axis=-1, keepdims=True)
    expd = jnp.exp(scores - row_max)
    summed = jnp.sum(expd, axis=-1, keepdims=True)
    probs = (expd / summed).astype(jnp.bfloat16)
    output = jnp.einsum("hqk,khe->qhe", probs, value_rows, preferred_element_type=jnp.float32)
    return (narrow(output).reshape(packed.shape[0], -1), (row_max + jnp.log(summed))[..., 0])


def attend_back(packed, same_doc, row_lse, grad_out, cosine, sine):
    query, key_rows, value_rows = split_heads(packed)
    grad_out = grad_out.reshape(packed.shape[0], -1, HEAD_DIM)
    scores = scores_of(query, key_rows, same_doc)
    probs = jnp.exp(scores - row_lse[..., None])
    value_grad = jnp.einsum(
        "hqk,qhe->khe", probs.astype(jnp.bfloat16), grad_out, preferred_element_type=jnp.float32
    )
    prob_grad = jnp.einsum("qhe,khe->hqk", grad_out, value_rows, preferred_element_type=jnp.float32)
    inner = jnp.sum(prob_grad * probs, axis=-1, keepdims=True)
    score_grad = (probs * (prob_grad - inner)).astype(jnp.bfloat16)
    query_grad = jnp.einsum(
        "hqk,khe->qhe", score_grad, key_rows, preferred_element_type=jnp.float32
    ) * HEAD_DIM ** (-0.5)
    key_grad = jnp.einsum(
        "hqk,qhe->khe", score_grad, query, preferred_element_type=jnp.float32
    ) * HEAD_DIM ** (-0.5)
    query_grad = rotate_heads(query_grad, cosine, -sine)
    key_grad = rotate_heads(key_grad, cosine, -sine)
    return narrow(jnp.stack([query_grad, key_grad, value_grad], axis=2).reshape(packed.shape))


def per_device(
    tokens,
    lengths,
    timesteps,
    masks,
    step_count,
    table,
    joint_weight,
    output_weight,
    upward_weight,
    downward_weight,
    gains,
    momentum_table,
    momentum_joint,
    momentum_output,
    momentum_upward,
    momentum_downward,
    momentum_gains,
    variance_table,
    variance_joint,
    variance_output,
    variance_upward,
    variance_downward,
    variance_gains,
):
    place = lax.axis_index("tensor")
    parts = lax.axis_size("tensor")
    rows = tokens.shape[0] // parts
    vocab_part, head_part = table.shape[0], joint_weight.shape[1]
    out_part, ff_part = output_weight.shape[0], upward_weight.shape[1]
    half_vocab = vocab_part // 2

    table_t = narrow(table).T
    left_half = gather_all(table_t[:, :half_vocab], True)
    right_half = gather_all(table_t[:, half_vocab:], False)
    gain_columns = jnp.pad(narrow(gains).T, ((0, 0), (0, 61)))
    first_group = gather_all(jnp.concatenate([narrow(joint_weight), gain_columns], axis=1), True)
    second_group = gather_all(
        jnp.concatenate(
            [narrow(upward_weight), narrow(downward_weight).T, narrow(output_weight).T], axis=1
        ),
        True,
    )
    table_q = [piece for pair in zip(left_half, right_half) for piece in pair]
    joint_q = [item[:, :head_part] for item in first_group]
    gain_full = wide(first_group[0][:, head_part : head_part + 3]).T
    up_q = [item[:, :ff_part] for item in second_group]
    down_q = [item[:, ff_part : 2 * ff_part] for item in second_group]
    out_all = jnp.concatenate([item[:, 2 * ff_part :] for item in second_group], axis=1)

    start = place * rows
    seq = start // SEQ_LEN
    mine = start - seq * SEQ_LEN
    cut = lambda array: lax.dynamic_slice(array, (start,), (rows,))
    targets = cut(tokens)
    corrupt = cut(masks) == 1
    inputs = jnp.where(corrupt, VOCAB - 1, targets)
    own_lengths = lax.dynamic_slice(lengths, (seq, 0), (1, DOCS))
    step_here = lax.dynamic_slice(timesteps, (seq,), (1,))
    theirs = mine ^ rows
    position = jnp.concatenate(
        [mine + jnp.arange(rows, dtype=jnp.int32), theirs + jnp.arange(rows, dtype=jnp.int32)]
    )
    doc_ends = jnp.cumsum(own_lengths[0])
    doc_starts = doc_ends - own_lengths[0]
    segment = jnp.sum((position[:, None] >= doc_ends[None, :]).astype(jnp.int32), axis=1)
    chosen = segment[:, None] == jnp.arange(DOCS, dtype=jnp.int32)[None, :]
    offset = position - jnp.sum(jnp.where(chosen, doc_starts[None, :], 0), axis=1)
    is_real = segment < DOCS - 1
    factor = jnp.where(step_here == 1, 1.0, T_DIFF / step_here.astype(jnp.float32))
    weights = jnp.where(corrupt & is_real[:rows], factor, 0.0)
    inverse_freq = 10000.0 ** (-jnp.arange(HEAD_DIM // 2, dtype=jnp.float32) / (HEAD_DIM // 2))
    angles = offset.astype(jnp.float32)[:, None] * inverse_freq
    cosine, sine = jnp.cos(angles), jnp.sin(angles)
    same_doc = segment[:, None] == segment[None, :]

    def hot(ids, piece):
        quarter, side = piece // 2, piece % 2
        owner = place ^ (2 * (quarter % 2) + quarter // 2)
        base = owner * vocab_part + side * half_vocab
        return (ids - base)[:, None] == jnp.arange(half_vocab, dtype=jnp.int32)[None, :]

    pieces = range(len(table_q))
    input_hot = [narrow(hot(inputs, piece)) for piece in pieces]
    looked = sum(mm_nt(input_hot[piece], table_q[piece]) for piece in pieces)
    embedded = looked * D**0.5
    normed_one = narrow(norm_apply(embedded, gain_full[0]))

    def turned(projected):
        projected = projected.reshape(rows, -1, 3, HEAD_DIM)
        query = rotate_heads(projected[:, :, 0], cosine[:rows], sine[:rows])
        key_rows = rotate_heads(projected[:, :, 1], cosine[:rows], sine[:rows])
        stacked = jnp.stack([query, key_rows, projected[:, :, 2]], axis=2)
        return narrow(stacked.reshape(rows, -1))

    packed = [turned(mm(normed_one, item)) for item in joint_q]
    whole = [
        jnp.concatenate([packed[side], swap(packed[2 + side], "tensor", 1)], axis=0)
        for side in range(2)
    ]
    attended, attn_lse = zip(*[attend(item, same_doc) for item in whole])
    attended_all = jnp.concatenate(
        [item[:rows] for item in attended]
        + [swap(item[rows:], "tensor", 1) for item in attended],
        axis=1,
    )
    after_attn = embedded + mm_nt(attended_all, out_all)
    normed_two = narrow(norm_apply(after_attn, gain_full[1]))
    pre_gelu = [mm(normed_two, item) for item in up_q]
    gelu_pairs = [jax.vjp(gelu_exact, item) for item in pre_gelu]
    activated = [narrow(item[0]) for item in gelu_pairs]
    after_mlp = after_attn + sum(mm_nt(activated[q], down_q[q]) for q in range(4))
    normed_out = narrow(norm_apply(after_mlp, gain_full[2]))
    logits = [mm(normed_out, item) for item in table_q]
    row_max = logits[0].max(axis=1)
    for item in logits[1:]:
        row_max = jnp.maximum(row_max, item.max(axis=1))
    row_sum = sum(jnp.sum(jnp.exp(item - row_max[:, None]), axis=1) for item in logits)
    target_hot = [hot(targets, piece) for piece in pieces]
    row_pick = sum(
        jnp.sum(jnp.where(target_hot[piece], logits[piece], 0.0), axis=1) for piece in pieces
    )
    row_lse = row_max + jnp.log(row_sum)
    loss_local = jnp.sum(weights * (row_lse - row_pick))
    count_local = jnp.sum(is_real[:rows].astype(jnp.float32))

    logit_grad = [
        narrow(
            weights[:, None]
            * (jnp.exp(logits[piece] - row_lse[:, None]) - target_hot[piece].astype(jnp.float32))
        )
        for piece in pieces
    ]
    out_grad = sum(mm_nt(logit_grad[piece], table_q[piece]) for piece in pieces)
    mlp_grad, gain_three = norm_back(after_mlp, gain_full[2], out_grad)
    mlp_branch = narrow(mlp_grad)
    down_grad = [narrow(mm_tn(mlp_branch, item)) for item in activated]
    down_sum = reduce_all(down_grad, True)
    up_input = [
        narrow(gelu_pairs[q][1](mm(mlp_branch, down_q[q]))[0]) for q in range(4)
    ]
    up_grad = [narrow(mm_tn(normed_two, item)) for item in up_input]
    up_sum = reduce_all(up_grad, False)
    normed_two_grad = sum(mm_nt(up_input[q], up_q[q]) for q in range(4))
    attn_in_grad, gain_two = norm_back(after_attn, gain_full[1], normed_two_grad)
    resid_one = mlp_grad + attn_in_grad
    attn_branch = narrow(resid_one)
    out_grads = narrow(mm_tn(attn_branch, attended_all))
    out_sum = reduce_all(
        [out_grads[:, q * out_part : (q + 1) * out_part] for q in range(4)], False
    )
    attended_grad = narrow(mm(attn_branch, out_all))
    grad_parts = [attended_grad[:, q * out_part : (q + 1) * out_part] for q in range(4)]
    proj_whole = [
        attend_back(
            whole[side],
            same_doc,
            attn_lse[side],
            jnp.concatenate(
                [grad_parts[side], swap(grad_parts[2 + side], "tensor", 1)], axis=0
            ),
            cosine,
            sine,
        )
        for side in range(2)
    ]
    proj_grad = [item[:rows] for item in proj_whole] + [
        swap(item[rows:], "tensor", 1) for item in proj_whole
    ]
    normed_one_grad = sum(mm_nt(proj_grad[q], joint_q[q]) for q in range(4))
    embed_in, gain_one = norm_back(embedded, gain_full[0], normed_one_grad)
    embed_grad = resid_one + embed_in
    gain_grad = jnp.pad(narrow(jnp.stack([gain_one, gain_two, gain_three])).T, ((0, 0), (0, 61)))
    joint_grad = [
        jnp.concatenate([narrow(mm_tn(normed_one, item)), gain_grad], axis=1) for item in proj_grad
    ]
    joint_sum = reduce_all(joint_grad, True)
    embed_scaled = narrow(embed_grad * D**0.5)
    table_grad = [
        narrow(mm_tn(normed_out, logit_grad[piece]) + mm_tn(embed_scaled, input_hot[piece]))
        for piece in pieces
    ]
    table_left = reduce_all(table_grad[0::2], True)
    table_right = reduce_all(table_grad[1::2], False)
    gain_sum = joint_sum[:, head_part : head_part + 3].T
    reduced = (
        jnp.concatenate([table_left, table_right], axis=1).T,
        joint_sum[:, :head_part],
        out_sum.T,
        up_sum,
        down_sum.T,
        gain_sum,
    )
    local_square = jnp.zeros((), jnp.float32)
    for grad_item in reduced[:5]:
        local_square = local_square + jnp.sum(grad_item * grad_item)
    local_square = local_square + jnp.sum(gain_sum * gain_sum) / parts
    totals = everyone_sum(jnp.stack([local_square, loss_local, count_local]))
    square_total, loss_total, count_total = totals[0], totals[1], totals[2]
    grad_norm = jnp.sqrt(square_total) / count_total
    clip_scale = jnp.minimum(1.0, clip_at / grad_norm)
    loss = loss_total / count_total
    step_float = step_count[0].astype(jnp.float32)
    fix_one = 1.0 - jnp.power(beta_one, step_float)
    fix_two = 1.0 - jnp.power(beta_two, step_float)
    masters = (table, joint_weight, output_weight, upward_weight, downward_weight, gains)
    moments_one = (
        momentum_table,
        momentum_joint,
        momentum_output,
        momentum_upward,
        momentum_downward,
        momentum_gains,
    )
    moments_two = (
        variance_table,
        variance_joint,
        variance_output,
        variance_upward,
        variance_downward,
        variance_gains,
    )
    updated = []
    for index in range(6):
        clipped = reduced[index] / count_total * clip_scale
        moment_one = beta_one * moments_one[index] + (1.0 - beta_one) * clipped
        moment_two = beta_two * moments_two[index] + (1.0 - beta_two) * clipped * clipped
        stepped = moment_one / fix_one / (jnp.sqrt(moment_two / fix_two) + adam_eps)
        master = masters[index]
        updated.extend(
            [moment_one, moment_two, master - rates[index] * (stepped + decays[index] * master)]
        )
    return tuple([loss, grad_norm] + updated)


def solution(mesh):
    placed = (
        P("dp"),
        P("dp", None),
        P("dp"),
        P("dp"),
        P(),
        P("tensor", "dp"),
        P("dp", "tensor"),
        P("tensor", "dp"),
        P("dp", "tensor"),
        P("tensor", "dp"),
        P(None, "dp"),
        P("tensor", "dp"),
        P("dp", "tensor"),
        P("tensor", "dp"),
        P("dp", "tensor"),
        P("tensor", "dp"),
        P(None, "dp"),
        P("tensor", "dp"),
        P("dp", "tensor"),
        P("tensor", "dp"),
        P("dp", "tensor"),
        P("tensor", "dp"),
        P(None, "dp"),
    )
    return jax.shard_map(
        per_device,
        mesh=mesh,
        in_specs=placed,
        out_specs=(
            P(),
            P(),
            P("tensor", "dp"),
            P("tensor", "dp"),
            P("tensor", "dp"),
            P("dp", "tensor"),
            P("dp", "tensor"),
            P("dp", "tensor"),
            P("tensor", "dp"),
            P("tensor", "dp"),
            P("tensor", "dp"),
            P("dp", "tensor"),
            P("dp", "tensor"),
            P("dp", "tensor"),
            P("tensor", "dp"),
            P("tensor", "dp"),
            P("tensor", "dp"),
            P(None, "dp"),
            P(None, "dp"),
            P(None, "dp"),
        ),
        check_vma=False,
    )
```

```python
import functools

import jax
import jax.numpy as jnp
from jax import lax
from jax.experimental import pallas as pl
from jax.experimental.pallas import tpu as pltpu
from jax.sharding import PartitionSpec as P

D = 768
HEAD_DIM = 64
VOCAB = 8192
SEQ_LEN = 1024
DOCS = 4
T_DIFF = 1000


eps_norm = 1e-06
neg_fill = -1000000000.0
beta_one = 0.9
beta_two = 0.999
adam_eps = 1e-08
clip_at = 0.02
rates = (0.05, 0.03, 0.25, 0.03, 0.03, 0.3)
decays = (0.1, 0.1, 0.1, 0.1, 0.1, 0.0)


def norm_apply(values, gain):
    inverse = lax.rsqrt(jnp.mean(values * values, axis=-1, keepdims=True) + eps_norm)
    return values * inverse * gain


def norm_back(values, gain, upstream):
    inverse = lax.rsqrt(jnp.mean(values * values, axis=-1, keepdims=True) + eps_norm)
    gain_grad = jnp.sum(upstream * values * inverse, axis=0)
    scaled = upstream * gain
    inner = jnp.mean(scaled * values, axis=-1, keepdims=True)
    return (inverse * (scaled - values * inverse * inverse * inner), gain_grad)


def rotate(values, cosine, sine):
    middle = values.shape[-1] // 2
    front_part = values[..., :middle]
    back_part = values[..., middle:]
    return jnp.concatenate(
        [front_part * cosine - back_part * sine, back_part * cosine + front_part * sine], axis=-1
    )


def groups_of(count):
    groups, bit, width = [], 1, 1
    while bit < count:
        masks = [bit]
        if width == 2 and bit * 2 < count:
            masks = [bit, 2 * bit, 3 * bit]
            bit = bit * 2
        groups.append(masks)
        bit, width = bit * 2, 2
    return groups


def swap(value, axis, mask):
    size = lax.axis_size(axis)
    return lax.ppermute(value, axis, [(place, place ^ mask) for place in range(size)])


def spread(value, masks):
    return jnp.concatenate([value] + [swap(value, "dp", mask) for mask in masks], axis=0)


def gather_all(value, x_last):
    groups = groups_of(lax.axis_size("dp"))
    for masks in groups[:0:-1]:
        value = spread(value, masks)
    if x_last:
        value = spread(value, groups[0])
        other = swap(value, "tensor", 2)
    else:
        other = swap(value, "tensor", 2)
        value = spread(value, groups[0])
        other = spread(other, groups[0])
    return [value, other, swap(value, "tensor", 1), swap(other, "tensor", 1)]


MESH = pl.DeviceIdType.MESH


def neighbours():
    column, row = lax.axis_index("dp"), lax.axis_index("tensor")
    return {
        "x": (column, (row + 2) % 4),
        "c": (column, row + 1 - 2 * (row % 2)),
        "y": (column + 1 - 2 * (column % 2), row),
        "up": (column + 2, row),
        "down": (column - 2, row),
    }


def meet(z, devices):
    barrier = pltpu.get_barrier_semaphore()

    def greet(name):
        pl.semaphore_signal(barrier, inc=1, device_id=devices[name], device_id_type=MESH)

    for name in ("x", "c", "y"):
        greet(name)
    pl.when(z < 3)(lambda: greet("up"))
    pl.when(z > 0)(lambda: greet("down"))
    pl.semaphore_wait(barrier, 3 + (z + 2) // 3 + (5 - z) // 3)


def gather_body(items, *refs):
    ins = refs[:items]
    outs = [refs[items + 4 * item : items + 4 * item + 4] for item in range(items)]
    side_sem, z_sem, recv_sem, own_sem = refs[5 * items :]
    column = lax.axis_index("dp")
    z = column // 2
    devices = neighbours()
    meet(z, devices)
    shard = [item.shape[0] for item in ins]
    piece = [item // 2 for item in shard]

    def mirror(source):
        return source + 1 - 2 * (source % 2)

    def view(item, part, quarter, source):
        start = pl.multiple_of(source * shard[item] + part * piece[item], 8)
        return outs[item][quarter].at[pl.ds(start, piece[item])]

    def copy(item, part, quarter, source, to_quarter, name, send, own=False):
        here = view(item, part, quarter, source)
        if own:
            here = ins[item].at[pl.ds(part * piece[item], piece[item])]
        return pltpu.make_async_remote_copy(
            src_ref=here,
            dst_ref=view(item, part, to_quarter, source),
            send_sem=send,
            recv_sem=recv_sem.at[item, part, to_quarter, source],
            device_id=devices[name],
            device_id_type=MESH,
        )

    def arrived(item, part, quarter, source):
        copy(item, part, quarter, source, quarter, "x", side_sem.at[0, item]).wait_recv()

    def send_x(item, part, source, own=False):
        copy(item, part, 0, source, 2, "x", side_sem.at[0, item], own).start()

    def send_y(item, part, quarter, source, own=False):
        copy(item, part, quarter, source, quarter, "y", side_sem.at[1, item], own).start()

    def send_c(item, part, quarter, source, own=False):
        copy(item, part, quarter, source, quarter + 1, "c", side_sem.at[2 + quarter // 2, item], own).start()

    def send_z(item, part, source, turn, upward, own=False):
        name = "up" if upward else "down"
        copy(item, part, 0, source, 0, name, z_sem.at[item, part, 1 - upward, turn], own).start()

    def slot(turn, action):
        pl.when(z >= turn)(lambda: action(column - 2 * turn, 1))
        pl.when(z + turn <= 3)(lambda: action(column + 2 * turn, 0))

    every = [(item, part) for item in range(items) for part in range(2)]
    local = [
        pltpu.make_async_copy(
            ins[item],
            outs[item][0].at[pl.ds(pl.multiple_of(column * shard[item], 8), shard[item])],
            own_sem.at[item],
        )
        for item in range(items)
    ]
    for item, part in every:
        pl.when(z < 3)(lambda: send_z(item, part, column, 0, 1, True))
        pl.when(z > 0)(lambda: send_z(item, part, column, 0, 0, True))
        send_x(item, part, column, True)
        send_y(item, part, 0, column, True)
        send_c(item, part, 0, column, True)
    for copied in local:
        copied.start()

    def from_z(item, part, turn, source, upward):
        arrived(item, part, 0, source)
        if turn < 3:
            ahead = z < 3 if upward else z > 0
            pl.when(ahead)(lambda: send_z(item, part, source, turn, upward))
        send_x(item, part, source)
        send_y(item, part, 0, source)
        send_c(item, part, 0, source)

    def second(item, source):
        arrived(item, 0, 0, mirror(source))
        send_x(item, 0, mirror(source))
        send_c(item, 0, 0, mirror(source))
        arrived(item, 1, 2, source)
        send_y(item, 1, 2, source)
        send_c(item, 1, 2, source)

    def third(item, source):
        arrived(item, 0, 2, source)
        send_c(item, 0, 2, source)
        arrived(item, 1, 0, mirror(source))
        send_c(item, 1, 0, mirror(source))
        for part in range(2):
            arrived(item, part, 2, mirror(source))
            send_c(item, part, 2, mirror(source))

    for item in range(items):
        for turn in (1, 2, 3):
            for part in range(2):
                slot(turn, lambda source, upward: from_z(item, part, turn, source, upward))
    for item in range(items):
        second(item, column)
        for turn in (1, 2, 3):
            slot(turn, lambda source, upward: second(item, source))
    for item in range(items):
        third(item, column)
        for turn in (1, 2, 3):
            slot(turn, lambda source, upward: third(item, source))
    for item, part in every:
        for source in range(8):
            for quarter in (1, 3):
                arrived(item, part, quarter, source)
    for copied in local:
        copied.wait()
    for item in range(items):
        for way, count in enumerate((12, 12, 16, 16)):
            lead = outs[item][0].at[pl.ds(0, count * piece[item])]
            pltpu.make_async_remote_copy(
                src_ref=lead,
                dst_ref=lead,
                send_sem=side_sem.at[way, item],
                recv_sem=recv_sem.at[item, 0, 0, 0],
                device_id=devices["x"],
                device_id_type=MESH,
            ).wait_send()
    for item, part in every:
        for turn in range(3):
            pl.when((z < 3) & (z >= turn))(
                lambda: copy(item, part, 0, column, 0, "up", z_sem.at[item, part, 0, turn], True).wait_send()
            )
            pl.when((z > 0) & (z + turn <= 3))(
                lambda: copy(item, part, 0, column, 0, "down", z_sem.at[item, part, 1, turn], True).wait_send()
            )


def gather_kernel(shards):
    items = len(shards)
    anywhere = pl.BlockSpec(memory_space=pl.ANY)
    whole = lax.axis_size("dp")
    shapes = [
        jax.ShapeDtypeStruct((item.shape[0] * whole, item.shape[1]), item.dtype)
        for item in shards
        for _ in range(4)
    ]
    flat = pl.pallas_call(
        functools.partial(gather_body, items),
        name="gather_weights",
        out_shape=shapes,
        in_specs=[anywhere] * items,
        out_specs=[anywhere] * (4 * items),
        scratch_shapes=[
            pltpu.SemaphoreType.DMA((4, items)),
            pltpu.SemaphoreType.DMA((items, 2, 2, 3)),
            pltpu.SemaphoreType.DMA((items, 2, 4, 8)),
            pltpu.SemaphoreType.DMA((items,)),
        ],
        compiler_params=pltpu.CompilerParams(collective_id=0, has_side_effects=True),
    )(*shards)
    return [flat[4 * item : 4 * item + 4] for item in range(items)]


def reduce_body(items, *refs):
    ins = [refs[4 * item : 4 * item + 4] for item in range(items)]
    outs = refs[4 * items : 5 * items]
    held = [refs[5 * items + 7 * item : 5 * items + 7 * item + 7] for item in range(items)]
    load_sem, side_sem, c_sem, x_sem, y_sem, zs_sem, zr_sem = refs[12 * items :]
    column = lax.axis_index("dp")
    z, y = column // 2, column % 2
    devices = neighbours()
    shard = [item.shape[0] for item in outs]
    piece = [item // 2 for item in shard]

    loads = []
    for item in range(items):
        for side in range(2):
            load = pltpu.make_async_copy(
                ins[item][2 * side], held[item][0].at[side], load_sem.at[item, side]
            )
            load.start()
            loads.append(load)
    meet(z, devices)

    def span(item, part, source):
        return pl.ds(pl.multiple_of(source * shard[item] + part * piece[item], 8), piece[item])

    def remote(src, dst, send, recv, name):
        return pltpu.make_async_remote_copy(
            src_ref=src, dst_ref=dst, send_sem=send, recv_sem=recv, device_id=devices[name], device_id_type=MESH
        )

    def c_copy(item, part, side, source):
        return remote(
            ins[item][2 * side + 1].at[span(item, part, source)],
            held[item][1].at[side, span(item, part, source)],
            side_sem.at[2 + side, item],
            c_sem.at[item, part, side, source],
            "c",
        )

    def x_copy(item, part, source):
        place = source if part == 0 else source // 2
        return remote(
            held[item][0].at[1, span(item, part, source)],
            held[item][2 + part].at[place],
            side_sem.at[0, item],
            x_sem.at[item, part, place],
            "x",
        )

    def y_copy(item, part, side, source):
        return remote(
            held[item][0].at[side, span(item, part, source)],
            held[item][4].at[source // 2] if part == 0 else held[item][5].at[side, source // 2],
            side_sem.at[1, item],
            y_sem.at[item, part + side, source // 2],
            "y",
        )

    def z_copy(item, part, source, away, upward):
        return remote(
            held[item][0].at[0, span(item, part, source)],
            held[item][6].at[1 - upward, part, away],
            zs_sem.at[item, part, 1 - upward, away],
            zr_sem.at[item, part, 1 - upward, away],
            "up" if upward else "down",
        )

    def add(item, side, part, source, *others):
        total = held[item][0]
        start = source * shard[item] + part * piece[item]
        step = 16

        def one(turn, _):
            here = pl.ds(pl.multiple_of(start + turn * step, 8), step)
            value = total[side, here].astype(jnp.float32)
            for other in others:
                value = value + other(turn * step, step)
            total[side, here] = value.astype(jnp.bfloat16)
            return 0

        lax.fori_loop(0, piece[item] // step, one, 0)

    def c_part(item, side, part, source):
        start = source * shard[item] + part * piece[item]
        return lambda at, step: held[item][1][side, pl.ds(pl.multiple_of(start + at, 8), step)].astype(jnp.float32)

    def of(ref, *place):
        return lambda at, step: ref[(*place, pl.ds(pl.multiple_of(at, 8), step))].astype(jnp.float32)

    def targets(action):
        def one(turn, _):
            away = 3 - turn // 2
            pl.when((turn % 2 == 0) & (z + away <= 3))(lambda: action(column + 2 * away, away, 1))
            pl.when((turn % 2 == 1) & (z >= away))(lambda: action(column - 2 * away, away, 0))
            return 0

        lax.fori_loop(0, 6, one, 0)
        action(column, 0, None)

    def mirror(source):
        return source + 1 - 2 * (source % 2)

    def send_c(item):
        def action(source, away, upward):
            c_copy(item, 0, 1, source).start()
            c_copy(item, 0, 1, mirror(source)).start()
            c_copy(item, 1, 1, mirror(source)).start()
            c_copy(item, 1, 0, mirror(source)).start()
            c_copy(item, 0, 0, source).start()
            c_copy(item, 0, 0, mirror(source)).start()
            c_copy(item, 1, 1, source).start()
            c_copy(item, 1, 0, source).start()

        targets(action)

    def first(item):
        def action(source, away, upward):
            for place in (source, mirror(source)):
                c_copy(item, 0, 1, place).wait_recv()
                add(item, 1, 0, place, c_part(item, 1, 0, place))
                x_copy(item, 0, place).start()
            for side in (1, 0):
                place = mirror(source)
                c_copy(item, 1, side, place).wait_recv()
                add(item, side, 1, place, c_part(item, side, 1, place))
                y_copy(item, 1, side, place).start()

        targets(action)

    def second(item):
        def action(source, away, upward):
            place = mirror(source)
            c_copy(item, 0, 0, place).wait_recv()
            x_copy(item, 0, place).wait_recv()
            add(item, 0, 0, place, c_part(item, 0, 0, place), of(held[item][2], place))
            y_copy(item, 0, 0, place).start()
            c_copy(item, 1, 1, source).wait_recv()
            y_copy(item, 1, 1, source).wait_recv()
            add(item, 1, 1, source, c_part(item, 1, 1, source), of(held[item][5], 1, source // 2))
            x_copy(item, 1, source).start()

        targets(action)

    def third(item):
        def action(source, away, upward):
            for part in range(2):
                c_copy(item, part, 0, source).wait_recv()
                x_copy(item, part, source).wait_recv()
                y_copy(item, part, 0, source).wait_recv()
                if part == 0:
                    terms = [of(held[item][2], source), of(held[item][4], source // 2)]
                else:
                    terms = [of(held[item][3], source // 2), of(held[item][5], 0, source // 2)]
                add(item, 0, part, source, c_part(item, 0, part, source), *terms)
                if upward is None:
                    continue
                behind = z > 0 if upward else z < 3

                def more():
                    z_copy(item, part, source, away, upward).wait_recv()
                    add(item, 0, part, source, of(held[item][6], 1 - upward, part, away))

                pl.when(behind)(more)
                z_copy(item, part, source, away - 1, upward).start()

        targets(action)

    def last(item):
        for part in range(2):
            for upward in (1, 0):
                pl.when(z > 0 if upward else z < 3)(
                    lambda: z_copy(item, part, column, 0, upward).wait_recv()
                )
            start = column * shard[item] + part * piece[item]

            def one(turn, _):
                at = pl.multiple_of(turn * 16, 8)
                value = held[item][0][0, pl.ds(pl.multiple_of(start + at, 8), 16)].astype(jnp.float32)
                below = held[item][6][0, part, 0, pl.ds(at, 16)].astype(jnp.float32)
                above = held[item][6][1, part, 0, pl.ds(at, 16)].astype(jnp.float32)
                value = value + jnp.where(z > 0, below, 0.0) + jnp.where(z < 3, above, 0.0)
                outs[item][pl.ds(pl.multiple_of(part * piece[item] + at, 8), 16)] = value
                return 0

            lax.fori_loop(0, piece[item] // 16, one, 0)

    for item in range(items):
        send_c(item)
    for load in loads:
        load.wait()
    for action in (first, second, third, last):
        for item in range(items):
            action(item)
    for item in range(items):
        for way, count in enumerate((12, 12, 16, 16)):
            lead = held[item][0].at[0, pl.ds(0, count * piece[item])]
            remote(lead, lead, side_sem.at[way, item], load_sem.at[item, 0], "x").wait_send()
        for part in range(2):
            for away in range(3):
                pl.when((z < 3) & (z + away + 1 <= 3))(
                    lambda: z_copy(item, part, column, away, 1).wait_send()
                )
                pl.when((z > 0) & (z - away - 1 >= 0))(
                    lambda: z_copy(item, part, column, away, 0).wait_send()
                )


def reduce_kernel(grads, tag):
    items = len(grads)
    anywhere = pl.BlockSpec(memory_space=pl.ANY)
    inside = pl.BlockSpec(memory_space=pltpu.VMEM)
    whole = lax.axis_size("dp")
    shapes, scratch = [], []
    for quarters in grads:
        rows, width = quarters[0].shape
        half = rows // (2 * whole)
        shapes.append(jax.ShapeDtypeStruct((rows // whole, width), jnp.float32))
        for lead in ((2, rows), (2, rows), (8, half), (4, half), (4, half), (2, 4, half), (2, 2, 3, half)):
            scratch.append(pltpu.VMEM((*lead, width), jnp.bfloat16))
    return pl.pallas_call(
        functools.partial(reduce_body, items),
        name="reduce_grads",
        out_shape=shapes,
        in_specs=[anywhere] * (4 * items),
        out_specs=[inside] * items,
        scratch_shapes=scratch
        + [
            pltpu.SemaphoreType.DMA((items, 2)),
            pltpu.SemaphoreType.DMA((4, items)),
            pltpu.SemaphoreType.DMA((items, 2, 2, 8)),
            pltpu.SemaphoreType.DMA((items, 2, 8)),
            pltpu.SemaphoreType.DMA((items, 3, 4)),
            pltpu.SemaphoreType.DMA((items, 2, 2, 3)),
            pltpu.SemaphoreType.DMA((items, 2, 2, 3)),
        ],
        compiler_params=pltpu.CompilerParams(
            collective_id=tag, has_side_effects=True, vmem_limit_bytes=60 << 20
        ),
    )(*[item for quarters in grads for item in quarters])


def known_mesh():
    return lax.axis_size("dp") == 8 and lax.axis_size("tensor") == 4


def gather_weights(shards):
    if not known_mesh():
        return [gather_all(item, True) for item in shards]
    return [[item[0], item[2], item[1], item[3]] for item in gather_kernel(shards)]


def reduce_grads(grads, tag):
    if not known_mesh():
        return [reduce_all(item, True) for item in grads]
    return reduce_kernel([[item[0], item[2], item[1], item[3]] for item in grads], tag)


def wide(value):
    return value.astype(jnp.float32)


def narrow(value):
    return value.astype(jnp.bfloat16)


def fold(value, masks, last):
    rows = value.shape[0] // (len(masks) + 1)
    total = wide(value[:rows])
    for place, mask in enumerate(masks):
        total = total + wide(swap(value[(place + 1) * rows : (place + 2) * rows], "dp", mask))
    return total if last else narrow(total)


def reduce_all(quarters, x_first):
    groups = groups_of(lax.axis_size("dp"))
    own = narrow(wide(quarters[0]) + wide(swap(quarters[2], "tensor", 1)))
    other = narrow(wide(quarters[1]) + wide(swap(quarters[3], "tensor", 1)))
    if x_first:
        own = narrow(wide(own) + wide(swap(other, "tensor", 2)))
        own = fold(own, groups[0], len(groups) == 1)
    else:
        own = fold(own, groups[0], False)
        other = fold(other, groups[0], False)
        own = narrow(wide(own) + wide(swap(other, "tensor", 2)))
    for place in range(1, len(groups)):
        own = fold(own, groups[place], place == len(groups) - 1)
    return wide(own)


def everyone_sum(value):
    for masks in groups_of(lax.axis_size("dp")):
        value = sum([swap(value, "dp", mask) for mask in masks], value)
    for mask in (1, 2):
        value = value + swap(value, "tensor", mask)
    return value


def mm(left, right):
    return jnp.dot(left, right, preferred_element_type=jnp.float32)


def mm_nt(left, right):
    return lax.dot_general(left, right, (((1,), (1,)), ((), ())), preferred_element_type=jnp.float32)


def mm_tn(left, right):
    return lax.dot_general(left, right, (((0,), (0,)), ((), ())), preferred_element_type=jnp.float32)


def gelu_exact(values):
    return jax.nn.gelu(values, approximate=False)


def rotate_heads(values, cosine, sine):
    return rotate(values, cosine[:, None, :], sine[:, None, :])


def scores_of(query, key_rows, same_doc):
    scores = jnp.einsum(
        "qhe,khe->hqk", query, key_rows, preferred_element_type=jnp.float32
    ) * HEAD_DIM ** (-0.5)
    return jnp.where(same_doc[None], scores, neg_fill)


def split_heads(packed):
    packed = packed.reshape(packed.shape[0], -1, 3, HEAD_DIM)
    return packed[:, :, 0], packed[:, :, 1], packed[:, :, 2]


def attend(packed, same_doc):
    query, key_rows, value_rows = split_heads(packed)
    scores = scores_of(query, key_rows, same_doc)
    row_max = jnp.max(scores, axis=-1, keepdims=True)
    expd = jnp.exp(scores - row_max)
    summed = jnp.sum(expd, axis=-1, keepdims=True)
    probs = (expd / summed).astype(jnp.bfloat16)
    output = jnp.einsum("hqk,khe->qhe", probs, value_rows, preferred_element_type=jnp.float32)
    return (narrow(output).reshape(packed.shape[0], -1), (row_max + jnp.log(summed))[..., 0])


def attend_back(packed, same_doc, row_lse, grad_out, cosine, sine):
    query, key_rows, value_rows = split_heads(packed)
    grad_out = grad_out.reshape(packed.shape[0], -1, HEAD_DIM)
    scores = scores_of(query, key_rows, same_doc)
    probs = jnp.exp(scores - row_lse[..., None])
    value_grad = jnp.einsum(
        "hqk,qhe->khe", probs.astype(jnp.bfloat16), grad_out, preferred_element_type=jnp.float32
    )
    prob_grad = jnp.einsum("qhe,khe->hqk", grad_out, value_rows, preferred_element_type=jnp.float32)
    inner = jnp.sum(prob_grad * probs, axis=-1, keepdims=True)
    score_grad = (probs * (prob_grad - inner)).astype(jnp.bfloat16)
    query_grad = jnp.einsum(
        "hqk,khe->qhe", score_grad, key_rows, preferred_element_type=jnp.float32
    ) * HEAD_DIM ** (-0.5)
    key_grad = jnp.einsum(
        "hqk,qhe->khe", score_grad, query, preferred_element_type=jnp.float32
    ) * HEAD_DIM ** (-0.5)
    query_grad = rotate_heads(query_grad, cosine, -sine)
    key_grad = rotate_heads(key_grad, cosine, -sine)
    return narrow(jnp.stack([query_grad, key_grad, value_grad], axis=2).reshape(packed.shape))


def per_device(
    tokens,
    lengths,
    timesteps,
    masks,
    step_count,
    table,
    joint_weight,
    output_weight,
    upward_weight,
    downward_weight,
    gains,
    momentum_table,
    momentum_joint,
    momentum_output,
    momentum_upward,
    momentum_downward,
    momentum_gains,
    variance_table,
    variance_joint,
    variance_output,
    variance_upward,
    variance_downward,
    variance_gains,
):
    place = lax.axis_index("tensor")
    parts = lax.axis_size("tensor")
    rows = tokens.shape[0] // parts
    vocab_part, head_part = table.shape[0], joint_weight.shape[1]
    out_part, ff_part = output_weight.shape[0], upward_weight.shape[1]

    gain_columns = jnp.pad(narrow(gains).T, ((0, 0), (0, 61)))
    shards = [
        narrow(table).T,
        jnp.concatenate([narrow(joint_weight), gain_columns], axis=1),
        jnp.concatenate(
            [narrow(upward_weight), narrow(downward_weight).T, narrow(output_weight).T], axis=1
        ),
    ]
    table_q, first_group, second_group = gather_weights(shards)
    joint_q = [item[:, :head_part] for item in first_group]
    gain_full = wide(first_group[0][:, head_part : head_part + 3]).T
    up_q = [item[:, :ff_part] for item in second_group]
    down_q = [item[:, ff_part : 2 * ff_part] for item in second_group]
    out_all = jnp.concatenate([item[:, 2 * ff_part :] for item in second_group], axis=1)

    start = place * rows
    seq = start // SEQ_LEN
    mine = start - seq * SEQ_LEN
    cut = lambda array: lax.dynamic_slice(array, (start,), (rows,))
    targets = cut(tokens)
    corrupt = cut(masks) == 1
    inputs = jnp.where(corrupt, VOCAB - 1, targets)
    own_lengths = lax.dynamic_slice(lengths, (seq, 0), (1, DOCS))
    step_here = lax.dynamic_slice(timesteps, (seq,), (1,))
    theirs = mine ^ rows
    position = jnp.concatenate(
        [mine + jnp.arange(rows, dtype=jnp.int32), theirs + jnp.arange(rows, dtype=jnp.int32)]
    )
    doc_ends = jnp.cumsum(own_lengths[0])
    doc_starts = doc_ends - own_lengths[0]
    segment = jnp.sum((position[:, None] >= doc_ends[None, :]).astype(jnp.int32), axis=1)
    chosen = segment[:, None] == jnp.arange(DOCS, dtype=jnp.int32)[None, :]
    offset = position - jnp.sum(jnp.where(chosen, doc_starts[None, :], 0), axis=1)
    is_real = segment < DOCS - 1
    factor = jnp.where(step_here == 1, 1.0, T_DIFF / step_here.astype(jnp.float32))
    weights = jnp.where(corrupt & is_real[:rows], factor, 0.0)
    inverse_freq = 10000.0 ** (-jnp.arange(HEAD_DIM // 2, dtype=jnp.float32) / (HEAD_DIM // 2))
    angles = offset.astype(jnp.float32)[:, None] * inverse_freq
    cosine, sine = jnp.cos(angles), jnp.sin(angles)
    same_doc = segment[:, None] == segment[None, :]

    def hot(ids, piece):
        base = (place ^ (2 * (piece % 2) + piece // 2)) * vocab_part
        return (ids - base)[:, None] == jnp.arange(vocab_part, dtype=jnp.int32)[None, :]

    pieces = range(len(table_q))
    input_hot = [narrow(hot(inputs, piece)) for piece in pieces]
    looked = sum(mm_nt(input_hot[piece], table_q[piece]) for piece in pieces)
    embedded = looked * D**0.5
    normed_one = narrow(norm_apply(embedded, gain_full[0]))

    def turned(projected):
        projected = projected.reshape(rows, -1, 3, HEAD_DIM)
        query = rotate_heads(projected[:, :, 0], cosine[:rows], sine[:rows])
        key_rows = rotate_heads(projected[:, :, 1], cosine[:rows], sine[:rows])
        stacked = jnp.stack([query, key_rows, projected[:, :, 2]], axis=2)
        return narrow(stacked.reshape(rows, -1))

    packed = [turned(mm(normed_one, item)) for item in joint_q]
    whole = [
        jnp.concatenate([packed[side], swap(packed[2 + side], "tensor", 1)], axis=0)
        for side in range(2)
    ]
    attended, attn_lse = zip(*[attend(item, same_doc) for item in whole])
    attended_all = jnp.concatenate(
        [item[:rows] for item in attended]
        + [swap(item[rows:], "tensor", 1) for item in attended],
        axis=1,
    )
    after_attn = embedded + mm_nt(attended_all, out_all)
    normed_two = narrow(norm_apply(after_attn, gain_full[1]))
    pre_gelu = [mm(normed_two, item) for item in up_q]
    gelu_pairs = [jax.vjp(gelu_exact, item) for item in pre_gelu]
    activated = [narrow(item[0]) for item in gelu_pairs]
    after_mlp = after_attn + sum(mm_nt(activated[q], down_q[q]) for q in range(4))
    normed_out = narrow(norm_apply(after_mlp, gain_full[2]))
    logits = [mm(normed_out, item) for item in table_q]
    row_max = logits[0].max(axis=1)
    for item in logits[1:]:
        row_max = jnp.maximum(row_max, item.max(axis=1))
    row_sum = sum(jnp.sum(jnp.exp(item - row_max[:, None]), axis=1) for item in logits)
    target_hot = [hot(targets, piece) for piece in pieces]
    row_pick = sum(
        jnp.sum(jnp.where(target_hot[piece], logits[piece], 0.0), axis=1) for piece in pieces
    )
    row_lse = row_max + jnp.log(row_sum)
    loss_local = jnp.sum(weights * (row_lse - row_pick))
    count_local = jnp.sum(is_real[:rows].astype(jnp.float32))

    logit_grad = [
        narrow(
            weights[:, None]
            * (jnp.exp(logits[piece] - row_lse[:, None]) - target_hot[piece].astype(jnp.float32))
        )
        for piece in pieces
    ]
    out_grad = sum(mm_nt(logit_grad[piece], table_q[piece]) for piece in pieces)
    mlp_grad, gain_three = norm_back(after_mlp, gain_full[2], out_grad)
    mlp_branch = narrow(mlp_grad)
    down_grad = [narrow(mm_tn(mlp_branch, item)) for item in activated]
    up_input = [
        narrow(gelu_pairs[q][1](mm(mlp_branch, down_q[q]))[0]) for q in range(4)
    ]
    up_grad = [narrow(mm_tn(normed_two, item)) for item in up_input]
    normed_two_grad = sum(mm_nt(up_input[q], up_q[q]) for q in range(4))
    attn_in_grad, gain_two = norm_back(after_attn, gain_full[1], normed_two_grad)
    resid_one = mlp_grad + attn_in_grad
    attn_branch = narrow(resid_one)
    out_grads = narrow(mm_tn(attn_branch, attended_all))
    out_grad_q = [out_grads[:, q * out_part : (q + 1) * out_part] for q in range(4)]
    attended_grad = narrow(mm(attn_branch, out_all))
    grad_parts = [attended_grad[:, q * out_part : (q + 1) * out_part] for q in range(4)]
    proj_whole = [
        attend_back(
            whole[side],
            same_doc,
            attn_lse[side],
            jnp.concatenate(
                [grad_parts[side], swap(grad_parts[2 + side], "tensor", 1)], axis=0
            ),
            cosine,
            sine,
        )
        for side in range(2)
    ]
    proj_grad = [item[:rows] for item in proj_whole] + [
        swap(item[rows:], "tensor", 1) for item in proj_whole
    ]
    normed_one_grad = sum(mm_nt(proj_grad[q], joint_q[q]) for q in range(4))
    embed_in, gain_one = norm_back(embedded, gain_full[0], normed_one_grad)
    embed_grad = resid_one + embed_in
    gain_grad = jnp.pad(narrow(jnp.stack([gain_one, gain_two, gain_three])).T, ((0, 0), (0, 61)))
    joint_grad = [
        jnp.concatenate([narrow(mm_tn(normed_one, item)), gain_grad], axis=1) for item in proj_grad
    ]
    embed_scaled = narrow(embed_grad * D**0.5)
    table_grad = [
        narrow(mm_tn(normed_out, logit_grad[piece]) + mm_tn(embed_scaled, input_hot[piece]))
        for piece in pieces
    ]
    table_sum, joint_sum, up_sum, down_sum, out_sum = reduce_grads(
        [table_grad, joint_grad, up_grad, down_grad, out_grad_q], 1
    )
    gain_sum = joint_sum[:, head_part : head_part + 3].T
    reduced = (
        table_sum.T,
        joint_sum[:, :head_part],
        out_sum.T,
        up_sum,
        down_sum.T,
        gain_sum,
    )
    local_square = jnp.zeros((), jnp.float32)
    for grad_item in reduced[:5]:
        local_square = local_square + jnp.sum(grad_item * grad_item)
    local_square = local_square + jnp.sum(gain_sum * gain_sum) / parts
    totals = everyone_sum(jnp.stack([local_square, loss_local, count_local]))
    square_total, loss_total, count_total = totals[0], totals[1], totals[2]
    grad_norm = jnp.sqrt(square_total) / count_total
    clip_scale = jnp.minimum(1.0, clip_at / grad_norm)
    loss = loss_total / count_total
    step_float = step_count[0].astype(jnp.float32)
    fix_one = 1.0 - jnp.power(beta_one, step_float)
    fix_two = 1.0 - jnp.power(beta_two, step_float)
    masters = (table, joint_weight, output_weight, upward_weight, downward_weight, gains)
    moments_one = (
        momentum_table,
        momentum_joint,
        momentum_output,
        momentum_upward,
        momentum_downward,
        momentum_gains,
    )
    moments_two = (
        variance_table,
        variance_joint,
        variance_output,
        variance_upward,
        variance_downward,
        variance_gains,
    )
    updated = []
    for index in range(6):
        clipped = reduced[index] / count_total * clip_scale
        moment_one = beta_one * moments_one[index] + (1.0 - beta_one) * clipped
        moment_two = beta_two * moments_two[index] + (1.0 - beta_two) * clipped * clipped
        stepped = moment_one / fix_one / (jnp.sqrt(moment_two / fix_two) + adam_eps)
        master = masters[index]
        updated.extend(
            [moment_one, moment_two, master - rates[index] * (stepped + decays[index] * master)]
        )
    return tuple([loss, grad_norm] + updated)


def solution(mesh):
    placed = (
        P("dp"),
        P("dp", None),
        P("dp"),
        P("dp"),
        P(),
        P("tensor", "dp"),
        P("dp", "tensor"),
        P("tensor", "dp"),
        P("dp", "tensor"),
        P("tensor", "dp"),
        P(None, "dp"),
        P("tensor", "dp"),
        P("dp", "tensor"),
        P("tensor", "dp"),
        P("dp", "tensor"),
        P("tensor", "dp"),
        P(None, "dp"),
        P("tensor", "dp"),
        P("dp", "tensor"),
        P("tensor", "dp"),
        P("dp", "tensor"),
        P("tensor", "dp"),
        P(None, "dp"),
    )
    return jax.shard_map(
        per_device,
        mesh=mesh,
        in_specs=placed,
        out_specs=(
            P(),
            P(),
            P("tensor", "dp"),
            P("tensor", "dp"),
            P("tensor", "dp"),
            P("dp", "tensor"),
            P("dp", "tensor"),
            P("dp", "tensor"),
            P("tensor", "dp"),
            P("tensor", "dp"),
            P("tensor", "dp"),
            P("dp", "tensor"),
            P("dp", "tensor"),
            P("dp", "tensor"),
            P("tensor", "dp"),
            P("tensor", "dp"),
            P("tensor", "dp"),
            P(None, "dp"),
            P(None, "dp"),
            P(None, "dp"),
        ),
        check_vma=False,
    )
```

```python
import functools

import jax
import jax.numpy as jnp
from jax import lax
from jax.experimental import pallas as pl
from jax.experimental.pallas import tpu as pltpu
from jax.sharding import PartitionSpec as P

D = 768
HEAD_DIM = 64
VOCAB = 8192
SEQ_LEN = 1024
DOCS = 4
T_DIFF = 1000


eps_norm = 1e-06
neg_fill = -1000000000.0
beta_one = 0.9
beta_two = 0.999
adam_eps = 1e-08
clip_at = 0.02
rates = (0.05, 0.03, 0.25, 0.03, 0.03, 0.3)
decays = (0.1, 0.1, 0.1, 0.1, 0.1, 0.0)


def norm_apply(values, gain):
    inverse = lax.rsqrt(jnp.mean(values * values, axis=-1, keepdims=True) + eps_norm)
    return values * inverse * gain


def norm_back(values, gain, upstream):
    inverse = lax.rsqrt(jnp.mean(values * values, axis=-1, keepdims=True) + eps_norm)
    gain_grad = jnp.sum(upstream * values * inverse, axis=0)
    scaled = upstream * gain
    inner = jnp.mean(scaled * values, axis=-1, keepdims=True)
    return (inverse * (scaled - values * inverse * inverse * inner), gain_grad)


def rotate(values, cosine, sine):
    middle = values.shape[-1] // 2
    front_part = values[..., :middle]
    back_part = values[..., middle:]
    return jnp.concatenate(
        [front_part * cosine - back_part * sine, back_part * cosine + front_part * sine], axis=-1
    )


def groups_of(count):
    groups, bit, width = [], 1, 1
    while bit < count:
        masks = [bit]
        if width == 2 and bit * 2 < count:
            masks = [bit, 2 * bit, 3 * bit]
            bit = bit * 2
        groups.append(masks)
        bit, width = bit * 2, 2
    return groups


def swap(value, axis, mask):
    size = lax.axis_size(axis)
    return lax.ppermute(value, axis, [(place, place ^ mask) for place in range(size)])


def spread(value, masks):
    return jnp.concatenate([value] + [swap(value, "dp", mask) for mask in masks], axis=0)


def gather_all(value, x_last):
    groups = groups_of(lax.axis_size("dp"))
    for masks in groups[:0:-1]:
        value = spread(value, masks)
    if x_last:
        value = spread(value, groups[0])
        other = swap(value, "tensor", 2)
    else:
        other = swap(value, "tensor", 2)
        value = spread(value, groups[0])
        other = spread(other, groups[0])
    return [value, other, swap(value, "tensor", 1), swap(other, "tensor", 1)]


MESH = pl.DeviceIdType.MESH


def neighbours():
    column, row = lax.axis_index("dp"), lax.axis_index("tensor")
    return {
        "x": (column, (row + 2) % 4),
        "c": (column, row + 1 - 2 * (row % 2)),
        "y": (column + 1 - 2 * (column % 2), row),
        "up": (column + 2, row),
        "down": (column - 2, row),
    }


def meet(z, devices):
    barrier = pltpu.get_barrier_semaphore()

    def greet(name):
        pl.semaphore_signal(barrier, inc=1, device_id=devices[name], device_id_type=MESH)

    for name in ("x", "c", "y"):
        greet(name)
    pl.when(z < 3)(lambda: greet("up"))
    pl.when(z > 0)(lambda: greet("down"))
    pl.semaphore_wait(barrier, 3 + (z + 2) // 3 + (5 - z) // 3)


def gather_body(items, *refs):
    ins = refs[:items]
    outs = [refs[items + 4 * item : items + 4 * item + 4] for item in range(items)]
    side_sem, z_sem, recv_sem, own_sem = refs[5 * items :]
    column = lax.axis_index("dp")
    z = column // 2
    devices = neighbours()
    meet(z, devices)
    shard = [item.shape[0] for item in ins]
    piece = [item // 2 for item in shard]

    def mirror(source):
        return source + 1 - 2 * (source % 2)

    def view(item, part, quarter, source):
        start = pl.multiple_of(source * shard[item] + part * piece[item], 8)
        return outs[item][quarter].at[pl.ds(start, piece[item])]

    def copy(item, part, quarter, source, to_quarter, name, send, own=False):
        here = view(item, part, quarter, source)
        if own:
            here = ins[item].at[pl.ds(part * piece[item], piece[item])]
        return pltpu.make_async_remote_copy(
            src_ref=here,
            dst_ref=view(item, part, to_quarter, source),
            send_sem=send,
            recv_sem=recv_sem.at[item, part, to_quarter, source],
            device_id=devices[name],
            device_id_type=MESH,
        )

    def arrived(item, part, quarter, source):
        copy(item, part, quarter, source, quarter, "x", side_sem.at[0, item]).wait_recv()

    def send_x(item, part, source, own=False):
        copy(item, part, 0, source, 2, "x", side_sem.at[0, item], own).start()

    def send_y(item, part, quarter, source, own=False):
        copy(item, part, quarter, source, quarter, "y", side_sem.at[1, item], own).start()

    def send_c(item, part, quarter, source, own=False):
        copy(item, part, quarter, source, quarter + 1, "c", side_sem.at[2 + quarter // 2, item], own).start()

    def send_z(item, part, source, turn, upward, own=False):
        name = "up" if upward else "down"
        copy(item, part, 0, source, 0, name, z_sem.at[item, part, 1 - upward, turn], own).start()

    def slot(turn, action):
        pl.when(z >= turn)(lambda: action(column - 2 * turn, 1))
        pl.when(z + turn <= 3)(lambda: action(column + 2 * turn, 0))

    every = [(item, part) for item in range(items) for part in range(2)]
    local = [
        pltpu.make_async_copy(
            ins[item],
            outs[item][0].at[pl.ds(pl.multiple_of(column * shard[item], 8), shard[item])],
            own_sem.at[item],
        )
        for item in range(items)
    ]
    for item, part in every:
        pl.when(z < 3)(lambda: send_z(item, part, column, 0, 1, True))
        pl.when(z > 0)(lambda: send_z(item, part, column, 0, 0, True))
        send_x(item, part, column, True)
        send_y(item, part, 0, column, True)
        send_c(item, part, 0, column, True)
    for copied in local:
        copied.start()

    def from_z(item, part, turn, source, upward):
        arrived(item, part, 0, source)
        if turn < 3:
            ahead = z < 3 if upward else z > 0
            pl.when(ahead)(lambda: send_z(item, part, source, turn, upward))
        send_x(item, part, source)
        send_y(item, part, 0, source)
        send_c(item, part, 0, source)

    def second(item, source):
        arrived(item, 0, 0, mirror(source))
        send_x(item, 0, mirror(source))
        send_c(item, 0, 0, mirror(source))
        arrived(item, 1, 2, source)
        send_y(item, 1, 2, source)
        send_c(item, 1, 2, source)

    def third(item, source):
        arrived(item, 0, 2, source)
        send_c(item, 0, 2, source)
        arrived(item, 1, 0, mirror(source))
        send_c(item, 1, 0, mirror(source))
        for part in range(2):
            arrived(item, part, 2, mirror(source))
            send_c(item, part, 2, mirror(source))

    for item in range(items):
        for turn in (1, 2, 3):
            for part in range(2):
                slot(turn, lambda source, upward: from_z(item, part, turn, source, upward))
    for item in range(items):
        second(item, column)
        for turn in (1, 2, 3):
            slot(turn, lambda source, upward: second(item, source))
    for item in range(items):
        third(item, column)
        for turn in (1, 2, 3):
            slot(turn, lambda source, upward: third(item, source))
    for item, part in every:
        for source in range(8):
            for quarter in (1, 3):
                arrived(item, part, quarter, source)
    for copied in local:
        copied.wait()
    for item in range(items):
        for way, count in enumerate((12, 12, 16, 16)):
            lead = outs[item][0].at[pl.ds(0, count * piece[item])]
            pltpu.make_async_remote_copy(
                src_ref=lead,
                dst_ref=lead,
                send_sem=side_sem.at[way, item],
                recv_sem=recv_sem.at[item, 0, 0, 0],
                device_id=devices["x"],
                device_id_type=MESH,
            ).wait_send()
    for item, part in every:
        for turn in range(3):
            pl.when((z < 3) & (z >= turn))(
                lambda: copy(item, part, 0, column, 0, "up", z_sem.at[item, part, 0, turn], True).wait_send()
            )
            pl.when((z > 0) & (z + turn <= 3))(
                lambda: copy(item, part, 0, column, 0, "down", z_sem.at[item, part, 1, turn], True).wait_send()
            )


def gather_kernel(shards):
    items = len(shards)
    anywhere = pl.BlockSpec(memory_space=pl.ANY)
    whole = lax.axis_size("dp")
    shapes = [
        jax.ShapeDtypeStruct((item.shape[0] * whole, item.shape[1]), item.dtype)
        for item in shards
        for _ in range(4)
    ]
    flat = pl.pallas_call(
        functools.partial(gather_body, items),
        name="gather_weights",
        out_shape=shapes,
        in_specs=[anywhere] * items,
        out_specs=[anywhere] * (4 * items),
        scratch_shapes=[
            pltpu.SemaphoreType.DMA((4, items)),
            pltpu.SemaphoreType.DMA((items, 2, 2, 3)),
            pltpu.SemaphoreType.DMA((items, 2, 4, 8)),
            pltpu.SemaphoreType.DMA((items,)),
        ],
        compiler_params=pltpu.CompilerParams(collective_id=0, has_side_effects=True),
    )(*shards)
    return [flat[4 * item : 4 * item + 4] for item in range(items)]


def reduce_body(layout, parts, gains_at, *refs):
    items, arrays = len(layout), sum([len(item) for item in layout])
    ins = [refs[4 * array : 4 * array + 4] for array in range(arrays)]
    facts = refs[4 * arrays]
    refs = refs[4 * arrays + 1 :]
    outs, totals = refs[:items], refs[items]
    refs = refs[items + 1 :]
    held = [refs[7 * item : 7 * item + 7] for item in range(items)]
    load_sem, side_sem, c_sem, x_sem, y_sem, zs_sem, zr_sem, whole_send, whole_recv = refs[7 * items : 7 * items + 9]
    tile, tile_row, tile_column, row_send, row_recv, column_send, column_recv = refs[7 * items + 9 :]
    column = lax.axis_index("dp")
    z, y = column // 2, column % 2
    devices = neighbours()
    shard = [item.shape[0] for item in outs]
    piece = [item // 2 for item in shard]

    loads = [[] for _ in range(items)]
    for item in range(items):
        for array, at, width in layout[item]:
            for side in range(2):
                load = pltpu.make_async_copy(
                    ins[array][2 * side],
                    held[item][0].at[side, :, pl.ds(at, width)],
                    load_sem.at[array, side],
                )
                load.start()
                loads[item].append(load)
    row = lax.axis_index("tensor")
    row_peers = [(column, (row + away) % 4) for away in (1, 2, 3)]
    column_peers = [((column + away) % 8, row) for away in range(1, 8)]
    barrier = pltpu.get_barrier_semaphore()
    for device in row_peers + column_peers:
        pl.semaphore_signal(barrier, inc=1, device_id=device, device_id_type=MESH)
    pl.semaphore_wait(barrier, 10)

    def span(item, part, source):
        return pl.ds(pl.multiple_of(source * shard[item] + part * piece[item], 8), piece[item])

    def remote(src, dst, send, recv, name):
        return pltpu.make_async_remote_copy(
            src_ref=src, dst_ref=dst, send_sem=send, recv_sem=recv, device_id=devices[name], device_id_type=MESH
        )

    def c_copy(item, part, side, source):
        array = layout[item][0][0]
        return remote(
            ins[array][2 * side + 1].at[span(item, part, source)],
            held[item][1].at[side, span(item, part, source)],
            side_sem.at[2 + side, item],
            c_sem.at[part, side, source],
            "c",
        )

    def c_whole(item):
        return [
            remote(
                ins[array][2 * side + 1],
                held[item][1].at[side, :, pl.ds(at, width)],
                whole_send.at[array, side],
                whole_recv.at[array, side],
                "c",
            )
            for array, at, width in layout[item]
            for side in range(2)
        ]

    def c_wait(item, part, side, source):
        if item == 0:
            c_copy(item, part, side, source).wait_recv()

    def x_copy(item, part, source):
        place = source if part == 0 else source // 2
        return remote(
            held[item][0].at[1, span(item, part, source)],
            held[item][2 + part].at[place],
            side_sem.at[0, item],
            x_sem.at[item, part, place],
            "x",
        )

    def y_copy(item, part, side, source):
        return remote(
            held[item][0].at[side, span(item, part, source)],
            held[item][4].at[source // 2] if part == 0 else held[item][5].at[side, source // 2],
            side_sem.at[1, item],
            y_sem.at[item, part + side, source // 2],
            "y",
        )

    def z_copy(item, part, source, away, upward):
        return remote(
            held[item][0].at[0, span(item, part, source)],
            held[item][6].at[1 - upward, part, away],
            zs_sem.at[item, part, 1 - upward, away],
            zr_sem.at[item, part, 1 - upward, away],
            "up" if upward else "down",
        )

    def add(item, side, part, source, *others):
        total = held[item][0]
        start = source * shard[item] + part * piece[item]
        step = 16

        def one(turn, _):
            here = pl.ds(pl.multiple_of(start + turn * step, 8), step)
            value = total[side, here].astype(jnp.float32)
            for other in others:
                value = value + other(turn * step, step)
            total[side, here] = value.astype(jnp.bfloat16)
            return 0

        lax.fori_loop(0, piece[item] // step, one, 0)

    def c_part(item, side, part, source):
        start = source * shard[item] + part * piece[item]
        return lambda at, step: held[item][1][side, pl.ds(pl.multiple_of(start + at, 8), step)].astype(jnp.float32)

    def of(ref, *place):
        return lambda at, step: ref[(*place, pl.ds(pl.multiple_of(at, 8), step))].astype(jnp.float32)

    def mirror(source):
        return source + 1 - 2 * (source % 2)

    def target(turn):
        low = 3 - turn if turn < 2 else jnp.where(z % 3 == 0, 3 - turn, turn - 2)
        return column + 2 * (jnp.where(z < 2, low, 3 - low) - z)

    def send_c(item, turn):
        source = target(turn)
        for part, side, place in (
            (0, 1, source),
            (1, 1, mirror(source)),
            (0, 1, mirror(source)),
            (1, 0, mirror(source)),
            (0, 0, mirror(source)),
            (1, 1, source),
            (0, 0, source),
            (1, 0, source),
        ):
            c_copy(item, part, side, place).start()

    def first(item, turn):
        source = target(turn)
        for x_place, y_side in ((source, 1), (mirror(source), 0)):
            c_wait(item, 0, 1, x_place)
            add(item, 1, 0, x_place, c_part(item, 1, 0, x_place))
            x_copy(item, 0, x_place).start()
            y_place = mirror(source)
            c_wait(item, 1, y_side, y_place)
            add(item, y_side, 1, y_place, c_part(item, y_side, 1, y_place))
            y_copy(item, 1, y_side, y_place).start()

    def second(item, turn):
        source = target(turn)
        place = mirror(source)
        c_wait(item, 0, 0, place)
        x_copy(item, 0, place).wait_recv()
        add(item, 0, 0, place, c_part(item, 0, 0, place), of(held[item][2], place))
        y_copy(item, 0, 0, place).start()
        c_wait(item, 1, 1, source)
        y_copy(item, 1, 1, source).wait_recv()
        add(item, 1, 1, source, c_part(item, 1, 1, source), of(held[item][5], 1, source // 2))
        x_copy(item, 1, source).start()

    def third(item, turn):
        source = target(turn)
        for part in range(2):
            c_wait(item, part, 0, source)
            x_copy(item, part, source).wait_recv()
            y_copy(item, part, 0, source).wait_recv()
            if part == 0:
                terms = [of(held[item][2], source), of(held[item][4], source // 2)]
            else:
                terms = [of(held[item][3], source // 2), of(held[item][5], 0, source // 2)]
            add(item, 0, part, source, c_part(item, 0, part, source), *terms)

    def fourth(item, turn):
        source = target(turn)
        away = jnp.where(source > column, source - column, column - source) // 2

        def along(upward):
            for part in range(2):

                def more():
                    z_copy(item, part, source, away, upward).wait_recv()
                    add(item, 0, part, source, of(held[item][6], 1 - upward, part, away))

                pl.when(z > 0 if upward else z < 3)(more)
                z_copy(item, part, source, away - 1, upward).start()

        pl.when(source > column)(lambda: along(1))
        pl.when(source < column)(lambda: along(0))

    def last(item):
        square = jnp.zeros((), jnp.float32)
        for part in range(2):
            for upward in (1, 0):
                pl.when(z > 0 if upward else z < 3)(
                    lambda: z_copy(item, part, column, 0, upward).wait_recv()
                )
            start = column * shard[item] + part * piece[item]

            def one(turn, square):
                at = pl.multiple_of(turn * 16, 8)
                value = held[item][0][0, pl.ds(pl.multiple_of(start + at, 8), 16)].astype(jnp.float32)
                below = held[item][6][0, part, 0, pl.ds(at, 16)].astype(jnp.float32)
                above = held[item][6][1, part, 0, pl.ds(at, 16)].astype(jnp.float32)
                value = value + jnp.where(z > 0, below, 0.0) + jnp.where(z < 3, above, 0.0)
                outs[item][pl.ds(pl.multiple_of(part * piece[item] + at, 8), 16)] = value
                square_here = value * value
                if item == gains_at[0]:
                    lane = lax.broadcasted_iota(jnp.int32, value.shape, 1)
                    repeated = (lane >= gains_at[1]) & (lane < gains_at[1] + gains_at[2])
                    square_here = jnp.where(repeated, square_here / parts, square_here)
                return square + jnp.sum(square_here)

            square = lax.fori_loop(0, piece[item] // 16, one, square)
        return square

    steps = [(item, turn) for item in range(items) for turn in range(4)]
    count = len(steps)
    for turn in range(3):
        send_c(*steps[turn])
    for turn in range(count + 3):
        if turn == 0:
            send_c(*steps[3])
        if turn % 4 == 0 and turn + 4 < count:
            for crossing in c_whole(turn // 4 + 1):
                crossing.start()
        if turn < count:
            if turn % 4 == 0:
                for load in loads[turn // 4]:
                    load.wait()
                if turn > 0:
                    for crossing in c_whole(turn // 4):
                        crossing.wait_recv()
            first(*steps[turn])
        if 0 <= turn - 1 < count:
            second(*steps[turn - 1])
        if 0 <= turn - 2 < count:
            third(*steps[turn - 2])
        if 0 <= turn - 3 < count and (turn - 3) % 4 < 3:
            fourth(*steps[turn - 3])
    square = sum([last(item) for item in range(items)])
    sublane = lax.broadcasted_iota(jnp.int32, (8, 128), 0)
    tile[...] = jnp.where(sublane == 0, square, facts[...])

    def exchange(value, slots, here, peers, sources, send, recv):
        slots[here] = value

        def crossing(place, device, source):
            return pltpu.make_async_remote_copy(
                src_ref=slots.at[here],
                dst_ref=slots.at[source],
                send_sem=send.at[place],
                recv_sem=recv.at[source],
                device_id=device,
                device_id_type=MESH,
            )

        for place, device in enumerate(peers):
            crossing(place, device, here).start()
        for place, device in enumerate(peers):
            crossing(place, device, sources[place]).wait_recv()
        total = slots[0]
        for place in range(1, len(peers) + 1):
            total = total + slots[place]
        for place, device in enumerate(peers):
            crossing(place, device, here).wait_send()
        return total

    along_row = exchange(
        tile[...], tile_row, row, row_peers, [(row + away) % 4 for away in (1, 2, 3)], row_send, row_recv
    )
    totals[...] = exchange(
        along_row,
        tile_column,
        column,
        column_peers,
        [(column + away) % 8 for away in range(1, 8)],
        column_send,
        column_recv,
    )
    for item in range(items):
        if item > 0:
            for crossing in c_whole(item):
                crossing.wait_send()
        for way, count in enumerate((12, 12, 16, 16) if item == 0 else (12, 12)):
            lead = held[item][0].at[0, pl.ds(0, count * piece[item])]
            remote(lead, lead, side_sem.at[way, item], load_sem.at[item, 0], "x").wait_send()
        for part in range(2):
            for away in range(3):
                pl.when((z < 3) & (z + away + 1 <= 3))(
                    lambda: z_copy(item, part, column, away, 1).wait_send()
                )
                pl.when((z > 0) & (z - away - 1 >= 0))(
                    lambda: z_copy(item, part, column, away, 0).wait_send()
                )


def reduce_kernel(layout, grads, facts, parts, gains_at, tag):
    items, arrays = len(layout), len(grads)
    anywhere = pl.BlockSpec(memory_space=pl.ANY)
    inside = pl.BlockSpec(memory_space=pltpu.VMEM)
    whole = lax.axis_size("dp")
    rows = grads[0][0].shape[0]
    half = rows // (2 * whole)
    shapes, scratch = [], []
    for item in layout:
        width = sum([part[2] for part in item])
        shapes.append(jax.ShapeDtypeStruct((rows // whole, width), jnp.float32))
        for lead in ((2, rows), (2, rows), (8, half), (4, half), (4, half), (2, 4, half), (2, 2, 3, half)):
            scratch.append(pltpu.VMEM((*lead, width), jnp.bfloat16))
    shapes.append(jax.ShapeDtypeStruct((8, 128), jnp.float32))
    found = pl.pallas_call(
        functools.partial(reduce_body, layout, parts, gains_at),
        name="reduce_grads",
        out_shape=shapes,
        in_specs=[anywhere] * (4 * arrays) + [inside],
        out_specs=[inside] * (items + 1),
        scratch_shapes=scratch
        + [
            pltpu.SemaphoreType.DMA((arrays, 2)),
            pltpu.SemaphoreType.DMA((4, items)),
            pltpu.SemaphoreType.DMA((2, 2, 8)),
            pltpu.SemaphoreType.DMA((items, 2, 8)),
            pltpu.SemaphoreType.DMA((items, 3, 4)),
            pltpu.SemaphoreType.DMA((items, 2, 2, 3)),
            pltpu.SemaphoreType.DMA((items, 2, 2, 3)),
            pltpu.SemaphoreType.DMA((arrays, 2)),
            pltpu.SemaphoreType.DMA((arrays, 2)),
            pltpu.VMEM((8, 128), jnp.float32),
            pltpu.VMEM((4, 8, 128), jnp.float32),
            pltpu.VMEM((8, 8, 128), jnp.float32),
            pltpu.SemaphoreType.DMA((3,)),
            pltpu.SemaphoreType.DMA((4,)),
            pltpu.SemaphoreType.DMA((7,)),
            pltpu.SemaphoreType.DMA((8,)),
        ],
        compiler_params=pltpu.CompilerParams(
            collective_id=tag, has_side_effects=True, vmem_limit_bytes=60 << 20
        ),
    )(*[item for quarters in grads for item in quarters], facts)
    return found[:-1], found[-1]


def update_body(sources, plans, *refs):
    count = len(plans)
    totals, fixes, grads = refs[0], refs[1], refs[2 : 2 + sources]
    refs = refs[2 + sources :]
    triples = [refs[3 * place : 3 * place + 3] for place in range(count)]
    outs = [refs[3 * (count + place) : 3 * (count + place) + 3] for place in range(count)]
    square, loss, real = totals[0:1, :], totals[1:2, :], totals[2:3, :]
    norm = jnp.sqrt(square) / real
    refs[6 * count][...] = jnp.concatenate([loss / real, norm] + [norm] * 6, axis=0)
    scale = (jnp.minimum(1.0, clip_at / norm) / real)[:, 0:1]
    over_one, over_two = fixes[0:1, 0:1], fixes[1:2, 0:1]

    def renew(place, grad, rows):
        source, turned, first, rate, decay = plans[place]
        weight, one, two = triples[place]
        clipped = grad * scale
        moment_one = beta_one * one[rows] + (1.0 - beta_one) * clipped
        moment_two = beta_two * two[rows] + (1.0 - beta_two) * clipped * clipped
        stepped = moment_one * over_one / (jnp.sqrt(moment_two * over_two) + adam_eps)
        outs[place][0][rows] = moment_one
        outs[place][1][rows] = moment_two
        outs[place][2][rows] = weight[rows] - rate * (stepped + decay * weight[rows])

    for place in range(count):
        source, turned, first, rate, decay = plans[place]
        rows, columns = triples[place][0].shape
        if turned and rows >= 128:
            for at in range(0, rows, 128):
                span = min(128, rows - at)
                block = grads[source][:, first + at : first + at + span].T
                renew(place, block, pl.ds(at, span))
        elif turned:
            start = first // 128 * 128
            block = grads[source][:, start : start + 128].T
            renew(place, block[first - start : first - start + rows], pl.ds(0, rows))
        else:
            for at in range(0, rows, 32):
                renew(place, grads[source][pl.ds(at, 32), first : first + columns], pl.ds(at, 32))


def update_kernel(totals, fixes, grads, plans, triples):
    inside = pl.BlockSpec(memory_space=pltpu.VMEM)
    flat = [item for triple in triples for item in triple]
    outs = [jax.ShapeDtypeStruct(item.shape, item.dtype) for item in flat] + [
        jax.ShapeDtypeStruct((8, 128), jnp.float32)
    ]
    found = pl.pallas_call(
        functools.partial(update_body, len(grads), plans),
        name="update_weights",
        out_shape=outs,
        in_specs=[inside] * (2 + len(grads) + len(flat)),
        out_specs=[inside] * len(outs),
        compiler_params=pltpu.CompilerParams(vmem_limit_bytes=60 << 20),
    )(totals, fixes, *grads, *flat)
    return found[:-1], found[-1]


def known_mesh():
    return lax.axis_size("dp") == 8 and lax.axis_size("tensor") == 4


def gather_weights(shards):
    if not known_mesh():
        return [gather_all(item, True) for item in shards]
    return [[item[0], item[2], item[1], item[3]] for item in gather_kernel(shards)]


def reduce_grads(layout, grads, facts, parts, gains_at):
    if known_mesh():
        ordered = [[item[0], item[2], item[1], item[3]] for item in grads]
        return reduce_kernel(layout, ordered, facts, parts, gains_at, 1)
    sums = [reduce_all(item, True) for item in grads]
    sums = [jnp.concatenate([sums[part[0]] for part in item], axis=1) for item in layout]
    square = sum(jnp.sum(item * item) for item in sums)
    repeated = sums[gains_at[0]][:, gains_at[1] : gains_at[1] + gains_at[2]]
    square = square - jnp.sum(repeated * repeated) * (1.0 - 1.0 / parts)
    tile = jnp.where(lax.broadcasted_iota(jnp.int32, (8, 128), 0) == 0, square, facts)
    return sums, everyone_sum(tile)


def wide(value):
    return value.astype(jnp.float32)


def narrow(value):
    return value.astype(jnp.bfloat16)


def fold(value, masks, last):
    rows = value.shape[0] // (len(masks) + 1)
    total = wide(value[:rows])
    for place, mask in enumerate(masks):
        total = total + wide(swap(value[(place + 1) * rows : (place + 2) * rows], "dp", mask))
    return total if last else narrow(total)


def reduce_all(quarters, x_first):
    groups = groups_of(lax.axis_size("dp"))
    own = narrow(wide(quarters[0]) + wide(swap(quarters[2], "tensor", 1)))
    other = narrow(wide(quarters[1]) + wide(swap(quarters[3], "tensor", 1)))
    if x_first:
        own = narrow(wide(own) + wide(swap(other, "tensor", 2)))
        own = fold(own, groups[0], len(groups) == 1)
    else:
        own = fold(own, groups[0], False)
        other = fold(other, groups[0], False)
        own = narrow(wide(own) + wide(swap(other, "tensor", 2)))
    for place in range(1, len(groups)):
        own = fold(own, groups[place], place == len(groups) - 1)
    return wide(own)


def everyone_sum(value):
    for masks in groups_of(lax.axis_size("dp")):
        value = sum([swap(value, "dp", mask) for mask in masks], value)
    for mask in (1, 2):
        value = value + swap(value, "tensor", mask)
    return value


def mm(left, right):
    return jnp.dot(left, right, preferred_element_type=jnp.float32)


def mm_nt(left, right):
    return lax.dot_general(left, right, (((1,), (1,)), ((), ())), preferred_element_type=jnp.float32)


def mm_tn(left, right):
    return lax.dot_general(left, right, (((0,), (0,)), ((), ())), preferred_element_type=jnp.float32)


def rotate_heads(values, cosine, sine):
    return rotate(values, cosine[:, None, :], sine[:, None, :])


def scores_of(query, key_rows, same_doc):
    scores = jnp.einsum(
        "qhe,khe->hqk", query, key_rows, preferred_element_type=jnp.float32
    ) * HEAD_DIM ** (-0.5)
    return jnp.where(same_doc[None], scores, neg_fill)


def split_heads(packed):
    packed = packed.reshape(packed.shape[0], -1, 3, HEAD_DIM)
    return packed[:, :, 0], packed[:, :, 1], packed[:, :, 2]


def attend(packed, same_doc):
    query, key_rows, value_rows = split_heads(packed)
    scores = scores_of(query, key_rows, same_doc)
    row_max = jnp.max(scores, axis=-1, keepdims=True)
    expd = jnp.exp(scores - row_max)
    summed = jnp.sum(expd, axis=-1, keepdims=True)
    probs = (expd / summed).astype(jnp.bfloat16)
    output = jnp.einsum("hqk,khe->qhe", probs, value_rows, preferred_element_type=jnp.float32)
    return (narrow(output).reshape(packed.shape[0], -1), (row_max + jnp.log(summed))[..., 0])


def attend_back(packed, same_doc, row_lse, grad_out, cosine, sine):
    query, key_rows, value_rows = split_heads(packed)
    grad_out = grad_out.reshape(packed.shape[0], -1, HEAD_DIM)
    scores = scores_of(query, key_rows, same_doc)
    probs = jnp.exp(scores - row_lse[..., None])
    value_grad = jnp.einsum(
        "hqk,qhe->khe", probs.astype(jnp.bfloat16), grad_out, preferred_element_type=jnp.float32
    )
    prob_grad = jnp.einsum("qhe,khe->hqk", grad_out, value_rows, preferred_element_type=jnp.float32)
    inner = jnp.sum(prob_grad * probs, axis=-1, keepdims=True)
    score_grad = (probs * (prob_grad - inner)).astype(jnp.bfloat16)
    query_grad = jnp.einsum(
        "hqk,khe->qhe", score_grad, key_rows, preferred_element_type=jnp.float32
    ) * HEAD_DIM ** (-0.5)
    key_grad = jnp.einsum(
        "hqk,qhe->khe", score_grad, query, preferred_element_type=jnp.float32
    ) * HEAD_DIM ** (-0.5)
    query_grad = rotate_heads(query_grad, cosine, -sine)
    key_grad = rotate_heads(key_grad, cosine, -sine)
    return narrow(jnp.stack([query_grad, key_grad, value_grad], axis=2).reshape(packed.shape))


def update_weights(totals, fixes, sums, plans, triples):
    if known_mesh():
        updated, results = update_kernel(totals, fixes, sums, plans, triples)
        return list(updated), results
    updated = []
    norm = jnp.sqrt(totals[0, 0]) / totals[2, 0]
    scale = jnp.minimum(1.0, clip_at / norm) / totals[2, 0]
    for (source, turned, first, rate, decay), (weight, one, two) in zip(plans, triples):
        columns = weight.shape[0] if turned else weight.shape[1]
        grad = sums[source][:, first : first + columns]
        clipped = (grad.T if turned else grad) * scale
        moment_one = beta_one * one + (1.0 - beta_one) * clipped
        moment_two = beta_two * two + (1.0 - beta_two) * clipped * clipped
        stepped = moment_one * fixes[0, 0] / (jnp.sqrt(moment_two * fixes[1, 0]) + adam_eps)
        updated.extend([moment_one, moment_two, weight - rate * (stepped + decay * weight)])
    return updated, jnp.stack([totals[1, 0] / totals[2, 0], norm])[:, None]


def per_device(
    tokens,
    lengths,
    timesteps,
    masks,
    step_count,
    table,
    joint_weight,
    output_weight,
    upward_weight,
    downward_weight,
    gains,
    momentum_table,
    momentum_joint,
    momentum_output,
    momentum_upward,
    momentum_downward,
    momentum_gains,
    variance_table,
    variance_joint,
    variance_output,
    variance_upward,
    variance_downward,
    variance_gains,
):
    place = lax.axis_index("tensor")
    parts = lax.axis_size("tensor")
    rows = tokens.shape[0] // parts
    vocab_part, head_part = table.shape[0], joint_weight.shape[1]
    out_part, ff_part = output_weight.shape[0], upward_weight.shape[1]

    gain_columns = jnp.pad(narrow(gains).T, ((0, 0), (0, 61)))
    shards = [
        narrow(table).T,
        jnp.concatenate([narrow(joint_weight), gain_columns], axis=1),
        narrow(upward_weight),
        narrow(downward_weight).T,
        narrow(output_weight).T,
    ]
    table_q, first_group, up_q, down_q, out_q = gather_weights(shards)
    joint_q = [item[:, :head_part] for item in first_group]
    gain_full = wide(first_group[0][:, head_part : head_part + 3]).T
    out_all = jnp.concatenate(out_q, axis=1)

    start = place * rows
    seq = start // SEQ_LEN
    mine = start - seq * SEQ_LEN
    cut = lambda array: lax.dynamic_slice(array, (start,), (rows,))
    targets = cut(tokens)
    corrupt = cut(masks) == 1
    inputs = jnp.where(corrupt, VOCAB - 1, targets)
    own_lengths = lax.dynamic_slice(lengths, (seq, 0), (1, DOCS))
    step_here = lax.dynamic_slice(timesteps, (seq,), (1,))
    theirs = mine ^ rows
    position = jnp.concatenate(
        [mine + jnp.arange(rows, dtype=jnp.int32), theirs + jnp.arange(rows, dtype=jnp.int32)]
    )
    doc_ends = jnp.cumsum(own_lengths[0])
    doc_starts = doc_ends - own_lengths[0]
    segment = jnp.sum((position[:, None] >= doc_ends[None, :]).astype(jnp.int32), axis=1)
    chosen = segment[:, None] == jnp.arange(DOCS, dtype=jnp.int32)[None, :]
    offset = position - jnp.sum(jnp.where(chosen, doc_starts[None, :], 0), axis=1)
    is_real = segment < DOCS - 1
    factor = jnp.where(step_here == 1, 1.0, T_DIFF / step_here.astype(jnp.float32))
    weights = jnp.where(corrupt & is_real[:rows], factor, 0.0)
    inverse_freq = 10000.0 ** (-jnp.arange(HEAD_DIM // 2, dtype=jnp.float32) / (HEAD_DIM // 2))
    angles = offset.astype(jnp.float32)[:, None] * inverse_freq
    cosine, sine = jnp.cos(angles), jnp.sin(angles)
    same_doc = segment[:, None] == segment[None, :]

    def hot(ids, piece):
        base = (place ^ (2 * (piece % 2) + piece // 2)) * vocab_part
        return (ids - base)[:, None] == jnp.arange(vocab_part, dtype=jnp.int32)[None, :]

    pieces = range(len(table_q))
    input_hot = [narrow(hot(inputs, piece)) for piece in pieces]
    looked = sum(mm_nt(input_hot[piece], table_q[piece]) for piece in pieces)
    embedded = looked * D**0.5
    normed_one = narrow(norm_apply(embedded, gain_full[0]))

    def turned(projected):
        projected = projected.reshape(rows, -1, 3, HEAD_DIM)
        query = rotate_heads(projected[:, :, 0], cosine[:rows], sine[:rows])
        key_rows = rotate_heads(projected[:, :, 1], cosine[:rows], sine[:rows])
        stacked = jnp.stack([query, key_rows, projected[:, :, 2]], axis=2)
        return narrow(stacked.reshape(rows, -1))

    packed = [turned(mm(normed_one, item)) for item in joint_q]
    whole = [
        jnp.concatenate([packed[side], swap(packed[2 + side], "tensor", 1)], axis=0)
        for side in range(2)
    ]
    attended, attn_lse = zip(*[attend(item, same_doc) for item in whole])
    attended_all = jnp.concatenate(
        [item[:rows] for item in attended]
        + [swap(item[rows:], "tensor", 1) for item in attended],
        axis=1,
    )
    after_attn = embedded + mm_nt(attended_all, out_all)
    normed_two = narrow(norm_apply(after_attn, gain_full[1]))
    pre_gelu = [mm(normed_two, item) for item in up_q]
    below = [0.5 + 0.5 * lax.erf(item * 0.5**0.5) for item in pre_gelu]
    slopes = [
        part + item * jnp.exp(-0.5 * item * item) * (0.5 / jnp.pi) ** 0.5
        for part, item in zip(below, pre_gelu)
    ]
    activated = [narrow(item * part) for part, item in zip(below, pre_gelu)]
    after_mlp = after_attn + sum(mm_nt(activated[q], down_q[q]) for q in range(4))
    normed_out = narrow(norm_apply(after_mlp, gain_full[2]))
    logits = [mm(normed_out, item) for item in table_q]
    row_max = logits[0].max(axis=1)
    for item in logits[1:]:
        row_max = jnp.maximum(row_max, item.max(axis=1))
    row_sum = sum(jnp.sum(jnp.exp(item - row_max[:, None]), axis=1) for item in logits)
    target_hot = [hot(targets, piece) for piece in pieces]
    row_pick = sum(
        jnp.sum(jnp.where(target_hot[piece], logits[piece], 0.0), axis=1) for piece in pieces
    )
    row_lse = row_max + jnp.log(row_sum)
    loss_local = jnp.sum(weights * (row_lse - row_pick))
    count_local = jnp.sum(is_real[:rows].astype(jnp.float32))

    logit_grad = [
        narrow(
            weights[:, None]
            * (jnp.exp(logits[piece] - row_lse[:, None]) - target_hot[piece].astype(jnp.float32))
        )
        for piece in pieces
    ]
    out_grad = sum(mm_nt(logit_grad[piece], table_q[piece]) for piece in pieces)
    mlp_grad, gain_three = norm_back(after_mlp, gain_full[2], out_grad)
    mlp_branch = narrow(mlp_grad)
    down_grad = [narrow(mm_tn(mlp_branch, item)) for item in activated]
    up_input = [
        narrow(slopes[q] * mm(mlp_branch, down_q[q])) for q in range(4)
    ]
    up_grad = [narrow(mm_tn(normed_two, item)) for item in up_input]
    normed_two_grad = sum(mm_nt(up_input[q], up_q[q]) for q in range(4))
    attn_in_grad, gain_two = norm_back(after_attn, gain_full[1], normed_two_grad)
    resid_one = mlp_grad + attn_in_grad
    attn_branch = narrow(resid_one)
    out_grads = narrow(mm_tn(attn_branch, attended_all))
    out_grad_q = [out_grads[:, q * out_part : (q + 1) * out_part] for q in range(4)]
    attended_grad = narrow(mm(attn_branch, out_all))
    grad_parts = [attended_grad[:, q * out_part : (q + 1) * out_part] for q in range(4)]
    proj_whole = [
        attend_back(
            whole[side],
            same_doc,
            attn_lse[side],
            jnp.concatenate(
                [grad_parts[side], swap(grad_parts[2 + side], "tensor", 1)], axis=0
            ),
            cosine,
            sine,
        )
        for side in range(2)
    ]
    proj_grad = [item[:rows] for item in proj_whole] + [
        swap(item[rows:], "tensor", 1) for item in proj_whole
    ]
    normed_one_grad = sum(mm_nt(proj_grad[q], joint_q[q]) for q in range(4))
    embed_in, gain_one = norm_back(embedded, gain_full[0], normed_one_grad)
    embed_grad = resid_one + embed_in
    gain_grad = jnp.pad(narrow(jnp.stack([gain_one, gain_two, gain_three])).T, ((0, 0), (0, 61)))
    joint_grad = [
        jnp.concatenate([narrow(mm_tn(normed_one, item)), gain_grad], axis=1) for item in proj_grad
    ]
    embed_scaled = narrow(embed_grad * D**0.5)
    table_grad = [
        narrow(mm_tn(normed_out, logit_grad[piece]) + mm_tn(embed_scaled, input_hot[piece]))
        for piece in pieces
    ]
    sublane = lax.broadcasted_iota(jnp.int32, (8, 128), 0)
    facts = jnp.where(sublane == 1, loss_local, jnp.where(sublane == 2, count_local, 0.0))
    joint_part = joint_grad[0].shape[1]
    layout = (
        ((0, 0, vocab_part),),
        ((2, 0, ff_part), (3, ff_part, ff_part)),
        ((1, 0, joint_part), (4, joint_part, out_part)),
    )
    sums, totals = reduce_grads(
        layout,
        [table_grad, joint_grad, up_grad, down_grad, out_grad_q],
        facts,
        parts,
        (2, head_part, joint_part - head_part),
    )
    step_float = step_count[0].astype(jnp.float32)
    fixes = jnp.where(
        sublane == 0,
        1.0 / (1.0 - jnp.power(beta_one, step_float)),
        1.0 / (1.0 - jnp.power(beta_two, step_float)),
    )
    plans = (
        (0, False, 0, rates[0], decays[0]),
        (2, False, 0, rates[1], decays[1]),
        (2, True, joint_part, rates[2], decays[2]),
        (1, False, 0, rates[3], decays[3]),
        (1, False, ff_part, rates[4], decays[4]),
        (2, True, head_part, rates[5], decays[5]),
    )
    triples = (
        (table.T, momentum_table.T, variance_table.T),
        (joint_weight, momentum_joint, variance_joint),
        (output_weight, momentum_output, variance_output),
        (upward_weight, momentum_upward, variance_upward),
        (downward_weight.T, momentum_downward.T, variance_downward.T),
        (gains, momentum_gains, variance_gains),
    )
    updated, results = update_weights(totals, fixes, sums, plans, triples)
    updated = [item.T if place // 3 in (0, 4) else item for place, item in enumerate(updated)]
    return tuple([results[0, 0], results[1, 0]] + updated)


def solution(mesh):
    placed = (
        P("dp"),
        P("dp", None),
        P("dp"),
        P("dp"),
        P(),
        P("tensor", "dp"),
        P("dp", "tensor"),
        P("tensor", "dp"),
        P("dp", "tensor"),
        P("tensor", "dp"),
        P(None, "dp"),
        P("tensor", "dp"),
        P("dp", "tensor"),
        P("tensor", "dp"),
        P("dp", "tensor"),
        P("tensor", "dp"),
        P(None, "dp"),
        P("tensor", "dp"),
        P("dp", "tensor"),
        P("tensor", "dp"),
        P("dp", "tensor"),
        P("tensor", "dp"),
        P(None, "dp"),
    )
    return jax.shard_map(
        per_device,
        mesh=mesh,
        in_specs=placed,
        out_specs=(
            P(),
            P(),
            P("tensor", "dp"),
            P("tensor", "dp"),
            P("tensor", "dp"),
            P("dp", "tensor"),
            P("dp", "tensor"),
            P("dp", "tensor"),
            P("tensor", "dp"),
            P("tensor", "dp"),
            P("tensor", "dp"),
            P("dp", "tensor"),
            P("dp", "tensor"),
            P("dp", "tensor"),
            P("tensor", "dp"),
            P("tensor", "dp"),
            P("tensor", "dp"),
            P(None, "dp"),
            P(None, "dp"),
            P(None, "dp"),
        ),
        check_vma=False,
    )
```

```python
import functools

import jax
import jax.numpy as jnp
from jax import lax
from jax.experimental import pallas as pl
from jax.experimental.pallas import tpu as pltpu
from jax.sharding import PartitionSpec as P

D = 768
HEAD_DIM = 64
VOCAB = 8192
SEQ_LEN = 1024
DOCS = 4
T_DIFF = 1000


eps_norm = 1e-06
neg_fill = -1000000000.0
beta_one = 0.9
beta_two = 0.999
adam_eps = 1e-08
clip_at = 0.02
rates = (0.05, 0.03, 0.25, 0.03, 0.03, 0.3)
decays = (0.1, 0.1, 0.1, 0.1, 0.1, 0.0)


def norm_apply(values, gain):
    inverse = lax.rsqrt(jnp.mean(values * values, axis=-1, keepdims=True) + eps_norm)
    return values * inverse * gain


def norm_back(values, gain, upstream):
    inverse = lax.rsqrt(jnp.mean(values * values, axis=-1, keepdims=True) + eps_norm)
    gain_grad = jnp.sum(upstream * values * inverse, axis=0)
    scaled = upstream * gain
    inner = jnp.mean(scaled * values, axis=-1, keepdims=True)
    return (inverse * (scaled - values * inverse * inverse * inner), gain_grad)


def rotate(values, cosine, sine):
    middle = values.shape[-1] // 2
    front_part = values[..., :middle]
    back_part = values[..., middle:]
    return jnp.concatenate(
        [front_part * cosine - back_part * sine, back_part * cosine + front_part * sine], axis=-1
    )


def groups_of(count):
    groups, bit, width = [], 1, 1
    while bit < count:
        masks = [bit]
        if width == 2 and bit * 2 < count:
            masks = [bit, 2 * bit, 3 * bit]
            bit = bit * 2
        groups.append(masks)
        bit, width = bit * 2, 2
    return groups


def swap(value, axis, mask):
    size = lax.axis_size(axis)
    return lax.ppermute(value, axis, [(place, place ^ mask) for place in range(size)])


def spread(value, masks):
    return jnp.concatenate([value] + [swap(value, "dp", mask) for mask in masks], axis=0)


def gather_all(value, x_last):
    groups = groups_of(lax.axis_size("dp"))
    for masks in groups[:0:-1]:
        value = spread(value, masks)
    if x_last:
        value = spread(value, groups[0])
        other = swap(value, "tensor", 2)
    else:
        other = swap(value, "tensor", 2)
        value = spread(value, groups[0])
        other = spread(other, groups[0])
    return [value, other, swap(value, "tensor", 1), swap(other, "tensor", 1)]


MESH = pl.DeviceIdType.MESH


def neighbours():
    column, row = lax.axis_index("dp"), lax.axis_index("tensor")
    return {
        "x": (column, (row + 2) % 4),
        "c": (column, row + 1 - 2 * (row % 2)),
        "y": (column + 1 - 2 * (column % 2), row),
        "up": (column + 2, row),
        "down": (column - 2, row),
    }


def meet(z, devices):
    barrier = pltpu.get_barrier_semaphore()

    def greet(name):
        pl.semaphore_signal(barrier, inc=1, device_id=devices[name], device_id_type=MESH)

    for name in ("x", "c", "y"):
        greet(name)
    pl.when(z < 3)(lambda: greet("up"))
    pl.when(z > 0)(lambda: greet("down"))
    pl.semaphore_wait(barrier, 3 + (z + 2) // 3 + (5 - z) // 3)


def gather_body(items, *refs):
    ins = refs[:items]
    outs = [refs[items + 4 * item : items + 4 * item + 4] for item in range(items)]
    side_sem, z_sem, recv_sem, own_sem = refs[5 * items :]
    column = lax.axis_index("dp")
    z = column // 2
    devices = neighbours()
    meet(z, devices)
    shard = [item.shape[0] for item in ins]
    piece = [item // 2 for item in shard]

    def mirror(source):
        return source + 1 - 2 * (source % 2)

    def view(item, part, quarter, source):
        start = pl.multiple_of(source * shard[item] + part * piece[item], 8)
        return outs[item][quarter].at[pl.ds(start, piece[item])]

    def copy(item, part, quarter, source, to_quarter, name, send, own=False):
        here = view(item, part, quarter, source)
        if own:
            here = ins[item].at[pl.ds(part * piece[item], piece[item])]
        return pltpu.make_async_remote_copy(
            src_ref=here,
            dst_ref=view(item, part, to_quarter, source),
            send_sem=send,
            recv_sem=recv_sem.at[item, part, to_quarter, source],
            device_id=devices[name],
            device_id_type=MESH,
        )

    def arrived(item, part, quarter, source):
        copy(item, part, quarter, source, quarter, "x", side_sem.at[0, item]).wait_recv()

    def send_x(item, part, source, own=False):
        copy(item, part, 0, source, 2, "x", side_sem.at[0, item], own).start()

    def send_y(item, part, quarter, source, own=False):
        copy(item, part, quarter, source, quarter, "y", side_sem.at[1, item], own).start()

    def send_c(item, part, quarter, source, own=False):
        copy(item, part, quarter, source, quarter + 1, "c", side_sem.at[2 + quarter // 2, item], own).start()

    def send_z(item, part, source, turn, upward, own=False):
        name = "up" if upward else "down"
        copy(item, part, 0, source, 0, name, z_sem.at[item, part, 1 - upward, turn], own).start()

    def slot(turn, action):
        pl.when(z >= turn)(lambda: action(column - 2 * turn, 1))
        pl.when(z + turn <= 3)(lambda: action(column + 2 * turn, 0))

    every = [(item, part) for item in range(items) for part in range(2)]
    local = [
        pltpu.make_async_copy(
            ins[item],
            outs[item][0].at[pl.ds(pl.multiple_of(column * shard[item], 8), shard[item])],
            own_sem.at[item],
        )
        for item in range(items)
    ]
    for item, part in every:
        pl.when(z < 3)(lambda: send_z(item, part, column, 0, 1, True))
        pl.when(z > 0)(lambda: send_z(item, part, column, 0, 0, True))
        send_x(item, part, column, True)
        send_y(item, part, 0, column, True)
        send_c(item, part, 0, column, True)
    for copied in local:
        copied.start()

    def from_z(item, part, turn, source, upward):
        arrived(item, part, 0, source)
        if turn < 3:
            ahead = z < 3 if upward else z > 0
            pl.when(ahead)(lambda: send_z(item, part, source, turn, upward))
        send_x(item, part, source)
        send_y(item, part, 0, source)
        send_c(item, part, 0, source)

    def second(item, source):
        arrived(item, 0, 0, mirror(source))
        send_x(item, 0, mirror(source))
        send_c(item, 0, 0, mirror(source))
        arrived(item, 1, 2, source)
        send_y(item, 1, 2, source)
        send_c(item, 1, 2, source)

    def third(item, source):
        arrived(item, 0, 2, source)
        send_c(item, 0, 2, source)
        arrived(item, 1, 0, mirror(source))
        send_c(item, 1, 0, mirror(source))
        for part in range(2):
            arrived(item, part, 2, mirror(source))
            send_c(item, part, 2, mirror(source))

    for item in range(items):
        for turn in (1, 2, 3):
            for part in range(2):
                slot(turn, lambda source, upward: from_z(item, part, turn, source, upward))
    for item in range(items):
        second(item, column)
        for turn in (1, 2, 3):
            slot(turn, lambda source, upward: second(item, source))
    for item in range(items):
        third(item, column)
        for turn in (1, 2, 3):
            slot(turn, lambda source, upward: third(item, source))
    for item, part in every:
        for source in range(8):
            for quarter in (1, 3):
                arrived(item, part, quarter, source)
    for copied in local:
        copied.wait()
    for item in range(items):
        for way, count in enumerate((12, 12, 16, 16)):
            lead = outs[item][0].at[pl.ds(0, count * piece[item])]
            pltpu.make_async_remote_copy(
                src_ref=lead,
                dst_ref=lead,
                send_sem=side_sem.at[way, item],
                recv_sem=recv_sem.at[item, 0, 0, 0],
                device_id=devices["x"],
                device_id_type=MESH,
            ).wait_send()
    for item, part in every:
        for turn in range(3):
            pl.when((z < 3) & (z >= turn))(
                lambda: copy(item, part, 0, column, 0, "up", z_sem.at[item, part, 0, turn], True).wait_send()
            )
            pl.when((z > 0) & (z + turn <= 3))(
                lambda: copy(item, part, 0, column, 0, "down", z_sem.at[item, part, 1, turn], True).wait_send()
            )


def gather_kernel(shards):
    items = len(shards)
    anywhere = pl.BlockSpec(memory_space=pl.ANY)
    whole = lax.axis_size("dp")
    shapes = [
        jax.ShapeDtypeStruct((item.shape[0] * whole, item.shape[1]), item.dtype)
        for item in shards
        for _ in range(4)
    ]
    flat = pl.pallas_call(
        functools.partial(gather_body, items),
        name="gather_weights",
        out_shape=shapes,
        in_specs=[anywhere] * items,
        out_specs=[anywhere] * (4 * items),
        scratch_shapes=[
            pltpu.SemaphoreType.DMA((4, items)),
            pltpu.SemaphoreType.DMA((items, 2, 2, 3)),
            pltpu.SemaphoreType.DMA((items, 2, 4, 8)),
            pltpu.SemaphoreType.DMA((items,)),
        ],
        compiler_params=pltpu.CompilerParams(collective_id=0, has_side_effects=True),
    )(*shards)
    return [flat[4 * item : 4 * item + 4] for item in range(items)]


def reduce_body(layout, parts, gains_at, *refs):
    items = len(layout)
    wide_refs = [refs[4 * item : 4 * item + 4] for item in range(items)]
    refs = refs[4 * items :]
    facts, places, extra = refs[:3]
    lefts = refs[3:9]
    refs = refs[9:]
    outs, totals = refs[:items], refs[items]
    refs = refs[items + 1 :]
    held = [refs[6 * item : 6 * item + 6] for item in range(items)]
    refs = refs[6 * items :]
    side_sem, c_send, c_sem, x_sem, y_sem, zs_sem, zr_sem, load_sem, free_sem = refs[:9]
    tile, tile_row, tile_column, row_send, row_recv, column_send, column_recv = refs[9:16]
    crossed, from_c, rights = refs[16:]
    column = lax.axis_index("dp")
    z, y = column // 2, column % 2
    devices = neighbours()
    shard = [item.shape[0] for item in outs]
    piece = [item // 2 for item in shard]
    width = [item.shape[1] for item in outs]

    def load(item, quarter):
        return pltpu.make_async_copy(
            wide_refs[item][quarter],
            rights.at[quarter, :, pl.ds(0, width[item])],
            load_sem.at[item, quarter],
        )

    for quarter in range(4):
        load(0, quarter).start()
    row = lax.axis_index("tensor")
    row_peers = [(column, (row + away) % 4) for away in (1, 2, 3)]
    column_peers = [((column + away) % 8, row) for away in range(1, 8)]
    barrier = pltpu.get_barrier_semaphore()
    for device in row_peers + column_peers:
        pl.semaphore_signal(barrier, inc=1, device_id=device, device_id_type=MESH)
    pl.semaphore_wait(barrier, 10)

    def span(item, part, source):
        return pl.ds(pl.multiple_of(source * shard[item] + part * piece[item], 8), piece[item])

    def remote(src, dst, send, recv, name):
        return pltpu.make_async_remote_copy(
            src_ref=src, dst_ref=dst, send_sem=send, recv_sem=recv, device_id=devices[name], device_id_type=MESH
        )

    def c_copy(item, part, side, source, slot=0):
        here = pl.ds(pl.multiple_of(source % 2 * shard[item] + part * piece[item], 8), piece[item])
        columns = pl.ds(0, width[item])
        return remote(
            crossed.at[side, slot, here, columns],
            from_c.at[side, span(item, part, source), columns],
            c_send.at[side, slot],
            c_sem.at[item, part, side, source],
            "c",
        )

    def c_wait(item, part, side, source):
        c_copy(item, part, side, source).wait_recv()

    def c_sent(item, slot):
        for side in range(2):
            lead = crossed.at[side, slot, :, pl.ds(0, width[item])]
            remote(lead, lead, c_send.at[side, slot], c_sem.at[0, 0, 0, 0], "c").wait_send()

    def x_copy(item, part, source):
        place = source if part == 0 else source // 2
        return remote(
            held[item][0].at[1, span(item, part, source)],
            held[item][1 + part].at[place],
            side_sem.at[0, item],
            x_sem.at[item, part, place],
            "x",
        )

    def y_copy(item, part, side, source):
        return remote(
            held[item][0].at[side, span(item, part, source)],
            held[item][3].at[source // 2] if part == 0 else held[item][4].at[side, source // 2],
            side_sem.at[1, item],
            y_sem.at[item, part + side, source // 2],
            "y",
        )

    def z_copy(item, part, source, away, upward):
        return remote(
            held[item][0].at[0, span(item, part, source)],
            held[item][5].at[1 - upward, part, away],
            zs_sem.at[item, part, 1 - upward, away],
            zr_sem.at[item, part, 1 - upward, away],
            "up" if upward else "down",
        )

    def add(item, side, part, source, *others):
        total = held[item][0]
        start = source * shard[item] + part * piece[item]
        step = 16

        def one(turn, _):
            here = pl.ds(pl.multiple_of(start + turn * step, 8), step)
            value = total[side, here].astype(jnp.float32)
            for other in others:
                value = value + other(turn * step, step)
            total[side, here] = value.astype(jnp.bfloat16)
            return 0

        lax.fori_loop(0, piece[item] // step, one, 0)

    def c_part(item, side, part, source):
        start = source * shard[item] + part * piece[item]

        def read(at, step):
            here = pl.ds(pl.multiple_of(start + at, 8), step)
            return from_c[side, here, pl.ds(0, width[item])].astype(jnp.float32)

        return read

    def of(ref, *place):
        return lambda at, step: ref[(*place, pl.ds(pl.multiple_of(at, 8), step))].astype(jnp.float32)

    def mirror(source):
        return source + 1 - 2 * (source % 2)

    def target(turn):
        low = 3 - turn if turn < 2 else jnp.where(z % 3 == 0, 3 - turn, turn - 2)
        return column + 2 * (jnp.where(z < 2, low, 3 - low) - z)

    def send_c(item, turn):
        source = target(turn)
        if item > 0:
            pl.semaphore_wait(free_sem, 1)
        for part, side, place in (
            (0, 1, source),
            (1, 1, mirror(source)),
            (0, 1, mirror(source)),
            (1, 0, mirror(source)),
            (0, 0, mirror(source)),
            (1, 1, source),
            (0, 0, source),
            (1, 0, source),
        ):
            c_copy(item, part, side, place, turn % 2).start()

    def make(item, turn):
        if 4 * item + turn >= 2:
            c_sent(item if turn >= 2 else item - 1, turn % 2)
        block = 2 * shard[item]
        rows = pl.ds(pl.multiple_of(target(turn) // 2 * block, 16), block)
        for quarter in range(4):
            if turn == 0:
                load(item, quarter).wait()
            for left, base, span_width, step in layout[item]:

                def one(chunk, _):
                    at = pl.ds(pl.multiple_of(base + chunk * step, 128), step)
                    found = jnp.dot(
                        lefts[left][rows], rights[quarter, :, at], preferred_element_type=jnp.float32
                    )
                    if item == 0:
                        spots = lax.broadcasted_iota(jnp.int32, (places.shape[0], step), 1) + chunk * step
                        hot = jnp.where(places[:, quarter : quarter + 1] == spots, 1.0, 0.0)
                        found += jnp.dot(
                            lefts[1][rows], hot.astype(jnp.bfloat16), preferred_element_type=jnp.float32
                        )
                    if item == gains_at[0] and base == 0:
                        found += extra[rows]
                    if quarter % 2:
                        crossed[quarter // 2, turn % 2, :, at] = found.astype(jnp.bfloat16)
                    else:
                        held[item][0][quarter // 2, rows, at] = found.astype(jnp.bfloat16)
                    return 0

                lax.fori_loop(0, span_width // step, one, 0)
        if turn == 3 and item + 1 < items:
            for quarter in range(4):
                load(item + 1, quarter).start()

    def first(item, turn):
        source = target(turn)
        for x_place, y_side in ((source, 1), (mirror(source), 0)):
            c_wait(item, 0, 1, x_place)
            add(item, 1, 0, x_place, c_part(item, 1, 0, x_place))
            x_copy(item, 0, x_place).start()
            y_place = mirror(source)
            c_wait(item, 1, y_side, y_place)
            add(item, y_side, 1, y_place, c_part(item, y_side, 1, y_place))
            y_copy(item, 1, y_side, y_place).start()

    def second(item, turn):
        source = target(turn)
        place = mirror(source)
        c_wait(item, 0, 0, place)
        x_copy(item, 0, place).wait_recv()
        add(item, 0, 0, place, c_part(item, 0, 0, place), of(held[item][1], place))
        y_copy(item, 0, 0, place).start()
        c_wait(item, 1, 1, source)
        y_copy(item, 1, 1, source).wait_recv()
        add(item, 1, 1, source, c_part(item, 1, 1, source), of(held[item][4], 1, source // 2))
        x_copy(item, 1, source).start()

    def third(item, turn):
        source = target(turn)
        for part in range(2):
            c_wait(item, part, 0, source)
            x_copy(item, part, source).wait_recv()
            y_copy(item, part, 0, source).wait_recv()
            if part == 0:
                terms = [of(held[item][1], source), of(held[item][3], source // 2)]
            else:
                terms = [of(held[item][2], source // 2), of(held[item][4], 0, source // 2)]
            add(item, 0, part, source, c_part(item, 0, part, source), *terms)
        if item + 1 < items:
            pl.semaphore_signal(free_sem, inc=1, device_id=devices["c"], device_id_type=MESH)

    def fourth(item, turn):
        source = target(turn)
        away = jnp.where(source > column, source - column, column - source) // 2

        def along(upward):
            for part in range(2):

                def more():
                    z_copy(item, part, source, away, upward).wait_recv()
                    add(item, 0, part, source, of(held[item][5], 1 - upward, part, away))

                pl.when(z > 0 if upward else z < 3)(more)
                z_copy(item, part, source, away - 1, upward).start()

        pl.when(source > column)(lambda: along(1))
        pl.when(source < column)(lambda: along(0))

    def last(item):
        square = jnp.zeros((), jnp.float32)
        for part in range(2):
            for upward in (1, 0):
                pl.when(z > 0 if upward else z < 3)(
                    lambda: z_copy(item, part, column, 0, upward).wait_recv()
                )
            start = column * shard[item] + part * piece[item]

            def one(turn, square):
                at = pl.multiple_of(turn * 16, 8)
                value = held[item][0][0, pl.ds(pl.multiple_of(start + at, 8), 16)].astype(jnp.float32)
                below = held[item][5][0, part, 0, pl.ds(at, 16)].astype(jnp.float32)
                above = held[item][5][1, part, 0, pl.ds(at, 16)].astype(jnp.float32)
                value = value + jnp.where(z > 0, below, 0.0) + jnp.where(z < 3, above, 0.0)
                outs[item][pl.ds(pl.multiple_of(part * piece[item] + at, 8), 16)] = value
                square_here = value * value
                if item == gains_at[0]:
                    lane = lax.broadcasted_iota(jnp.int32, value.shape, 1)
                    repeated = (lane >= gains_at[1]) & (lane < gains_at[1] + gains_at[2])
                    square_here = jnp.where(repeated, square_here / parts, square_here)
                return square + jnp.sum(square_here)

            square = lax.fori_loop(0, piece[item] // 16, one, square)
        return square

    steps = [(item, turn) for item in range(items) for turn in range(4)]
    count = len(steps)
    make(*steps[0])
    send_c(*steps[0])
    for turn in range(count + 3):
        if turn < count:
            first(*steps[turn])
        if turn + 1 < count:
            make(*steps[turn + 1])
            send_c(*steps[turn + 1])
        if 0 <= turn - 1 < count:
            second(*steps[turn - 1])
        if 0 <= turn - 2 < count:
            third(*steps[turn - 2])
        if 0 <= turn - 3 < count and (turn - 3) % 4 < 3:
            fourth(*steps[turn - 3])
    square = sum([last(item) for item in range(items)])
    sublane = lax.broadcasted_iota(jnp.int32, (8, 128), 0)
    tile[...] = jnp.where(sublane == 0, square, facts[...])

    def exchange(value, slots, here, peers, sources, send, recv):
        slots[here] = value

        def crossing(place, device, source):
            return pltpu.make_async_remote_copy(
                src_ref=slots.at[here],
                dst_ref=slots.at[source],
                send_sem=send.at[place],
                recv_sem=recv.at[source],
                device_id=device,
                device_id_type=MESH,
            )

        for place, device in enumerate(peers):
            crossing(place, device, here).start()
        for place, device in enumerate(peers):
            crossing(place, device, sources[place]).wait_recv()
        total = slots[0]
        for place in range(1, len(peers) + 1):
            total = total + slots[place]
        for place, device in enumerate(peers):
            crossing(place, device, here).wait_send()
        return total

    along_row = exchange(
        tile[...], tile_row, row, row_peers, [(row + away) % 4 for away in (1, 2, 3)], row_send, row_recv
    )
    totals[...] = exchange(
        along_row,
        tile_column,
        column,
        column_peers,
        [(column + away) % 8 for away in range(1, 8)],
        column_send,
        column_recv,
    )
    for slot in range(2):
        c_sent(items - 1, slot)
    for item in range(items):
        for way, count in enumerate((12, 12)):
            lead = held[item][0].at[0, pl.ds(0, count * piece[item])]
            remote(lead, lead, side_sem.at[way, item], c_sem.at[item, 0, 0, 0], "x").wait_send()
        for part in range(2):
            for away in range(3):
                pl.when((z < 3) & (z + away + 1 <= 3))(
                    lambda: z_copy(item, part, column, away, 1).wait_send()
                )
                pl.when((z > 0) & (z - away - 1 >= 0))(
                    lambda: z_copy(item, part, column, away, 0).wait_send()
                )


def reduce_kernel(layout, lefts, rights, places, extra, facts, parts, gains_at, tag):
    items = len(layout)
    anywhere = pl.BlockSpec(memory_space=pl.ANY)
    inside = pl.BlockSpec(memory_space=pltpu.VMEM)
    whole = lax.axis_size("dp")
    rows, depth = lefts[0].shape
    half = rows // (2 * whole)
    widths = [item[0].shape[1] for item in rights]
    shapes, scratch = [], []
    for width in widths:
        shapes.append(jax.ShapeDtypeStruct((rows // whole, width), jnp.float32))
        for lead in ((2, rows), (8, half), (4, half), (4, half), (2, 4, half), (2, 2, 3, half)):
            scratch.append(pltpu.VMEM((*lead, width), jnp.bfloat16))
    shapes.append(jax.ShapeDtypeStruct((8, 128), jnp.float32))
    found = pl.pallas_call(
        functools.partial(reduce_body, layout, parts, gains_at),
        name="reduce_grads",
        out_shape=shapes,
        in_specs=[anywhere] * (4 * items) + [inside] * (3 + len(lefts)),
        out_specs=[inside] * (items + 1),
        scratch_shapes=scratch
        + [
            pltpu.SemaphoreType.DMA((2, items)),
            pltpu.SemaphoreType.DMA((2, 2)),
            pltpu.SemaphoreType.DMA((items, 2, 2, 8)),
            pltpu.SemaphoreType.DMA((items, 2, 8)),
            pltpu.SemaphoreType.DMA((items, 3, 4)),
            pltpu.SemaphoreType.DMA((items, 2, 2, 3)),
            pltpu.SemaphoreType.DMA((items, 2, 2, 3)),
            pltpu.SemaphoreType.DMA((items, 4)),
            pltpu.SemaphoreType.REGULAR,
            pltpu.VMEM((8, 128), jnp.float32),
            pltpu.VMEM((4, 8, 128), jnp.float32),
            pltpu.VMEM((8, 8, 128), jnp.float32),
            pltpu.SemaphoreType.DMA((3,)),
            pltpu.SemaphoreType.DMA((4,)),
            pltpu.SemaphoreType.DMA((7,)),
            pltpu.SemaphoreType.DMA((8,)),
            pltpu.VMEM((2, 2, 4 * half, max(widths)), jnp.bfloat16),
            pltpu.VMEM((2, rows, max(widths)), jnp.bfloat16),
            pltpu.VMEM((4, depth, max(widths)), jnp.bfloat16),
        ],
        compiler_params=pltpu.CompilerParams(
            collective_id=tag, has_side_effects=True, vmem_limit_bytes=60 << 20
        ),
    )(*[item for quarters in rights for item in quarters], facts, places, extra, *lefts)
    return found[:-1], found[-1]


def update_body(sources, plans, *refs):
    count = len(plans)
    totals, fixes, grads = refs[0], refs[1], refs[2 : 2 + sources]
    refs = refs[2 + sources :]
    triples = [refs[3 * place : 3 * place + 3] for place in range(count)]
    outs = [refs[3 * (count + place) : 3 * (count + place) + 3] for place in range(count)]
    square, loss, real = totals[0:1, :], totals[1:2, :], totals[2:3, :]
    norm = jnp.sqrt(square) / real
    refs[6 * count][...] = jnp.concatenate([loss / real, norm] + [norm] * 6, axis=0)
    scale = (jnp.minimum(1.0, clip_at / norm) / real)[:, 0:1]
    over_one, over_two = fixes[0:1, 0:1], fixes[1:2, 0:1]

    def renew(place, grad, rows):
        source, turned, first, rate, decay = plans[place]
        weight, one, two = triples[place]
        clipped = grad * scale
        moment_one = beta_one * one[rows] + (1.0 - beta_one) * clipped
        moment_two = beta_two * two[rows] + (1.0 - beta_two) * clipped * clipped
        stepped = moment_one * over_one / (jnp.sqrt(moment_two * over_two) + adam_eps)
        outs[place][0][rows] = moment_one
        outs[place][1][rows] = moment_two
        outs[place][2][rows] = weight[rows] - rate * (stepped + decay * weight[rows])

    for place in range(count):
        source, turned, first, rate, decay = plans[place]
        rows, columns = triples[place][0].shape
        if turned and rows >= 128:
            for at in range(0, rows, 128):
                span = min(128, rows - at)
                block = grads[source][:, first + at : first + at + span].T
                renew(place, block, pl.ds(at, span))
        elif turned:
            start = first // 128 * 128
            block = grads[source][:, start : start + 128].T
            renew(place, block[first - start : first - start + rows], pl.ds(0, rows))
        else:
            for at in range(0, rows, 32):
                renew(place, grads[source][pl.ds(at, 32), first : first + columns], pl.ds(at, 32))


def update_kernel(totals, fixes, grads, plans, triples):
    inside = pl.BlockSpec(memory_space=pltpu.VMEM)
    flat = [item for triple in triples for item in triple]
    outs = [jax.ShapeDtypeStruct(item.shape, item.dtype) for item in flat] + [
        jax.ShapeDtypeStruct((8, 128), jnp.float32)
    ]
    found = pl.pallas_call(
        functools.partial(update_body, len(grads), plans),
        name="update_weights",
        out_shape=outs,
        in_specs=[inside] * (2 + len(grads) + len(flat)),
        out_specs=[inside] * len(outs),
        compiler_params=pltpu.CompilerParams(vmem_limit_bytes=60 << 20),
    )(totals, fixes, *grads, *flat)
    return found[:-1], found[-1]


def turn_halves(tile, cosine, sine):
    lane = lax.broadcasted_iota(jnp.int32, tile.shape, 1)
    other = jnp.where(lane % 64 < 32, pltpu.roll(tile, 96, 1), pltpu.roll(tile, 32, 1))
    return tile * cosine + other * sine


def greet_core(device):
    barrier = pltpu.get_barrier_semaphore()
    pl.semaphore_signal(barrier, inc=1, device_id=device, device_id_type=MESH)
    pl.semaphore_wait(barrier, 1)


def attend_body(normed, j0, j1, j2, j3, cosine, sine, seg_row, seg_col, packed, lse, attended, leaving, heads_out, heads_in, send_sem, recv_sem, out_send, out_recv):
    device = neighbours()["c"]
    rows = normed.shape[0]
    greet_core(device)

    def project(joint, put):
        found = jnp.dot(normed[...], joint[...], preferred_element_type=jnp.float32)
        for head in range(3):
            pair = turn_halves(found[:, 192 * head : 192 * head + 128], cosine[...], sine[...])
            value = found[:, 192 * head + 128 : 192 * head + 192]
            put(head, pair.astype(jnp.bfloat16), value.astype(jnp.bfloat16))

    def crossing(place):
        return pltpu.make_async_remote_copy(
            src_ref=leaving.at[place],
            dst_ref=packed.at[place, pl.ds(rows, rows)],
            send_sem=send_sem.at[place],
            recv_sem=recv_sem.at[place],
            device_id=device,
            device_id_type=MESH,
        )

    for side, joint in enumerate((j1, j3)):

        def put(head, pair, value):
            leaving[3 * side + head, :, 0:128] = pair
            leaving[3 * side + head, :, 128:192] = value
            crossing(3 * side + head).start()

        project(joint, put)
    for side, joint in enumerate((j0, j2)):

        def put(head, pair, value):
            packed[3 * side + head, pl.ds(0, rows), 0:128] = pair
            packed[3 * side + head, pl.ds(0, rows), 128:192] = value

        project(joint, put)

    def one_head(place):
        keys = packed[place, :, 0:128][:, 64:128]
        values_t = packed[place, :, 128:256][:, 0:64].astype(jnp.float32).T.astype(jnp.bfloat16)

        def block(turn, _):
            at = pl.ds(pl.multiple_of(turn * 256, 256), 256)
            query = packed[place, at, 0:128][:, 0:64]
            scores = lax.dot_general(
                keys, query, (((1,), (1,)), ((), ())), preferred_element_type=jnp.float32
            ) * HEAD_DIM ** (-0.5)
            scores = jnp.where(seg_col[:, 0:1] == seg_row[0:1, at], scores, neg_fill)
            top = jnp.max(scores, axis=0, keepdims=True)
            expd = jnp.exp(scores - top)
            summed = jnp.sum(expd, axis=0, keepdims=True)
            probs = (expd * (1.0 / summed)).astype(jnp.bfloat16)
            found = jnp.dot(values_t, probs, preferred_element_type=jnp.float32)
            lse[pl.ds(place, 1), at] = top + jnp.log(summed)
            heads_out[place, at, 0:64] = found.T.astype(jnp.bfloat16)
            return 0

        lax.fori_loop(0, 2 * rows // 256, block, 0)

    for place in range(6):
        crossing(place).wait_recv()

    def heads(place, _):
        one_head(place)
        return 0

    lax.fori_loop(0, 6, heads, 0)

    def returning(place):
        return pltpu.make_async_remote_copy(
            src_ref=heads_out.at[place, pl.ds(rows, rows)],
            dst_ref=heads_in.at[place],
            send_sem=out_send.at[place],
            recv_sem=out_recv.at[place],
            device_id=device,
            device_id_type=MESH,
        )

    for place in range(6):
        returning(place).start()
    for place in range(6):
        attended[:, 64 * place : 64 * place + 64] = heads_out[place, pl.ds(0, rows), 0:64]
    for place in range(6):
        returning(place).wait_recv()
        attended[:, 384 + 64 * place : 448 + 64 * place] = heads_in[place, :, 0:64]
    for place in range(6):
        crossing(place).wait_send()
        returning(place).wait_send()


def attend_kernel(normed, joints, cosine, sine, seg_row, seg_col):
    rows = normed.shape[0]
    inside = pl.BlockSpec(memory_space=pltpu.VMEM)
    return pl.pallas_call(
        attend_body,
        name="attend",
        out_shape=(
            jax.ShapeDtypeStruct((6, 2 * rows, 256), jnp.bfloat16),
            jax.ShapeDtypeStruct((8, 2 * rows), jnp.float32),
            jax.ShapeDtypeStruct((rows, 768), jnp.bfloat16),
        ),
        in_specs=[inside] * 9,
        out_specs=(inside, inside, inside),
        scratch_shapes=[
            pltpu.VMEM((6, rows, 256), jnp.bfloat16),
            pltpu.VMEM((6, 2 * rows, 128), jnp.bfloat16),
            pltpu.VMEM((6, rows, 128), jnp.bfloat16),
            pltpu.SemaphoreType.DMA((6,)),
            pltpu.SemaphoreType.DMA((6,)),
            pltpu.SemaphoreType.DMA((6,)),
            pltpu.SemaphoreType.DMA((6,)),
        ],
        compiler_params=pltpu.CompilerParams(
            collective_id=2, has_side_effects=True, vmem_limit_bytes=48 << 20
        ),
    )(normed, *joints, cosine, sine, seg_row, seg_col)


def attend_back_body(grad_out, packed, lse, attended, cosine, sine, seg_row, seg_col, p0, p1, p2, p3, r0, r1, r2, r3, grads, leaving, keys_t, probs, prob_grads, found, going, coming, send_sem, recv_sem, out_send, out_recv):
    device = neighbours()["c"]
    rows = grad_out.shape[0]
    greet_core(device)

    def crossing(place):
        return pltpu.make_async_remote_copy(
            src_ref=leaving.at[place],
            dst_ref=grads.at[place, pl.ds(rows, rows)],
            send_sem=send_sem.at[place],
            recv_sem=recv_sem.at[place],
            device_id=device,
            device_id_type=MESH,
        )

    for place in range(6):
        leaving[place, :, 0:64] = grad_out[:, 384 + 64 * place : 448 + 64 * place]
        crossing(place).start()
        grads[place, pl.ds(0, rows), 0:64] = grad_out[:, 64 * place : 64 * place + 64]
    nothing = jnp.zeros((rows, 64), jnp.bfloat16)
    for order, (part, right) in enumerate(((p0, r0), (p2, r2), (p1, r1), (p3, r3))):
        part[:, 576:640] = nothing
        right[:, 576:640] = nothing
        right[:, 640:832] = attended[:, 192 * order : 192 * order + 192]
        right[:, 832:896] = nothing
    for place in range(6):
        crossing(place).wait_recv()

    def one_head(place):
        query = packed[place, :, 0:128][:, 0:64]
        wide_keys = packed[place, :, 0:128][:, 64:128].astype(jnp.float32)
        keys_t[...] = wide_keys.T.astype(jnp.bfloat16)
        grad = grads[place, :, 0:64]
        stat = lse[pl.ds(place, 1), :]

        def score(turn, inner):
            at = pl.ds(pl.multiple_of(turn * 256, 256), 256)
            keys = packed[place, at, 0:128][:, 64:128]
            values = packed[place, at, 128:256][:, 0:64]
            scores = lax.dot_general(
                keys, query, (((1,), (1,)), ((), ())), preferred_element_type=jnp.float32
            ) * HEAD_DIM ** (-0.5)
            scores = jnp.where(seg_col[at, 0:1] == seg_row[0:1, :], scores, neg_fill)
            prob = jnp.exp(scores - stat)
            prob_grad = lax.dot_general(
                values, grad, (((1,), (1,)), ((), ())), preferred_element_type=jnp.float32
            )
            probs[at] = prob
            prob_grads[at] = prob_grad
            value_grad = jnp.dot(prob.astype(jnp.bfloat16), grad, preferred_element_type=jnp.float32)
            found[place, at, 128:192] = value_grad
            return inner + jnp.sum(prob * prob_grad, axis=0, keepdims=True)

        inner = lax.fori_loop(0, 2 * rows // 256, score, jnp.zeros((1, 2 * rows), jnp.float32))

        def spread_back(turn, query_grad):
            at = pl.ds(pl.multiple_of(turn * 256, 256), 256)
            score_grad = (probs[at] * (prob_grads[at] - inner)).astype(jnp.bfloat16)
            key_grad = jnp.dot(score_grad, query, preferred_element_type=jnp.float32)
            found[place, at, 64:128] = key_grad * HEAD_DIM ** (-0.5)
            return query_grad + jnp.dot(keys_t[:, at], score_grad, preferred_element_type=jnp.float32)

        query_grad = lax.fori_loop(
            0, 2 * rows // 256, spread_back, jnp.zeros((64, 2 * rows), jnp.float32)
        )
        found[place, :, 0:64] = query_grad.T * HEAD_DIM ** (-0.5)

    def heads(place, _):
        one_head(place)
        return 0

    lax.fori_loop(0, 6, heads, 0)

    def returning(side):
        return pltpu.make_async_remote_copy(
            src_ref=going.at[side],
            dst_ref=coming.at[side],
            send_sem=out_send.at[side],
            recv_sem=out_recv.at[side],
            device_id=device,
            device_id_type=MESH,
        )

    for half in (1, 0):
        at = pl.ds(half * rows, rows)
        for side in range(2):
            for head in range(3):
                place = 3 * side + head
                pair = turn_halves(found[place, at, 0:128], cosine[at], -sine[at]).astype(jnp.bfloat16)
                value = found[place, at, 128:192].astype(jnp.bfloat16)
                puts = [going.at[side]] if half else [(p0, p2)[side], (r0, r2)[side]]
                for put in puts:
                    put[:, 192 * head : 192 * head + 128] = pair
                    put[:, 192 * head + 128 : 192 * head + 192] = value
            if half:
                returning(side).start()
    for side in range(2):
        returning(side).wait_recv()
        for put in ((p1, p3)[side], (r1, r3)[side]):
            put[:, 0:576] = coming[side, :, 0:576]
    for place in range(6):
        crossing(place).wait_send()
    for side in range(2):
        returning(side).wait_send()


def attend_back_kernel(grad_out, packed, lse, attended, cosine, sine, seg_row, seg_col):
    rows = grad_out.shape[0]
    inside = pl.BlockSpec(memory_space=pltpu.VMEM)
    found = pl.pallas_call(
        attend_back_body,
        name="attend_back",
        out_shape=[jax.ShapeDtypeStruct((rows, 640), jnp.bfloat16)] * 4
        + [jax.ShapeDtypeStruct((rows, 896), jnp.bfloat16)] * 4,
        in_specs=[inside] * 8,
        out_specs=[inside] * 8,
        scratch_shapes=[
            pltpu.VMEM((6, 2 * rows, 128), jnp.bfloat16),
            pltpu.VMEM((6, rows, 128), jnp.bfloat16),
            pltpu.VMEM((64, 2 * rows), jnp.bfloat16),
            pltpu.VMEM((2 * rows, 2 * rows), jnp.float32),
            pltpu.VMEM((2 * rows, 2 * rows), jnp.float32),
            pltpu.VMEM((6, 2 * rows, 256), jnp.float32),
            pltpu.VMEM((2, rows, 640), jnp.bfloat16),
            pltpu.VMEM((2, rows, 640), jnp.bfloat16),
            pltpu.SemaphoreType.DMA((6,)),
            pltpu.SemaphoreType.DMA((6,)),
            pltpu.SemaphoreType.DMA((2,)),
            pltpu.SemaphoreType.DMA((2,)),
        ],
        compiler_params=pltpu.CompilerParams(
            collective_id=3, has_side_effects=True, vmem_limit_bytes=56 << 20
        ),
    )(grad_out, packed, lse, attended, cosine, sine, seg_row, seg_col)
    return found[:4], found[4:]


def known_mesh():
    return lax.axis_size("dp") == 8 and lax.axis_size("tensor") == 4


def gather_weights(shards):
    if not known_mesh():
        return [gather_all(item, True) for item in shards]
    return [[item[0], item[2], item[1], item[3]] for item in gather_kernel(shards)]


def reduce_grads(layout, lefts, rights, places, extra, facts, parts, gains_at):
    if known_mesh():
        ordered = [[item[0], item[2], item[1], item[3]] for item in rights]
        return reduce_kernel(layout, lefts, ordered, places, extra, facts, parts, gains_at, 1)
    sums = []
    for item, products in enumerate(layout):
        quarters = []
        for quarter, mask in enumerate((0, 2, 1, 3)):
            right = rights[item][quarter]
            found = [mm(lefts[at], right[:, base : base + width]) for at, base, width, _ in products]
            if item == 0:
                spots = jnp.arange(right.shape[1], dtype=jnp.int32)[None, :]
                found[0] += mm(lefts[1], narrow(places[:, mask : mask + 1] == spots))
            if item == gains_at[0]:
                found[0] += extra
            quarters.append(narrow(jnp.concatenate(found, axis=1)))
        sums.append(reduce_all(quarters, True))
    square = sum(jnp.sum(item * item) for item in sums)
    repeated = sums[gains_at[0]][:, gains_at[1] : gains_at[1] + gains_at[2]]
    square = square - jnp.sum(repeated * repeated) * (1.0 - 1.0 / parts)
    tile = jnp.where(lax.broadcasted_iota(jnp.int32, (8, 128), 0) == 0, square, facts)
    return sums, everyone_sum(tile)


def wide(value):
    return value.astype(jnp.float32)


def narrow(value):
    return value.astype(jnp.bfloat16)


def fold(value, masks, last):
    rows = value.shape[0] // (len(masks) + 1)
    total = wide(value[:rows])
    for place, mask in enumerate(masks):
        total = total + wide(swap(value[(place + 1) * rows : (place + 2) * rows], "dp", mask))
    return total if last else narrow(total)


def reduce_all(quarters, x_first):
    groups = groups_of(lax.axis_size("dp"))
    own = narrow(wide(quarters[0]) + wide(swap(quarters[2], "tensor", 1)))
    other = narrow(wide(quarters[1]) + wide(swap(quarters[3], "tensor", 1)))
    if x_first:
        own = narrow(wide(own) + wide(swap(other, "tensor", 2)))
        own = fold(own, groups[0], len(groups) == 1)
    else:
        own = fold(own, groups[0], False)
        other = fold(other, groups[0], False)
        own = narrow(wide(own) + wide(swap(other, "tensor", 2)))
    for place in range(1, len(groups)):
        own = fold(own, groups[place], place == len(groups) - 1)
    return wide(own)


def everyone_sum(value):
    for masks in groups_of(lax.axis_size("dp")):
        value = sum([swap(value, "dp", mask) for mask in masks], value)
    for mask in (1, 2):
        value = value + swap(value, "tensor", mask)
    return value


def mm(left, right):
    return jnp.dot(left, right, preferred_element_type=jnp.float32)


def mm_nt(left, right):
    return lax.dot_general(left, right, (((1,), (1,)), ((), ())), preferred_element_type=jnp.float32)


def mm_tn(left, right):
    return lax.dot_general(left, right, (((0,), (0,)), ((), ())), preferred_element_type=jnp.float32)


def rotate_heads(values, cosine, sine):
    return rotate(values, cosine[:, None, :], sine[:, None, :])


def scores_of(query, key_rows, same_doc):
    scores = jnp.einsum(
        "qhe,khe->hqk", query, key_rows, preferred_element_type=jnp.float32
    ) * HEAD_DIM ** (-0.5)
    return jnp.where(same_doc[None], scores, neg_fill)


def split_heads(packed):
    packed = packed.reshape(packed.shape[0], -1, 3, HEAD_DIM)
    return packed[:, :, 0], packed[:, :, 1], packed[:, :, 2]


def attend(packed, same_doc):
    query, key_rows, value_rows = split_heads(packed)
    scores = scores_of(query, key_rows, same_doc)
    row_max = jnp.max(scores, axis=-1, keepdims=True)
    expd = jnp.exp(scores - row_max)
    summed = jnp.sum(expd, axis=-1, keepdims=True)
    probs = (expd / summed).astype(jnp.bfloat16)
    output = jnp.einsum("hqk,khe->qhe", probs, value_rows, preferred_element_type=jnp.float32)
    return (narrow(output).reshape(packed.shape[0], -1), (row_max + jnp.log(summed))[..., 0])


def attend_back(packed, same_doc, row_lse, grad_out, cosine, sine):
    query, key_rows, value_rows = split_heads(packed)
    grad_out = grad_out.reshape(packed.shape[0], -1, HEAD_DIM)
    scores = scores_of(query, key_rows, same_doc)
    probs = jnp.exp(scores - row_lse[..., None])
    value_grad = jnp.einsum(
        "hqk,qhe->khe", probs.astype(jnp.bfloat16), grad_out, preferred_element_type=jnp.float32
    )
    prob_grad = jnp.einsum("qhe,khe->hqk", grad_out, value_rows, preferred_element_type=jnp.float32)
    inner = jnp.sum(prob_grad * probs, axis=-1, keepdims=True)
    score_grad = (probs * (prob_grad - inner)).astype(jnp.bfloat16)
    query_grad = jnp.einsum(
        "hqk,khe->qhe", score_grad, key_rows, preferred_element_type=jnp.float32
    ) * HEAD_DIM ** (-0.5)
    key_grad = jnp.einsum(
        "hqk,qhe->khe", score_grad, query, preferred_element_type=jnp.float32
    ) * HEAD_DIM ** (-0.5)
    query_grad = rotate_heads(query_grad, cosine, -sine)
    key_grad = rotate_heads(key_grad, cosine, -sine)
    return narrow(jnp.stack([query_grad, key_grad, value_grad], axis=2).reshape(packed.shape))


def update_weights(totals, fixes, sums, plans, triples):
    if known_mesh():
        updated, results = update_kernel(totals, fixes, sums, plans, triples)
        return list(updated), results
    updated = []
    norm = jnp.sqrt(totals[0, 0]) / totals[2, 0]
    scale = jnp.minimum(1.0, clip_at / norm) / totals[2, 0]
    for (source, turned, first, rate, decay), (weight, one, two) in zip(plans, triples):
        columns = weight.shape[0] if turned else weight.shape[1]
        grad = sums[source][:, first : first + columns]
        clipped = (grad.T if turned else grad) * scale
        moment_one = beta_one * one + (1.0 - beta_one) * clipped
        moment_two = beta_two * two + (1.0 - beta_two) * clipped * clipped
        stepped = moment_one * fixes[0, 0] / (jnp.sqrt(moment_two * fixes[1, 0]) + adam_eps)
        updated.extend([moment_one, moment_two, weight - rate * (stepped + decay * weight)])
    return updated, jnp.stack([totals[1, 0] / totals[2, 0], norm])[:, None]


def per_device(
    tokens,
    lengths,
    timesteps,
    masks,
    step_count,
    table,
    joint_weight,
    output_weight,
    upward_weight,
    downward_weight,
    gains,
    momentum_table,
    momentum_joint,
    momentum_output,
    momentum_upward,
    momentum_downward,
    momentum_gains,
    variance_table,
    variance_joint,
    variance_output,
    variance_upward,
    variance_downward,
    variance_gains,
):
    place = lax.axis_index("tensor")
    parts = lax.axis_size("tensor")
    rows = tokens.shape[0] // parts
    vocab_part, head_part = table.shape[0], joint_weight.shape[1]
    out_part, ff_part = output_weight.shape[0], upward_weight.shape[1]

    gain_columns = jnp.pad(narrow(gains).T, ((0, 0), (0, 61)))
    shards = [
        narrow(table).T,
        jnp.concatenate([narrow(joint_weight), gain_columns], axis=1),
        narrow(upward_weight),
        narrow(downward_weight).T,
        narrow(output_weight).T,
    ]
    table_q, first_group, up_q, down_q, out_q = gather_weights(shards)
    joint_q = [item[:, :head_part] for item in first_group]
    gain_full = wide(first_group[0][:, head_part : head_part + 3]).T
    out_all = jnp.concatenate(out_q, axis=1)

    start = place * rows
    seq = start // SEQ_LEN
    mine = start - seq * SEQ_LEN
    cut = lambda array: lax.dynamic_slice(array, (start,), (rows,))
    targets = cut(tokens)
    corrupt = cut(masks) == 1
    inputs = jnp.where(corrupt, VOCAB - 1, targets)
    own_lengths = lax.dynamic_slice(lengths, (seq, 0), (1, DOCS))
    step_here = lax.dynamic_slice(timesteps, (seq,), (1,))
    theirs = mine ^ rows
    position = jnp.concatenate(
        [mine + jnp.arange(rows, dtype=jnp.int32), theirs + jnp.arange(rows, dtype=jnp.int32)]
    )
    doc_ends = jnp.cumsum(own_lengths[0])
    doc_starts = doc_ends - own_lengths[0]
    segment = jnp.sum((position[:, None] >= doc_ends[None, :]).astype(jnp.int32), axis=1)
    chosen = segment[:, None] == jnp.arange(DOCS, dtype=jnp.int32)[None, :]
    offset = position - jnp.sum(jnp.where(chosen, doc_starts[None, :], 0), axis=1)
    is_real = segment < DOCS - 1
    factor = jnp.where(step_here == 1, 1.0, T_DIFF / step_here.astype(jnp.float32))
    weights = jnp.where(corrupt & is_real[:rows], factor, 0.0)
    inverse_freq = 10000.0 ** (-jnp.arange(HEAD_DIM // 2, dtype=jnp.float32) / (HEAD_DIM // 2))
    angles = offset.astype(jnp.float32)[:, None] * inverse_freq
    cosine, sine = jnp.cos(angles), jnp.sin(angles)
    same_doc = segment[:, None] == segment[None, :]

    def hot(ids, piece):
        base = (place ^ (2 * (piece % 2) + piece // 2)) * vocab_part
        return (ids - base)[:, None] == jnp.arange(vocab_part, dtype=jnp.int32)[None, :]

    pieces = range(len(table_q))
    input_hot = [narrow(hot(inputs, piece)) for piece in pieces]
    looked = sum(mm_nt(input_hot[piece], table_q[piece]) for piece in pieces)
    embedded = looked * D**0.5
    normed_one = narrow(norm_apply(embedded, gain_full[0]))

    on_known = known_mesh()
    if on_known:
        double = lambda array: jnp.concatenate([array] * 4, axis=1)
        cosines = double(cosine)
        sines = jnp.concatenate([-sine, sine] * 2, axis=1)
        seg_row = jnp.broadcast_to(segment[None, :], (8, 2 * rows))
        seg_col = jnp.broadcast_to(segment[:, None], (2 * rows, 128))
        packed, attn_lse, attended_all = attend_kernel(
            normed_one,
            [first_group[q] for q in (0, 2, 1, 3)],
            cosines[:rows],
            sines[:rows],
            seg_row,
            seg_col,
        )
    else:
        def turned(projected):
            projected = projected.reshape(rows, -1, 3, HEAD_DIM)
            query = rotate_heads(projected[:, :, 0], cosine[:rows], sine[:rows])
            key_rows = rotate_heads(projected[:, :, 1], cosine[:rows], sine[:rows])
            stacked = jnp.stack([query, key_rows, projected[:, :, 2]], axis=2)
            return narrow(stacked.reshape(rows, -1))

        packed = [turned(mm(normed_one, item)) for item in joint_q]
        whole = [
            jnp.concatenate([packed[side], swap(packed[2 + side], "tensor", 1)], axis=0)
            for side in range(2)
        ]
        attended, attn_lse = zip(*[attend(item, same_doc) for item in whole])
        attended_all = jnp.concatenate(
            [item[:rows] for item in attended]
            + [swap(item[rows:], "tensor", 1) for item in attended],
            axis=1,
        )
    after_attn = embedded + mm_nt(attended_all, out_all)
    normed_two = narrow(norm_apply(after_attn, gain_full[1]))
    pre_gelu = [mm(normed_two, item) for item in up_q]
    below = [0.5 + 0.5 * lax.erf(item * 0.5**0.5) for item in pre_gelu]
    slopes = [
        part + item * jnp.exp(-0.5 * item * item) * (0.5 / jnp.pi) ** 0.5
        for part, item in zip(below, pre_gelu)
    ]
    activated = [narrow(item * part) for part, item in zip(below, pre_gelu)]
    after_mlp = after_attn + sum(mm_nt(activated[q], down_q[q]) for q in range(4))
    normed_out = narrow(norm_apply(after_mlp, gain_full[2]))
    logits = [mm(normed_out, item) for item in table_q]
    row_max = logits[0].max(axis=1)
    for item in logits[1:]:
        row_max = jnp.maximum(row_max, item.max(axis=1))
    row_sum = sum(jnp.sum(jnp.exp(item - row_max[:, None]), axis=1) for item in logits)
    target_hot = [hot(targets, piece) for piece in pieces]
    row_pick = sum(
        jnp.sum(jnp.where(target_hot[piece], logits[piece], 0.0), axis=1) for piece in pieces
    )
    row_lse = row_max + jnp.log(row_sum)
    loss_local = jnp.sum(weights * (row_lse - row_pick))
    count_local = jnp.sum(is_real[:rows].astype(jnp.float32))

    logit_grad = [
        narrow(
            weights[:, None]
            * (jnp.exp(logits[piece] - row_lse[:, None]) - target_hot[piece].astype(jnp.float32))
        )
        for piece in pieces
    ]
    out_grad = sum(mm_nt(logit_grad[piece], table_q[piece]) for piece in pieces)
    mlp_grad, gain_three = norm_back(after_mlp, gain_full[2], out_grad)
    mlp_branch = narrow(mlp_grad)
    up_input = [
        narrow(slopes[q] * mm(mlp_branch, down_q[q])) for q in range(4)
    ]
    normed_two_grad = sum(mm_nt(up_input[q], up_q[q]) for q in range(4))
    attn_in_grad, gain_two = norm_back(after_attn, gain_full[1], normed_two_grad)
    resid_one = mlp_grad + attn_in_grad
    attn_branch = narrow(resid_one)
    attended_grad = narrow(mm(attn_branch, out_all))
    if on_known:
        proj_grad, last_rights = attend_back_kernel(
            attended_grad, packed, attn_lse, attended_all, cosines, sines, seg_row, seg_col
        )
        proj_grad = [proj_grad[q] for q in (0, 2, 1, 3)]
        last_rights = [last_rights[q] for q in (0, 2, 1, 3)]
        joint_back = first_group
    else:
        grad_parts = [attended_grad[:, q * out_part : (q + 1) * out_part] for q in range(4)]
        proj_whole = [
            attend_back(
                whole[side],
                same_doc,
                attn_lse[side],
                jnp.concatenate(
                    [grad_parts[side], swap(grad_parts[2 + side], "tensor", 1)], axis=0
                ),
                cosine,
                sine,
            )
            for side in range(2)
        ]
        proj_grad = [item[:rows] for item in proj_whole] + [
            swap(item[rows:], "tensor", 1) for item in proj_whole
        ]
        joint_back = joint_q
    normed_one_grad = sum(mm_nt(proj_grad[q], joint_back[q]) for q in range(4))
    embed_in, gain_one = norm_back(embedded, gain_full[0], normed_one_grad)
    embed_grad = resid_one + embed_in
    embed_scaled = narrow(embed_grad * D**0.5)
    places = jnp.pad(
        jnp.stack([inputs - (place ^ mask) * vocab_part for mask in range(4)], axis=1),
        ((0, 0), (0, 124)),
    )
    sublane = lax.broadcasted_iota(jnp.int32, (8, 128), 0)
    facts = jnp.where(sublane == 1, loss_local, jnp.where(sublane == 2, count_local, 0.0))
    gains_end = (head_part + gains.shape[0] + 127) // 128 * 128
    out_fill = (out_part + 127) // 128 * 128
    fill = lambda array, columns: jnp.pad(array, ((0, 0), (0, columns - array.shape[1])))
    extra = jnp.pad(
        jnp.stack([gain_one, gain_two, gain_three]).T,
        ((0, 0), (head_part, gains_end - head_part - gains.shape[0])),
    )
    if not on_known:
        attended_q = [attended_all[:, q * out_part : (q + 1) * out_part] for q in range(4)]
        last_rights = [
            jnp.concatenate([fill(proj_grad[q], gains_end), fill(attended_q[q], out_fill)], axis=1)
            for q in range(4)
        ]
    lefts = [
        item.T
        for item in (normed_out, embed_scaled, normed_two, mlp_branch, normed_one, attn_branch)
    ]
    rights = [
        logit_grad,
        [jnp.concatenate([up_input[q], activated[q]], axis=1) for q in range(4)],
        last_rights,
    ]
    half_ff = ff_part // 2
    layout = (
        ((0, 0, vocab_part, 512),),
        ((2, 0, ff_part, half_ff), (3, ff_part, ff_part, half_ff)),
        ((4, 0, gains_end, gains_end), (5, gains_end, out_fill, out_fill)),
    )
    sums, totals = reduce_grads(
        layout, lefts, rights, places, extra, facts, parts, (2, head_part, gains_end - head_part)
    )
    step_float = step_count[0].astype(jnp.float32)
    fixes = jnp.where(
        sublane == 0,
        1.0 / (1.0 - jnp.power(beta_one, step_float)),
        1.0 / (1.0 - jnp.power(beta_two, step_float)),
    )
    plans = (
        (0, False, 0, rates[0], decays[0]),
        (2, False, 0, rates[1], decays[1]),
        (2, True, gains_end, rates[2], decays[2]),
        (1, False, 0, rates[3], decays[3]),
        (1, False, ff_part, rates[4], decays[4]),
        (2, True, head_part, rates[5], decays[5]),
    )
    triples = (
        (table.T, momentum_table.T, variance_table.T),
        (joint_weight, momentum_joint, variance_joint),
        (output_weight, momentum_output, variance_output),
        (upward_weight, momentum_upward, variance_upward),
        (downward_weight.T, momentum_downward.T, variance_downward.T),
        (gains, momentum_gains, variance_gains),
    )
    updated, results = update_weights(totals, fixes, sums, plans, triples)
    updated = [item.T if place // 3 in (0, 4) else item for place, item in enumerate(updated)]
    return tuple([results[0, 0], results[1, 0]] + updated)


def solution(mesh):
    placed = (
        P("dp"),
        P("dp", None),
        P("dp"),
        P("dp"),
        P(),
        P("tensor", "dp"),
        P("dp", "tensor"),
        P("tensor", "dp"),
        P("dp", "tensor"),
        P("tensor", "dp"),
        P(None, "dp"),
        P("tensor", "dp"),
        P("dp", "tensor"),
        P("tensor", "dp"),
        P("dp", "tensor"),
        P("tensor", "dp"),
        P(None, "dp"),
        P("tensor", "dp"),
        P("dp", "tensor"),
        P("tensor", "dp"),
        P("dp", "tensor"),
        P("tensor", "dp"),
        P(None, "dp"),
    )
    return jax.shard_map(
        per_device,
        mesh=mesh,
        in_specs=placed,
        out_specs=(
            P(),
            P(),
            P("tensor", "dp"),
            P("tensor", "dp"),
            P("tensor", "dp"),
            P("dp", "tensor"),
            P("dp", "tensor"),
            P("dp", "tensor"),
            P("tensor", "dp"),
            P("tensor", "dp"),
            P("tensor", "dp"),
            P("dp", "tensor"),
            P("dp", "tensor"),
            P("dp", "tensor"),
            P("tensor", "dp"),
            P("tensor", "dp"),
            P("tensor", "dp"),
            P(None, "dp"),
            P(None, "dp"),
            P(None, "dp"),
        ),
        check_vma=False,
    )
```

```python
import functools

import jax
import jax.numpy as jnp
from jax import lax
from jax.experimental import pallas as pl
from jax.experimental.pallas import tpu as pltpu
from jax.sharding import PartitionSpec as P

D = 768
HEAD_DIM = 64
VOCAB = 8192
SEQ_LEN = 1024
DOCS = 4
T_DIFF = 1000


eps_norm = 1e-06
neg_fill = -1000000000.0
beta_one = 0.9
beta_two = 0.999
adam_eps = 1e-08
clip_at = 0.02
rates = (0.05, 0.03, 0.25, 0.03, 0.03, 0.3)
decays = (0.1, 0.1, 0.1, 0.1, 0.1, 0.0)


def norm_apply(values, gain):
    inverse = lax.rsqrt(jnp.mean(values * values, axis=-1, keepdims=True) + eps_norm)
    return values * inverse * gain


def norm_back(values, gain, upstream):
    inverse = lax.rsqrt(jnp.mean(values * values, axis=-1, keepdims=True) + eps_norm)
    gain_grad = jnp.sum(upstream * values * inverse, axis=0)
    scaled = upstream * gain
    inner = jnp.mean(scaled * values, axis=-1, keepdims=True)
    return (inverse * (scaled - values * inverse * inverse * inner), gain_grad)


def rotate(values, cosine, sine):
    middle = values.shape[-1] // 2
    front_part = values[..., :middle]
    back_part = values[..., middle:]
    return jnp.concatenate(
        [front_part * cosine - back_part * sine, back_part * cosine + front_part * sine], axis=-1
    )


def groups_of(count):
    groups, bit, width = [], 1, 1
    while bit < count:
        masks = [bit]
        if width == 2 and bit * 2 < count:
            masks = [bit, 2 * bit, 3 * bit]
            bit = bit * 2
        groups.append(masks)
        bit, width = bit * 2, 2
    return groups


def swap(value, axis, mask):
    size = lax.axis_size(axis)
    return lax.ppermute(value, axis, [(place, place ^ mask) for place in range(size)])


def spread(value, masks):
    return jnp.concatenate([value] + [swap(value, "dp", mask) for mask in masks], axis=0)


def gather_all(value, x_last):
    groups = groups_of(lax.axis_size("dp"))
    for masks in groups[:0:-1]:
        value = spread(value, masks)
    if x_last:
        value = spread(value, groups[0])
        other = swap(value, "tensor", 2)
    else:
        other = swap(value, "tensor", 2)
        value = spread(value, groups[0])
        other = spread(other, groups[0])
    return [value, other, swap(value, "tensor", 1), swap(other, "tensor", 1)]


MESH = pl.DeviceIdType.MESH


def neighbours():
    column, row = lax.axis_index("dp"), lax.axis_index("tensor")
    return {
        "x": (column, (row + 2) % 4),
        "c": (column, row + 1 - 2 * (row % 2)),
        "y": (column + 1 - 2 * (column % 2), row),
        "up": (column + 2, row),
        "down": (column - 2, row),
    }


def meet(z, devices):
    barrier = pltpu.get_barrier_semaphore()

    def greet(name):
        pl.semaphore_signal(barrier, inc=1, device_id=devices[name], device_id_type=MESH)

    for name in ("x", "c", "y"):
        greet(name)
    pl.when(z < 3)(lambda: greet("up"))
    pl.when(z > 0)(lambda: greet("down"))
    pl.semaphore_wait(barrier, 3 + (z + 2) // 3 + (5 - z) // 3)


def start_body(items, *refs):
    ins = refs[:items]
    places, cosine, sine, seg_row, seg_col = refs[items : items + 5]
    refs = refs[items + 5 :]
    outs = [refs[4 * item : 4 * item + 4] for item in range(items)]
    embedded_out, normed, packed, lse, attended = refs[4 * items : 4 * items + 5]
    refs = refs[4 * items + 5 :]
    side_sem, z_sem, recv_sem, own_sem, keep_sem = refs[:5]
    staged = refs[5:7]
    attend_refs = refs[7:]
    column = lax.axis_index("dp")
    z = column // 2
    devices = neighbours()
    meet(z, devices)
    shard = [item.shape[0] for item in ins]
    piece = [item // 2 for item in shard]

    def base(item, quarter):
        return staged[item].at[quarter] if item < 2 else outs[item][quarter]

    def mirror(source):
        return source + 1 - 2 * (source % 2)

    def view(item, part, quarter, source):
        start = pl.multiple_of(source * shard[item] + part * piece[item], 8)
        return base(item, quarter).at[pl.ds(start, piece[item])]

    def copy(item, part, quarter, source, to_quarter, name, send, own=False):
        here = view(item, part, quarter, source)
        if own:
            here = ins[item].at[pl.ds(part * piece[item], piece[item])]
        return pltpu.make_async_remote_copy(
            src_ref=here,
            dst_ref=view(item, part, to_quarter, source),
            send_sem=send,
            recv_sem=recv_sem.at[item, part, to_quarter, source],
            device_id=devices[name],
            device_id_type=MESH,
        )

    def arrived(item, part, quarter, source):
        copy(item, part, quarter, source, quarter, "x", side_sem.at[0, item]).wait_recv()

    def send_x(item, part, source, own=False):
        copy(item, part, 0, source, 2, "x", side_sem.at[0, item], own).start()

    def send_y(item, part, quarter, source, own=False):
        copy(item, part, quarter, source, quarter, "y", side_sem.at[1, item], own).start()

    def send_c(item, part, quarter, source, own=False):
        copy(item, part, quarter, source, quarter + 1, "c", side_sem.at[2 + quarter // 2, item], own).start()

    def send_z(item, part, source, turn, upward, own=False):
        name = "up" if upward else "down"
        copy(item, part, 0, source, 0, name, z_sem.at[item, part, 1 - upward, turn], own).start()

    def slot(turn, action):
        pl.when(z >= turn)(lambda: action(column - 2 * turn, 1))
        pl.when(z + turn <= 3)(lambda: action(column + 2 * turn, 0))

    every = [(item, part) for item in range(items) for part in range(2)]

    def local(item):
        return pltpu.make_async_copy(
            ins[item],
            base(item, 0).at[pl.ds(pl.multiple_of(column * shard[item], 8), shard[item])],
            own_sem.at[item],
        )

    def keep(item, quarter):
        return pltpu.make_async_copy(staged[item].at[quarter], outs[item][quarter], keep_sem.at[item, quarter])

    def begin(item):
        for part in range(2):
            pl.when(z < 3)(lambda: send_z(item, part, column, 0, 1, True))
            pl.when(z > 0)(lambda: send_z(item, part, column, 0, 0, True))
            send_x(item, part, column, True)
            send_y(item, part, 0, column, True)
            send_c(item, part, 0, column, True)
        local(item).start()

    def from_z(item, part, turn, source, upward):
        arrived(item, part, 0, source)
        if turn < 3:
            ahead = z < 3 if upward else z > 0
            pl.when(ahead)(lambda: send_z(item, part, source, turn, upward))
        send_x(item, part, source)
        send_y(item, part, 0, source)
        send_c(item, part, 0, source)

    def second(item, source):
        arrived(item, 0, 0, mirror(source))
        send_x(item, 0, mirror(source))
        send_c(item, 0, 0, mirror(source))
        arrived(item, 1, 2, source)
        send_y(item, 1, 2, source)
        send_c(item, 1, 2, source)

    def third(item, source):
        arrived(item, 0, 2, source)
        send_c(item, 0, 2, source)
        arrived(item, 1, 0, mirror(source))
        send_c(item, 1, 0, mirror(source))
        for part in range(2):
            arrived(item, part, 2, mirror(source))
            send_c(item, part, 2, mirror(source))

    def along_z(item, turn):
        for part in range(2):
            slot(turn, lambda source, upward: from_z(item, part, turn, source, upward))

    def onward(action, item, turn):
        if turn == 0:
            action(item, column)
        else:
            slot(turn, lambda source, upward: action(item, source))

    def complete(item):
        for part in range(2):
            for source in range(8):
                for quarter in (1, 3):
                    arrived(item, part, quarter, source)
        local(item).wait()
        if item < 2:
            for quarter in range(4):
                keep(item, quarter).start()

    rest = range(2, items)
    begin(0)
    for turn in (1, 2, 3):
        along_z(0, turn)
    begin(1)
    for turn in range(4):
        onward(second, 0, turn)
    for turn in (1, 2, 3):
        along_z(1, turn)
    for turn in range(4):
        onward(third, 0, turn)
    for item in rest:
        begin(item)
    complete(0)

    def look_up(quarter):
        def one(chunk, _):
            at = pl.ds(pl.multiple_of(chunk * 512, 512), 512)
            spots = lax.broadcasted_iota(jnp.int32, (places.shape[0], 512), 1) + chunk * 512
            hot = jnp.where(places[:, quarter : quarter + 1] == spots, 1.0, 0.0).astype(jnp.bfloat16)
            embedded_out[...] += lax.dot_general(
                hot, staged[0][quarter, :, at], (((1,), (1,)), ((), ())), preferred_element_type=jnp.float32
            )
            return 0

        lax.fori_loop(0, staged[0].shape[2] // 512, one, 0)

    embedded_out[...] = jnp.zeros_like(embedded_out)
    look_up(0)
    for turn in range(4):
        onward(second, 1, turn)
    look_up(2)
    for item in rest:
        along_z(item, 1)
    look_up(1)
    for turn in range(4):
        onward(third, 1, turn)
    for item in rest:
        along_z(item, 2)
    look_up(3)
    complete(1)
    gain = staged[1][0, :, 512:640].astype(jnp.float32).T[64:65]
    value = embedded_out[...] * D**0.5
    embedded_out[...] = value
    inverse = lax.rsqrt(jnp.mean(value * value, axis=-1, keepdims=True) + eps_norm)
    normed[...] = (value * inverse * gain).astype(jnp.bfloat16)
    for item in rest:
        along_z(item, 3)

    def between(stage):
        for item in rest:
            if stage == 0:
                onward(second, item, 0)
                onward(second, item, 1)
            if stage == 1:
                onward(second, item, 2)
                onward(second, item, 3)
            if stage in (3, 4, 5):
                onward(third, item, (0, 1, 2)[stage - 3])
            if stage == 6:
                onward(third, item, 3)

    attend_steps(
        normed, [staged[1].at[q] for q in range(4)], cosine, sine, seg_row, seg_col, packed, lse, attended, between, *attend_refs
    )
    for item in rest:
        complete(item)
    for item in range(2):
        for quarter in range(4):
            keep(item, quarter).wait()
    for item in range(items):
        for way, count in enumerate((12, 12, 16, 16)):
            lead = base(item, 0).at[pl.ds(0, count * piece[item])]
            pltpu.make_async_remote_copy(
                src_ref=lead,
                dst_ref=lead,
                send_sem=side_sem.at[way, item],
                recv_sem=recv_sem.at[item, 0, 0, 0],
                device_id=devices["x"],
                device_id_type=MESH,
            ).wait_send()
    for item, part in every:
        for turn in range(3):
            pl.when((z < 3) & (z >= turn))(
                lambda: copy(item, part, 0, column, 0, "up", z_sem.at[item, part, 0, turn], True).wait_send()
            )
            pl.when((z > 0) & (z + turn <= 3))(
                lambda: copy(item, part, 0, column, 0, "down", z_sem.at[item, part, 1, turn], True).wait_send()
            )


def start_kernel(shards, places, cosine, sine, seg_row, seg_col):
    items = len(shards)
    anywhere = pl.BlockSpec(memory_space=pl.ANY)
    inside = pl.BlockSpec(memory_space=pltpu.VMEM)
    whole, rows = lax.axis_size("dp"), places.shape[0]
    full = [(item.shape[0] * whole, item.shape[1]) for item in shards]
    shapes = [jax.ShapeDtypeStruct(shape, jnp.bfloat16) for shape in full for _ in range(4)]
    flat = pl.pallas_call(
        functools.partial(start_body, items),
        name="start",
        out_shape=shapes
        + [
            jax.ShapeDtypeStruct((rows, full[0][0]), jnp.float32),
            jax.ShapeDtypeStruct((rows, full[0][0]), jnp.bfloat16),
            jax.ShapeDtypeStruct((6, 2 * rows, 256), jnp.bfloat16),
            jax.ShapeDtypeStruct((8, 2 * rows), jnp.float32),
            jax.ShapeDtypeStruct((rows, 768), jnp.bfloat16),
        ],
        in_specs=[anywhere] * items + [inside] * 5,
        out_specs=[anywhere] * (4 * items) + [inside] * 5,
        scratch_shapes=[
            pltpu.SemaphoreType.DMA((4, items)),
            pltpu.SemaphoreType.DMA((items, 2, 2, 3)),
            pltpu.SemaphoreType.DMA((items, 2, 4, 8)),
            pltpu.SemaphoreType.DMA((items,)),
            pltpu.SemaphoreType.DMA((2, 4)),
            pltpu.VMEM((4, *full[0]), jnp.bfloat16),
            pltpu.VMEM((4, *full[1]), jnp.bfloat16),
            pltpu.VMEM((6, rows, 256), jnp.bfloat16),
            pltpu.VMEM((6, 2 * rows, 128), jnp.bfloat16),
            pltpu.VMEM((6, rows, 128), jnp.bfloat16),
            pltpu.SemaphoreType.DMA((6,)),
            pltpu.SemaphoreType.DMA((6,)),
            pltpu.SemaphoreType.DMA((6,)),
            pltpu.SemaphoreType.DMA((6,)),
        ],
        compiler_params=pltpu.CompilerParams(
            collective_id=0, has_side_effects=True, vmem_limit_bytes=56 << 20
        ),
    )(*shards, places, cosine, sine, seg_row, seg_col)
    return [flat[4 * item : 4 * item + 4] for item in range(items)], flat[4 * items :]


def reduce_body(layout, parts, gains_at, *refs):
    items = len(layout)
    wide_refs = [refs[4 * item : 4 * item + 4] for item in range(items)]
    refs = refs[4 * items :]
    facts, places, extra = refs[:3]
    lefts = refs[3:9]
    refs = refs[9:]
    outs, totals = refs[:items], refs[items]
    refs = refs[items + 1 :]
    held = [refs[6 * item : 6 * item + 6] for item in range(items)]
    refs = refs[6 * items :]
    side_sem, c_send, c_sem, x_sem, y_sem, zs_sem, zr_sem, load_sem, free_sem = refs[:9]
    tile, tile_row, tile_column, row_send, row_recv, column_send, column_recv = refs[9:16]
    crossed, from_c, rights = refs[16:]
    column = lax.axis_index("dp")
    z, y = column // 2, column % 2
    devices = neighbours()
    shard = [item.shape[0] for item in outs]
    piece = [item // 2 for item in shard]
    width = [item.shape[1] for item in outs]

    def load(item, quarter):
        return pltpu.make_async_copy(
            wide_refs[item][quarter],
            rights.at[quarter, :, pl.ds(0, width[item])],
            load_sem.at[item, quarter],
        )

    for quarter in range(4):
        load(0, quarter).start()
    row = lax.axis_index("tensor")
    row_peers = [(column, (row + away) % 4) for away in (1, 2, 3)]
    column_peers = [((column + away) % 8, row) for away in range(1, 8)]
    barrier = pltpu.get_barrier_semaphore()
    for device in row_peers + column_peers:
        pl.semaphore_signal(barrier, inc=1, device_id=device, device_id_type=MESH)
    pl.semaphore_wait(barrier, 10)

    def span(item, part, source):
        return pl.ds(pl.multiple_of(source * shard[item] + part * piece[item], 8), piece[item])

    def remote(src, dst, send, recv, name):
        return pltpu.make_async_remote_copy(
            src_ref=src, dst_ref=dst, send_sem=send, recv_sem=recv, device_id=devices[name], device_id_type=MESH
        )

    def c_copy(item, part, side, source, slot=0):
        here = pl.ds(pl.multiple_of(source % 2 * shard[item] + part * piece[item], 8), piece[item])
        columns = pl.ds(0, width[item])
        return remote(
            crossed.at[side, slot, here, columns],
            from_c.at[side, span(item, part, source), columns],
            c_send.at[side, slot],
            c_sem.at[item, part, side, source],
            "c",
        )

    def c_wait(item, part, side, source):
        c_copy(item, part, side, source).wait_recv()

    def c_sent(item, slot):
        for side in range(2):
            lead = crossed.at[side, slot, :, pl.ds(0, width[item])]
            remote(lead, lead, c_send.at[side, slot], c_sem.at[0, 0, 0, 0], "c").wait_send()

    def x_copy(item, part, source):
        place = source if part == 0 else source // 2
        return remote(
            held[item][0].at[1, span(item, part, source)],
            held[item][1 + part].at[place],
            side_sem.at[0, item],
            x_sem.at[item, part, place],
            "x",
        )

    def y_copy(item, part, side, source):
        return remote(
            held[item][0].at[side, span(item, part, source)],
            held[item][3].at[source // 2] if part == 0 else held[item][4].at[side, source // 2],
            side_sem.at[1, item],
            y_sem.at[item, part + side, source // 2],
            "y",
        )

    def z_copy(item, part, source, away, upward):
        return remote(
            held[item][0].at[0, span(item, part, source)],
            held[item][5].at[1 - upward, part, away],
            zs_sem.at[item, part, 1 - upward, away],
            zr_sem.at[item, part, 1 - upward, away],
            "up" if upward else "down",
        )

    def add(item, side, part, source, *others):
        total = held[item][0]
        start = source * shard[item] + part * piece[item]
        step = 16

        def one(turn, _):
            here = pl.ds(pl.multiple_of(start + turn * step, 8), step)
            value = total[side, here].astype(jnp.float32)
            for other in others:
                value = value + other(turn * step, step)
            total[side, here] = value.astype(jnp.bfloat16)
            return 0

        lax.fori_loop(0, piece[item] // step, one, 0)

    def c_part(item, side, part, source):
        start = source * shard[item] + part * piece[item]

        def read(at, step):
            here = pl.ds(pl.multiple_of(start + at, 8), step)
            return from_c[side, here, pl.ds(0, width[item])].astype(jnp.float32)

        return read

    def of(ref, *place):
        return lambda at, step: ref[(*place, pl.ds(pl.multiple_of(at, 8), step))].astype(jnp.float32)

    def mirror(source):
        return source + 1 - 2 * (source % 2)

    def target(turn):
        low = 3 - turn if turn < 2 else jnp.where(z % 3 == 0, 3 - turn, turn - 2)
        return column + 2 * (jnp.where(z < 2, low, 3 - low) - z)

    def send_c(item, turn):
        source = target(turn)
        if item > 0:
            pl.semaphore_wait(free_sem, 1)
        for part, side, place in (
            (0, 1, source),
            (1, 1, mirror(source)),
            (0, 1, mirror(source)),
            (1, 0, mirror(source)),
            (0, 0, mirror(source)),
            (1, 1, source),
            (0, 0, source),
            (1, 0, source),
        ):
            c_copy(item, part, side, place, turn % 2).start()

    def make(item, turn):
        if 4 * item + turn >= 2:
            c_sent(item if turn >= 2 else item - 1, turn % 2)
        block = 2 * shard[item]
        rows = pl.ds(pl.multiple_of(target(turn) // 2 * block, 16), block)
        for quarter in range(4):
            if turn == 0:
                load(item, quarter).wait()
            for left, base, span_width, step in layout[item]:

                def one(chunk, _):
                    at = pl.ds(pl.multiple_of(base + chunk * step, 128), step)
                    found = jnp.dot(
                        lefts[left][rows], rights[quarter, :, at], preferred_element_type=jnp.float32
                    )
                    if item == 0:
                        spots = lax.broadcasted_iota(jnp.int32, (places.shape[0], step), 1) + chunk * step
                        hot = jnp.where(places[:, quarter : quarter + 1] == spots, 1.0, 0.0)
                        found += jnp.dot(
                            lefts[1][rows], hot.astype(jnp.bfloat16), preferred_element_type=jnp.float32
                        )
                    if item == gains_at[0] and base == 0:
                        found += extra[rows]
                    if quarter % 2:
                        crossed[quarter // 2, turn % 2, :, at] = found.astype(jnp.bfloat16)
                    else:
                        held[item][0][quarter // 2, rows, at] = found.astype(jnp.bfloat16)
                    return 0

                lax.fori_loop(0, span_width // step, one, 0)
        if turn == 3 and item + 1 < items:
            for quarter in range(4):
                load(item + 1, quarter).start()

    def first(item, turn):
        source = target(turn)
        for x_place, y_side in ((source, 1), (mirror(source), 0)):
            c_wait(item, 0, 1, x_place)
            add(item, 1, 0, x_place, c_part(item, 1, 0, x_place))
            x_copy(item, 0, x_place).start()
            y_place = mirror(source)
            c_wait(item, 1, y_side, y_place)
            add(item, y_side, 1, y_place, c_part(item, y_side, 1, y_place))
            y_copy(item, 1, y_side, y_place).start()

    def second(item, turn):
        source = target(turn)
        place = mirror(source)
        c_wait(item, 0, 0, place)
        x_copy(item, 0, place).wait_recv()
        add(item, 0, 0, place, c_part(item, 0, 0, place), of(held[item][1], place))
        y_copy(item, 0, 0, place).start()
        c_wait(item, 1, 1, source)
        y_copy(item, 1, 1, source).wait_recv()
        add(item, 1, 1, source, c_part(item, 1, 1, source), of(held[item][4], 1, source // 2))
        x_copy(item, 1, source).start()

    def third(item, turn):
        source = target(turn)
        for part in range(2):
            c_wait(item, part, 0, source)
            x_copy(item, part, source).wait_recv()
            y_copy(item, part, 0, source).wait_recv()
            if part == 0:
                terms = [of(held[item][1], source), of(held[item][3], source // 2)]
            else:
                terms = [of(held[item][2], source // 2), of(held[item][4], 0, source // 2)]
            add(item, 0, part, source, c_part(item, 0, part, source), *terms)
        if item + 1 < items:
            pl.semaphore_signal(free_sem, inc=1, device_id=devices["c"], device_id_type=MESH)

    def fourth(item, turn):
        source = target(turn)
        away = jnp.where(source > column, source - column, column - source) // 2

        def along(upward):
            for part in range(2):

                def more():
                    z_copy(item, part, source, away, upward).wait_recv()
                    add(item, 0, part, source, of(held[item][5], 1 - upward, part, away))

                pl.when(z > 0 if upward else z < 3)(more)
                z_copy(item, part, source, away - 1, upward).start()

        pl.when(source > column)(lambda: along(1))
        pl.when(source < column)(lambda: along(0))

    def last(item):
        square = jnp.zeros((), jnp.float32)
        for part in range(2):
            for upward in (1, 0):
                pl.when(z > 0 if upward else z < 3)(
                    lambda: z_copy(item, part, column, 0, upward).wait_recv()
                )
            start = column * shard[item] + part * piece[item]

            def one(turn, square):
                at = pl.multiple_of(turn * 16, 8)
                value = held[item][0][0, pl.ds(pl.multiple_of(start + at, 8), 16)].astype(jnp.float32)
                below = held[item][5][0, part, 0, pl.ds(at, 16)].astype(jnp.float32)
                above = held[item][5][1, part, 0, pl.ds(at, 16)].astype(jnp.float32)
                value = value + jnp.where(z > 0, below, 0.0) + jnp.where(z < 3, above, 0.0)
                outs[item][pl.ds(pl.multiple_of(part * piece[item] + at, 8), 16)] = value
                square_here = value * value
                if item == gains_at[0]:
                    lane = lax.broadcasted_iota(jnp.int32, value.shape, 1)
                    repeated = (lane >= gains_at[1]) & (lane < gains_at[1] + gains_at[2])
                    square_here = jnp.where(repeated, square_here / parts, square_here)
                return square + jnp.sum(square_here)

            square = lax.fori_loop(0, piece[item] // 16, one, square)
        return square

    steps = [(item, turn) for item in range(items) for turn in range(4)]
    count = len(steps)
    make(*steps[0])
    send_c(*steps[0])
    for turn in range(count + 3):
        if turn < count:
            first(*steps[turn])
        if turn + 1 < count:
            make(*steps[turn + 1])
            send_c(*steps[turn + 1])
        if 0 <= turn - 1 < count:
            second(*steps[turn - 1])
        if 0 <= turn - 2 < count:
            third(*steps[turn - 2])
        if 0 <= turn - 3 < count and (turn - 3) % 4 < 3:
            fourth(*steps[turn - 3])
    square = sum([last(item) for item in range(items)])
    sublane = lax.broadcasted_iota(jnp.int32, (8, 128), 0)
    tile[...] = jnp.where(sublane == 0, square, facts[...])

    def exchange(value, slots, here, peers, sources, send, recv):
        slots[here] = value

        def crossing(place, device, source):
            return pltpu.make_async_remote_copy(
                src_ref=slots.at[here],
                dst_ref=slots.at[source],
                send_sem=send.at[place],
                recv_sem=recv.at[source],
                device_id=device,
                device_id_type=MESH,
            )

        for place, device in enumerate(peers):
            crossing(place, device, here).start()
        for place, device in enumerate(peers):
            crossing(place, device, sources[place]).wait_recv()
        total = slots[0]
        for place in range(1, len(peers) + 1):
            total = total + slots[place]
        for place, device in enumerate(peers):
            crossing(place, device, here).wait_send()
        return total

    along_row = exchange(
        tile[...], tile_row, row, row_peers, [(row + away) % 4 for away in (1, 2, 3)], row_send, row_recv
    )
    totals[...] = exchange(
        along_row,
        tile_column,
        column,
        column_peers,
        [(column + away) % 8 for away in range(1, 8)],
        column_send,
        column_recv,
    )
    for slot in range(2):
        c_sent(items - 1, slot)
    for item in range(items):
        for way, count in enumerate((12, 12)):
            lead = held[item][0].at[0, pl.ds(0, count * piece[item])]
            remote(lead, lead, side_sem.at[way, item], c_sem.at[item, 0, 0, 0], "x").wait_send()
        for part in range(2):
            for away in range(3):
                pl.when((z < 3) & (z + away + 1 <= 3))(
                    lambda: z_copy(item, part, column, away, 1).wait_send()
                )
                pl.when((z > 0) & (z - away - 1 >= 0))(
                    lambda: z_copy(item, part, column, away, 0).wait_send()
                )


def reduce_kernel(layout, lefts, rights, places, extra, facts, parts, gains_at, tag):
    items = len(layout)
    anywhere = pl.BlockSpec(memory_space=pl.ANY)
    inside = pl.BlockSpec(memory_space=pltpu.VMEM)
    whole = lax.axis_size("dp")
    rows, depth = lefts[0].shape
    half = rows // (2 * whole)
    widths = [item[0].shape[1] for item in rights]
    shapes, scratch = [], []
    for width in widths:
        shapes.append(jax.ShapeDtypeStruct((rows // whole, width), jnp.float32))
        for lead in ((2, rows), (8, half), (4, half), (4, half), (2, 4, half), (2, 2, 3, half)):
            scratch.append(pltpu.VMEM((*lead, width), jnp.bfloat16))
    shapes.append(jax.ShapeDtypeStruct((8, 128), jnp.float32))
    found = pl.pallas_call(
        functools.partial(reduce_body, layout, parts, gains_at),
        name="reduce_grads",
        out_shape=shapes,
        in_specs=[anywhere] * (4 * items) + [inside] * (3 + len(lefts)),
        out_specs=[inside] * (items + 1),
        scratch_shapes=scratch
        + [
            pltpu.SemaphoreType.DMA((2, items)),
            pltpu.SemaphoreType.DMA((2, 2)),
            pltpu.SemaphoreType.DMA((items, 2, 2, 8)),
            pltpu.SemaphoreType.DMA((items, 2, 8)),
            pltpu.SemaphoreType.DMA((items, 3, 4)),
            pltpu.SemaphoreType.DMA((items, 2, 2, 3)),
            pltpu.SemaphoreType.DMA((items, 2, 2, 3)),
            pltpu.SemaphoreType.DMA((items, 4)),
            pltpu.SemaphoreType.REGULAR,
            pltpu.VMEM((8, 128), jnp.float32),
            pltpu.VMEM((4, 8, 128), jnp.float32),
            pltpu.VMEM((8, 8, 128), jnp.float32),
            pltpu.SemaphoreType.DMA((3,)),
            pltpu.SemaphoreType.DMA((4,)),
            pltpu.SemaphoreType.DMA((7,)),
            pltpu.SemaphoreType.DMA((8,)),
            pltpu.VMEM((2, 2, 4 * half, max(widths)), jnp.bfloat16),
            pltpu.VMEM((2, rows, max(widths)), jnp.bfloat16),
            pltpu.VMEM((4, depth, max(widths)), jnp.bfloat16),
        ],
        compiler_params=pltpu.CompilerParams(
            collective_id=tag, has_side_effects=True, vmem_limit_bytes=60 << 20
        ),
    )(*[item for quarters in rights for item in quarters], facts, places, extra, *lefts)
    return found[:-1], found[-1]


def update_body(sources, plans, *refs):
    count = len(plans)
    totals, fixes, grads = refs[0], refs[1], refs[2 : 2 + sources]
    refs = refs[2 + sources :]
    triples = [refs[3 * place : 3 * place + 3] for place in range(count)]
    outs = [refs[3 * (count + place) : 3 * (count + place) + 3] for place in range(count)]
    square, loss, real = totals[0:1, :], totals[1:2, :], totals[2:3, :]
    norm = jnp.sqrt(square) / real
    refs[6 * count][...] = jnp.concatenate([loss / real, norm] + [norm] * 6, axis=0)
    scale = (jnp.minimum(1.0, clip_at / norm) / real)[:, 0:1]
    over_one, over_two = fixes[0:1, 0:1], fixes[1:2, 0:1]

    def renew(place, grad, rows):
        source, turned, first, rate, decay = plans[place]
        weight, one, two = triples[place]
        clipped = grad * scale
        moment_one = beta_one * one[rows] + (1.0 - beta_one) * clipped
        moment_two = beta_two * two[rows] + (1.0 - beta_two) * clipped * clipped
        stepped = moment_one * over_one / (jnp.sqrt(moment_two * over_two) + adam_eps)
        outs[place][0][rows] = moment_one
        outs[place][1][rows] = moment_two
        outs[place][2][rows] = weight[rows] - rate * (stepped + decay * weight[rows])

    for place in range(count):
        source, turned, first, rate, decay = plans[place]
        rows, columns = triples[place][0].shape
        if turned and rows >= 128:
            for at in range(0, rows, 128):
                span = min(128, rows - at)
                block = grads[source][:, first + at : first + at + span].T
                renew(place, block, pl.ds(at, span))
        elif turned:
            start = first // 128 * 128
            block = grads[source][:, start : start + 128].T
            renew(place, block[first - start : first - start + rows], pl.ds(0, rows))
        else:
            for at in range(0, rows, 32):
                renew(place, grads[source][pl.ds(at, 32), first : first + columns], pl.ds(at, 32))


def update_kernel(totals, fixes, grads, plans, triples):
    inside = pl.BlockSpec(memory_space=pltpu.VMEM)
    flat = [item for triple in triples for item in triple]
    outs = [jax.ShapeDtypeStruct(item.shape, item.dtype) for item in flat] + [
        jax.ShapeDtypeStruct((8, 128), jnp.float32)
    ]
    found = pl.pallas_call(
        functools.partial(update_body, len(grads), plans),
        name="update_weights",
        out_shape=outs,
        in_specs=[inside] * (2 + len(grads) + len(flat)),
        out_specs=[inside] * len(outs),
        compiler_params=pltpu.CompilerParams(vmem_limit_bytes=60 << 20),
    )(totals, fixes, *grads, *flat)
    return found[:-1], found[-1]


def turn_halves(tile, cosine, sine):
    lane = lax.broadcasted_iota(jnp.int32, tile.shape, 1)
    other = jnp.where(lane % 64 < 32, pltpu.roll(tile, 96, 1), pltpu.roll(tile, 32, 1))
    return tile * cosine + other * sine


def greet_core(device):
    barrier = pltpu.get_barrier_semaphore()
    pl.semaphore_signal(barrier, inc=1, device_id=device, device_id_type=MESH)
    pl.semaphore_wait(barrier, 1)


def attend_steps(normed, joints, cosine, sine, seg_row, seg_col, packed, lse, attended, between, leaving, heads_out, heads_in, send_sem, recv_sem, out_send, out_recv):
    device = neighbours()["c"]
    rows = normed.shape[0]

    def project(joint, put):
        found = jnp.dot(normed[...], joint[...], preferred_element_type=jnp.float32)
        for head in range(3):
            pair = turn_halves(found[:, 192 * head : 192 * head + 128], cosine[...], sine[...])
            value = found[:, 192 * head + 128 : 192 * head + 192]
            put(head, pair.astype(jnp.bfloat16), value.astype(jnp.bfloat16))

    def crossing(place):
        return pltpu.make_async_remote_copy(
            src_ref=leaving.at[place],
            dst_ref=packed.at[place, pl.ds(rows, rows)],
            send_sem=send_sem.at[place],
            recv_sem=recv_sem.at[place],
            device_id=device,
            device_id_type=MESH,
        )

    for side, joint in enumerate((joints[1], joints[3])):

        def put(head, pair, value):
            leaving[3 * side + head, :, 0:128] = pair
            leaving[3 * side + head, :, 128:192] = value
            crossing(3 * side + head).start()

        project(joint, put)
    for side, joint in enumerate((joints[0], joints[2])):

        def put(head, pair, value):
            packed[3 * side + head, pl.ds(0, rows), 0:128] = pair
            packed[3 * side + head, pl.ds(0, rows), 128:192] = value

        project(joint, put)

    def one_head(place):
        keys = packed[place, :, 0:128][:, 64:128]
        values_t = packed[place, :, 128:256][:, 0:64].astype(jnp.float32).T.astype(jnp.bfloat16)

        def block(turn, _):
            at = pl.ds(pl.multiple_of(turn * 256, 256), 256)
            query = packed[place, at, 0:128][:, 0:64]
            scores = lax.dot_general(
                keys, query, (((1,), (1,)), ((), ())), preferred_element_type=jnp.float32
            ) * HEAD_DIM ** (-0.5)
            scores = jnp.where(seg_col[:, 0:1] == seg_row[0:1, at], scores, neg_fill)
            top = jnp.max(scores, axis=0, keepdims=True)
            expd = jnp.exp(scores - top)
            summed = jnp.sum(expd, axis=0, keepdims=True)
            probs = (expd * (1.0 / summed)).astype(jnp.bfloat16)
            found = jnp.dot(values_t, probs, preferred_element_type=jnp.float32)
            lse[pl.ds(place, 1), at] = top + jnp.log(summed)
            heads_out[place, at, 0:64] = found.T.astype(jnp.bfloat16)
            return 0

        lax.fori_loop(0, 2 * rows // 256, block, 0)

    between(0)
    for place in range(6):
        crossing(place).wait_recv()
    for place in range(6):
        one_head(place)
        between(1 + place)

    def returning(place):
        return pltpu.make_async_remote_copy(
            src_ref=heads_out.at[place, pl.ds(rows, rows)],
            dst_ref=heads_in.at[place],
            send_sem=out_send.at[place],
            recv_sem=out_recv.at[place],
            device_id=device,
            device_id_type=MESH,
        )

    for place in range(6):
        returning(place).start()
    for place in range(6):
        attended[:, 64 * place : 64 * place + 64] = heads_out[place, pl.ds(0, rows), 0:64]
    for place in range(6):
        returning(place).wait_recv()
        attended[:, 384 + 64 * place : 448 + 64 * place] = heads_in[place, :, 0:64]
    for place in range(6):
        crossing(place).wait_send()
        returning(place).wait_send()


def attend_back_body(grad_out, packed, lse, attended, cosine, sine, seg_row, seg_col, p0, p1, p2, p3, r0, r1, r2, r3, grads, leaving, keys_t, probs, prob_grads, found, going, coming, send_sem, recv_sem, out_send, out_recv):
    device = neighbours()["c"]
    rows = grad_out.shape[0]
    greet_core(device)

    def crossing(place):
        return pltpu.make_async_remote_copy(
            src_ref=leaving.at[place],
            dst_ref=grads.at[place, pl.ds(rows, rows)],
            send_sem=send_sem.at[place],
            recv_sem=recv_sem.at[place],
            device_id=device,
            device_id_type=MESH,
        )

    for place in range(6):
        leaving[place, :, 0:64] = grad_out[:, 384 + 64 * place : 448 + 64 * place]
        crossing(place).start()
        grads[place, pl.ds(0, rows), 0:64] = grad_out[:, 64 * place : 64 * place + 64]
    nothing = jnp.zeros((rows, 64), jnp.bfloat16)
    for order, (part, right) in enumerate(((p0, r0), (p2, r2), (p1, r1), (p3, r3))):
        part[:, 576:640] = nothing
        right[:, 576:640] = nothing
        right[:, 640:832] = attended[:, 192 * order : 192 * order + 192]
        right[:, 832:896] = nothing
    for place in range(6):
        crossing(place).wait_recv()

    def one_head(place):
        query = packed[place, :, 0:128][:, 0:64]
        wide_keys = packed[place, :, 0:128][:, 64:128].astype(jnp.float32)
        keys_t[...] = wide_keys.T.astype(jnp.bfloat16)
        grad = grads[place, :, 0:64]
        stat = lse[pl.ds(place, 1), :]

        def score(turn, inner):
            at = pl.ds(pl.multiple_of(turn * 256, 256), 256)
            keys = packed[place, at, 0:128][:, 64:128]
            values = packed[place, at, 128:256][:, 0:64]
            scores = lax.dot_general(
                keys, query, (((1,), (1,)), ((), ())), preferred_element_type=jnp.float32
            ) * HEAD_DIM ** (-0.5)
            scores = jnp.where(seg_col[at, 0:1] == seg_row[0:1, :], scores, neg_fill)
            prob = jnp.exp(scores - stat)
            prob_grad = lax.dot_general(
                values, grad, (((1,), (1,)), ((), ())), preferred_element_type=jnp.float32
            )
            probs[at] = prob
            prob_grads[at] = prob_grad
            value_grad = jnp.dot(prob.astype(jnp.bfloat16), grad, preferred_element_type=jnp.float32)
            found[place, at, 128:192] = value_grad
            return inner + jnp.sum(prob * prob_grad, axis=0, keepdims=True)

        inner = lax.fori_loop(0, 2 * rows // 256, score, jnp.zeros((1, 2 * rows), jnp.float32))

        def spread_back(turn, query_grad):
            at = pl.ds(pl.multiple_of(turn * 256, 256), 256)
            score_grad = (probs[at] * (prob_grads[at] - inner)).astype(jnp.bfloat16)
            key_grad = jnp.dot(score_grad, query, preferred_element_type=jnp.float32)
            found[place, at, 64:128] = key_grad * HEAD_DIM ** (-0.5)
            return query_grad + jnp.dot(keys_t[:, at], score_grad, preferred_element_type=jnp.float32)

        query_grad = lax.fori_loop(
            0, 2 * rows // 256, spread_back, jnp.zeros((64, 2 * rows), jnp.float32)
        )
        found[place, :, 0:64] = query_grad.T * HEAD_DIM ** (-0.5)

    def heads(place, _):
        one_head(place)
        return 0

    lax.fori_loop(0, 6, heads, 0)

    def returning(side):
        return pltpu.make_async_remote_copy(
            src_ref=going.at[side],
            dst_ref=coming.at[side],
            send_sem=out_send.at[side],
            recv_sem=out_recv.at[side],
            device_id=device,
            device_id_type=MESH,
        )

    for half in (1, 0):
        at = pl.ds(half * rows, rows)
        for side in range(2):
            for head in range(3):
                place = 3 * side + head
                pair = turn_halves(found[place, at, 0:128], cosine[at], -sine[at]).astype(jnp.bfloat16)
                value = found[place, at, 128:192].astype(jnp.bfloat16)
                puts = [going.at[side]] if half else [(p0, p2)[side], (r0, r2)[side]]
                for put in puts:
                    put[:, 192 * head : 192 * head + 128] = pair
                    put[:, 192 * head + 128 : 192 * head + 192] = value
            if half:
                returning(side).start()
    for side in range(2):
        returning(side).wait_recv()
        for put in ((p1, p3)[side], (r1, r3)[side]):
            put[:, 0:576] = coming[side, :, 0:576]
    for place in range(6):
        crossing(place).wait_send()
    for side in range(2):
        returning(side).wait_send()


def attend_back_kernel(grad_out, packed, lse, attended, cosine, sine, seg_row, seg_col):
    rows = grad_out.shape[0]
    inside = pl.BlockSpec(memory_space=pltpu.VMEM)
    found = pl.pallas_call(
        attend_back_body,
        name="attend_back",
        out_shape=[jax.ShapeDtypeStruct((rows, 640), jnp.bfloat16)] * 4
        + [jax.ShapeDtypeStruct((rows, 896), jnp.bfloat16)] * 4,
        in_specs=[inside] * 8,
        out_specs=[inside] * 8,
        scratch_shapes=[
            pltpu.VMEM((6, 2 * rows, 128), jnp.bfloat16),
            pltpu.VMEM((6, rows, 128), jnp.bfloat16),
            pltpu.VMEM((64, 2 * rows), jnp.bfloat16),
            pltpu.VMEM((2 * rows, 2 * rows), jnp.float32),
            pltpu.VMEM((2 * rows, 2 * rows), jnp.float32),
            pltpu.VMEM((6, 2 * rows, 256), jnp.float32),
            pltpu.VMEM((2, rows, 640), jnp.bfloat16),
            pltpu.VMEM((2, rows, 640), jnp.bfloat16),
            pltpu.SemaphoreType.DMA((6,)),
            pltpu.SemaphoreType.DMA((6,)),
            pltpu.SemaphoreType.DMA((2,)),
            pltpu.SemaphoreType.DMA((2,)),
        ],
        compiler_params=pltpu.CompilerParams(
            collective_id=3, has_side_effects=True, vmem_limit_bytes=56 << 20
        ),
    )(grad_out, packed, lse, attended, cosine, sine, seg_row, seg_col)
    return found[:4], found[4:]


def known_mesh():
    return lax.axis_size("dp") == 8 and lax.axis_size("tensor") == 4


def reduce_grads(layout, lefts, rights, places, extra, facts, parts, gains_at):
    if known_mesh():
        ordered = [[item[0], item[2], item[1], item[3]] for item in rights]
        return reduce_kernel(layout, lefts, ordered, places, extra, facts, parts, gains_at, 1)
    sums = []
    for item, products in enumerate(layout):
        quarters = []
        for quarter, mask in enumerate((0, 2, 1, 3)):
            right = rights[item][quarter]
            found = [mm(lefts[at], right[:, base : base + width]) for at, base, width, _ in products]
            if item == 0:
                spots = jnp.arange(right.shape[1], dtype=jnp.int32)[None, :]
                found[0] += mm(lefts[1], narrow(places[:, mask : mask + 1] == spots))
            if item == gains_at[0]:
                found[0] += extra
            quarters.append(narrow(jnp.concatenate(found, axis=1)))
        sums.append(reduce_all(quarters, True))
    square = sum(jnp.sum(item * item) for item in sums)
    repeated = sums[gains_at[0]][:, gains_at[1] : gains_at[1] + gains_at[2]]
    square = square - jnp.sum(repeated * repeated) * (1.0 - 1.0 / parts)
    tile = jnp.where(lax.broadcasted_iota(jnp.int32, (8, 128), 0) == 0, square, facts)
    return sums, everyone_sum(tile)


def wide(value):
    return value.astype(jnp.float32)


def narrow(value):
    return value.astype(jnp.bfloat16)


def fold(value, masks, last):
    rows = value.shape[0] // (len(masks) + 1)
    total = wide(value[:rows])
    for place, mask in enumerate(masks):
        total = total + wide(swap(value[(place + 1) * rows : (place + 2) * rows], "dp", mask))
    return total if last else narrow(total)


def reduce_all(quarters, x_first):
    groups = groups_of(lax.axis_size("dp"))
    own = narrow(wide(quarters[0]) + wide(swap(quarters[2], "tensor", 1)))
    other = narrow(wide(quarters[1]) + wide(swap(quarters[3], "tensor", 1)))
    if x_first:
        own = narrow(wide(own) + wide(swap(other, "tensor", 2)))
        own = fold(own, groups[0], len(groups) == 1)
    else:
        own = fold(own, groups[0], False)
        other = fold(other, groups[0], False)
        own = narrow(wide(own) + wide(swap(other, "tensor", 2)))
    for place in range(1, len(groups)):
        own = fold(own, groups[place], place == len(groups) - 1)
    return wide(own)


def everyone_sum(value):
    for masks in groups_of(lax.axis_size("dp")):
        value = sum([swap(value, "dp", mask) for mask in masks], value)
    for mask in (1, 2):
        value = value + swap(value, "tensor", mask)
    return value


def mm(left, right):
    return jnp.dot(left, right, preferred_element_type=jnp.float32)


def mm_nt(left, right):
    return lax.dot_general(left, right, (((1,), (1,)), ((), ())), preferred_element_type=jnp.float32)


def mm_tn(left, right):
    return lax.dot_general(left, right, (((0,), (0,)), ((), ())), preferred_element_type=jnp.float32)


def rotate_heads(values, cosine, sine):
    return rotate(values, cosine[:, None, :], sine[:, None, :])


def scores_of(query, key_rows, same_doc):
    scores = jnp.einsum(
        "qhe,khe->hqk", query, key_rows, preferred_element_type=jnp.float32
    ) * HEAD_DIM ** (-0.5)
    return jnp.where(same_doc[None], scores, neg_fill)


def split_heads(packed):
    packed = packed.reshape(packed.shape[0], -1, 3, HEAD_DIM)
    return packed[:, :, 0], packed[:, :, 1], packed[:, :, 2]


def attend(packed, same_doc):
    query, key_rows, value_rows = split_heads(packed)
    scores = scores_of(query, key_rows, same_doc)
    row_max = jnp.max(scores, axis=-1, keepdims=True)
    expd = jnp.exp(scores - row_max)
    summed = jnp.sum(expd, axis=-1, keepdims=True)
    probs = (expd / summed).astype(jnp.bfloat16)
    output = jnp.einsum("hqk,khe->qhe", probs, value_rows, preferred_element_type=jnp.float32)
    return (narrow(output).reshape(packed.shape[0], -1), (row_max + jnp.log(summed))[..., 0])


def attend_back(packed, same_doc, row_lse, grad_out, cosine, sine):
    query, key_rows, value_rows = split_heads(packed)
    grad_out = grad_out.reshape(packed.shape[0], -1, HEAD_DIM)
    scores = scores_of(query, key_rows, same_doc)
    probs = jnp.exp(scores - row_lse[..., None])
    value_grad = jnp.einsum(
        "hqk,qhe->khe", probs.astype(jnp.bfloat16), grad_out, preferred_element_type=jnp.float32
    )
    prob_grad = jnp.einsum("qhe,khe->hqk", grad_out, value_rows, preferred_element_type=jnp.float32)
    inner = jnp.sum(prob_grad * probs, axis=-1, keepdims=True)
    score_grad = (probs * (prob_grad - inner)).astype(jnp.bfloat16)
    query_grad = jnp.einsum(
        "hqk,khe->qhe", score_grad, key_rows, preferred_element_type=jnp.float32
    ) * HEAD_DIM ** (-0.5)
    key_grad = jnp.einsum(
        "hqk,qhe->khe", score_grad, query, preferred_element_type=jnp.float32
    ) * HEAD_DIM ** (-0.5)
    query_grad = rotate_heads(query_grad, cosine, -sine)
    key_grad = rotate_heads(key_grad, cosine, -sine)
    return narrow(jnp.stack([query_grad, key_grad, value_grad], axis=2).reshape(packed.shape))


def update_weights(totals, fixes, sums, plans, triples):
    if known_mesh():
        updated, results = update_kernel(totals, fixes, sums, plans, triples)
        return list(updated), results
    updated = []
    norm = jnp.sqrt(totals[0, 0]) / totals[2, 0]
    scale = jnp.minimum(1.0, clip_at / norm) / totals[2, 0]
    for (source, turned, first, rate, decay), (weight, one, two) in zip(plans, triples):
        columns = weight.shape[0] if turned else weight.shape[1]
        grad = sums[source][:, first : first + columns]
        clipped = (grad.T if turned else grad) * scale
        moment_one = beta_one * one + (1.0 - beta_one) * clipped
        moment_two = beta_two * two + (1.0 - beta_two) * clipped * clipped
        stepped = moment_one * fixes[0, 0] / (jnp.sqrt(moment_two * fixes[1, 0]) + adam_eps)
        updated.extend([moment_one, moment_two, weight - rate * (stepped + decay * weight)])
    return updated, jnp.stack([totals[1, 0] / totals[2, 0], norm])[:, None]


def per_device(
    tokens,
    lengths,
    timesteps,
    masks,
    step_count,
    table,
    joint_weight,
    output_weight,
    upward_weight,
    downward_weight,
    gains,
    momentum_table,
    momentum_joint,
    momentum_output,
    momentum_upward,
    momentum_downward,
    momentum_gains,
    variance_table,
    variance_joint,
    variance_output,
    variance_upward,
    variance_downward,
    variance_gains,
):
    place = lax.axis_index("tensor")
    parts = lax.axis_size("tensor")
    rows = tokens.shape[0] // parts
    vocab_part, head_part = table.shape[0], joint_weight.shape[1]
    out_part, ff_part = output_weight.shape[0], upward_weight.shape[1]

    gain_columns = jnp.pad(narrow(gains).T, ((0, 0), (0, 61)))
    shards = [
        narrow(table).T,
        jnp.concatenate([narrow(joint_weight), gain_columns], axis=1),
        narrow(upward_weight),
        narrow(downward_weight).T,
        narrow(output_weight).T,
    ]
    start = place * rows
    seq = start // SEQ_LEN
    mine = start - seq * SEQ_LEN
    cut = lambda array: lax.dynamic_slice(array, (start,), (rows,))
    targets = cut(tokens)
    corrupt = cut(masks) == 1
    inputs = jnp.where(corrupt, VOCAB - 1, targets)
    own_lengths = lax.dynamic_slice(lengths, (seq, 0), (1, DOCS))
    step_here = lax.dynamic_slice(timesteps, (seq,), (1,))
    theirs = mine ^ rows
    position = jnp.concatenate(
        [mine + jnp.arange(rows, dtype=jnp.int32), theirs + jnp.arange(rows, dtype=jnp.int32)]
    )
    doc_ends = jnp.cumsum(own_lengths[0])
    doc_starts = doc_ends - own_lengths[0]
    segment = jnp.sum((position[:, None] >= doc_ends[None, :]).astype(jnp.int32), axis=1)
    chosen = segment[:, None] == jnp.arange(DOCS, dtype=jnp.int32)[None, :]
    offset = position - jnp.sum(jnp.where(chosen, doc_starts[None, :], 0), axis=1)
    is_real = segment < DOCS - 1
    factor = jnp.where(step_here == 1, 1.0, T_DIFF / step_here.astype(jnp.float32))
    weights = jnp.where(corrupt & is_real[:rows], factor, 0.0)
    inverse_freq = 10000.0 ** (-jnp.arange(HEAD_DIM // 2, dtype=jnp.float32) / (HEAD_DIM // 2))
    angles = offset.astype(jnp.float32)[:, None] * inverse_freq
    cosine, sine = jnp.cos(angles), jnp.sin(angles)
    same_doc = segment[:, None] == segment[None, :]

    def hot(ids, piece):
        base = (place ^ (2 * (piece % 2) + piece // 2)) * vocab_part
        return (ids - base)[:, None] == jnp.arange(vocab_part, dtype=jnp.int32)[None, :]

    pieces = range(4)
    places = jnp.pad(
        jnp.stack([inputs - (place ^ mask) * vocab_part for mask in range(4)], axis=1),
        ((0, 0), (0, 124)),
    )

    on_known = known_mesh()
    if on_known:
        cosines = jnp.concatenate([cosine] * 4, axis=1)
        sines = jnp.concatenate([-sine, sine] * 2, axis=1)
        seg_row = jnp.broadcast_to(segment[None, :], (8, 2 * rows))
        seg_col = jnp.broadcast_to(segment[:, None], (2 * rows, 128))
        groups, (embedded, normed_one, packed, attn_lse, attended_all) = start_kernel(
            shards, places, cosines[:rows], sines[:rows], seg_row, seg_col
        )
        groups = [[item[0], item[2], item[1], item[3]] for item in groups]
    else:
        groups = [gather_all(item, True) for item in shards]
    table_q, first_group, up_q, down_q, out_q = groups
    gain_full = wide(first_group[0][:, head_part : head_part + 3]).T
    out_all = jnp.concatenate(out_q, axis=1)
    if not on_known:
        joint_q = [item[:, :head_part] for item in first_group]
        looked = sum(mm_nt(narrow(hot(inputs, piece)), table_q[piece]) for piece in pieces)
        embedded = looked * D**0.5
        normed_one = narrow(norm_apply(embedded, gain_full[0]))

        def turned(projected):
            projected = projected.reshape(rows, -1, 3, HEAD_DIM)
            query = rotate_heads(projected[:, :, 0], cosine[:rows], sine[:rows])
            key_rows = rotate_heads(projected[:, :, 1], cosine[:rows], sine[:rows])
            stacked = jnp.stack([query, key_rows, projected[:, :, 2]], axis=2)
            return narrow(stacked.reshape(rows, -1))

        packed = [turned(mm(normed_one, item)) for item in joint_q]
        whole = [
            jnp.concatenate([packed[side], swap(packed[2 + side], "tensor", 1)], axis=0)
            for side in range(2)
        ]
        attended, attn_lse = zip(*[attend(item, same_doc) for item in whole])
        attended_all = jnp.concatenate(
            [item[:rows] for item in attended]
            + [swap(item[rows:], "tensor", 1) for item in attended],
            axis=1,
        )
    after_attn = embedded + mm_nt(attended_all, out_all)
    normed_two = narrow(norm_apply(after_attn, gain_full[1]))
    pre_gelu = [mm(normed_two, item) for item in up_q]
    below = [0.5 + 0.5 * lax.erf(item * 0.5**0.5) for item in pre_gelu]
    slopes = [
        part + item * jnp.exp(-0.5 * item * item) * (0.5 / jnp.pi) ** 0.5
        for part, item in zip(below, pre_gelu)
    ]
    activated = [narrow(item * part) for part, item in zip(below, pre_gelu)]
    after_mlp = after_attn + sum(mm_nt(activated[q], down_q[q]) for q in range(4))
    normed_out = narrow(norm_apply(after_mlp, gain_full[2]))
    logits = [mm(normed_out, item) for item in table_q]
    row_max = logits[0].max(axis=1)
    for item in logits[1:]:
        row_max = jnp.maximum(row_max, item.max(axis=1))
    row_sum = sum(jnp.sum(jnp.exp(item - row_max[:, None]), axis=1) for item in logits)
    target_hot = [hot(targets, piece) for piece in pieces]
    row_pick = sum(
        jnp.sum(jnp.where(target_hot[piece], logits[piece], 0.0), axis=1) for piece in pieces
    )
    row_lse = row_max + jnp.log(row_sum)
    loss_local = jnp.sum(weights * (row_lse - row_pick))
    count_local = jnp.sum(is_real[:rows].astype(jnp.float32))

    logit_grad = [
        narrow(
            weights[:, None]
            * (jnp.exp(logits[piece] - row_lse[:, None]) - target_hot[piece].astype(jnp.float32))
        )
        for piece in pieces
    ]
    out_grad = sum(mm_nt(logit_grad[piece], table_q[piece]) for piece in pieces)
    mlp_grad, gain_three = norm_back(after_mlp, gain_full[2], out_grad)
    mlp_branch = narrow(mlp_grad)
    up_input = [
        narrow(slopes[q] * mm(mlp_branch, down_q[q])) for q in range(4)
    ]
    normed_two_grad = sum(mm_nt(up_input[q], up_q[q]) for q in range(4))
    attn_in_grad, gain_two = norm_back(after_attn, gain_full[1], normed_two_grad)
    resid_one = mlp_grad + attn_in_grad
    attn_branch = narrow(resid_one)
    attended_grad = narrow(mm(attn_branch, out_all))
    if on_known:
        proj_grad, last_rights = attend_back_kernel(
            attended_grad, packed, attn_lse, attended_all, cosines, sines, seg_row, seg_col
        )
        proj_grad = [proj_grad[q] for q in (0, 2, 1, 3)]
        last_rights = [last_rights[q] for q in (0, 2, 1, 3)]
        joint_back = first_group
    else:
        grad_parts = [attended_grad[:, q * out_part : (q + 1) * out_part] for q in range(4)]
        proj_whole = [
            attend_back(
                whole[side],
                same_doc,
                attn_lse[side],
                jnp.concatenate(
                    [grad_parts[side], swap(grad_parts[2 + side], "tensor", 1)], axis=0
                ),
                cosine,
                sine,
            )
            for side in range(2)
        ]
        proj_grad = [item[:rows] for item in proj_whole] + [
            swap(item[rows:], "tensor", 1) for item in proj_whole
        ]
        joint_back = joint_q
    normed_one_grad = sum(mm_nt(proj_grad[q], joint_back[q]) for q in range(4))
    embed_in, gain_one = norm_back(embedded, gain_full[0], normed_one_grad)
    embed_grad = resid_one + embed_in
    embed_scaled = narrow(embed_grad * D**0.5)
    sublane = lax.broadcasted_iota(jnp.int32, (8, 128), 0)
    facts = jnp.where(sublane == 1, loss_local, jnp.where(sublane == 2, count_local, 0.0))
    gains_end = (head_part + gains.shape[0] + 127) // 128 * 128
    out_fill = (out_part + 127) // 128 * 128
    fill = lambda array, columns: jnp.pad(array, ((0, 0), (0, columns - array.shape[1])))
    extra = jnp.pad(
        jnp.stack([gain_one, gain_two, gain_three]).T,
        ((0, 0), (head_part, gains_end - head_part - gains.shape[0])),
    )
    if not on_known:
        attended_q = [attended_all[:, q * out_part : (q + 1) * out_part] for q in range(4)]
        last_rights = [
            jnp.concatenate([fill(proj_grad[q], gains_end), fill(attended_q[q], out_fill)], axis=1)
            for q in range(4)
        ]
    lefts = [
        item.T
        for item in (normed_out, embed_scaled, normed_two, mlp_branch, normed_one, attn_branch)
    ]
    rights = [
        logit_grad,
        [jnp.concatenate([up_input[q], activated[q]], axis=1) for q in range(4)],
        last_rights,
    ]
    half_ff = ff_part // 2
    layout = (
        ((0, 0, vocab_part, 512),),
        ((2, 0, ff_part, half_ff), (3, ff_part, ff_part, half_ff)),
        ((4, 0, gains_end, gains_end), (5, gains_end, out_fill, out_fill)),
    )
    sums, totals = reduce_grads(
        layout, lefts, rights, places, extra, facts, parts, (2, head_part, gains_end - head_part)
    )
    step_float = step_count[0].astype(jnp.float32)
    fixes = jnp.where(
        sublane == 0,
        1.0 / (1.0 - jnp.power(beta_one, step_float)),
        1.0 / (1.0 - jnp.power(beta_two, step_float)),
    )
    plans = (
        (0, False, 0, rates[0], decays[0]),
        (2, False, 0, rates[1], decays[1]),
        (2, True, gains_end, rates[2], decays[2]),
        (1, False, 0, rates[3], decays[3]),
        (1, False, ff_part, rates[4], decays[4]),
        (2, True, head_part, rates[5], decays[5]),
    )
    triples = (
        (table.T, momentum_table.T, variance_table.T),
        (joint_weight, momentum_joint, variance_joint),
        (output_weight, momentum_output, variance_output),
        (upward_weight, momentum_upward, variance_upward),
        (downward_weight.T, momentum_downward.T, variance_downward.T),
        (gains, momentum_gains, variance_gains),
    )
    updated, results = update_weights(totals, fixes, sums, plans, triples)
    updated = [item.T if place // 3 in (0, 4) else item for place, item in enumerate(updated)]
    return tuple([results[0, 0], results[1, 0]] + updated)


def solution(mesh):
    placed = (
        P("dp"),
        P("dp", None),
        P("dp"),
        P("dp"),
        P(),
        P("tensor", "dp"),
        P("dp", "tensor"),
        P("tensor", "dp"),
        P("dp", "tensor"),
        P("tensor", "dp"),
        P(None, "dp"),
        P("tensor", "dp"),
        P("dp", "tensor"),
        P("tensor", "dp"),
        P("dp", "tensor"),
        P("tensor", "dp"),
        P(None, "dp"),
        P("tensor", "dp"),
        P("dp", "tensor"),
        P("tensor", "dp"),
        P("dp", "tensor"),
        P("tensor", "dp"),
        P(None, "dp"),
    )
    return jax.shard_map(
        per_device,
        mesh=mesh,
        in_specs=placed,
        out_specs=(
            P(),
            P(),
            P("tensor", "dp"),
            P("tensor", "dp"),
            P("tensor", "dp"),
            P("dp", "tensor"),
            P("dp", "tensor"),
            P("dp", "tensor"),
            P("tensor", "dp"),
            P("tensor", "dp"),
            P("tensor", "dp"),
            P("dp", "tensor"),
            P("dp", "tensor"),
            P("dp", "tensor"),
            P("tensor", "dp"),
            P("tensor", "dp"),
            P("tensor", "dp"),
            P(None, "dp"),
            P(None, "dp"),
            P(None, "dp"),
        ),
        check_vma=False,
    )
```

```python
import functools

import jax
import jax.numpy as jnp
from jax import lax
from jax.experimental import pallas as pl
from jax.experimental.pallas import tpu as pltpu
from jax.sharding import PartitionSpec as P

D = 768
HEAD_DIM = 64
VOCAB = 8192
SEQ_LEN = 1024
DOCS = 4
T_DIFF = 1000


eps_norm = 1e-06
neg_fill = -1000000000.0
beta_one = 0.9
beta_two = 0.999
adam_eps = 1e-08
clip_at = 0.02
rates = (0.05, 0.03, 0.25, 0.03, 0.03, 0.3)
decays = (0.1, 0.1, 0.1, 0.1, 0.1, 0.0)


def norm_apply(values, gain):
    inverse = lax.rsqrt(jnp.mean(values * values, axis=-1, keepdims=True) + eps_norm)
    return values * inverse * gain


def norm_back(values, gain, upstream):
    inverse = lax.rsqrt(jnp.mean(values * values, axis=-1, keepdims=True) + eps_norm)
    gain_grad = jnp.sum(upstream * values * inverse, axis=0)
    scaled = upstream * gain
    inner = jnp.mean(scaled * values, axis=-1, keepdims=True)
    return (inverse * (scaled - values * inverse * inverse * inner), gain_grad)


def rotate(values, cosine, sine):
    middle = values.shape[-1] // 2
    front_part = values[..., :middle]
    back_part = values[..., middle:]
    return jnp.concatenate(
        [front_part * cosine - back_part * sine, back_part * cosine + front_part * sine], axis=-1
    )


def groups_of(count):
    groups, bit, width = [], 1, 1
    while bit < count:
        masks = [bit]
        if width == 2 and bit * 2 < count:
            masks = [bit, 2 * bit, 3 * bit]
            bit = bit * 2
        groups.append(masks)
        bit, width = bit * 2, 2
    return groups


def swap(value, axis, mask):
    size = lax.axis_size(axis)
    return lax.ppermute(value, axis, [(place, place ^ mask) for place in range(size)])


def spread(value, masks):
    return jnp.concatenate([value] + [swap(value, "dp", mask) for mask in masks], axis=0)


def gather_all(value, x_last):
    groups = groups_of(lax.axis_size("dp"))
    for masks in groups[:0:-1]:
        value = spread(value, masks)
    if x_last:
        value = spread(value, groups[0])
        other = swap(value, "tensor", 2)
    else:
        other = swap(value, "tensor", 2)
        value = spread(value, groups[0])
        other = spread(other, groups[0])
    return [value, other, swap(value, "tensor", 1), swap(other, "tensor", 1)]


MESH = pl.DeviceIdType.MESH


def neighbours():
    column, row = lax.axis_index("dp"), lax.axis_index("tensor")
    return {
        "x": (column, (row + 2) % 4),
        "c": (column, row + 1 - 2 * (row % 2)),
        "y": (column + 1 - 2 * (column % 2), row),
        "up": (column + 2, row),
        "down": (column - 2, row),
    }


def meet(z, devices):
    barrier = pltpu.get_barrier_semaphore()

    def greet(name):
        pl.semaphore_signal(barrier, inc=1, device_id=devices[name], device_id_type=MESH)

    for name in ("x", "c", "y"):
        greet(name)
    pl.when(z < 3)(lambda: greet("up"))
    pl.when(z > 0)(lambda: greet("down"))
    pl.semaphore_wait(barrier, 3 + (z + 2) // 3 + (5 - z) // 3)


def start_body(items, *refs):
    ins = refs[:items]
    places, cosine, sine, seg_row, seg_col = refs[items : items + 5]
    refs = refs[items + 5 :]
    outs = [refs[4 * item : 4 * item + 4] for item in range(items)]
    embedded_out, normed, packed, lse, attended = refs[4 * items : 4 * items + 5]
    refs = refs[4 * items + 5 :]
    side_sem, z_sem, recv_sem, own_sem, keep_sem = refs[:5]
    staged = refs[5:7]
    attend_refs = refs[7:]
    column = lax.axis_index("dp")
    z = column // 2
    devices = neighbours()
    meet(z, devices)
    shard = [item.shape[0] for item in ins]
    piece = [item // 2 for item in shard]

    def base(item, quarter):
        return staged[item].at[quarter] if item < 2 else outs[item][quarter]

    def mirror(source):
        return source + 1 - 2 * (source % 2)

    def view(item, part, quarter, source):
        start = pl.multiple_of(source * shard[item] + part * piece[item], 8)
        return base(item, quarter).at[pl.ds(start, piece[item])]

    def copy(item, part, quarter, source, to_quarter, name, send, own=False):
        here = view(item, part, quarter, source)
        if own:
            here = ins[item].at[pl.ds(part * piece[item], piece[item])]
        return pltpu.make_async_remote_copy(
            src_ref=here,
            dst_ref=view(item, part, to_quarter, source),
            send_sem=send,
            recv_sem=recv_sem.at[item, part, to_quarter, source],
            device_id=devices[name],
            device_id_type=MESH,
        )

    def arrived(item, part, quarter, source):
        copy(item, part, quarter, source, quarter, "x", side_sem.at[0, item]).wait_recv()

    def send_x(item, part, source, own=False):
        copy(item, part, 0, source, 2, "x", side_sem.at[0, item], own).start()

    def send_y(item, part, quarter, source, own=False):
        copy(item, part, quarter, source, quarter, "y", side_sem.at[1, item], own).start()

    def send_c(item, part, quarter, source, own=False):
        copy(item, part, quarter, source, quarter + 1, "c", side_sem.at[2 + quarter // 2, item], own).start()

    def send_z(item, part, source, turn, upward, own=False):
        name = "up" if upward else "down"
        copy(item, part, 0, source, 0, name, z_sem.at[item, part, 1 - upward, turn], own).start()

    def slot(turn, action):
        pl.when(z >= turn)(lambda: action(column - 2 * turn, 1))
        pl.when(z + turn <= 3)(lambda: action(column + 2 * turn, 0))

    every = [(item, part) for item in range(items) for part in range(2)]

    def local(item):
        return pltpu.make_async_copy(
            ins[item],
            base(item, 0).at[pl.ds(pl.multiple_of(column * shard[item], 8), shard[item])],
            own_sem.at[item],
        )

    def keep(item, quarter):
        return pltpu.make_async_copy(staged[item].at[quarter], outs[item][quarter], keep_sem.at[item, quarter])

    def begin(item):
        for part in range(2):
            pl.when(z < 3)(lambda: send_z(item, part, column, 0, 1, True))
            pl.when(z > 0)(lambda: send_z(item, part, column, 0, 0, True))
            send_x(item, part, column, True)
            send_y(item, part, 0, column, True)
            send_c(item, part, 0, column, True)
        local(item).start()

    def from_z(item, part, turn, source, upward):
        arrived(item, part, 0, source)
        if turn < 3:
            ahead = z < 3 if upward else z > 0
            pl.when(ahead)(lambda: send_z(item, part, source, turn, upward))
        send_x(item, part, source)
        send_y(item, part, 0, source)
        send_c(item, part, 0, source)

    def second(item, source):
        arrived(item, 0, 0, mirror(source))
        send_x(item, 0, mirror(source))
        send_c(item, 0, 0, mirror(source))
        arrived(item, 1, 2, source)
        send_y(item, 1, 2, source)
        send_c(item, 1, 2, source)

    def third(item, source):
        arrived(item, 0, 2, source)
        send_c(item, 0, 2, source)
        arrived(item, 1, 0, mirror(source))
        send_c(item, 1, 0, mirror(source))
        for part in range(2):
            arrived(item, part, 2, mirror(source))
            send_c(item, part, 2, mirror(source))

    def along_z(item, turn):
        for part in range(2):
            slot(turn, lambda source, upward: from_z(item, part, turn, source, upward))

    def onward(action, item, turn):
        if turn == 0:
            action(item, column)
        else:
            slot(turn, lambda source, upward: action(item, source))

    def complete(item):
        for part in range(2):
            for source in range(8):
                for quarter in (1, 3):
                    arrived(item, part, quarter, source)
        local(item).wait()
        if item < 2:
            for quarter in range(4):
                keep(item, quarter).start()

    rest = range(2, items)
    begin(0)
    for turn in (1, 2, 3):
        along_z(0, turn)
    begin(1)
    for turn in range(4):
        onward(second, 0, turn)
    for turn in (1, 2, 3):
        along_z(1, turn)
    for turn in range(4):
        onward(third, 0, turn)
    for item in rest:
        begin(item)
    complete(0)

    def look_up(quarter):
        def one(chunk, _):
            at = pl.ds(pl.multiple_of(chunk * 512, 512), 512)
            spots = lax.broadcasted_iota(jnp.int32, (places.shape[0], 512), 1) + chunk * 512
            hot = jnp.where(places[:, quarter : quarter + 1] == spots, 1.0, 0.0).astype(jnp.bfloat16)
            embedded_out[...] += lax.dot_general(
                hot, staged[0][quarter, :, at], (((1,), (1,)), ((), ())), preferred_element_type=jnp.float32
            )
            return 0

        lax.fori_loop(0, staged[0].shape[2] // 512, one, 0)

    embedded_out[...] = jnp.zeros_like(embedded_out)
    look_up(0)
    for turn in range(4):
        onward(second, 1, turn)
    look_up(2)
    for item in rest:
        along_z(item, 1)
    look_up(1)
    for turn in range(4):
        onward(third, 1, turn)
    for item in rest:
        along_z(item, 2)
    look_up(3)
    complete(1)
    gain = staged[1][0, :, 512:640].astype(jnp.float32).T[64:65]
    value = embedded_out[...] * D**0.5
    embedded_out[...] = value
    inverse = lax.rsqrt(jnp.mean(value * value, axis=-1, keepdims=True) + eps_norm)
    normed[...] = (value * inverse * gain).astype(jnp.bfloat16)
    for item in rest:
        along_z(item, 3)

    def between(stage):
        for item in rest:
            if stage == 0:
                onward(second, item, 0)
                onward(second, item, 1)
            if stage == 1:
                onward(second, item, 2)
                onward(second, item, 3)
            if stage in (3, 4, 5):
                onward(third, item, (0, 1, 2)[stage - 3])
            if stage == 6:
                onward(third, item, 3)

    attend_steps(
        normed, [staged[1].at[q] for q in range(4)], cosine, sine, seg_row, seg_col, packed, lse, attended, between, *attend_refs
    )
    for item in rest:
        complete(item)
    for item in range(2):
        for quarter in range(4):
            keep(item, quarter).wait()
    for item in range(items):
        for way, count in enumerate((12, 12, 16, 16)):
            lead = base(item, 0).at[pl.ds(0, count * piece[item])]
            pltpu.make_async_remote_copy(
                src_ref=lead,
                dst_ref=lead,
                send_sem=side_sem.at[way, item],
                recv_sem=recv_sem.at[item, 0, 0, 0],
                device_id=devices["x"],
                device_id_type=MESH,
            ).wait_send()
    for item, part in every:
        for turn in range(3):
            pl.when((z < 3) & (z >= turn))(
                lambda: copy(item, part, 0, column, 0, "up", z_sem.at[item, part, 0, turn], True).wait_send()
            )
            pl.when((z > 0) & (z + turn <= 3))(
                lambda: copy(item, part, 0, column, 0, "down", z_sem.at[item, part, 1, turn], True).wait_send()
            )


def start_kernel(shards, places, cosine, sine, seg_row, seg_col):
    items = len(shards)
    anywhere = pl.BlockSpec(memory_space=pl.ANY)
    inside = pl.BlockSpec(memory_space=pltpu.VMEM)
    whole, rows = lax.axis_size("dp"), places.shape[0]
    full = [(item.shape[0] * whole, item.shape[1]) for item in shards]
    shapes = [jax.ShapeDtypeStruct(shape, jnp.bfloat16) for shape in full for _ in range(4)]
    flat = pl.pallas_call(
        functools.partial(start_body, items),
        name="start",
        out_shape=shapes
        + [
            jax.ShapeDtypeStruct((rows, full[0][0]), jnp.float32),
            jax.ShapeDtypeStruct((rows, full[0][0]), jnp.bfloat16),
            jax.ShapeDtypeStruct((6, 2 * rows, 256), jnp.bfloat16),
            jax.ShapeDtypeStruct((8, 2 * rows), jnp.float32),
            jax.ShapeDtypeStruct((rows, 768), jnp.bfloat16),
        ],
        in_specs=[anywhere] * items + [inside] * 5,
        out_specs=[anywhere] * (4 * items) + [inside] * 5,
        scratch_shapes=[
            pltpu.SemaphoreType.DMA((4, items)),
            pltpu.SemaphoreType.DMA((items, 2, 2, 3)),
            pltpu.SemaphoreType.DMA((items, 2, 4, 8)),
            pltpu.SemaphoreType.DMA((items,)),
            pltpu.SemaphoreType.DMA((2, 4)),
            pltpu.VMEM((4, *full[0]), jnp.bfloat16),
            pltpu.VMEM((4, *full[1]), jnp.bfloat16),
            pltpu.VMEM((6, rows, 256), jnp.bfloat16),
            pltpu.VMEM((6, 2 * rows, 128), jnp.bfloat16),
            pltpu.VMEM((6, rows, 128), jnp.bfloat16),
            pltpu.SemaphoreType.DMA((6,)),
            pltpu.SemaphoreType.DMA((6,)),
            pltpu.SemaphoreType.DMA((6,)),
            pltpu.SemaphoreType.DMA((6,)),
        ],
        compiler_params=pltpu.CompilerParams(
            collective_id=0, has_side_effects=True, vmem_limit_bytes=56 << 20
        ),
    )(*shards, places, cosine, sine, seg_row, seg_col)
    return [flat[4 * item : 4 * item + 4] for item in range(items)], flat[4 * items :]


def reduce_tools(layout, gains_at, parts, places, extra, lefts, wide_refs, outs, refs):
    items = len(layout)
    held = [refs[6 * item : 6 * item + 6] for item in range(items)]
    refs = refs[6 * items :]
    side_sem, c_send, c_sem, x_sem, y_sem, zs_sem, zr_sem, load_sem, free_sem = refs[:9]
    crossed, from_c, rights = refs[9:]
    column = lax.axis_index("dp")
    z = column // 2
    devices = neighbours()
    shard = [item.shape[0] for item in outs]
    piece = [item // 2 for item in shard]
    width = [item.shape[1] for item in outs]

    def load(item, quarter, which):
        sources, first_column, span = wide_refs[item][which]
        before = sum([part[2] for part in wide_refs[item][:which]])
        return pltpu.make_async_copy(
            sources[quarter].at[:, pl.ds(first_column, span)],
            rights.at[quarter, :, pl.ds(before, span)],
            load_sem.at[item, quarter, which],
        )

    def start_loads(item):
        for quarter in range(4):
            for which in range(len(wide_refs[item])):
                load(item, quarter, which).start()

    def span(item, part, source):
        return pl.ds(pl.multiple_of(source * shard[item] + part * piece[item], 8), piece[item])

    def remote(src, dst, send, recv, name):
        return pltpu.make_async_remote_copy(
            src_ref=src, dst_ref=dst, send_sem=send, recv_sem=recv, device_id=devices[name], device_id_type=MESH
        )

    def c_copy(item, side, source, slot=0):
        columns = pl.ds(0, width[item])
        block = 2 * shard[item]
        there = pl.ds(pl.multiple_of(source // 2 * block, 16), block)
        return remote(
            crossed.at[side, slot, :, columns],
            from_c.at[side, there, columns],
            c_send.at[side, slot],
            c_sem.at[item, side, source // 2],
            "c",
        )

    def c_sent(item, slot):
        for side in range(2):
            c_copy(item, side, 0, slot).wait_send()

    def x_copy(item, part, source):
        place = source if part == 0 else source // 2
        return remote(
            held[item][0].at[1, span(item, part, source)],
            held[item][1 + part].at[place],
            side_sem.at[0, item],
            x_sem.at[item, part, place],
            "x",
        )

    def y_copy(item, part, side, source):
        return remote(
            held[item][0].at[side, span(item, part, source)],
            held[item][3].at[source // 2] if part == 0 else held[item][4].at[side, source // 2],
            side_sem.at[1, item],
            y_sem.at[item, part + side, source // 2],
            "y",
        )

    def z_copy(item, part, source, away, upward):
        return remote(
            held[item][0].at[0, span(item, part, source)],
            held[item][5].at[1 - upward, part, away],
            zs_sem.at[item, part, 1 - upward, away],
            zr_sem.at[item, part, 1 - upward, away],
            "up" if upward else "down",
        )

    def add(item, side, part, source, *others):
        total = held[item][0]
        start = source * shard[item] + part * piece[item]
        step = 16

        def one(turn, _):
            here = pl.ds(pl.multiple_of(start + turn * step, 8), step)
            value = total[side, here]
            for other in others:
                value = value + other(turn * step, step)
            total[side, here] = value
            return 0

        lax.fori_loop(0, piece[item] // step, one, 0)

    def c_part(item, side, part, source):
        start = source * shard[item] + part * piece[item]

        def read(at, step):
            here = pl.ds(pl.multiple_of(start + at, 8), step)
            return from_c[side, here, pl.ds(0, width[item])]

        return read

    def of(ref, *place):
        return lambda at, step: ref[(*place, pl.ds(pl.multiple_of(at, 8), step))]

    def mirror(source):
        return source + 1 - 2 * (source % 2)

    def target(turn):
        low = 3 - turn if turn < 2 else jnp.where(z % 3 == 0, 3 - turn, turn - 2)
        return column + 2 * (jnp.where(z < 2, low, 3 - low) - z)

    def send_c(item, turn):
        source = target(turn)
        if item > 0:
            pl.semaphore_wait(free_sem, 1)
        for side in (1, 0):
            c_copy(item, side, source, turn % 2).start()

    def make(item, turn):
        if 4 * item + turn >= 2:
            c_sent(item if turn >= 2 else item - 1, turn % 2)
        block = 2 * shard[item]
        rows = pl.ds(pl.multiple_of(target(turn) // 2 * block, 16), block)
        for quarter in range(4):
            if turn == 0:
                for which in range(len(wide_refs[item])):
                    load(item, quarter, which).wait()
            for left, base, span_width, step in layout[item][1]:

                def one(chunk, _):
                    at = pl.ds(pl.multiple_of(base + chunk * step, 128), step)
                    found = jnp.dot(
                        lefts[left][rows], rights[quarter, :, at], preferred_element_type=jnp.float32
                    )
                    if layout[item][0] is not None:
                        spots = lax.broadcasted_iota(jnp.int32, (places.shape[0], step), 1)
                        spots = spots + (layout[item][0] + chunk * step)
                        hot = jnp.where(places[:, quarter : quarter + 1] == spots, 1.0, 0.0)
                        found += jnp.dot(
                            lefts[1][rows], hot.astype(jnp.bfloat16), preferred_element_type=jnp.float32
                        )
                    if extra is not None and item == gains_at[0] and base == 0:
                        found += extra[rows]
                    if quarter % 2:
                        crossed[quarter // 2, turn % 2, :, at] = found.astype(jnp.bfloat16)
                    else:
                        held[item][0][quarter // 2, rows, at] = found.astype(jnp.bfloat16)
                    return 0

                lax.fori_loop(0, span_width // step, one, 0)
        if turn == 3 and item + 1 < items:
            start_loads(item + 1)

    def first(item, turn):
        source = target(turn)
        for side in (1, 0):
            c_copy(item, side, source).wait_recv()
        for x_place, y_side in ((source, 1), (mirror(source), 0)):
            add(item, 1, 0, x_place, c_part(item, 1, 0, x_place))
            x_copy(item, 0, x_place).start()
            y_place = mirror(source)
            add(item, y_side, 1, y_place, c_part(item, y_side, 1, y_place))
            y_copy(item, 1, y_side, y_place).start()

    def second(item, turn):
        source = target(turn)
        place = mirror(source)
        x_copy(item, 0, place).wait_recv()
        add(item, 0, 0, place, c_part(item, 0, 0, place), of(held[item][1], place))
        y_copy(item, 0, 0, place).start()
        y_copy(item, 1, 1, source).wait_recv()
        add(item, 1, 1, source, c_part(item, 1, 1, source), of(held[item][4], 1, source // 2))
        x_copy(item, 1, source).start()

    def third(item, turn):
        source = target(turn)
        for part in range(2):
            x_copy(item, part, source).wait_recv()
            y_copy(item, part, 0, source).wait_recv()
            if part == 0:
                terms = [of(held[item][1], source), of(held[item][3], source // 2)]
            else:
                terms = [of(held[item][2], source // 2), of(held[item][4], 0, source // 2)]
            add(item, 0, part, source, c_part(item, 0, part, source), *terms)
        if item + 1 < items:
            pl.semaphore_signal(free_sem, inc=1, device_id=devices["c"], device_id_type=MESH)

    def fourth(item, turn):
        source = target(turn)
        away = jnp.where(source > column, source - column, column - source) // 2

        def along(upward):
            for part in range(2):

                def more():
                    z_copy(item, part, source, away, upward).wait_recv()
                    add(item, 0, part, source, of(held[item][5], 1 - upward, part, away))

                pl.when(z > 0 if upward else z < 3)(more)
                z_copy(item, part, source, away - 1, upward).start()

        pl.when(source > column)(lambda: along(1))
        pl.when(source < column)(lambda: along(0))

    def last(item):
        square = jnp.zeros((), jnp.float32)
        for part in range(2):
            for upward in (1, 0):
                pl.when(z > 0 if upward else z < 3)(
                    lambda: z_copy(item, part, column, 0, upward).wait_recv()
                )
            start = column * shard[item] + part * piece[item]

            def one(turn, square):
                at = pl.multiple_of(turn * 16, 8)
                value = held[item][0][0, pl.ds(pl.multiple_of(start + at, 8), 16)].astype(jnp.float32)
                below = held[item][5][0, part, 0, pl.ds(at, 16)].astype(jnp.float32)
                above = held[item][5][1, part, 0, pl.ds(at, 16)].astype(jnp.float32)
                value = value + jnp.where(z > 0, below, 0.0) + jnp.where(z < 3, above, 0.0)
                outs[item][pl.ds(pl.multiple_of(part * piece[item] + at, 8), 16)] = value
                square_here = value * value
                if extra is not None and item == gains_at[0]:
                    lane = lax.broadcasted_iota(jnp.int32, value.shape, 1)
                    repeated = (lane >= gains_at[1]) & (lane < gains_at[1] + gains_at[2])
                    square_here = jnp.where(repeated, square_here / parts, square_here)
                return square + jnp.sum(square_here)

            square = lax.fori_loop(0, piece[item] // 16, one, square)
        return square

    steps = [(item, turn) for item in range(items) for turn in range(4)]
    count = len(steps)
    def begin():
        make(*steps[0])
        send_c(*steps[0])

    def advance(turn):
        if turn < count:
            first(*steps[turn])
        if turn + 1 < count:
            make(*steps[turn + 1])
            send_c(*steps[turn + 1])
        if 0 <= turn - 1 < count:
            second(*steps[turn - 1])
        if 0 <= turn - 2 < count:
            third(*steps[turn - 2])
        if 0 <= turn - 3 < count and (turn - 3) % 4 < 3:
            fourth(*steps[turn - 3])

    def finish():
        return sum([last(item) for item in range(items)])

    def drain():
        for slot in range(2):
            c_sent(items - 1, slot)
        for item in range(items):
            for way, count in enumerate((12, 12)):
                lead = held[item][0].at[0, pl.ds(0, count * piece[item])]
                remote(lead, lead, side_sem.at[way, item], c_sem.at[item, 0, 0], "x").wait_send()
            for part in range(2):
                for away in range(3):
                    pl.when((z < 3) & (z + away + 1 <= 3))(
                        lambda: z_copy(item, part, column, away, 1).wait_send()
                    )
                    pl.when((z > 0) & (z - away - 1 >= 0))(
                        lambda: z_copy(item, part, column, away, 0).wait_send()
                    )

    return lambda: start_loads(0), begin, advance, count + 3, finish, drain


def reduce_body(layout, parts, gains_at, *refs):
    table_rights, last_rights = refs[:4], refs[4:8]
    facts, places, extra = refs[8:11]
    lefts = refs[11:15]
    table_out, last_out, totals = refs[15:18]
    refs = refs[18:]
    outs, wide_refs = [], []
    for at, products in layout:
        span = sum([product[2] for product in products])
        outs.append(last_out if at is None else table_out.at[:, pl.ds(at, span)])
        wide_refs.append([(last_rights if at is None else table_rights, at or 0, span)])
    tile, tile_row, tile_column, row_send, row_recv, column_send, column_recv = refs[:7]
    start_loads, begin, advance, turns, finish, drain = reduce_tools(
        layout, gains_at, parts, places, extra, lefts, wide_refs, outs, refs[7:]
    )
    start_loads()
    column = lax.axis_index("dp")
    row = lax.axis_index("tensor")
    row_peers = [(column, (row + away) % 4) for away in (1, 2, 3)]
    column_peers = [((column + away) % 8, row) for away in range(1, 8)]
    barrier = pltpu.get_barrier_semaphore()
    for device in row_peers + column_peers:
        pl.semaphore_signal(barrier, inc=1, device_id=device, device_id_type=MESH)
    pl.semaphore_wait(barrier, 10)
    begin()
    for turn in range(turns):
        advance(turn)
    square = finish()
    sublane = lax.broadcasted_iota(jnp.int32, (8, 128), 0)
    tile[...] = facts[...] + jnp.where(sublane == 0, square, 0.0)

    def exchange(value, slots, here, peers, sources, send, recv):
        slots[here] = value

        def crossing(place, device, source):
            return pltpu.make_async_remote_copy(
                src_ref=slots.at[here],
                dst_ref=slots.at[source],
                send_sem=send.at[place],
                recv_sem=recv.at[source],
                device_id=device,
                device_id_type=MESH,
            )

        for place, device in enumerate(peers):
            crossing(place, device, here).start()
        for place, device in enumerate(peers):
            crossing(place, device, sources[place]).wait_recv()
        total = slots[0]
        for place in range(1, len(peers) + 1):
            total = total + slots[place]
        for place, device in enumerate(peers):
            crossing(place, device, here).wait_send()
        return total

    along_row = exchange(
        tile[...], tile_row, row, row_peers, [(row + away) % 4 for away in (1, 2, 3)], row_send, row_recv
    )
    totals[...] = exchange(
        along_row,
        tile_column,
        column,
        column_peers,
        [(column + away) % 8 for away in range(1, 8)],
        column_send,
        column_recv,
    )
    drain()


def reduce_scratch(widths, products, rows, depth):
    whole = lax.axis_size("dp")
    items, half = len(widths), rows // (2 * whole)
    scratch = [
        pltpu.VMEM((*lead, width), jnp.bfloat16)
        for width in widths
        for lead in ((2, rows), (8, half), (4, half), (4, half), (2, 4, half), (2, 2, 3, half))
    ]
    return scratch + [
        pltpu.SemaphoreType.DMA((2, items)),
        pltpu.SemaphoreType.DMA((2, 2)),
        pltpu.SemaphoreType.DMA((items, 2, 4)),
        pltpu.SemaphoreType.DMA((items, 2, 8)),
        pltpu.SemaphoreType.DMA((items, 3, 4)),
        pltpu.SemaphoreType.DMA((items, 2, 2, 3)),
        pltpu.SemaphoreType.DMA((items, 2, 2, 3)),
        pltpu.SemaphoreType.DMA((items, 4, products)),
        pltpu.SemaphoreType.REGULAR,
        pltpu.VMEM((2, 2, 4 * half, max(widths)), jnp.bfloat16),
        pltpu.VMEM((2, rows, max(widths)), jnp.bfloat16),
        pltpu.VMEM((4, depth, max(widths)), jnp.bfloat16),
    ]


def reduce_kernel(layout, lefts, rights, places, extra, facts, parts, gains_at, tag):
    anywhere = pl.BlockSpec(memory_space=pl.ANY)
    inside = pl.BlockSpec(memory_space=pltpu.VMEM)
    rows, depth = lefts[0].shape
    widths = [sum([product[2] for product in products]) for _, products in layout]
    shapes = [
        jax.ShapeDtypeStruct((rows // lax.axis_size("dp"), item[0].shape[1]), jnp.float32)
        for item in rights
    ]
    shapes.append(jax.ShapeDtypeStruct((8, 128), jnp.float32))
    found = pl.pallas_call(
        functools.partial(reduce_body, layout, parts, gains_at),
        name="reduce_grads",
        out_shape=shapes,
        in_specs=[anywhere] * 8 + [inside] * (3 + len(lefts)),
        out_specs=[inside] * 3,
        scratch_shapes=[
            pltpu.VMEM((8, 128), jnp.float32),
            pltpu.VMEM((4, 8, 128), jnp.float32),
            pltpu.VMEM((8, 8, 128), jnp.float32),
            pltpu.SemaphoreType.DMA((3,)),
            pltpu.SemaphoreType.DMA((4,)),
            pltpu.SemaphoreType.DMA((7,)),
            pltpu.SemaphoreType.DMA((8,)),
        ]
        + reduce_scratch(widths, 1, rows, depth),
        compiler_params=pltpu.CompilerParams(
            collective_id=tag, has_side_effects=True, vmem_limit_bytes=60 << 20
        ),
    )(*[item for quarters in rights for item in quarters], facts, places, extra, *lefts)
    return found[:-1], found[-1]


def update_body(sources, plans, *refs):
    count = len(plans)
    totals, fixes, grads = refs[0], refs[1], refs[2 : 2 + sources]
    refs = refs[2 + sources :]
    triples = [refs[3 * place : 3 * place + 3] for place in range(count)]
    outs = [refs[3 * (count + place) : 3 * (count + place) + 3] for place in range(count)]
    square, loss, real = totals[0:1, :], totals[1:2, :], totals[2:3, :]
    norm = jnp.sqrt(square) / real
    refs[6 * count][...] = jnp.concatenate([loss / real, norm] + [norm] * 6, axis=0)
    scale = (jnp.minimum(1.0, clip_at / norm) / real)[:, 0:1]
    over_one, over_two = fixes[0:1, 0:1], fixes[1:2, 0:1]

    def renew(place, grad, rows):
        source, turned, first, rate, decay = plans[place]
        weight, one, two = triples[place]
        clipped = grad * scale
        moment_one = beta_one * one[rows] + (1.0 - beta_one) * clipped
        moment_two = beta_two * two[rows] + (1.0 - beta_two) * clipped * clipped
        stepped = moment_one * over_one / (jnp.sqrt(moment_two * over_two) + adam_eps)
        outs[place][0][rows] = moment_one
        outs[place][1][rows] = moment_two
        outs[place][2][rows] = weight[rows] - rate * (stepped + decay * weight[rows])

    for place in range(count):
        source, turned, first, rate, decay = plans[place]
        rows, columns = triples[place][0].shape
        if turned and rows >= 128:
            for at in range(0, rows, 128):
                span = min(128, rows - at)
                block = grads[source][:, first + at : first + at + span].T
                renew(place, block, pl.ds(at, span))
        elif turned:
            start = first // 128 * 128
            block = grads[source][:, start : start + 128].T
            renew(place, block[first - start : first - start + rows], pl.ds(0, rows))
        else:
            for at in range(0, rows, 32):
                renew(place, grads[source][pl.ds(at, 32), first : first + columns], pl.ds(at, 32))


def update_kernel(totals, fixes, grads, plans, triples):
    inside = pl.BlockSpec(memory_space=pltpu.VMEM)
    flat = [item for triple in triples for item in triple]
    outs = [jax.ShapeDtypeStruct(item.shape, item.dtype) for item in flat] + [
        jax.ShapeDtypeStruct((8, 128), jnp.float32)
    ]
    found = pl.pallas_call(
        functools.partial(update_body, len(grads), plans),
        name="update_weights",
        out_shape=outs,
        in_specs=[inside] * (2 + len(grads) + len(flat)),
        out_specs=[inside] * len(outs),
        compiler_params=pltpu.CompilerParams(vmem_limit_bytes=60 << 20),
    )(totals, fixes, *grads, *flat)
    return found[:-1], found[-1]


def turn_halves(tile, cosine, sine):
    lane = lax.broadcasted_iota(jnp.int32, tile.shape, 1)
    other = jnp.where(lane % 64 < 32, pltpu.roll(tile, 96, 1), pltpu.roll(tile, 32, 1))
    return tile * cosine + other * sine


def attend_steps(normed, joints, cosine, sine, seg_row, seg_col, packed, lse, attended, between, leaving, heads_out, heads_in, send_sem, recv_sem, out_send, out_recv):
    device = neighbours()["c"]
    rows = normed.shape[0]

    def project(joint, put):
        found = jnp.dot(normed[...], joint[...], preferred_element_type=jnp.float32)
        for head in range(3):
            pair = turn_halves(found[:, 192 * head : 192 * head + 128], cosine[0:rows], sine[0:rows])
            value = found[:, 192 * head + 128 : 192 * head + 192]
            put(head, pair.astype(jnp.bfloat16), value.astype(jnp.bfloat16))

    def crossing(place):
        return pltpu.make_async_remote_copy(
            src_ref=leaving.at[place],
            dst_ref=packed.at[place, pl.ds(rows, rows)],
            send_sem=send_sem.at[place],
            recv_sem=recv_sem.at[place],
            device_id=device,
            device_id_type=MESH,
        )

    for side, joint in enumerate((joints[1], joints[3])):

        def put(head, pair, value):
            leaving[3 * side + head, :, 0:128] = pair
            leaving[3 * side + head, :, 128:192] = value
            crossing(3 * side + head).start()

        project(joint, put)
    for side, joint in enumerate((joints[0], joints[2])):

        def put(head, pair, value):
            packed[3 * side + head, pl.ds(0, rows), 0:128] = pair
            packed[3 * side + head, pl.ds(0, rows), 128:192] = value

        project(joint, put)

    def one_head(place):
        keys = packed[place, :, 0:128][:, 64:128]
        values_t = packed[place, :, 128:256][:, 0:64].astype(jnp.float32).T.astype(jnp.bfloat16)

        def block(turn, _):
            at = pl.ds(pl.multiple_of(turn * 256, 256), 256)
            query = packed[place, at, 0:128][:, 0:64] * jnp.bfloat16(HEAD_DIM ** (-0.5))
            scores = lax.dot_general(
                keys, query, (((1,), (1,)), ((), ())), preferred_element_type=jnp.float32
            )
            scores = jnp.where(seg_col[:, 0:1] == seg_row[0:1, at], scores, neg_fill)
            top = jnp.max(scores, axis=0, keepdims=True)
            expd = jnp.exp(scores - top)
            summed = jnp.sum(expd, axis=0, keepdims=True)
            probs = (expd * (1.0 / summed)).astype(jnp.bfloat16)
            found = jnp.dot(values_t, probs, preferred_element_type=jnp.float32)
            lse[pl.ds(place, 1), at] = top + jnp.log(summed)
            heads_out[place, at, 0:64] = found.T.astype(jnp.bfloat16)
            return 0

        lax.fori_loop(0, 2 * rows // 256, block, 0)

    between(0)
    for place in range(6):
        crossing(place).wait_recv()
    for place in range(6):
        one_head(place)
        between(1 + place)

    def returning(place):
        return pltpu.make_async_remote_copy(
            src_ref=heads_out.at[place, pl.ds(rows, rows)],
            dst_ref=heads_in.at[place],
            send_sem=out_send.at[place],
            recv_sem=out_recv.at[place],
            device_id=device,
            device_id_type=MESH,
        )

    for place in range(6):
        returning(place).start()
    for place in range(6):
        attended[:, 64 * place : 64 * place + 64] = heads_out[place, pl.ds(0, rows), 0:64]
    for place in range(6):
        returning(place).wait_recv()
        attended[:, 384 + 64 * place : 448 + 64 * place] = heads_in[place, :, 0:64]
    for place in range(6):
        crossing(place).wait_send()
        returning(place).wait_send()


def attend_back_body(layout, *refs):
    grad_out, packed, lse, attended, cosine, sine, seg_row, seg_col, left_up, left_down = refs[:10]
    ups, downs = refs[10:14], refs[14:18]
    p0, p1, p2, p3, r0, r1, r2, r3, summed, square_out = refs[18:28]
    grads, leaving, keys_t, probs, prob_grads, found, going, coming = refs[28:36]
    send_sem, recv_sem, out_send, out_recv = refs[36:40]
    span = ups[0].shape[1]
    outs = [summed.at[:, pl.ds(0, span)], summed.at[:, pl.ds(span, span)]]
    wide_refs = [[(ups, 0, span)], [(downs, 0, span)]]
    start_loads, begin, advance, turns, finish, drain = reduce_tools(
        layout, None, None, None, None, (left_up, left_down), wide_refs, outs, refs[40:]
    )
    start_loads()
    device = neighbours()["c"]
    rows = grad_out.shape[0]
    meet(lax.axis_index("dp") // 2, neighbours())

    def crossing(place):
        return pltpu.make_async_remote_copy(
            src_ref=leaving.at[place],
            dst_ref=grads.at[place, pl.ds(rows, rows)],
            send_sem=send_sem.at[place],
            recv_sem=recv_sem.at[place],
            device_id=device,
            device_id_type=MESH,
        )

    for place in range(6):
        leaving[place, :, 0:64] = grad_out[:, 384 + 64 * place : 448 + 64 * place]
        crossing(place).start()
        grads[place, pl.ds(0, rows), 0:64] = grad_out[:, 64 * place : 64 * place + 64]
    nothing = jnp.zeros((rows, 64), jnp.bfloat16)
    for order, (part, right) in enumerate(((p0, r0), (p2, r2), (p1, r1), (p3, r3))):
        part[:, 576:640] = nothing
        right[:, 576:640] = nothing
        right[:, 640:832] = attended[:, 192 * order : 192 * order + 192]
        right[:, 832:896] = nothing
    begin()
    for place in range(6):
        crossing(place).wait_recv()

    def one_head(place):
        query = packed[place, :, 0:128][:, 0:64]
        scaled = query * jnp.bfloat16(HEAD_DIM ** (-0.5))
        wide_keys = packed[place, :, 0:128][:, 64:128].astype(jnp.float32)
        keys_t[...] = wide_keys.T.astype(jnp.bfloat16)
        grad = grads[place, :, 0:64]
        stat = lse[pl.ds(place, 1), :]

        def score(turn, inner):
            at = pl.ds(pl.multiple_of(turn * 256, 256), 256)
            keys = packed[place, at, 0:128][:, 64:128]
            values = packed[place, at, 128:256][:, 0:64]
            scores = lax.dot_general(
                keys, scaled, (((1,), (1,)), ((), ())), preferred_element_type=jnp.float32
            )
            scores = jnp.where(seg_col[at, 0:1] == seg_row[0:1, :], scores, neg_fill)
            prob = jnp.exp(scores - stat)
            prob_grad = lax.dot_general(
                values, grad, (((1,), (1,)), ((), ())), preferred_element_type=jnp.float32
            )
            probs[at] = prob
            prob_grads[at] = prob_grad
            value_grad = jnp.dot(prob.astype(jnp.bfloat16), grad, preferred_element_type=jnp.float32)
            found[place, at, 128:192] = value_grad
            return inner + jnp.sum(prob * prob_grad, axis=0, keepdims=True)

        inner = lax.fori_loop(0, 2 * rows // 256, score, jnp.zeros((1, 2 * rows), jnp.float32))

        def spread_back(turn, query_grad):
            at = pl.ds(pl.multiple_of(turn * 256, 256), 256)
            score_grad = (probs[at] * (prob_grads[at] - inner)).astype(jnp.bfloat16)
            key_grad = jnp.dot(score_grad, scaled, preferred_element_type=jnp.float32)
            found[place, at, 64:128] = key_grad
            return query_grad + jnp.dot(keys_t[:, at], score_grad, preferred_element_type=jnp.float32)

        query_grad = lax.fori_loop(
            0, 2 * rows // 256, spread_back, jnp.zeros((64, 2 * rows), jnp.float32)
        )
        found[place, :, 0:64] = query_grad.T * HEAD_DIM ** (-0.5)

    for place in range(6):
        advance(2 * place)
        if 2 * place + 1 < turns:
            advance(2 * place + 1)
        one_head(place)
    for turn in range(12, turns):
        advance(turn)

    def returning(side):
        return pltpu.make_async_remote_copy(
            src_ref=going.at[side],
            dst_ref=coming.at[side],
            send_sem=out_send.at[side],
            recv_sem=out_recv.at[side],
            device_id=device,
            device_id_type=MESH,
        )

    for half in (1, 0):
        at = pl.ds(half * rows, rows)
        for side in range(2):
            for head in range(3):
                place = 3 * side + head
                pair = turn_halves(found[place, at, 0:128], cosine[at], -sine[at]).astype(jnp.bfloat16)
                value = found[place, at, 128:192].astype(jnp.bfloat16)
                puts = [going.at[side]] if half else [(p0, p2)[side], (r0, r2)[side]]
                for put in puts:
                    put[:, 192 * head : 192 * head + 128] = pair
                    put[:, 192 * head + 128 : 192 * head + 192] = value
            if half:
                returning(side).start()
    square_out[...] = jnp.full(square_out.shape, finish(), jnp.float32)
    for side in range(2):
        returning(side).wait_recv()
        for put in ((p1, p3)[side], (r1, r3)[side]):
            put[:, 0:576] = coming[side, :, 0:576]
    for place in range(6):
        crossing(place).wait_send()
    for side in range(2):
        returning(side).wait_send()
    drain()


def attend_back_kernel(layout, grad_out, packed, lse, attended, cosine, sine, seg_row, seg_col, lefts, ups, downs):
    rows = grad_out.shape[0]
    anywhere = pl.BlockSpec(memory_space=pl.ANY)
    width = ups[0].shape[1] + downs[0].shape[1]
    inside = pl.BlockSpec(memory_space=pltpu.VMEM)
    found = pl.pallas_call(
        functools.partial(attend_back_body, layout),
        name="attend_back",
        out_shape=[jax.ShapeDtypeStruct((rows, 640), jnp.bfloat16)] * 4
        + [jax.ShapeDtypeStruct((rows, 896), jnp.bfloat16)] * 4
        + [
            jax.ShapeDtypeStruct((lefts[0].shape[0] // lax.axis_size("dp"), width), jnp.float32),
            jax.ShapeDtypeStruct((8, 128), jnp.float32),
        ],
        in_specs=[inside] * 10 + [anywhere] * 8,
        out_specs=[inside] * 10,
        scratch_shapes=[
            pltpu.VMEM((6, 2 * rows, 128), jnp.bfloat16),
            pltpu.VMEM((6, rows, 128), jnp.bfloat16),
            pltpu.VMEM((64, 2 * rows), jnp.bfloat16),
            pltpu.VMEM((2 * rows, 2 * rows), jnp.float32),
            pltpu.VMEM((2 * rows, 2 * rows), jnp.float32),
            pltpu.VMEM((6, 2 * rows, 256), jnp.float32),
            pltpu.VMEM((2, rows, 640), jnp.bfloat16),
            pltpu.VMEM((2, rows, 640), jnp.bfloat16),
            pltpu.SemaphoreType.DMA((6,)),
            pltpu.SemaphoreType.DMA((6,)),
            pltpu.SemaphoreType.DMA((2,)),
            pltpu.SemaphoreType.DMA((2,)),
        ]
        + reduce_scratch([width // 2] * 2, 1, *lefts[0].shape),
        compiler_params=pltpu.CompilerParams(
            collective_id=3, has_side_effects=True, vmem_limit_bytes=62 << 20
        ),
    )(grad_out, packed, lse, attended, cosine, sine, seg_row, seg_col, *lefts, *ups, *downs)
    return found[:4], found[4:8], found[8], found[9]


def pieces_of(width):
    pieces, at = [], 0
    for span in (768, 640, 640):
        pieces.append((at, span, span // 2 if span % 256 == 0 else span))
        at += span
    return pieces


def known_mesh():
    return lax.axis_size("dp") == 8 and lax.axis_size("tensor") == 4


def reduce_grads(layout, lefts, rights, places, extra, facts, parts, gains_at):
    if known_mesh():
        ordered = [[item[0], item[2], item[1], item[3]] for item in rights]
        return reduce_kernel(layout, lefts, ordered, places, extra, facts, parts, gains_at, 1)
    sums = []
    for item, (_, products) in enumerate(layout):
        quarters = []
        for quarter, mask in enumerate((0, 2, 1, 3)):
            right = rights[item][quarter]
            found = [mm(lefts[at], right[:, base : base + width]) for at, base, width, _ in products]
            if item == 0:
                spots = jnp.arange(right.shape[1], dtype=jnp.int32)[None, :]
                found[0] += mm(lefts[1], narrow(places[:, mask : mask + 1] == spots))
            if item == gains_at[0]:
                found[0] += extra
            quarters.append(narrow(jnp.concatenate(found, axis=1)))
        sums.append(reduce_all(quarters, True))
    square = sum(jnp.sum(item * item) for item in sums)
    repeated = sums[gains_at[0]][:, gains_at[1] : gains_at[1] + gains_at[2]]
    square = square - jnp.sum(repeated * repeated) * (1.0 - 1.0 / parts)
    tile = jnp.where(lax.broadcasted_iota(jnp.int32, (8, 128), 0) == 0, square, facts)
    return sums, everyone_sum(tile)


def wide(value):
    return value.astype(jnp.float32)


def narrow(value):
    return value.astype(jnp.bfloat16)


def fold(value, masks, last):
    rows = value.shape[0] // (len(masks) + 1)
    total = wide(value[:rows])
    for place, mask in enumerate(masks):
        total = total + wide(swap(value[(place + 1) * rows : (place + 2) * rows], "dp", mask))
    return total if last else narrow(total)


def reduce_all(quarters, x_first):
    groups = groups_of(lax.axis_size("dp"))
    own = narrow(wide(quarters[0]) + wide(swap(quarters[2], "tensor", 1)))
    other = narrow(wide(quarters[1]) + wide(swap(quarters[3], "tensor", 1)))
    if x_first:
        own = narrow(wide(own) + wide(swap(other, "tensor", 2)))
        own = fold(own, groups[0], len(groups) == 1)
    else:
        own = fold(own, groups[0], False)
        other = fold(other, groups[0], False)
        own = narrow(wide(own) + wide(swap(other, "tensor", 2)))
    for place in range(1, len(groups)):
        own = fold(own, groups[place], place == len(groups) - 1)
    return wide(own)


def everyone_sum(value):
    for masks in groups_of(lax.axis_size("dp")):
        value = sum([swap(value, "dp", mask) for mask in masks], value)
    for mask in (1, 2):
        value = value + swap(value, "tensor", mask)
    return value


def mm(left, right):
    return jnp.dot(left, right, preferred_element_type=jnp.float32)


def mm_nt(left, right):
    return lax.dot_general(left, right, (((1,), (1,)), ((), ())), preferred_element_type=jnp.float32)


def mm_tn(left, right):
    return lax.dot_general(left, right, (((0,), (0,)), ((), ())), preferred_element_type=jnp.float32)


def rotate_heads(values, cosine, sine):
    return rotate(values, cosine[:, None, :], sine[:, None, :])


def scores_of(query, key_rows, same_doc):
    scores = jnp.einsum(
        "qhe,khe->hqk", query, key_rows, preferred_element_type=jnp.float32
    ) * HEAD_DIM ** (-0.5)
    return jnp.where(same_doc[None], scores, neg_fill)


def split_heads(packed):
    packed = packed.reshape(packed.shape[0], -1, 3, HEAD_DIM)
    return packed[:, :, 0], packed[:, :, 1], packed[:, :, 2]


def attend(packed, same_doc):
    query, key_rows, value_rows = split_heads(packed)
    scores = scores_of(query, key_rows, same_doc)
    row_max = jnp.max(scores, axis=-1, keepdims=True)
    expd = jnp.exp(scores - row_max)
    summed = jnp.sum(expd, axis=-1, keepdims=True)
    probs = (expd / summed).astype(jnp.bfloat16)
    output = jnp.einsum("hqk,khe->qhe", probs, value_rows, preferred_element_type=jnp.float32)
    return (narrow(output).reshape(packed.shape[0], -1), (row_max + jnp.log(summed))[..., 0])


def attend_back(packed, same_doc, row_lse, grad_out, cosine, sine):
    query, key_rows, value_rows = split_heads(packed)
    grad_out = grad_out.reshape(packed.shape[0], -1, HEAD_DIM)
    scores = scores_of(query, key_rows, same_doc)
    probs = jnp.exp(scores - row_lse[..., None])
    value_grad = jnp.einsum(
        "hqk,qhe->khe", probs.astype(jnp.bfloat16), grad_out, preferred_element_type=jnp.float32
    )
    prob_grad = jnp.einsum("qhe,khe->hqk", grad_out, value_rows, preferred_element_type=jnp.float32)
    inner = jnp.sum(prob_grad * probs, axis=-1, keepdims=True)
    score_grad = (probs * (prob_grad - inner)).astype(jnp.bfloat16)
    query_grad = jnp.einsum(
        "hqk,khe->qhe", score_grad, key_rows, preferred_element_type=jnp.float32
    ) * HEAD_DIM ** (-0.5)
    key_grad = jnp.einsum(
        "hqk,qhe->khe", score_grad, query, preferred_element_type=jnp.float32
    ) * HEAD_DIM ** (-0.5)
    query_grad = rotate_heads(query_grad, cosine, -sine)
    key_grad = rotate_heads(key_grad, cosine, -sine)
    return narrow(jnp.stack([query_grad, key_grad, value_grad], axis=2).reshape(packed.shape))


def update_weights(totals, fixes, sums, plans, triples):
    if known_mesh():
        updated, results = update_kernel(totals, fixes, sums, plans, triples)
        return list(updated), results
    updated = []
    norm = jnp.sqrt(totals[0, 0]) / totals[2, 0]
    scale = jnp.minimum(1.0, clip_at / norm) / totals[2, 0]
    for (source, turned, first, rate, decay), (weight, one, two) in zip(plans, triples):
        columns = weight.shape[0] if turned else weight.shape[1]
        grad = sums[source][:, first : first + columns]
        clipped = (grad.T if turned else grad) * scale
        moment_one = beta_one * one + (1.0 - beta_one) * clipped
        moment_two = beta_two * two + (1.0 - beta_two) * clipped * clipped
        stepped = moment_one * fixes[0, 0] / (jnp.sqrt(moment_two * fixes[1, 0]) + adam_eps)
        updated.extend([moment_one, moment_two, weight - rate * (stepped + decay * weight)])
    return updated, jnp.stack([totals[1, 0] / totals[2, 0], norm])[:, None]


def per_device(
    tokens,
    lengths,
    timesteps,
    masks,
    step_count,
    table,
    joint_weight,
    output_weight,
    upward_weight,
    downward_weight,
    gains,
    momentum_table,
    momentum_joint,
    momentum_output,
    momentum_upward,
    momentum_downward,
    momentum_gains,
    variance_table,
    variance_joint,
    variance_output,
    variance_upward,
    variance_downward,
    variance_gains,
):
    place = lax.axis_index("tensor")
    parts = lax.axis_size("tensor")
    rows = tokens.shape[0] // parts
    vocab_part, head_part = table.shape[0], joint_weight.shape[1]
    out_part, ff_part = output_weight.shape[0], upward_weight.shape[1]

    gain_columns = jnp.pad(narrow(gains).T, ((0, 0), (0, 61)))
    shards = [
        narrow(table).T,
        jnp.concatenate([narrow(joint_weight), gain_columns], axis=1),
        narrow(upward_weight),
        narrow(downward_weight).T,
        narrow(output_weight).T,
    ]
    start = place * rows
    seq = start // SEQ_LEN
    mine = start - seq * SEQ_LEN
    cut = lambda array: lax.dynamic_slice(array, (start,), (rows,))
    targets = cut(tokens)
    corrupt = cut(masks) == 1
    inputs = jnp.where(corrupt, VOCAB - 1, targets)
    own_lengths = lax.dynamic_slice(lengths, (seq, 0), (1, DOCS))
    step_here = lax.dynamic_slice(timesteps, (seq,), (1,))
    theirs = mine ^ rows
    position = jnp.concatenate(
        [mine + jnp.arange(rows, dtype=jnp.int32), theirs + jnp.arange(rows, dtype=jnp.int32)]
    )
    doc_ends = jnp.cumsum(own_lengths[0])
    doc_starts = doc_ends - own_lengths[0]
    segment = jnp.sum((position[:, None] >= doc_ends[None, :]).astype(jnp.int32), axis=1)
    chosen = segment[:, None] == jnp.arange(DOCS, dtype=jnp.int32)[None, :]
    offset = position - jnp.sum(jnp.where(chosen, doc_starts[None, :], 0), axis=1)
    is_real = segment < DOCS - 1
    factor = jnp.where(step_here == 1, 1.0, T_DIFF / step_here.astype(jnp.float32))
    weights = jnp.where(corrupt & is_real[:rows], factor, 0.0)
    inverse_freq = 10000.0 ** (-jnp.arange(HEAD_DIM // 2, dtype=jnp.float32) / (HEAD_DIM // 2))
    angles = offset.astype(jnp.float32)[:, None] * inverse_freq
    cosine, sine = jnp.cos(angles), jnp.sin(angles)
    same_doc = segment[:, None] == segment[None, :]

    def hot(ids, piece):
        base = (place ^ (2 * (piece % 2) + piece // 2)) * vocab_part
        return (ids - base)[:, None] == jnp.arange(vocab_part, dtype=jnp.int32)[None, :]

    pieces = range(4)
    lane = jnp.arange(128, dtype=jnp.int32)[None, :]
    places = inputs[:, None] - (place ^ (lane % 4)) * vocab_part

    on_known = known_mesh()
    if on_known:
        cosines = jnp.concatenate([cosine] * 4, axis=1)
        sines = jnp.concatenate([-sine, sine] * 2, axis=1)
        seg_row = jnp.broadcast_to(segment[None, :], (8, 2 * rows))
        seg_col = jnp.broadcast_to(segment[:, None], (2 * rows, 128))
        groups, (embedded, normed_one, packed, attn_lse, attended_all) = start_kernel(
            shards, places, cosines, sines, seg_row, seg_col
        )
        groups = [[item[0], item[2], item[1], item[3]] for item in groups]
    else:
        groups = [gather_all(item, True) for item in shards]
    table_q, first_group, up_q, down_q, out_q = groups
    gain_full = wide(first_group[0][:, head_part : head_part + 3]).T
    out_all = jnp.concatenate(out_q, axis=1)
    if not on_known:
        joint_q = [item[:, :head_part] for item in first_group]
        looked = sum(mm_nt(narrow(hot(inputs, piece)), table_q[piece]) for piece in pieces)
        embedded = looked * D**0.5
        normed_one = narrow(norm_apply(embedded, gain_full[0]))

        def turned(projected):
            projected = projected.reshape(rows, -1, 3, HEAD_DIM)
            query = rotate_heads(projected[:, :, 0], cosine[:rows], sine[:rows])
            key_rows = rotate_heads(projected[:, :, 1], cosine[:rows], sine[:rows])
            stacked = jnp.stack([query, key_rows, projected[:, :, 2]], axis=2)
            return narrow(stacked.reshape(rows, -1))

        packed = [turned(mm(normed_one, item)) for item in joint_q]
        whole = [
            jnp.concatenate([packed[side], swap(packed[2 + side], "tensor", 1)], axis=0)
            for side in range(2)
        ]
        attended, attn_lse = zip(*[attend(item, same_doc) for item in whole])
        attended_all = jnp.concatenate(
            [item[:rows] for item in attended]
            + [swap(item[rows:], "tensor", 1) for item in attended],
            axis=1,
        )
    after_attn = embedded + mm_nt(attended_all, out_all)
    normed_two = narrow(norm_apply(after_attn, gain_full[1]))
    pre_gelu = [mm(normed_two, item) for item in up_q]
    below = [0.5 + 0.5 * lax.erf(item * 0.5**0.5) for item in pre_gelu]
    slopes = [
        part + item * jnp.exp(-0.5 * item * item) * (0.5 / jnp.pi) ** 0.5
        for part, item in zip(below, pre_gelu)
    ]
    activated = [narrow(item * part) for part, item in zip(below, pre_gelu)]
    after_mlp = after_attn + sum(mm_nt(activated[q], down_q[q]) for q in range(4))
    normed_out = narrow(norm_apply(after_mlp, gain_full[2]))
    logits = [mm(normed_out, item) for item in table_q]
    row_max = logits[0].max(axis=1)
    for item in logits[1:]:
        row_max = jnp.maximum(row_max, item.max(axis=1))
    row_sum = sum(jnp.sum(jnp.exp(item - row_max[:, None]), axis=1) for item in logits)
    target_hot = [hot(targets, piece) for piece in pieces]
    row_pick = sum(
        jnp.sum(jnp.where(target_hot[piece], logits[piece], 0.0), axis=1) for piece in pieces
    )
    row_lse = row_max + jnp.log(row_sum)
    loss_local = jnp.sum(weights * (row_lse - row_pick))
    count_local = jnp.sum(is_real[:rows].astype(jnp.float32))

    logit_grad = [
        narrow(
            weights[:, None]
            * (jnp.exp(logits[piece] - row_lse[:, None]) - target_hot[piece].astype(jnp.float32))
        )
        for piece in pieces
    ]
    out_grad = sum(mm_nt(logit_grad[piece], table_q[piece]) for piece in pieces)
    mlp_grad, gain_three = norm_back(after_mlp, gain_full[2], out_grad)
    mlp_branch = narrow(mlp_grad)
    up_input = [
        narrow(slopes[q] * mm(mlp_branch, down_q[q])) for q in range(4)
    ]
    normed_two_grad = sum(mm_nt(up_input[q], up_q[q]) for q in range(4))
    attn_in_grad, gain_two = norm_back(after_attn, gain_full[1], normed_two_grad)
    resid_one = mlp_grad + attn_in_grad
    attn_branch = narrow(resid_one)
    attended_grad = narrow(mm(attn_branch, out_all))
    if on_known:
        proj_grad, last_rights, middle_sum, middle_square = attend_back_kernel(
            ((None, ((0, 0, ff_part, ff_part // 2),)), (None, ((1, 0, ff_part, ff_part // 2),))),
            attended_grad,
            packed,
            attn_lse,
            attended_all,
            cosines,
            sines,
            seg_row,
            seg_col,
            [normed_two.T, mlp_branch.T],
            [up_input[q] for q in (0, 2, 1, 3)],
            [activated[q] for q in (0, 2, 1, 3)],
        )
        proj_grad = [proj_grad[q] for q in (0, 2, 1, 3)]
        last_rights = [last_rights[q] for q in (0, 2, 1, 3)]
        joint_back = first_group
    else:
        grad_parts = [attended_grad[:, q * out_part : (q + 1) * out_part] for q in range(4)]
        proj_whole = [
            attend_back(
                whole[side],
                same_doc,
                attn_lse[side],
                jnp.concatenate(
                    [grad_parts[side], swap(grad_parts[2 + side], "tensor", 1)], axis=0
                ),
                cosine,
                sine,
            )
            for side in range(2)
        ]
        proj_grad = [item[:rows] for item in proj_whole] + [
            swap(item[rows:], "tensor", 1) for item in proj_whole
        ]
        joint_back = joint_q
    normed_one_grad = sum(mm_nt(proj_grad[q], joint_back[q]) for q in range(4))
    embed_in, gain_one = norm_back(embedded, gain_full[0], normed_one_grad)
    embed_grad = resid_one + embed_in
    embed_scaled = narrow(embed_grad * D**0.5)
    sublane = lax.broadcasted_iota(jnp.int32, (8, 128), 0)
    facts = jnp.where(sublane == 1, loss_local, jnp.where(sublane == 2, count_local, 0.0))
    gains_end = (head_part + gains.shape[0] + 127) // 128 * 128
    out_fill = (out_part + 127) // 128 * 128
    fill = lambda array, columns: jnp.pad(array, ((0, 0), (0, columns - array.shape[1])))
    extra = jnp.pad(
        jnp.stack([gain_one, gain_two, gain_three]).T,
        ((0, 0), (head_part, gains_end - head_part - gains.shape[0])),
    )
    if not on_known:
        attended_q = [attended_all[:, q * out_part : (q + 1) * out_part] for q in range(4)]
        last_rights = [
            jnp.concatenate([fill(proj_grad[q], gains_end), fill(attended_q[q], out_fill)], axis=1)
            for q in range(4)
        ]
    lefts = [normed_out, embed_scaled, normed_one, attn_branch]
    rights = [logit_grad, last_rights]
    layout = (
        (None, ((2, 0, gains_end, gains_end), (3, gains_end, out_fill, out_fill))),
        *((at, ((0, 0, span, step),)) for at, span, step in pieces_of(vocab_part)),
    )
    gains_at = (0, head_part, gains_end - head_part)
    if on_known:
        facts = facts + jnp.where(sublane == 0, middle_square, 0.0)
    else:
        layout = (
            (0, ((0, 0, vocab_part, vocab_part),)),
            (None, ((2, 0, gains_end, gains_end), (3, gains_end, out_fill, out_fill))),
            (None, ((4, 0, ff_part, ff_part), (5, ff_part, ff_part, ff_part))),
        )
        gains_at = (1, head_part, gains_end - head_part)
        lefts = lefts + [normed_two, mlp_branch]
        rights = rights + [[jnp.concatenate([up_input[q], activated[q]], axis=1) for q in range(4)]]
    sums, totals = reduce_grads(
        layout, [item.T for item in lefts], rights, places, extra, facts, parts, gains_at
    )
    if on_known:
        sums = [*sums, middle_sum]
    step_float = step_count[0].astype(jnp.float32)
    fixes = jnp.where(
        sublane == 0,
        1.0 / (1.0 - jnp.power(beta_one, step_float)),
        1.0 / (1.0 - jnp.power(beta_two, step_float)),
    )
    plans = (
        (0, False, 0, rates[0], decays[0]),
        (1, False, 0, rates[1], decays[1]),
        (1, True, gains_end, rates[2], decays[2]),
        (2, False, 0, rates[3], decays[3]),
        (2, False, ff_part, rates[4], decays[4]),
        (1, True, head_part, rates[5], decays[5]),
    )
    triples = (
        (table.T, momentum_table.T, variance_table.T),
        (joint_weight, momentum_joint, variance_joint),
        (output_weight, momentum_output, variance_output),
        (upward_weight, momentum_upward, variance_upward),
        (downward_weight.T, momentum_downward.T, variance_downward.T),
        (gains, momentum_gains, variance_gains),
    )
    updated, results = update_weights(totals, fixes, sums, plans, triples)
    updated = [item.T if place // 3 in (0, 4) else item for place, item in enumerate(updated)]
    return tuple([results[0, 0], results[1, 0]] + updated)


def solution(mesh):
    placed = (
        P("dp"),
        P("dp", None),
        P("dp"),
        P("dp"),
        P(),
        P("tensor", "dp"),
        P("dp", "tensor"),
        P("tensor", "dp"),
        P("dp", "tensor"),
        P("tensor", "dp"),
        P(None, "dp"),
        P("tensor", "dp"),
        P("dp", "tensor"),
        P("tensor", "dp"),
        P("dp", "tensor"),
        P("tensor", "dp"),
        P(None, "dp"),
        P("tensor", "dp"),
        P("dp", "tensor"),
        P("tensor", "dp"),
        P("dp", "tensor"),
        P("tensor", "dp"),
        P(None, "dp"),
    )
    return jax.shard_map(
        per_device,
        mesh=mesh,
        in_specs=placed,
        out_specs=(
            P(),
            P(),
            P("tensor", "dp"),
            P("tensor", "dp"),
            P("tensor", "dp"),
            P("dp", "tensor"),
            P("dp", "tensor"),
            P("dp", "tensor"),
            P("tensor", "dp"),
            P("tensor", "dp"),
            P("tensor", "dp"),
            P("dp", "tensor"),
            P("dp", "tensor"),
            P("dp", "tensor"),
            P("tensor", "dp"),
            P("tensor", "dp"),
            P("tensor", "dp"),
            P(None, "dp"),
            P(None, "dp"),
            P(None, "dp"),
        ),
        check_vma=False,
    )
```

```python
import functools

import jax
import jax.numpy as jnp
from jax import lax
from jax.experimental import pallas as pl
from jax.experimental.pallas import tpu as pltpu
from jax.sharding import PartitionSpec as P

D = 768
HEAD_DIM = 64
VOCAB = 8192
SEQ_LEN = 1024
DOCS = 4
T_DIFF = 1000


eps_norm = 1e-06
neg_fill = -1000000000.0
beta_one = 0.9
beta_two = 0.999
adam_eps = 1e-08
clip_at = 0.02
rates = (0.05, 0.03, 0.25, 0.03, 0.03, 0.3)
decays = (0.1, 0.1, 0.1, 0.1, 0.1, 0.0)


def norm_apply(values, gain):
    inverse = lax.rsqrt(jnp.mean(values * values, axis=-1, keepdims=True) + eps_norm)
    return values * inverse * gain


def norm_back(values, gain, upstream):
    inverse = lax.rsqrt(jnp.mean(values * values, axis=-1, keepdims=True) + eps_norm)
    gain_grad = jnp.sum(upstream * values * inverse, axis=0)
    scaled = upstream * gain
    inner = jnp.mean(scaled * values, axis=-1, keepdims=True)
    return (inverse * (scaled - values * inverse * inverse * inner), gain_grad)


def rotate(values, cosine, sine):
    middle = values.shape[-1] // 2
    front_part = values[..., :middle]
    back_part = values[..., middle:]
    return jnp.concatenate(
        [front_part * cosine - back_part * sine, back_part * cosine + front_part * sine], axis=-1
    )


def groups_of(count):
    groups, bit, width = [], 1, 1
    while bit < count:
        masks = [bit]
        if width == 2 and bit * 2 < count:
            masks = [bit, 2 * bit, 3 * bit]
            bit = bit * 2
        groups.append(masks)
        bit, width = bit * 2, 2
    return groups


def swap(value, axis, mask):
    size = lax.axis_size(axis)
    return lax.ppermute(value, axis, [(place, place ^ mask) for place in range(size)])


def spread(value, masks):
    return jnp.concatenate([value] + [swap(value, "dp", mask) for mask in masks], axis=0)


def gather_all(value, x_last):
    groups = groups_of(lax.axis_size("dp"))
    for masks in groups[:0:-1]:
        value = spread(value, masks)
    if x_last:
        value = spread(value, groups[0])
        other = swap(value, "tensor", 2)
    else:
        other = swap(value, "tensor", 2)
        value = spread(value, groups[0])
        other = spread(other, groups[0])
    return [value, other, swap(value, "tensor", 1), swap(other, "tensor", 1)]


MESH = pl.DeviceIdType.MESH


def neighbours():
    column, row = lax.axis_index("dp"), lax.axis_index("tensor")
    return {
        "x": (column, (row + 2) % 4),
        "c": (column, row + 1 - 2 * (row % 2)),
        "y": (column + 1 - 2 * (column % 2), row),
        "up": (column + 2, row),
        "down": (column - 2, row),
    }


def meet(z, devices):
    barrier = pltpu.get_barrier_semaphore()

    def greet(name):
        pl.semaphore_signal(barrier, inc=1, device_id=devices[name], device_id_type=MESH)

    for name in ("x", "c", "y"):
        greet(name)
    pl.when(z < 3)(lambda: greet("up"))
    pl.when(z > 0)(lambda: greet("down"))
    pl.semaphore_wait(barrier, 3 + (z + 2) // 3 + (5 - z) // 3)


def start_body(items, *refs):
    arrays = items - 1
    given = refs[:arrays]
    places, cosine, sine, seg_row, seg_col = refs[arrays : arrays + 5]
    refs = refs[arrays + 5 :]
    kept = [refs[4 * array : 4 * array + 4] for array in range(arrays)]
    embedded_out, normed, packed, lse, attended = refs[4 * arrays : 4 * arrays + 5]
    refs = refs[4 * arrays + 5 :]
    side_sem, z_sem, late_sem, recv_sem, own_sem, keep_sem = refs[:6]
    staged = refs[6:8]
    attend_refs = refs[8:]
    late = (1, 3)
    cut = given[0].shape[1] - 256
    columns = [pl.ds(0, cut), pl.ds(cut, 256)] + [pl.ds(0, item.shape[1]) for item in given[1:]]
    ins = [given[0].at[:, columns[0]], given[0].at[:, columns[1]], *given[1:]]
    column = lax.axis_index("dp")
    z = column // 2
    devices = neighbours()
    meet(z, devices)
    shard = [given[0].shape[0]] * items
    piece = [item // 2 for item in shard]

    def base(item, quarter, rows):
        if item < 3:
            return staged[item // 2].at[quarter, rows, columns[item]]
        return kept[item - 1][quarter].at[rows]

    def mirror(source):
        return source + 1 - 2 * (source % 2)

    def view(item, part, quarter, source):
        start = pl.multiple_of(source * shard[item] + part * piece[item], 8)
        return base(item, quarter, pl.ds(start, piece[item]))

    def copy(item, part, quarter, source, to_quarter, name, send, own=False):
        here = view(item, part, quarter, source)
        if own:
            own_rows = pl.ds(part * piece[item], piece[item])
            here = given[0].at[own_rows, columns[item]] if item < 2 else given[item - 1].at[own_rows]
        return pltpu.make_async_remote_copy(
            src_ref=here,
            dst_ref=view(item, part, to_quarter, source),
            send_sem=send,
            recv_sem=recv_sem.at[item, part, to_quarter, source],
            device_id=devices[name],
            device_id_type=MESH,
        )

    def arrived(item, part, quarter, source):
        copy(item, part, quarter, source, quarter, "x", side_sem.at[0, item]).wait_recv()

    def send_x(item, part, source, own=False):
        copy(item, part, 0, source, 2, "x", side_sem.at[0, item], own).start()

    def send_y(item, part, quarter, source, own=False):
        copy(item, part, quarter, source, quarter, "y", side_sem.at[1, item], own).start()

    def send_c(item, part, quarter, source, own=False):
        copy(item, part, quarter, source, quarter + 1, "c", side_sem.at[2 + quarter // 2, item], own).start()

    def send_z(item, part, source, turn, upward, own=False, quarter=0, kind=0):
        name = "up" if upward else "down"
        sem = z_sem.at[item, part, 1 - upward, turn]
        if item in late:
            sem = late_sem.at[item // 2, part, 1 - upward, turn, kind]
        copy(item, part, quarter, source, quarter, name, sem, own).start()

    def slot(turn, action):
        pl.when(z >= turn)(lambda: action(column - 2 * turn, 1))
        pl.when(z + turn <= 3)(lambda: action(column + 2 * turn, 0))

    every = [(item, part) for item in range(items) for part in range(2)]

    def local(item):
        return pltpu.make_async_copy(
            ins[item],
            base(item, 0, pl.ds(pl.multiple_of(column * shard[item], 8), shard[item])),
            own_sem.at[item],
        )

    def keep(item, quarter):
        return pltpu.make_async_copy(staged[item].at[quarter], kept[item][quarter], keep_sem.at[item, quarter])

    def begin(item):
        for part in range(2):
            pl.when(z < 3)(lambda: send_z(item, part, column, 0, 1, True))
            pl.when(z > 0)(lambda: send_z(item, part, column, 0, 0, True))
            send_x(item, part, column, True)
            send_y(item, part, 0, column, True)
            send_c(item, part, 0, column, True)
        local(item).start()

    def from_z(item, part, turn, source, upward):
        arrived(item, part, 0, source)
        if turn < 3:
            ahead = z < 3 if upward else z > 0
            pl.when(ahead)(lambda: send_z(item, part, source, turn, upward))
        send_x(item, part, source)
        send_y(item, part, 0, source)
        send_c(item, part, 0, source)

    def second(item, source):
        arrived(item, 0, 0, mirror(source))
        send_x(item, 0, mirror(source))
        send_c(item, 0, 0, mirror(source))
        arrived(item, 1, 2, source)
        send_y(item, 1, 2, source)
        send_c(item, 1, 2, source)

    def third(item, source):
        arrived(item, 0, 2, source)
        send_c(item, 0, 2, source)
        arrived(item, 1, 0, mirror(source))
        send_c(item, 1, 0, mirror(source))
        for part in range(2):
            arrived(item, part, 2, mirror(source))
            send_c(item, part, 2, mirror(source))

    def along_z(item, turn):
        for part in range(2):
            slot(turn, lambda source, upward: from_z(item, part, turn, source, upward))

    def onward(action, item, turn):
        if turn == 0:
            action(item, column)
        else:
            slot(turn, lambda source, upward: action(item, source))

    def complete(item):
        for part in range(2):
            for source in range(8):
                for quarter in (1, 3):
                    arrived(item, part, quarter, source)
        local(item).wait()
        if item in (1, 2):
            for quarter in range(4):
                keep(item - 1, quarter).start()

    def kinds(source):
        return ((0, source), (2, source), (0, mirror(source)), (2, mirror(source)))

    def both_ways(item, part, kind):
        quarter, source = kinds(column)[kind]
        pl.when(z < 3)(lambda: send_z(item, part, source, 0, 1, False, quarter, kind))
        pl.when(z > 0)(lambda: send_z(item, part, source, 0, 0, False, quarter, kind))
        send_c(item, part, quarter, source)

    def late_first(item):
        other = mirror(column)
        arrived(item, 0, 2, column)
        send_y(item, 0, 2, column)
        both_ways(item, 0, 1)
        arrived(item, 1, 0, other)
        send_x(item, 1, other)
        both_ways(item, 1, 2)
        arrived(item, 0, 0, other)
        both_ways(item, 0, 2)
        arrived(item, 1, 2, column)
        both_ways(item, 1, 1)

    def late_second(item):
        for part in range(2):
            arrived(item, part, 2, mirror(column))
            both_ways(item, part, 3)

    def late_z(item, turn):
        def action(place, upward):
            for kind, (quarter, source) in enumerate(kinds(place)):
                for part in range(2):
                    arrived(item, part, quarter, source)
                    if turn < 3:
                        ahead = z < 3 if upward else z > 0
                        pl.when(ahead)(lambda: send_z(item, part, source, turn, upward, False, quarter, kind))
                    send_c(item, part, quarter, source)

        slot(turn, action)

    rest = range(4, items)
    begin(0)
    begin(1)
    late_first(1)
    along_z(0, 1)
    late_second(1)
    for turn in (2, 3):
        along_z(0, turn)
    late_z(1, 1)
    begin(2)
    for turn in range(4):
        onward(second, 0, turn)
    late_z(1, 2)
    for turn in (1, 2, 3):
        along_z(2, turn)
    late_z(1, 3)
    for turn in range(4):
        onward(third, 0, turn)
    for item in range(3, items):
        begin(item)
    complete(0)
    complete(1)

    def look_up(quarter):
        def one(chunk, _):
            at = pl.ds(pl.multiple_of(chunk * 512, 512), 512)
            spots = lax.broadcasted_iota(jnp.int32, (places.shape[0], 512), 1) + chunk * 512
            hot = jnp.where(places[:, quarter : quarter + 1] == spots, 1.0, 0.0).astype(jnp.bfloat16)
            embedded_out[...] += lax.dot_general(
                hot, staged[0][quarter, :, at], (((1,), (1,)), ((), ())), preferred_element_type=jnp.float32
            )
            return 0

        lax.fori_loop(0, staged[0].shape[2] // 512, one, 0)

    embedded_out[...] = jnp.zeros_like(embedded_out)
    look_up(0)
    late_first(3)
    for turn in range(4):
        onward(second, 2, turn)
    look_up(2)
    for item in rest:
        along_z(item, 1)
    late_second(3)
    look_up(1)
    for turn in range(4):
        onward(third, 2, turn)
    for item in rest:
        along_z(item, 2)
    late_z(3, 1)
    look_up(3)
    complete(2)
    gain = staged[1][0, :, 512:640].astype(jnp.float32).T[64:65]
    value = embedded_out[...] * D**0.5
    embedded_out[...] = value
    inverse = lax.rsqrt(jnp.mean(value * value, axis=-1, keepdims=True) + eps_norm)
    normed[...] = (value * inverse * gain).astype(jnp.bfloat16)
    for item in rest:
        along_z(item, 3)

    def between(stage):
        if stage in (2, 5):
            late_z(3, 2 if stage == 2 else 3)
        for item in rest:
            if stage == 0:
                onward(second, item, 0)
                onward(second, item, 1)
            if stage == 1:
                onward(second, item, 2)
                onward(second, item, 3)
            if stage == 6:
                for turn in range(4):
                    onward(third, item, turn)

    attend_steps(
        normed, [staged[1].at[q] for q in range(4)], cosine, sine, seg_row, seg_col, packed, lse, attended, between, *attend_refs
    )
    for item in range(3, items):
        complete(item)
    for item in range(2):
        for quarter in range(4):
            keep(item, quarter).wait()
    for item in range(items):
        for way, count in enumerate((3, 3, 16, 16) if item in late else (12, 12, 16, 16)):
            lead = base(item, 0, pl.ds(0, count * piece[item]))
            pltpu.make_async_remote_copy(
                src_ref=lead,
                dst_ref=lead,
                send_sem=side_sem.at[way, item],
                recv_sem=recv_sem.at[item, 0, 0, 0],
                device_id=devices["x"],
                device_id_type=MESH,
            ).wait_send()
    for item, part in every:
        for turn in range(3):
            for kind in range(4 if item in late else 1):
                sems = [
                    late_sem.at[item // 2, part, way, turn, kind] if item in late else z_sem.at[item, part, way, turn]
                    for way in range(2)
                ]
                pl.when((z < 3) & (z >= turn))(
                    lambda: copy(item, part, 0, column, 0, "up", sems[0], True).wait_send()
                )
                pl.when((z > 0) & (z + turn <= 3))(
                    lambda: copy(item, part, 0, column, 0, "down", sems[1], True).wait_send()
                )


def start_kernel(shards, places, cosine, sine, seg_row, seg_col):
    arrays = len(shards)
    items = arrays + 1
    anywhere = pl.BlockSpec(memory_space=pl.ANY)
    inside = pl.BlockSpec(memory_space=pltpu.VMEM)
    whole, rows = lax.axis_size("dp"), places.shape[0]
    full = [(item.shape[0] * whole, item.shape[1]) for item in shards]
    shapes = [jax.ShapeDtypeStruct(shape, jnp.bfloat16) for shape in full for _ in range(4)]
    flat = pl.pallas_call(
        functools.partial(start_body, items),
        name="start",
        out_shape=shapes
        + [
            jax.ShapeDtypeStruct((rows, full[0][0]), jnp.float32),
            jax.ShapeDtypeStruct((rows, full[0][0]), jnp.bfloat16),
            jax.ShapeDtypeStruct((6, 2 * rows, 256), jnp.bfloat16),
            jax.ShapeDtypeStruct((8, 2 * rows), jnp.float32),
            jax.ShapeDtypeStruct((rows, 768), jnp.bfloat16),
        ],
        in_specs=[anywhere] * arrays + [inside] * 5,
        out_specs=[anywhere] * (4 * arrays) + [inside] * 5,
        scratch_shapes=[
            pltpu.SemaphoreType.DMA((4, items)),
            pltpu.SemaphoreType.DMA((items, 2, 2, 3)),
            pltpu.SemaphoreType.DMA((2, 2, 2, 3, 4)),
            pltpu.SemaphoreType.DMA((items, 2, 4, 8)),
            pltpu.SemaphoreType.DMA((items,)),
            pltpu.SemaphoreType.DMA((2, 4)),
            pltpu.VMEM((4, *full[0]), jnp.bfloat16),
            pltpu.VMEM((4, *full[1]), jnp.bfloat16),
            pltpu.VMEM((6, rows, 256), jnp.bfloat16),
            pltpu.VMEM((6, 2 * rows, 128), jnp.bfloat16),
            pltpu.VMEM((6, rows, 128), jnp.bfloat16),
            pltpu.SemaphoreType.DMA((6,)),
            pltpu.SemaphoreType.DMA((6,)),
            pltpu.SemaphoreType.DMA((6,)),
            pltpu.SemaphoreType.DMA((6,)),
        ],
        compiler_params=pltpu.CompilerParams(
            collective_id=0, has_side_effects=True, vmem_limit_bytes=56 << 20
        ),
    )(*shards, places, cosine, sine, seg_row, seg_col)
    return [flat[4 * array : 4 * array + 4] for array in range(arrays)], flat[4 * arrays :]


def reduce_tools(layout, gains_at, parts, places, extra, lefts, wide_refs, outs, refs):
    items = len(layout)
    held = [refs[6 * item : 6 * item + 6] for item in range(items)]
    refs = refs[6 * items :]
    side_sem, c_send, c_sem, x_sem, y_sem, zs_sem, zr_sem, load_sem, free_sem = refs[:9]
    crossed, from_c, rights = refs[9:]
    column = lax.axis_index("dp")
    z = column // 2
    devices = neighbours()
    shard = [item.shape[0] for item in outs]
    piece = [item // 2 for item in shard]
    width = [item.shape[1] for item in outs]

    def load(item, quarter, which):
        sources, first_column, span = wide_refs[item][which]
        before = sum([part[2] for part in wide_refs[item][:which]])
        return pltpu.make_async_copy(
            sources[quarter].at[:, pl.ds(first_column, span)],
            rights.at[quarter, :, pl.ds(before, span)],
            load_sem.at[item, quarter, which],
        )

    def start_loads(item):
        for quarter in range(4):
            for which in range(len(wide_refs[item])):
                load(item, quarter, which).start()

    def span(item, part, source):
        return pl.ds(pl.multiple_of(source * shard[item] + part * piece[item], 8), piece[item])

    def remote(src, dst, send, recv, name):
        return pltpu.make_async_remote_copy(
            src_ref=src, dst_ref=dst, send_sem=send, recv_sem=recv, device_id=devices[name], device_id_type=MESH
        )

    def c_copy(item, side, source, slot=0):
        columns = pl.ds(0, width[item])
        block = 2 * shard[item]
        there = pl.ds(pl.multiple_of(source // 2 * block, 16), block)
        return remote(
            crossed.at[side, slot, :, columns],
            from_c.at[side, there, columns],
            c_send.at[side, slot],
            c_sem.at[item, side, source // 2],
            "c",
        )

    def c_sent(item, slot):
        for side in range(2):
            c_copy(item, side, 0, slot).wait_send()

    def x_copy(item, part, source):
        place = source if part == 0 else source // 2
        return remote(
            held[item][0].at[1, span(item, part, source)],
            held[item][1 + part].at[place],
            side_sem.at[0, item],
            x_sem.at[item, part, place],
            "x",
        )

    def y_copy(item, part, side, source):
        return remote(
            held[item][0].at[side, span(item, part, source)],
            held[item][3].at[source // 2] if part == 0 else held[item][4].at[side, source // 2],
            side_sem.at[1, item],
            y_sem.at[item, part + side, source // 2],
            "y",
        )

    def z_copy(item, part, source, away, upward):
        return remote(
            held[item][0].at[0, span(item, part, source)],
            held[item][5].at[1 - upward, part, away],
            zs_sem.at[item, part, 1 - upward, away],
            zr_sem.at[item, part, 1 - upward, away],
            "up" if upward else "down",
        )

    def add(item, side, part, source, *others):
        total = held[item][0]
        start = source * shard[item] + part * piece[item]
        step = 16

        def one(turn, _):
            here = pl.ds(pl.multiple_of(start + turn * step, 8), step)
            value = total[side, here]
            for other in others:
                value = value + other(turn * step, step)
            total[side, here] = value
            return 0

        lax.fori_loop(0, piece[item] // step, one, 0)

    def c_part(item, side, part, source):
        start = source * shard[item] + part * piece[item]

        def read(at, step):
            here = pl.ds(pl.multiple_of(start + at, 8), step)
            return from_c[side, here, pl.ds(0, width[item])]

        return read

    def of(ref, *place):
        return lambda at, step: ref[(*place, pl.ds(pl.multiple_of(at, 8), step))]

    def mirror(source):
        return source + 1 - 2 * (source % 2)

    def target(turn):
        low = 3 - turn if turn < 2 else jnp.where(z % 3 == 0, 3 - turn, turn - 2)
        return column + 2 * (jnp.where(z < 2, low, 3 - low) - z)

    def send_c(item, turn):
        source = target(turn)
        if item > 0:
            pl.semaphore_wait(free_sem, 1)
        for side in (1, 0):
            c_copy(item, side, source, turn % 2).start()

    def make(item, turn):
        if 4 * item + turn >= 2:
            c_sent(item if turn >= 2 else item - 1, turn % 2)
        block = 2 * shard[item]
        rows = pl.ds(pl.multiple_of(target(turn) // 2 * block, 16), block)
        for quarter in range(4):
            if turn == 0:
                for which in range(len(wide_refs[item])):
                    load(item, quarter, which).wait()
            for left, base, span_width, step in layout[item][1]:

                def one(chunk, _):
                    at = pl.ds(pl.multiple_of(base + chunk * step, 128), step)
                    found = jnp.dot(
                        lefts[left][rows], rights[quarter, :, at], preferred_element_type=jnp.float32
                    )
                    if layout[item][0] is not None:
                        spots = lax.broadcasted_iota(jnp.int32, (places.shape[0], step), 1)
                        spots = spots + (layout[item][0] + chunk * step)
                        hot = jnp.where(places[:, quarter : quarter + 1] == spots, 1.0, 0.0)
                        found += jnp.dot(
                            lefts[1][rows], hot.astype(jnp.bfloat16), preferred_element_type=jnp.float32
                        )
                    if extra is not None and item == gains_at[0] and base == 0:
                        found += extra[rows]
                    if quarter % 2:
                        crossed[quarter // 2, turn % 2, :, at] = found.astype(jnp.bfloat16)
                    else:
                        held[item][0][quarter // 2, rows, at] = found.astype(jnp.bfloat16)
                    return 0

                lax.fori_loop(0, span_width // step, one, 0)
        if turn == 3 and item + 1 < items:
            start_loads(item + 1)

    def first(item, turn):
        source = target(turn)
        for side in (1, 0):
            c_copy(item, side, source).wait_recv()
        for x_place, y_side in ((source, 1), (mirror(source), 0)):
            add(item, 1, 0, x_place, c_part(item, 1, 0, x_place))
            x_copy(item, 0, x_place).start()
            y_place = mirror(source)
            add(item, y_side, 1, y_place, c_part(item, y_side, 1, y_place))
            y_copy(item, 1, y_side, y_place).start()

    def second(item, turn):
        source = target(turn)
        place = mirror(source)
        x_copy(item, 0, place).wait_recv()
        add(item, 0, 0, place, c_part(item, 0, 0, place), of(held[item][1], place))
        y_copy(item, 0, 0, place).start()
        y_copy(item, 1, 1, source).wait_recv()
        add(item, 1, 1, source, c_part(item, 1, 1, source), of(held[item][4], 1, source // 2))
        x_copy(item, 1, source).start()

    def third(item, turn):
        source = target(turn)
        for part in range(2):
            x_copy(item, part, source).wait_recv()
            y_copy(item, part, 0, source).wait_recv()
            if part == 0:
                terms = [of(held[item][1], source), of(held[item][3], source // 2)]
            else:
                terms = [of(held[item][2], source // 2), of(held[item][4], 0, source // 2)]
            add(item, 0, part, source, c_part(item, 0, part, source), *terms)
        if item + 1 < items:
            pl.semaphore_signal(free_sem, inc=1, device_id=devices["c"], device_id_type=MESH)

    def fourth(item, turn):
        source = target(turn)
        away = jnp.where(source > column, source - column, column - source) // 2

        def along(upward):
            for part in range(2):

                def more():
                    z_copy(item, part, source, away, upward).wait_recv()
                    add(item, 0, part, source, of(held[item][5], 1 - upward, part, away))

                pl.when(z > 0 if upward else z < 3)(more)
                z_copy(item, part, source, away - 1, upward).start()

        pl.when(source > column)(lambda: along(1))
        pl.when(source < column)(lambda: along(0))

    def last(item):
        square = jnp.zeros((), jnp.float32)
        for part in range(2):
            for upward in (1, 0):
                pl.when(z > 0 if upward else z < 3)(
                    lambda: z_copy(item, part, column, 0, upward).wait_recv()
                )
            start = column * shard[item] + part * piece[item]

            def one(turn, square):
                at = pl.multiple_of(turn * 16, 8)
                value = held[item][0][0, pl.ds(pl.multiple_of(start + at, 8), 16)].astype(jnp.float32)
                below = held[item][5][0, part, 0, pl.ds(at, 16)].astype(jnp.float32)
                above = held[item][5][1, part, 0, pl.ds(at, 16)].astype(jnp.float32)
                value = value + jnp.where(z > 0, below, 0.0) + jnp.where(z < 3, above, 0.0)
                outs[item][pl.ds(pl.multiple_of(part * piece[item] + at, 8), 16)] = value
                square_here = value * value
                if extra is not None and item == gains_at[0]:
                    lane = lax.broadcasted_iota(jnp.int32, value.shape, 1)
                    repeated = (lane >= gains_at[1]) & (lane < gains_at[1] + gains_at[2])
                    square_here = jnp.where(repeated, square_here / parts, square_here)
                return square + jnp.sum(square_here)

            square = lax.fori_loop(0, piece[item] // 16, one, square)
        return square

    steps = [(item, turn) for item in range(items) for turn in range(4)]
    count = len(steps)
    def begin():
        make(*steps[0])
        send_c(*steps[0])

    def advance(turn):
        if turn < count:
            first(*steps[turn])
        if turn + 1 < count:
            make(*steps[turn + 1])
            send_c(*steps[turn + 1])
        if 0 <= turn - 1 < count:
            second(*steps[turn - 1])
        if 0 <= turn - 2 < count:
            third(*steps[turn - 2])
        if 0 <= turn - 3 < count and (turn - 3) % 4 < 3:
            fourth(*steps[turn - 3])

    def finish():
        return sum([last(item) for item in range(items)])

    def drain():
        for slot in range(2):
            c_sent(items - 1, slot)
        for item in range(items):
            for way, count in enumerate((12, 12)):
                lead = held[item][0].at[0, pl.ds(0, count * piece[item])]
                remote(lead, lead, side_sem.at[way, item], c_sem.at[item, 0, 0], "x").wait_send()
            for part in range(2):
                for away in range(3):
                    pl.when((z < 3) & (z + away + 1 <= 3))(
                        lambda: z_copy(item, part, column, away, 1).wait_send()
                    )
                    pl.when((z > 0) & (z - away - 1 >= 0))(
                        lambda: z_copy(item, part, column, away, 0).wait_send()
                    )

    return lambda: start_loads(0), begin, advance, count + 3, finish, drain


def reduce_body(layout, parts, gains_at, *refs):
    table_rights, last_rights = refs[:4], refs[4:8]
    facts, places, extra = refs[8:11]
    lefts = refs[11:15]
    table_out, last_out, totals = refs[15:18]
    refs = refs[18:]
    outs, wide_refs = [], []
    for at, products in layout:
        span = sum([product[2] for product in products])
        outs.append(last_out if at is None else table_out.at[:, pl.ds(at, span)])
        wide_refs.append([(last_rights if at is None else table_rights, at or 0, span)])
    tile, tile_row, tile_column, row_send, row_recv, column_send, column_recv = refs[:7]
    start_loads, begin, advance, turns, finish, drain = reduce_tools(
        layout, gains_at, parts, places, extra, lefts, wide_refs, outs, refs[7:]
    )
    start_loads()
    column = lax.axis_index("dp")
    row = lax.axis_index("tensor")
    row_peers = [(column, (row + away) % 4) for away in (1, 2, 3)]
    column_peers = [((column + away) % 8, row) for away in range(1, 8)]
    barrier = pltpu.get_barrier_semaphore()
    for device in row_peers + column_peers:
        pl.semaphore_signal(barrier, inc=1, device_id=device, device_id_type=MESH)
    pl.semaphore_wait(barrier, 10)
    begin()
    for turn in range(turns):
        advance(turn)
    square = finish()
    sublane = lax.broadcasted_iota(jnp.int32, (8, 128), 0)
    tile[...] = facts[...] + jnp.where(sublane == 0, square, 0.0)

    def exchange(value, slots, here, peers, sources, send, recv):
        slots[here] = value

        def crossing(place, device, source):
            return pltpu.make_async_remote_copy(
                src_ref=slots.at[here],
                dst_ref=slots.at[source],
                send_sem=send.at[place],
                recv_sem=recv.at[source],
                device_id=device,
                device_id_type=MESH,
            )

        for place, device in enumerate(peers):
            crossing(place, device, here).start()
        for place, device in enumerate(peers):
            crossing(place, device, sources[place]).wait_recv()
        total = slots[0]
        for place in range(1, len(peers) + 1):
            total = total + slots[place]
        for place, device in enumerate(peers):
            crossing(place, device, here).wait_send()
        return total

    along_row = exchange(
        tile[...], tile_row, row, row_peers, [(row + away) % 4 for away in (1, 2, 3)], row_send, row_recv
    )
    totals[...] = exchange(
        along_row,
        tile_column,
        column,
        column_peers,
        [(column + away) % 8 for away in range(1, 8)],
        column_send,
        column_recv,
    )
    drain()


def reduce_scratch(widths, products, rows, depth):
    whole = lax.axis_size("dp")
    items, half = len(widths), rows // (2 * whole)
    scratch = [
        pltpu.VMEM((*lead, width), jnp.bfloat16)
        for width in widths
        for lead in ((2, rows), (8, half), (4, half), (4, half), (2, 4, half), (2, 2, 3, half))
    ]
    return scratch + [
        pltpu.SemaphoreType.DMA((2, items)),
        pltpu.SemaphoreType.DMA((2, 2)),
        pltpu.SemaphoreType.DMA((items, 2, 4)),
        pltpu.SemaphoreType.DMA((items, 2, 8)),
        pltpu.SemaphoreType.DMA((items, 3, 4)),
        pltpu.SemaphoreType.DMA((items, 2, 2, 3)),
        pltpu.SemaphoreType.DMA((items, 2, 2, 3)),
        pltpu.SemaphoreType.DMA((items, 4, products)),
        pltpu.SemaphoreType.REGULAR,
        pltpu.VMEM((2, 2, 4 * half, max(widths)), jnp.bfloat16),
        pltpu.VMEM((2, rows, max(widths)), jnp.bfloat16),
        pltpu.VMEM((4, depth, max(widths)), jnp.bfloat16),
    ]


def reduce_kernel(layout, lefts, rights, places, extra, facts, parts, gains_at, tag):
    anywhere = pl.BlockSpec(memory_space=pl.ANY)
    inside = pl.BlockSpec(memory_space=pltpu.VMEM)
    rows, depth = lefts[0].shape
    widths = [sum([product[2] for product in products]) for _, products in layout]
    shapes = [
        jax.ShapeDtypeStruct((rows // lax.axis_size("dp"), item[0].shape[1]), jnp.float32)
        for item in rights
    ]
    shapes.append(jax.ShapeDtypeStruct((8, 128), jnp.float32))
    found = pl.pallas_call(
        functools.partial(reduce_body, layout, parts, gains_at),
        name="reduce_grads",
        out_shape=shapes,
        in_specs=[anywhere] * 8 + [inside] * (3 + len(lefts)),
        out_specs=[inside] * 3,
        scratch_shapes=[
            pltpu.VMEM((8, 128), jnp.float32),
            pltpu.VMEM((4, 8, 128), jnp.float32),
            pltpu.VMEM((8, 8, 128), jnp.float32),
            pltpu.SemaphoreType.DMA((3,)),
            pltpu.SemaphoreType.DMA((4,)),
            pltpu.SemaphoreType.DMA((7,)),
            pltpu.SemaphoreType.DMA((8,)),
        ]
        + reduce_scratch(widths, 1, rows, depth),
        compiler_params=pltpu.CompilerParams(
            collective_id=tag, has_side_effects=True, vmem_limit_bytes=60 << 20
        ),
    )(*[item for quarters in rights for item in quarters], facts, places, extra, *lefts)
    return found[:-1], found[-1]


def update_body(sources, plans, *refs):
    count = len(plans)
    totals, fixes, grads = refs[0], refs[1], refs[2 : 2 + sources]
    refs = refs[2 + sources :]
    triples = [refs[3 * place : 3 * place + 3] for place in range(count)]
    outs = [refs[3 * (count + place) : 3 * (count + place) + 3] for place in range(count)]
    square, loss, real = totals[0:1, :], totals[1:2, :], totals[2:3, :]
    norm = jnp.sqrt(square) / real
    refs[6 * count][...] = jnp.concatenate([loss / real, norm] + [norm] * 6, axis=0)
    scale = (jnp.minimum(1.0, clip_at / norm) / real)[:, 0:1]
    over_one, over_two = fixes[0:1, 0:1], fixes[1:2, 0:1]

    def renew(place, grad, rows):
        source, turned, first, rate, decay = plans[place]
        weight, one, two = triples[place]
        clipped = grad * scale
        moment_one = beta_one * one[rows] + (1.0 - beta_one) * clipped
        moment_two = beta_two * two[rows] + (1.0 - beta_two) * clipped * clipped
        stepped = moment_one * over_one / (jnp.sqrt(moment_two * over_two) + adam_eps)
        outs[place][0][rows] = moment_one
        outs[place][1][rows] = moment_two
        outs[place][2][rows] = weight[rows] - rate * (stepped + decay * weight[rows])

    for place in range(count):
        source, turned, first, rate, decay = plans[place]
        rows, columns = triples[place][0].shape
        if turned and rows >= 128:
            for at in range(0, rows, 128):
                span = min(128, rows - at)
                block = grads[source][:, first + at : first + at + span].T
                renew(place, block, pl.ds(at, span))
        elif turned:
            start = first // 128 * 128
            block = grads[source][:, start : start + 128].T
            renew(place, block[first - start : first - start + rows], pl.ds(0, rows))
        else:
            for at in range(0, rows, 32):
                renew(place, grads[source][pl.ds(at, 32), first : first + columns], pl.ds(at, 32))


def update_kernel(totals, fixes, grads, plans, triples):
    inside = pl.BlockSpec(memory_space=pltpu.VMEM)
    flat = [item for triple in triples for item in triple]
    outs = [jax.ShapeDtypeStruct(item.shape, item.dtype) for item in flat] + [
        jax.ShapeDtypeStruct((8, 128), jnp.float32)
    ]
    found = pl.pallas_call(
        functools.partial(update_body, len(grads), plans),
        name="update_weights",
        out_shape=outs,
        in_specs=[inside] * (2 + len(grads) + len(flat)),
        out_specs=[inside] * len(outs),
        compiler_params=pltpu.CompilerParams(vmem_limit_bytes=60 << 20),
    )(totals, fixes, *grads, *flat)
    return found[:-1], found[-1]


def turn_halves(tile, cosine, sine):
    lane = lax.broadcasted_iota(jnp.int32, tile.shape, 1)
    other = jnp.where(lane % 64 < 32, pltpu.roll(tile, 96, 1), pltpu.roll(tile, 32, 1))
    return tile * cosine + other * sine


def attend_steps(normed, joints, cosine, sine, seg_row, seg_col, packed, lse, attended, between, leaving, heads_out, heads_in, send_sem, recv_sem, out_send, out_recv):
    device = neighbours()["c"]
    rows = normed.shape[0]

    def project(joint, put):
        found = jnp.dot(normed[...], joint[...], preferred_element_type=jnp.float32)
        for head in range(3):
            pair = turn_halves(found[:, 192 * head : 192 * head + 128], cosine[0:rows], sine[0:rows])
            value = found[:, 192 * head + 128 : 192 * head + 192]
            put(head, pair.astype(jnp.bfloat16), value.astype(jnp.bfloat16))

    def crossing(place):
        return pltpu.make_async_remote_copy(
            src_ref=leaving.at[place],
            dst_ref=packed.at[place, pl.ds(rows, rows)],
            send_sem=send_sem.at[place],
            recv_sem=recv_sem.at[place],
            device_id=device,
            device_id_type=MESH,
        )

    for side, joint in enumerate((joints[1], joints[3])):

        def put(head, pair, value):
            leaving[3 * side + head, :, 0:128] = pair
            leaving[3 * side + head, :, 128:192] = value
            crossing(3 * side + head).start()

        project(joint, put)
    for side, joint in enumerate((joints[0], joints[2])):

        def put(head, pair, value):
            packed[3 * side + head, pl.ds(0, rows), 0:128] = pair
            packed[3 * side + head, pl.ds(0, rows), 128:192] = value

        project(joint, put)

    def one_head(place):
        keys = packed[place, :, 0:128][:, 64:128]
        values_t = packed[place, :, 128:256][:, 0:64].astype(jnp.float32).T.astype(jnp.bfloat16)

        def block(turn, _):
            at = pl.ds(pl.multiple_of(turn * 256, 256), 256)
            query = packed[place, at, 0:128][:, 0:64] * jnp.bfloat16(HEAD_DIM ** (-0.5))
            scores = lax.dot_general(
                keys, query, (((1,), (1,)), ((), ())), preferred_element_type=jnp.float32
            )
            scores = jnp.where(seg_col[:, 0:1] == seg_row[0:1, at], scores, neg_fill)
            top = jnp.max(scores, axis=0, keepdims=True)
            expd = jnp.exp(scores - top)
            summed = jnp.sum(expd, axis=0, keepdims=True)
            probs = (expd * (1.0 / summed)).astype(jnp.bfloat16)
            found = jnp.dot(values_t, probs, preferred_element_type=jnp.float32)
            lse[pl.ds(place, 1), at] = top + jnp.log(summed)
            heads_out[place, at, 0:64] = found.T.astype(jnp.bfloat16)
            return 0

        lax.fori_loop(0, 2 * rows // 256, block, 0)

    between(0)
    for place in range(6):
        crossing(place).wait_recv()
    for place in range(6):
        one_head(place)
        between(1 + place)

    def returning(place):
        return pltpu.make_async_remote_copy(
            src_ref=heads_out.at[place, pl.ds(rows, rows)],
            dst_ref=heads_in.at[place],
            send_sem=out_send.at[place],
            recv_sem=out_recv.at[place],
            device_id=device,
            device_id_type=MESH,
        )

    for place in range(6):
        returning(place).start()
    for place in range(6):
        attended[:, 64 * place : 64 * place + 64] = heads_out[place, pl.ds(0, rows), 0:64]
    for place in range(6):
        returning(place).wait_recv()
        attended[:, 384 + 64 * place : 448 + 64 * place] = heads_in[place, :, 0:64]
    for place in range(6):
        crossing(place).wait_send()
        returning(place).wait_send()


def attend_back_body(layout, *refs):
    grad_out, packed, lse, attended, cosine, sine, seg_row, seg_col, left_up, left_down = refs[:10]
    ups, downs = refs[10:14], refs[14:18]
    p0, p1, p2, p3, r0, r1, r2, r3, summed, square_out = refs[18:28]
    grads, leaving, keys_t, probs, prob_grads, found, going, coming = refs[28:36]
    send_sem, recv_sem, out_send, out_recv = refs[36:40]
    span = ups[0].shape[1]
    outs = [summed.at[:, pl.ds(0, span)], summed.at[:, pl.ds(span, span)]]
    wide_refs = [[(ups, 0, span)], [(downs, 0, span)]]
    start_loads, begin, advance, turns, finish, drain = reduce_tools(
        layout, None, None, None, None, (left_up, left_down), wide_refs, outs, refs[40:]
    )
    start_loads()
    device = neighbours()["c"]
    rows = grad_out.shape[0]
    meet(lax.axis_index("dp") // 2, neighbours())

    def crossing(place):
        return pltpu.make_async_remote_copy(
            src_ref=leaving.at[place],
            dst_ref=grads.at[place, pl.ds(rows, rows)],
            send_sem=send_sem.at[place],
            recv_sem=recv_sem.at[place],
            device_id=device,
            device_id_type=MESH,
        )

    for place in range(6):
        leaving[place, :, 0:64] = grad_out[:, 384 + 64 * place : 448 + 64 * place]
        crossing(place).start()
        grads[place, pl.ds(0, rows), 0:64] = grad_out[:, 64 * place : 64 * place + 64]
    nothing = jnp.zeros((rows, 64), jnp.bfloat16)
    for order, (part, right) in enumerate(((p0, r0), (p2, r2), (p1, r1), (p3, r3))):
        part[:, 576:640] = nothing
        right[:, 576:640] = nothing
        right[:, 640:832] = attended[:, 192 * order : 192 * order + 192]
        right[:, 832:896] = nothing
    begin()
    for place in range(6):
        crossing(place).wait_recv()

    def one_head(place):
        query = packed[place, :, 0:128][:, 0:64]
        scaled = query * jnp.bfloat16(HEAD_DIM ** (-0.5))
        wide_keys = packed[place, :, 0:128][:, 64:128].astype(jnp.float32)
        keys_t[...] = wide_keys.T.astype(jnp.bfloat16)
        grad = grads[place, :, 0:64]
        stat = lse[pl.ds(place, 1), :]

        def score(turn, inner):
            at = pl.ds(pl.multiple_of(turn * 256, 256), 256)
            keys = packed[place, at, 0:128][:, 64:128]
            values = packed[place, at, 128:256][:, 0:64]
            scores = lax.dot_general(
                keys, scaled, (((1,), (1,)), ((), ())), preferred_element_type=jnp.float32
            )
            scores = jnp.where(seg_col[at, 0:1] == seg_row[0:1, :], scores, neg_fill)
            prob = jnp.exp(scores - stat)
            prob_grad = lax.dot_general(
                values, grad, (((1,), (1,)), ((), ())), preferred_element_type=jnp.float32
            )
            probs[at] = prob
            prob_grads[at] = prob_grad
            value_grad = jnp.dot(prob.astype(jnp.bfloat16), grad, preferred_element_type=jnp.float32)
            found[place, at, 128:192] = value_grad
            return inner + jnp.sum(prob * prob_grad, axis=0, keepdims=True)

        inner = lax.fori_loop(0, 2 * rows // 256, score, jnp.zeros((1, 2 * rows), jnp.float32))

        def spread_back(turn, query_grad):
            at = pl.ds(pl.multiple_of(turn * 256, 256), 256)
            score_grad = (probs[at] * (prob_grads[at] - inner)).astype(jnp.bfloat16)
            key_grad = jnp.dot(score_grad, scaled, preferred_element_type=jnp.float32)
            found[place, at, 64:128] = key_grad
            return query_grad + jnp.dot(keys_t[:, at], score_grad, preferred_element_type=jnp.float32)

        query_grad = lax.fori_loop(
            0, 2 * rows // 256, spread_back, jnp.zeros((64, 2 * rows), jnp.float32)
        )
        found[place, :, 0:64] = query_grad.T * HEAD_DIM ** (-0.5)

    for place in range(6):
        advance(2 * place)
        if 2 * place + 1 < turns:
            advance(2 * place + 1)
        one_head(place)
    for turn in range(12, turns):
        advance(turn)

    def returning(side):
        return pltpu.make_async_remote_copy(
            src_ref=going.at[side],
            dst_ref=coming.at[side],
            send_sem=out_send.at[side],
            recv_sem=out_recv.at[side],
            device_id=device,
            device_id_type=MESH,
        )

    for half in (1, 0):
        at = pl.ds(half * rows, rows)
        for side in range(2):
            for head in range(3):
                place = 3 * side + head
                pair = turn_halves(found[place, at, 0:128], cosine[at], -sine[at]).astype(jnp.bfloat16)
                value = found[place, at, 128:192].astype(jnp.bfloat16)
                puts = [going.at[side]] if half else [(p0, p2)[side], (r0, r2)[side]]
                for put in puts:
                    put[:, 192 * head : 192 * head + 128] = pair
                    put[:, 192 * head + 128 : 192 * head + 192] = value
            if half:
                returning(side).start()
    square_out[...] = jnp.full(square_out.shape, finish(), jnp.float32)
    for side in range(2):
        returning(side).wait_recv()
        for put in ((p1, p3)[side], (r1, r3)[side]):
            put[:, 0:576] = coming[side, :, 0:576]
    for place in range(6):
        crossing(place).wait_send()
    for side in range(2):
        returning(side).wait_send()
    drain()


def attend_back_kernel(layout, grad_out, packed, lse, attended, cosine, sine, seg_row, seg_col, lefts, ups, downs):
    rows = grad_out.shape[0]
    anywhere = pl.BlockSpec(memory_space=pl.ANY)
    width = ups[0].shape[1] + downs[0].shape[1]
    inside = pl.BlockSpec(memory_space=pltpu.VMEM)
    found = pl.pallas_call(
        functools.partial(attend_back_body, layout),
        name="attend_back",
        out_shape=[jax.ShapeDtypeStruct((rows, 640), jnp.bfloat16)] * 4
        + [jax.ShapeDtypeStruct((rows, 896), jnp.bfloat16)] * 4
        + [
            jax.ShapeDtypeStruct((lefts[0].shape[0] // lax.axis_size("dp"), width), jnp.float32),
            jax.ShapeDtypeStruct((8, 128), jnp.float32),
        ],
        in_specs=[inside] * 10 + [anywhere] * 8,
        out_specs=[inside] * 10,
        scratch_shapes=[
            pltpu.VMEM((6, 2 * rows, 128), jnp.bfloat16),
            pltpu.VMEM((6, rows, 128), jnp.bfloat16),
            pltpu.VMEM((64, 2 * rows), jnp.bfloat16),
            pltpu.VMEM((2 * rows, 2 * rows), jnp.float32),
            pltpu.VMEM((2 * rows, 2 * rows), jnp.float32),
            pltpu.VMEM((6, 2 * rows, 256), jnp.float32),
            pltpu.VMEM((2, rows, 640), jnp.bfloat16),
            pltpu.VMEM((2, rows, 640), jnp.bfloat16),
            pltpu.SemaphoreType.DMA((6,)),
            pltpu.SemaphoreType.DMA((6,)),
            pltpu.SemaphoreType.DMA((2,)),
            pltpu.SemaphoreType.DMA((2,)),
        ]
        + reduce_scratch([width // 2] * 2, 1, *lefts[0].shape),
        compiler_params=pltpu.CompilerParams(
            collective_id=3, has_side_effects=True, vmem_limit_bytes=62 << 20
        ),
    )(grad_out, packed, lse, attended, cosine, sine, seg_row, seg_col, *lefts, *ups, *downs)
    return found[:4], found[4:8], found[8], found[9]


def pieces_of(width):
    pieces, at = [], 0
    for span in (1024, 1024):
        pieces.append((at, span, span // 2 if span % 256 == 0 else span))
        at += span
    return pieces


def known_mesh():
    return lax.axis_size("dp") == 8 and lax.axis_size("tensor") == 4


def reduce_grads(layout, lefts, rights, places, extra, facts, parts, gains_at):
    if known_mesh():
        ordered = [[item[0], item[2], item[1], item[3]] for item in rights]
        return reduce_kernel(layout, lefts, ordered, places, extra, facts, parts, gains_at, 1)
    sums = []
    for item, (_, products) in enumerate(layout):
        quarters = []
        for quarter, mask in enumerate((0, 2, 1, 3)):
            right = rights[item][quarter]
            found = [mm(lefts[at], right[:, base : base + width]) for at, base, width, _ in products]
            if item == 0:
                spots = jnp.arange(right.shape[1], dtype=jnp.int32)[None, :]
                found[0] += mm(lefts[1], narrow(places[:, mask : mask + 1] == spots))
            if item == gains_at[0]:
                found[0] += extra
            quarters.append(narrow(jnp.concatenate(found, axis=1)))
        sums.append(reduce_all(quarters, True))
    square = sum(jnp.sum(item * item) for item in sums)
    repeated = sums[gains_at[0]][:, gains_at[1] : gains_at[1] + gains_at[2]]
    square = square - jnp.sum(repeated * repeated) * (1.0 - 1.0 / parts)
    tile = jnp.where(lax.broadcasted_iota(jnp.int32, (8, 128), 0) == 0, square, facts)
    return sums, everyone_sum(tile)


def wide(value):
    return value.astype(jnp.float32)


def narrow(value):
    return value.astype(jnp.bfloat16)


def fold(value, masks, last):
    rows = value.shape[0] // (len(masks) + 1)
    total = wide(value[:rows])
    for place, mask in enumerate(masks):
        total = total + wide(swap(value[(place + 1) * rows : (place + 2) * rows], "dp", mask))
    return total if last else narrow(total)


def reduce_all(quarters, x_first):
    groups = groups_of(lax.axis_size("dp"))
    own = narrow(wide(quarters[0]) + wide(swap(quarters[2], "tensor", 1)))
    other = narrow(wide(quarters[1]) + wide(swap(quarters[3], "tensor", 1)))
    if x_first:
        own = narrow(wide(own) + wide(swap(other, "tensor", 2)))
        own = fold(own, groups[0], len(groups) == 1)
    else:
        own = fold(own, groups[0], False)
        other = fold(other, groups[0], False)
        own = narrow(wide(own) + wide(swap(other, "tensor", 2)))
    for place in range(1, len(groups)):
        own = fold(own, groups[place], place == len(groups) - 1)
    return wide(own)


def everyone_sum(value):
    for masks in groups_of(lax.axis_size("dp")):
        value = sum([swap(value, "dp", mask) for mask in masks], value)
    for mask in (1, 2):
        value = value + swap(value, "tensor", mask)
    return value


def mm(left, right):
    return jnp.dot(left, right, preferred_element_type=jnp.float32)


def mm_nt(left, right):
    return lax.dot_general(left, right, (((1,), (1,)), ((), ())), preferred_element_type=jnp.float32)


def mm_tn(left, right):
    return lax.dot_general(left, right, (((0,), (0,)), ((), ())), preferred_element_type=jnp.float32)


def rotate_heads(values, cosine, sine):
    return rotate(values, cosine[:, None, :], sine[:, None, :])


def scores_of(query, key_rows, same_doc):
    scores = jnp.einsum(
        "qhe,khe->hqk", query, key_rows, preferred_element_type=jnp.float32
    ) * HEAD_DIM ** (-0.5)
    return jnp.where(same_doc[None], scores, neg_fill)


def split_heads(packed):
    packed = packed.reshape(packed.shape[0], -1, 3, HEAD_DIM)
    return packed[:, :, 0], packed[:, :, 1], packed[:, :, 2]


def attend(packed, same_doc):
    query, key_rows, value_rows = split_heads(packed)
    scores = scores_of(query, key_rows, same_doc)
    row_max = jnp.max(scores, axis=-1, keepdims=True)
    expd = jnp.exp(scores - row_max)
    summed = jnp.sum(expd, axis=-1, keepdims=True)
    probs = (expd / summed).astype(jnp.bfloat16)
    output = jnp.einsum("hqk,khe->qhe", probs, value_rows, preferred_element_type=jnp.float32)
    return (narrow(output).reshape(packed.shape[0], -1), (row_max + jnp.log(summed))[..., 0])


def attend_back(packed, same_doc, row_lse, grad_out, cosine, sine):
    query, key_rows, value_rows = split_heads(packed)
    grad_out = grad_out.reshape(packed.shape[0], -1, HEAD_DIM)
    scores = scores_of(query, key_rows, same_doc)
    probs = jnp.exp(scores - row_lse[..., None])
    value_grad = jnp.einsum(
        "hqk,qhe->khe", probs.astype(jnp.bfloat16), grad_out, preferred_element_type=jnp.float32
    )
    prob_grad = jnp.einsum("qhe,khe->hqk", grad_out, value_rows, preferred_element_type=jnp.float32)
    inner = jnp.sum(prob_grad * probs, axis=-1, keepdims=True)
    score_grad = (probs * (prob_grad - inner)).astype(jnp.bfloat16)
    query_grad = jnp.einsum(
        "hqk,khe->qhe", score_grad, key_rows, preferred_element_type=jnp.float32
    ) * HEAD_DIM ** (-0.5)
    key_grad = jnp.einsum(
        "hqk,qhe->khe", score_grad, query, preferred_element_type=jnp.float32
    ) * HEAD_DIM ** (-0.5)
    query_grad = rotate_heads(query_grad, cosine, -sine)
    key_grad = rotate_heads(key_grad, cosine, -sine)
    return narrow(jnp.stack([query_grad, key_grad, value_grad], axis=2).reshape(packed.shape))


def update_weights(totals, fixes, sums, plans, triples):
    if known_mesh():
        updated, results = update_kernel(totals, fixes, sums, plans, triples)
        return list(updated), results
    updated = []
    norm = jnp.sqrt(totals[0, 0]) / totals[2, 0]
    scale = jnp.minimum(1.0, clip_at / norm) / totals[2, 0]
    for (source, turned, first, rate, decay), (weight, one, two) in zip(plans, triples):
        columns = weight.shape[0] if turned else weight.shape[1]
        grad = sums[source][:, first : first + columns]
        clipped = (grad.T if turned else grad) * scale
        moment_one = beta_one * one + (1.0 - beta_one) * clipped
        moment_two = beta_two * two + (1.0 - beta_two) * clipped * clipped
        stepped = moment_one * fixes[0, 0] / (jnp.sqrt(moment_two * fixes[1, 0]) + adam_eps)
        updated.extend([moment_one, moment_two, weight - rate * (stepped + decay * weight)])
    return updated, jnp.stack([totals[1, 0] / totals[2, 0], norm])[:, None]


def per_device(
    tokens,
    lengths,
    timesteps,
    masks,
    step_count,
    table,
    joint_weight,
    output_weight,
    upward_weight,
    downward_weight,
    gains,
    momentum_table,
    momentum_joint,
    momentum_output,
    momentum_upward,
    momentum_downward,
    momentum_gains,
    variance_table,
    variance_joint,
    variance_output,
    variance_upward,
    variance_downward,
    variance_gains,
):
    place = lax.axis_index("tensor")
    parts = lax.axis_size("tensor")
    rows = tokens.shape[0] // parts
    vocab_part, head_part = table.shape[0], joint_weight.shape[1]
    out_part, ff_part = output_weight.shape[0], upward_weight.shape[1]

    gain_columns = jnp.pad(narrow(gains).T, ((0, 0), (0, 61)))
    shards = [
        narrow(table).T,
        jnp.concatenate([narrow(joint_weight), gain_columns], axis=1),
        narrow(upward_weight),
        narrow(downward_weight).T,
        narrow(output_weight).T,
    ]
    start = place * rows
    seq = start // SEQ_LEN
    mine = start - seq * SEQ_LEN
    cut = lambda array: lax.dynamic_slice(array, (start,), (rows,))
    targets = cut(tokens)
    corrupt = cut(masks) == 1
    inputs = jnp.where(corrupt, VOCAB - 1, targets)
    own_lengths = lax.dynamic_slice(lengths, (seq, 0), (1, DOCS))
    step_here = lax.dynamic_slice(timesteps, (seq,), (1,))
    theirs = mine ^ rows
    position = jnp.concatenate(
        [mine + jnp.arange(rows, dtype=jnp.int32), theirs + jnp.arange(rows, dtype=jnp.int32)]
    )
    doc_ends = jnp.cumsum(own_lengths[0])
    doc_starts = doc_ends - own_lengths[0]
    segment = jnp.sum((position[:, None] >= doc_ends[None, :]).astype(jnp.int32), axis=1)
    chosen = segment[:, None] == jnp.arange(DOCS, dtype=jnp.int32)[None, :]
    offset = position - jnp.sum(jnp.where(chosen, doc_starts[None, :], 0), axis=1)
    is_real = segment < DOCS - 1
    factor = jnp.where(step_here == 1, 1.0, T_DIFF / step_here.astype(jnp.float32))
    weights = jnp.where(corrupt & is_real[:rows], factor, 0.0)
    inverse_freq = 10000.0 ** (-jnp.arange(HEAD_DIM // 2, dtype=jnp.float32) / (HEAD_DIM // 2))
    angles = offset.astype(jnp.float32)[:, None] * inverse_freq
    cosine, sine = jnp.cos(angles), jnp.sin(angles)
    same_doc = segment[:, None] == segment[None, :]

    def hot(ids, piece):
        base = (place ^ (2 * (piece % 2) + piece // 2)) * vocab_part
        return (ids - base)[:, None] == jnp.arange(vocab_part, dtype=jnp.int32)[None, :]

    pieces = range(4)
    lane = jnp.arange(128, dtype=jnp.int32)[None, :]
    places = inputs[:, None] - (place ^ (lane % 4)) * vocab_part

    on_known = known_mesh()
    if on_known:
        cosines = jnp.concatenate([cosine] * 4, axis=1)
        sines = jnp.concatenate([-sine, sine] * 2, axis=1)
        seg_row = jnp.broadcast_to(segment[None, :], (8, 2 * rows))
        seg_col = jnp.broadcast_to(segment[:, None], (2 * rows, 128))
        groups, (embedded, normed_one, packed, attn_lse, attended_all) = start_kernel(
            shards, places, cosines, sines, seg_row, seg_col
        )
        groups = [[item[0], item[2], item[1], item[3]] for item in groups]
    else:
        groups = [gather_all(item, True) for item in shards]
    table_q, first_group, up_q, down_q, out_q = groups
    gain_full = wide(first_group[0][:, head_part : head_part + 3]).T
    out_all = jnp.concatenate(out_q, axis=1)
    if not on_known:
        joint_q = [item[:, :head_part] for item in first_group]
        looked = sum(mm_nt(narrow(hot(inputs, piece)), table_q[piece]) for piece in pieces)
        embedded = looked * D**0.5
        normed_one = narrow(norm_apply(embedded, gain_full[0]))

        def turned(projected):
            projected = projected.reshape(rows, -1, 3, HEAD_DIM)
            query = rotate_heads(projected[:, :, 0], cosine[:rows], sine[:rows])
            key_rows = rotate_heads(projected[:, :, 1], cosine[:rows], sine[:rows])
            stacked = jnp.stack([query, key_rows, projected[:, :, 2]], axis=2)
            return narrow(stacked.reshape(rows, -1))

        packed = [turned(mm(normed_one, item)) for item in joint_q]
        whole = [
            jnp.concatenate([packed[side], swap(packed[2 + side], "tensor", 1)], axis=0)
            for side in range(2)
        ]
        attended, attn_lse = zip(*[attend(item, same_doc) for item in whole])
        attended_all = jnp.concatenate(
            [item[:rows] for item in attended]
            + [swap(item[rows:], "tensor", 1) for item in attended],
            axis=1,
        )
    after_attn = embedded + mm_nt(attended_all, out_all)
    normed_two = narrow(norm_apply(after_attn, gain_full[1]))
    pre_gelu = [mm(normed_two, item) for item in up_q]
    below = [0.5 + 0.5 * lax.erf(item * 0.5**0.5) for item in pre_gelu]
    slopes = [
        part + item * jnp.exp(-0.5 * item * item) * (0.5 / jnp.pi) ** 0.5
        for part, item in zip(below, pre_gelu)
    ]
    activated = [narrow(item * part) for part, item in zip(below, pre_gelu)]
    after_mlp = after_attn + sum(mm_nt(activated[q], down_q[q]) for q in range(4))
    normed_out = narrow(norm_apply(after_mlp, gain_full[2]))
    logits = [mm(normed_out, item) for item in table_q]
    row_max = logits[0].max(axis=1)
    for item in logits[1:]:
        row_max = jnp.maximum(row_max, item.max(axis=1))
    row_sum = sum(jnp.sum(jnp.exp(item - row_max[:, None]), axis=1) for item in logits)
    target_hot = [hot(targets, piece) for piece in pieces]
    row_pick = sum(
        jnp.sum(jnp.where(target_hot[piece], logits[piece], 0.0), axis=1) for piece in pieces
    )
    row_lse = row_max + jnp.log(row_sum)
    loss_local = jnp.sum(weights * (row_lse - row_pick))
    count_local = jnp.sum(is_real[:rows].astype(jnp.float32))

    logit_grad = [
        narrow(
            weights[:, None]
            * (jnp.exp(logits[piece] - row_lse[:, None]) - target_hot[piece].astype(jnp.float32))
        )
        for piece in pieces
    ]
    out_grad = sum(mm_nt(logit_grad[piece], table_q[piece]) for piece in pieces)
    mlp_grad, gain_three = norm_back(after_mlp, gain_full[2], out_grad)
    mlp_branch = narrow(mlp_grad)
    up_input = [
        narrow(slopes[q] * mm(mlp_branch, down_q[q])) for q in range(4)
    ]
    normed_two_grad = sum(mm_nt(up_input[q], up_q[q]) for q in range(4))
    attn_in_grad, gain_two = norm_back(after_attn, gain_full[1], normed_two_grad)
    resid_one = mlp_grad + attn_in_grad
    attn_branch = narrow(resid_one)
    attended_grad = narrow(mm(attn_branch, out_all))
    if on_known:
        proj_grad, last_rights, middle_sum, middle_square = attend_back_kernel(
            ((None, ((0, 0, ff_part, ff_part // 2),)), (None, ((1, 0, ff_part, ff_part // 2),))),
            attended_grad,
            packed,
            attn_lse,
            attended_all,
            cosines,
            sines,
            seg_row,
            seg_col,
            [normed_two.T, mlp_branch.T],
            [up_input[q] for q in (0, 2, 1, 3)],
            [activated[q] for q in (0, 2, 1, 3)],
        )
        proj_grad = [proj_grad[q] for q in (0, 2, 1, 3)]
        last_rights = [last_rights[q] for q in (0, 2, 1, 3)]
        joint_back = first_group
    else:
        grad_parts = [attended_grad[:, q * out_part : (q + 1) * out_part] for q in range(4)]
        proj_whole = [
            attend_back(
                whole[side],
                same_doc,
                attn_lse[side],
                jnp.concatenate(
                    [grad_parts[side], swap(grad_parts[2 + side], "tensor", 1)], axis=0
                ),
                cosine,
                sine,
            )
            for side in range(2)
        ]
        proj_grad = [item[:rows] for item in proj_whole] + [
            swap(item[rows:], "tensor", 1) for item in proj_whole
        ]
        joint_back = joint_q
    normed_one_grad = sum(mm_nt(proj_grad[q], joint_back[q]) for q in range(4))
    embed_in, gain_one = norm_back(embedded, gain_full[0], normed_one_grad)
    embed_grad = resid_one + embed_in
    embed_scaled = narrow(embed_grad * D**0.5)
    sublane = lax.broadcasted_iota(jnp.int32, (8, 128), 0)
    facts = jnp.where(sublane == 1, loss_local, jnp.where(sublane == 2, count_local, 0.0))
    gains_end = (head_part + gains.shape[0] + 127) // 128 * 128
    out_fill = (out_part + 127) // 128 * 128
    fill = lambda array, columns: jnp.pad(array, ((0, 0), (0, columns - array.shape[1])))
    extra = jnp.pad(
        jnp.stack([gain_one, gain_two, gain_three]).T,
        ((0, 0), (head_part, gains_end - head_part - gains.shape[0])),
    )
    if not on_known:
        attended_q = [attended_all[:, q * out_part : (q + 1) * out_part] for q in range(4)]
        last_rights = [
            jnp.concatenate([fill(proj_grad[q], gains_end), fill(attended_q[q], out_fill)], axis=1)
            for q in range(4)
        ]
    lefts = [normed_out, embed_scaled, normed_one, attn_branch]
    rights = [logit_grad, last_rights]
    layout = (
        (None, ((2, 0, gains_end, gains_end), (3, gains_end, out_fill, out_fill))),
        *((at, ((0, 0, span, step),)) for at, span, step in pieces_of(vocab_part)),
    )
    gains_at = (0, head_part, gains_end - head_part)
    if on_known:
        facts = facts + jnp.where(sublane == 0, middle_square, 0.0)
    else:
        layout = (
            (0, ((0, 0, vocab_part, vocab_part),)),
            (None, ((2, 0, gains_end, gains_end), (3, gains_end, out_fill, out_fill))),
            (None, ((4, 0, ff_part, ff_part), (5, ff_part, ff_part, ff_part))),
        )
        gains_at = (1, head_part, gains_end - head_part)
        lefts = lefts + [normed_two, mlp_branch]
        rights = rights + [[jnp.concatenate([up_input[q], activated[q]], axis=1) for q in range(4)]]
    sums, totals = reduce_grads(
        layout, [item.T for item in lefts], rights, places, extra, facts, parts, gains_at
    )
    if on_known:
        sums = [*sums, middle_sum]
    step_float = step_count[0].astype(jnp.float32)
    fixes = jnp.where(
        sublane == 0,
        1.0 / (1.0 - jnp.power(beta_one, step_float)),
        1.0 / (1.0 - jnp.power(beta_two, step_float)),
    )
    plans = (
        (0, False, 0, rates[0], decays[0]),
        (1, False, 0, rates[1], decays[1]),
        (1, True, gains_end, rates[2], decays[2]),
        (2, False, 0, rates[3], decays[3]),
        (2, False, ff_part, rates[4], decays[4]),
        (1, True, head_part, rates[5], decays[5]),
    )
    triples = (
        (table.T, momentum_table.T, variance_table.T),
        (joint_weight, momentum_joint, variance_joint),
        (output_weight, momentum_output, variance_output),
        (upward_weight, momentum_upward, variance_upward),
        (downward_weight.T, momentum_downward.T, variance_downward.T),
        (gains, momentum_gains, variance_gains),
    )
    updated, results = update_weights(totals, fixes, sums, plans, triples)
    updated = [item.T if place // 3 in (0, 4) else item for place, item in enumerate(updated)]
    return tuple([results[0, 0], results[1, 0]] + updated)


def solution(mesh):
    placed = (
        P("dp"),
        P("dp", None),
        P("dp"),
        P("dp"),
        P(),
        P("tensor", "dp"),
        P("dp", "tensor"),
        P("tensor", "dp"),
        P("dp", "tensor"),
        P("tensor", "dp"),
        P(None, "dp"),
        P("tensor", "dp"),
        P("dp", "tensor"),
        P("tensor", "dp"),
        P("dp", "tensor"),
        P("tensor", "dp"),
        P(None, "dp"),
        P("tensor", "dp"),
        P("dp", "tensor"),
        P("tensor", "dp"),
        P("dp", "tensor"),
        P("tensor", "dp"),
        P(None, "dp"),
    )
    return jax.shard_map(
        per_device,
        mesh=mesh,
        in_specs=placed,
        out_specs=(
            P(),
            P(),
            P("tensor", "dp"),
            P("tensor", "dp"),
            P("tensor", "dp"),
            P("dp", "tensor"),
            P("dp", "tensor"),
            P("dp", "tensor"),
            P("tensor", "dp"),
            P("tensor", "dp"),
            P("tensor", "dp"),
            P("dp", "tensor"),
            P("dp", "tensor"),
            P("dp", "tensor"),
            P("tensor", "dp"),
            P("tensor", "dp"),
            P("tensor", "dp"),
            P(None, "dp"),
            P(None, "dp"),
            P(None, "dp"),
        ),
        check_vma=False,
    )
```

```python
import functools

import jax
import jax.numpy as jnp
from jax import lax
from jax.experimental import pallas as pl
from jax.experimental.pallas import tpu as pltpu
from jax.sharding import PartitionSpec as P

D = 768
HEAD_DIM = 64
VOCAB = 8192
SEQ_LEN = 1024
DOCS = 4
T_DIFF = 1000


eps_norm = 1e-06
neg_fill = -1000000000.0
beta_one = 0.9
beta_two = 0.999
adam_eps = 1e-08
clip_at = 0.02
rates = (0.05, 0.03, 0.25, 0.03, 0.03, 0.3)
decays = (0.1, 0.1, 0.1, 0.1, 0.1, 0.0)


def norm_apply(values, gain):
    inverse = lax.rsqrt(jnp.mean(values * values, axis=-1, keepdims=True) + eps_norm)
    return values * inverse * gain


def norm_back(values, gain, upstream):
    inverse = lax.rsqrt(jnp.mean(values * values, axis=-1, keepdims=True) + eps_norm)
    gain_grad = jnp.sum(upstream * values * inverse, axis=0)
    scaled = upstream * gain
    inner = jnp.mean(scaled * values, axis=-1, keepdims=True)
    return (inverse * (scaled - values * inverse * inverse * inner), gain_grad)


def rotate(values, cosine, sine):
    middle = values.shape[-1] // 2
    front_part = values[..., :middle]
    back_part = values[..., middle:]
    return jnp.concatenate(
        [front_part * cosine - back_part * sine, back_part * cosine + front_part * sine], axis=-1
    )


def groups_of(count):
    groups, bit, width = [], 1, 1
    while bit < count:
        masks = [bit]
        if width == 2 and bit * 2 < count:
            masks = [bit, 2 * bit, 3 * bit]
            bit = bit * 2
        groups.append(masks)
        bit, width = bit * 2, 2
    return groups


def swap(value, axis, mask):
    size = lax.axis_size(axis)
    return lax.ppermute(value, axis, [(place, place ^ mask) for place in range(size)])


def spread(value, masks):
    return jnp.concatenate([value] + [swap(value, "dp", mask) for mask in masks], axis=0)


def gather_all(value, x_last):
    groups = groups_of(lax.axis_size("dp"))
    for masks in groups[:0:-1]:
        value = spread(value, masks)
    if x_last:
        value = spread(value, groups[0])
        other = swap(value, "tensor", 2)
    else:
        other = swap(value, "tensor", 2)
        value = spread(value, groups[0])
        other = spread(other, groups[0])
    return [value, other, swap(value, "tensor", 1), swap(other, "tensor", 1)]


MESH = pl.DeviceIdType.MESH


def neighbours():
    column, row = lax.axis_index("dp"), lax.axis_index("tensor")
    return {
        "x": (column, (row + 2) % 4),
        "c": (column, row + 1 - 2 * (row % 2)),
        "y": (column + 1 - 2 * (column % 2), row),
        "up": (column + 2, row),
        "down": (column - 2, row),
    }


def meet(z, devices):
    barrier = pltpu.get_barrier_semaphore()

    def greet(name):
        pl.semaphore_signal(barrier, inc=1, device_id=devices[name], device_id_type=MESH)

    for name in ("x", "c", "y"):
        greet(name)
    pl.when(z < 3)(lambda: greet("up"))
    pl.when(z > 0)(lambda: greet("down"))
    pl.semaphore_wait(barrier, 3 + (z + 2) // 3 + (5 - z) // 3)


def start_body(items, *refs):
    arrays = items - 1
    given = refs[:arrays]
    places, cosine, sine, seg_row, seg_col = refs[arrays : arrays + 5]
    refs = refs[arrays + 5 :]
    kept = [refs[4 * array : 4 * array + 4] for array in range(arrays)]
    embedded_out, normed, packed, lse, attended = refs[4 * arrays : 4 * arrays + 5]
    refs = refs[4 * arrays + 5 :]
    side_sem, z_sem, late_sem, recv_sem, own_sem, keep_sem = refs[:6]
    staged = refs[6:8]
    attend_refs = refs[8:]
    late = (1, 3)
    cut = given[0].shape[1] - 256
    columns = [pl.ds(0, cut), pl.ds(cut, 256)] + [pl.ds(0, item.shape[1]) for item in given[1:]]
    ins = [given[0].at[:, columns[0]], given[0].at[:, columns[1]], *given[1:]]
    column = lax.axis_index("dp")
    z = column // 2
    devices = neighbours()
    meet(z, devices)
    shard = [given[0].shape[0]] * items
    piece = [item // 2 for item in shard]

    def base(item, quarter, rows):
        if item < 3:
            return staged[item // 2].at[quarter, rows, columns[item]]
        return kept[item - 1][quarter].at[rows]

    def mirror(source):
        return source + 1 - 2 * (source % 2)

    def view(item, part, quarter, source):
        start = pl.multiple_of(source * shard[item] + part * piece[item], 8)
        return base(item, quarter, pl.ds(start, piece[item]))

    def copy(item, part, quarter, source, to_quarter, name, send, own=False):
        here = view(item, part, quarter, source)
        if own:
            own_rows = pl.ds(part * piece[item], piece[item])
            here = given[0].at[own_rows, columns[item]] if item < 2 else given[item - 1].at[own_rows]
        return pltpu.make_async_remote_copy(
            src_ref=here,
            dst_ref=view(item, part, to_quarter, source),
            send_sem=send,
            recv_sem=recv_sem.at[item, part, to_quarter, source],
            device_id=devices[name],
            device_id_type=MESH,
        )

    def arrived(item, part, quarter, source):
        copy(item, part, quarter, source, quarter, "x", side_sem.at[0, item]).wait_recv()

    def send_x(item, part, source, own=False):
        copy(item, part, 0, source, 2, "x", side_sem.at[0, item], own).start()

    def send_y(item, part, quarter, source, own=False):
        copy(item, part, quarter, source, quarter, "y", side_sem.at[1, item], own).start()

    def send_c(item, part, quarter, source, own=False):
        copy(item, part, quarter, source, quarter + 1, "c", side_sem.at[2 + quarter // 2, item], own).start()

    def send_z(item, part, source, turn, upward, own=False, quarter=0, kind=0):
        name = "up" if upward else "down"
        sem = z_sem.at[item, part, 1 - upward, turn]
        if item in late:
            sem = late_sem.at[item // 2, part, 1 - upward, turn, kind]
        copy(item, part, quarter, source, quarter, name, sem, own).start()

    def slot(turn, action):
        pl.when(z >= turn)(lambda: action(column - 2 * turn, 1))
        pl.when(z + turn <= 3)(lambda: action(column + 2 * turn, 0))

    every = [(item, part) for item in range(items) for part in range(2)]

    def local(item):
        return pltpu.make_async_copy(
            ins[item],
            base(item, 0, pl.ds(pl.multiple_of(column * shard[item], 8), shard[item])),
            own_sem.at[item],
        )

    def keep(item, quarter):
        return pltpu.make_async_copy(staged[item].at[quarter], kept[item][quarter], keep_sem.at[item, quarter])

    def begin(item):
        for part in range(2):
            pl.when(z < 3)(lambda: send_z(item, part, column, 0, 1, True))
            pl.when(z > 0)(lambda: send_z(item, part, column, 0, 0, True))
            send_x(item, part, column, True)
            send_y(item, part, 0, column, True)
            send_c(item, part, 0, column, True)
        local(item).start()

    def from_z(item, part, turn, source, upward):
        arrived(item, part, 0, source)
        if turn < 3:
            ahead = z < 3 if upward else z > 0
            pl.when(ahead)(lambda: send_z(item, part, source, turn, upward))
        send_x(item, part, source)
        send_y(item, part, 0, source)
        send_c(item, part, 0, source)

    def second(item, source):
        arrived(item, 0, 0, mirror(source))
        send_x(item, 0, mirror(source))
        send_c(item, 0, 0, mirror(source))
        arrived(item, 1, 2, source)
        send_y(item, 1, 2, source)
        send_c(item, 1, 2, source)

    def third(item, source):
        arrived(item, 0, 2, source)
        send_c(item, 0, 2, source)
        arrived(item, 1, 0, mirror(source))
        send_c(item, 1, 0, mirror(source))
        for part in range(2):
            arrived(item, part, 2, mirror(source))
            send_c(item, part, 2, mirror(source))

    def along_z(item, turn):
        for part in range(2):
            slot(turn, lambda source, upward: from_z(item, part, turn, source, upward))

    def onward(action, item, turn):
        if turn == 0:
            action(item, column)
        else:
            slot(turn, lambda source, upward: action(item, source))

    def complete(item):
        for part in range(2):
            for source in range(8):
                for quarter in (1, 3):
                    arrived(item, part, quarter, source)
        local(item).wait()
        if item in (1, 2):
            for quarter in range(4):
                keep(item - 1, quarter).start()

    def kinds(source):
        return ((0, source), (2, source), (0, mirror(source)), (2, mirror(source)))

    def both_ways(item, part, kind):
        quarter, source = kinds(column)[kind]
        pl.when(z < 3)(lambda: send_z(item, part, source, 0, 1, False, quarter, kind))
        pl.when(z > 0)(lambda: send_z(item, part, source, 0, 0, False, quarter, kind))
        send_c(item, part, quarter, source)

    def late_first(item):
        other = mirror(column)
        arrived(item, 0, 2, column)
        send_y(item, 0, 2, column)
        both_ways(item, 0, 1)
        arrived(item, 1, 0, other)
        send_x(item, 1, other)
        both_ways(item, 1, 2)
        arrived(item, 0, 0, other)
        both_ways(item, 0, 2)
        arrived(item, 1, 2, column)
        both_ways(item, 1, 1)

    def late_second(item):
        for part in range(2):
            arrived(item, part, 2, mirror(column))
            both_ways(item, part, 3)

    def late_z(item, turn):
        def action(place, upward):
            for kind, (quarter, source) in enumerate(kinds(place)):
                for part in range(2):
                    arrived(item, part, quarter, source)
                    if turn < 3:
                        ahead = z < 3 if upward else z > 0
                        pl.when(ahead)(lambda: send_z(item, part, source, turn, upward, False, quarter, kind))
                    send_c(item, part, quarter, source)

        slot(turn, action)

    rest = range(4, items)
    begin(0)
    begin(1)
    late_first(1)
    along_z(0, 1)
    late_second(1)
    for turn in (2, 3):
        along_z(0, turn)
    late_z(1, 1)
    begin(2)
    for turn in range(4):
        onward(second, 0, turn)
    late_z(1, 2)
    for turn in (1, 2, 3):
        along_z(2, turn)
    late_z(1, 3)
    for turn in range(4):
        onward(third, 0, turn)
    for item in range(3, items):
        begin(item)
    complete(0)
    complete(1)

    def look_up(quarter):
        def one(chunk, _):
            at = pl.ds(pl.multiple_of(chunk * 512, 512), 512)
            spots = lax.broadcasted_iota(jnp.int32, (places.shape[0], 512), 1) + chunk * 512
            hot = jnp.where(places[:, quarter : quarter + 1] == spots, 1.0, 0.0).astype(jnp.bfloat16)
            embedded_out[...] += lax.dot_general(
                hot, staged[0][quarter, :, at], (((1,), (1,)), ((), ())), preferred_element_type=jnp.float32
            )
            return 0

        lax.fori_loop(0, staged[0].shape[2] // 512, one, 0)

    embedded_out[...] = jnp.zeros_like(embedded_out)
    look_up(0)
    late_first(3)
    for turn in range(4):
        onward(second, 2, turn)
    look_up(2)
    for item in rest:
        along_z(item, 1)
    late_second(3)
    look_up(1)
    for turn in range(4):
        onward(third, 2, turn)
    for item in rest:
        along_z(item, 2)
    late_z(3, 1)
    look_up(3)
    complete(2)
    gain = staged[1][0, :, 512:640].astype(jnp.float32).T[64:65]
    value = embedded_out[...] * D**0.5
    embedded_out[...] = value
    inverse = lax.rsqrt(jnp.mean(value * value, axis=-1, keepdims=True) + eps_norm)
    normed[...] = (value * inverse * gain).astype(jnp.bfloat16)
    for item in rest:
        along_z(item, 3)

    def between(stage):
        if stage in (2, 5):
            late_z(3, 2 if stage == 2 else 3)
        for item in rest:
            if stage == 0:
                onward(second, item, 0)
                onward(second, item, 1)
            if stage == 1:
                onward(second, item, 2)
                onward(second, item, 3)
            if stage == 6:
                for turn in range(4):
                    onward(third, item, turn)

    attend_steps(
        normed, [staged[1].at[q] for q in range(4)], cosine, sine, seg_row, seg_col, packed, lse, attended, between, *attend_refs
    )
    for item in range(3, items):
        complete(item)
    for item in range(2):
        for quarter in range(4):
            keep(item, quarter).wait()
    for item in range(items):
        for way, count in enumerate((3, 3, 16, 16) if item in late else (12, 12, 16, 16)):
            lead = base(item, 0, pl.ds(0, count * piece[item]))
            pltpu.make_async_remote_copy(
                src_ref=lead,
                dst_ref=lead,
                send_sem=side_sem.at[way, item],
                recv_sem=recv_sem.at[item, 0, 0, 0],
                device_id=devices["x"],
                device_id_type=MESH,
            ).wait_send()
    for item, part in every:
        for turn in range(3):
            for kind in range(4 if item in late else 1):
                sems = [
                    late_sem.at[item // 2, part, way, turn, kind] if item in late else z_sem.at[item, part, way, turn]
                    for way in range(2)
                ]
                pl.when((z < 3) & (z >= turn))(
                    lambda: copy(item, part, 0, column, 0, "up", sems[0], True).wait_send()
                )
                pl.when((z > 0) & (z + turn <= 3))(
                    lambda: copy(item, part, 0, column, 0, "down", sems[1], True).wait_send()
                )


def start_kernel(shards, places, cosine, sine, seg_row, seg_col):
    arrays = len(shards)
    items = arrays + 1
    anywhere = pl.BlockSpec(memory_space=pl.ANY)
    inside = pl.BlockSpec(memory_space=pltpu.VMEM)
    whole, rows = lax.axis_size("dp"), places.shape[0]
    full = [(item.shape[0] * whole, item.shape[1]) for item in shards]
    shapes = [jax.ShapeDtypeStruct(shape, jnp.bfloat16) for shape in full for _ in range(4)]
    flat = pl.pallas_call(
        functools.partial(start_body, items),
        name="start",
        out_shape=shapes
        + [
            jax.ShapeDtypeStruct((rows, full[0][0]), jnp.float32),
            jax.ShapeDtypeStruct((rows, full[0][0]), jnp.bfloat16),
            jax.ShapeDtypeStruct((6, 2 * rows, 256), jnp.bfloat16),
            jax.ShapeDtypeStruct((8, 2 * rows), jnp.float32),
            jax.ShapeDtypeStruct((rows, 768), jnp.bfloat16),
        ],
        in_specs=[anywhere] * arrays + [inside] * 5,
        out_specs=[anywhere] * (4 * arrays) + [inside] * 5,
        scratch_shapes=[
            pltpu.SemaphoreType.DMA((4, items)),
            pltpu.SemaphoreType.DMA((items, 2, 2, 3)),
            pltpu.SemaphoreType.DMA((2, 2, 2, 3, 4)),
            pltpu.SemaphoreType.DMA((items, 2, 4, 8)),
            pltpu.SemaphoreType.DMA((items,)),
            pltpu.SemaphoreType.DMA((2, 4)),
            pltpu.VMEM((4, *full[0]), jnp.bfloat16),
            pltpu.VMEM((4, *full[1]), jnp.bfloat16),
            pltpu.VMEM((6, rows, 256), jnp.bfloat16),
            pltpu.VMEM((6, 2 * rows, 128), jnp.bfloat16),
            pltpu.VMEM((6, rows, 128), jnp.bfloat16),
            pltpu.SemaphoreType.DMA((6,)),
            pltpu.SemaphoreType.DMA((6,)),
            pltpu.SemaphoreType.DMA((6,)),
            pltpu.SemaphoreType.DMA((6,)),
        ],
        compiler_params=pltpu.CompilerParams(
            collective_id=0, has_side_effects=True, vmem_limit_bytes=56 << 20
        ),
    )(*shards, places, cosine, sine, seg_row, seg_col)
    return [flat[4 * array : 4 * array + 4] for array in range(arrays)], flat[4 * arrays :]


def reduce_tools(layout, gains_at, parts, places, extra, lefts, wide_refs, outs, refs):
    items = len(layout)
    held = [refs[6 * item : 6 * item + 6] for item in range(items)]
    refs = refs[6 * items :]
    side_sem, c_send, c_sem, x_sem, y_sem, zs_sem, zr_sem, load_sem, free_sem = refs[:9]
    crossed, from_c, rights = refs[9:]
    column = lax.axis_index("dp")
    z = column // 2
    devices = neighbours()
    shard = [item.shape[0] for item in outs]
    piece = [item // 2 for item in shard]
    width = [item.shape[1] for item in outs]

    def load(item, quarter, which):
        sources, first_column, span = wide_refs[item][which]
        before = sum([part[2] for part in wide_refs[item][:which]])
        return pltpu.make_async_copy(
            sources[quarter].at[:, pl.ds(first_column, span)],
            rights.at[quarter, :, pl.ds(before, span)],
            load_sem.at[item, quarter, which],
        )

    def start_loads(item):
        for quarter in range(4):
            for which in range(len(wide_refs[item])):
                load(item, quarter, which).start()

    def span(item, part, source):
        return pl.ds(pl.multiple_of(source * shard[item] + part * piece[item], 8), piece[item])

    def remote(src, dst, send, recv, name):
        return pltpu.make_async_remote_copy(
            src_ref=src, dst_ref=dst, send_sem=send, recv_sem=recv, device_id=devices[name], device_id_type=MESH
        )

    def c_copy(item, side, source, slot=0):
        columns = pl.ds(0, width[item])
        block = 2 * shard[item]
        there = pl.ds(pl.multiple_of(source // 2 * block, 16), block)
        return remote(
            crossed.at[side, slot, :, columns],
            from_c.at[side, there, columns],
            c_send.at[side, slot],
            c_sem.at[item, side, source // 2],
            "c",
        )

    def c_sent(item, slot):
        for side in range(2):
            c_copy(item, side, 0, slot).wait_send()

    def x_copy(item, part, source):
        place = source if part == 0 else source // 2
        return remote(
            held[item][0].at[1, span(item, part, source)],
            held[item][1 + part].at[place],
            side_sem.at[0, item],
            x_sem.at[item, part, place],
            "x",
        )

    def y_copy(item, part, side, source):
        return remote(
            held[item][0].at[side, span(item, part, source)],
            held[item][3].at[source // 2] if part == 0 else held[item][4].at[side, source // 2],
            side_sem.at[1, item],
            y_sem.at[item, part + side, source // 2],
            "y",
        )

    def z_copy(item, part, source, away, upward):
        return remote(
            held[item][0].at[0, span(item, part, source)],
            held[item][5].at[1 - upward, part, away],
            zs_sem.at[item, part, 1 - upward, away],
            zr_sem.at[item, part, 1 - upward, away],
            "up" if upward else "down",
        )

    def add(item, side, part, source, *others):
        total = held[item][0]
        start = source * shard[item] + part * piece[item]
        step = 16

        def one(turn, _):
            here = pl.ds(pl.multiple_of(start + turn * step, 8), step)
            value = total[side, here]
            for other in others:
                value = value + other(turn * step, step)
            total[side, here] = value
            return 0

        lax.fori_loop(0, piece[item] // step, one, 0)

    def c_part(item, side, part, source):
        start = source * shard[item] + part * piece[item]

        def read(at, step):
            here = pl.ds(pl.multiple_of(start + at, 8), step)
            return from_c[side, here, pl.ds(0, width[item])]

        return read

    def of(ref, *place):
        return lambda at, step: ref[(*place, pl.ds(pl.multiple_of(at, 8), step))]

    def mirror(source):
        return source + 1 - 2 * (source % 2)

    def target(turn):
        low = 3 - turn if turn < 2 else jnp.where(z % 3 == 0, 3 - turn, turn - 2)
        return column + 2 * (jnp.where(z < 2, low, 3 - low) - z)

    def send_c(item, turn):
        source = target(turn)
        if item > 0:
            pl.semaphore_wait(free_sem, 1)
        for side in (1, 0):
            c_copy(item, side, source, turn % 2).start()

    def make(item, turn):
        if 4 * item + turn >= 2:
            c_sent(item if turn >= 2 else item - 1, turn % 2)
        block = 2 * shard[item]
        rows = pl.ds(pl.multiple_of(target(turn) // 2 * block, 16), block)
        for quarter in range(4):
            if turn == 0:
                for which in range(len(wide_refs[item])):
                    load(item, quarter, which).wait()
            for left, base, span_width, step in layout[item][1]:

                def one(chunk, _):
                    at = pl.ds(pl.multiple_of(base + chunk * step, 128), step)
                    found = jnp.dot(
                        lefts[left][rows], rights[quarter, :, at], preferred_element_type=jnp.float32
                    )
                    if layout[item][0] is not None:
                        spots = lax.broadcasted_iota(jnp.int32, (places.shape[0], step), 1)
                        spots = spots + (layout[item][0] + chunk * step)
                        hot = jnp.where(places[:, quarter : quarter + 1] == spots, 1.0, 0.0)
                        found += jnp.dot(
                            lefts[1][rows], hot.astype(jnp.bfloat16), preferred_element_type=jnp.float32
                        )
                    if extra is not None and item == gains_at[0] and base == 0:
                        found += extra[rows]
                    if quarter % 2:
                        crossed[quarter // 2, turn % 2, :, at] = found.astype(jnp.bfloat16)
                    else:
                        held[item][0][quarter // 2, rows, at] = found.astype(jnp.bfloat16)
                    return 0

                lax.fori_loop(0, span_width // step, one, 0)
        if turn == 3 and item + 1 < items:
            start_loads(item + 1)

    def first(item, turn):
        source = target(turn)
        for side in (1, 0):
            c_copy(item, side, source).wait_recv()
        for x_place, y_side in ((source, 1), (mirror(source), 0)):
            add(item, 1, 0, x_place, c_part(item, 1, 0, x_place))
            x_copy(item, 0, x_place).start()
            y_place = mirror(source)
            add(item, y_side, 1, y_place, c_part(item, y_side, 1, y_place))
            y_copy(item, 1, y_side, y_place).start()

    def second(item, turn):
        source = target(turn)
        place = mirror(source)
        x_copy(item, 0, place).wait_recv()
        add(item, 0, 0, place, c_part(item, 0, 0, place), of(held[item][1], place))
        y_copy(item, 0, 0, place).start()
        y_copy(item, 1, 1, source).wait_recv()
        add(item, 1, 1, source, c_part(item, 1, 1, source), of(held[item][4], 1, source // 2))
        x_copy(item, 1, source).start()

    def third(item, turn):
        source = target(turn)
        for part in range(2):
            x_copy(item, part, source).wait_recv()
            y_copy(item, part, 0, source).wait_recv()
            if part == 0:
                terms = [of(held[item][1], source), of(held[item][3], source // 2)]
            else:
                terms = [of(held[item][2], source // 2), of(held[item][4], 0, source // 2)]
            add(item, 0, part, source, c_part(item, 0, part, source), *terms)
        if item + 1 < items:
            pl.semaphore_signal(free_sem, inc=1, device_id=devices["c"], device_id_type=MESH)

    def fourth(item, turn):
        source = target(turn)
        away = jnp.where(source > column, source - column, column - source) // 2

        def along(upward):
            for part in range(2):

                def more():
                    z_copy(item, part, source, away, upward).wait_recv()
                    add(item, 0, part, source, of(held[item][5], 1 - upward, part, away))

                pl.when(z > 0 if upward else z < 3)(more)
                z_copy(item, part, source, away - 1, upward).start()

        pl.when(source > column)(lambda: along(1))
        pl.when(source < column)(lambda: along(0))

    def last(item):
        square = jnp.zeros((), jnp.float32)
        for part in range(2):
            for upward in (1, 0):
                pl.when(z > 0 if upward else z < 3)(
                    lambda: z_copy(item, part, column, 0, upward).wait_recv()
                )
            start = column * shard[item] + part * piece[item]

            def one(turn, square):
                at = pl.multiple_of(turn * 16, 8)
                value = held[item][0][0, pl.ds(pl.multiple_of(start + at, 8), 16)].astype(jnp.float32)
                below = held[item][5][0, part, 0, pl.ds(at, 16)].astype(jnp.float32)
                above = held[item][5][1, part, 0, pl.ds(at, 16)].astype(jnp.float32)
                value = value + jnp.where(z > 0, below, 0.0) + jnp.where(z < 3, above, 0.0)
                outs[item][pl.ds(pl.multiple_of(part * piece[item] + at, 8), 16)] = value
                square_here = value * value
                if extra is not None and item == gains_at[0]:
                    lane = lax.broadcasted_iota(jnp.int32, value.shape, 1)
                    repeated = (lane >= gains_at[1]) & (lane < gains_at[1] + gains_at[2])
                    square_here = jnp.where(repeated, square_here / parts, square_here)
                return square + jnp.sum(square_here)

            square = lax.fori_loop(0, piece[item] // 16, one, square)
        return square

    steps = [(item, turn) for item in range(items) for turn in range(4)]
    count = len(steps)
    def begin():
        make(*steps[0])
        send_c(*steps[0])

    def advance(turn):
        if turn < count:
            first(*steps[turn])
        if turn + 1 < count:
            make(*steps[turn + 1])
            send_c(*steps[turn + 1])
        if 0 <= turn - 1 < count:
            second(*steps[turn - 1])
        if 0 <= turn - 2 < count:
            third(*steps[turn - 2])
        if 0 <= turn - 3 < count and (turn - 3) % 4 < 3:
            fourth(*steps[turn - 3])

    def finish():
        return sum([last(item) for item in range(items)])

    def drain():
        for slot in range(2):
            c_sent(items - 1, slot)
        for item in range(items):
            for way, count in enumerate((12, 12)):
                lead = held[item][0].at[0, pl.ds(0, count * piece[item])]
                remote(lead, lead, side_sem.at[way, item], c_sem.at[item, 0, 0], "x").wait_send()
            for part in range(2):
                for away in range(3):
                    pl.when((z < 3) & (z + away + 1 <= 3))(
                        lambda: z_copy(item, part, column, away, 1).wait_send()
                    )
                    pl.when((z > 0) & (z - away - 1 >= 0))(
                        lambda: z_copy(item, part, column, away, 0).wait_send()
                    )

    return lambda: start_loads(0), begin, advance, count + 3, finish, drain


def reduce_body(layout, parts, gains_at, *refs):
    table_rights, last_rights = refs[:4], refs[4:8]
    facts, places, extra = refs[8:11]
    lefts = refs[11:15]
    table_out, last_out, totals = refs[15:18]
    refs = refs[18:]
    outs, wide_refs = [], []
    for at, products in layout:
        span = sum([product[2] for product in products])
        outs.append(last_out if at is None else table_out.at[:, pl.ds(at, span)])
        wide_refs.append([(last_rights if at is None else table_rights, at or 0, span)])
    tile, tile_row, tile_column, row_send, row_recv, column_send, column_recv = refs[:7]
    start_loads, begin, advance, turns, finish, drain = reduce_tools(
        layout, gains_at, parts, places, extra, lefts, wide_refs, outs, refs[7:]
    )
    start_loads()
    column = lax.axis_index("dp")
    row = lax.axis_index("tensor")
    row_peers = [(column, (row + away) % 4) for away in (1, 2, 3)]
    column_peers = [((column + away) % 8, row) for away in range(1, 8)]
    barrier = pltpu.get_barrier_semaphore()
    for device in row_peers + column_peers:
        pl.semaphore_signal(barrier, inc=1, device_id=device, device_id_type=MESH)
    pl.semaphore_wait(barrier, 10)
    begin()
    for turn in range(turns):
        advance(turn)
    square = finish()
    sublane = lax.broadcasted_iota(jnp.int32, (8, 128), 0)
    tile[...] = facts[...] + jnp.where(sublane == 0, square, 0.0)

    def exchange(value, slots, here, peers, sources, send, recv):
        slots[here] = value

        def crossing(place, device, source):
            return pltpu.make_async_remote_copy(
                src_ref=slots.at[here],
                dst_ref=slots.at[source],
                send_sem=send.at[place],
                recv_sem=recv.at[source],
                device_id=device,
                device_id_type=MESH,
            )

        for place, device in enumerate(peers):
            crossing(place, device, here).start()
        for place, device in enumerate(peers):
            crossing(place, device, sources[place]).wait_recv()
        total = slots[0]
        for place in range(1, len(peers) + 1):
            total = total + slots[place]
        for place, device in enumerate(peers):
            crossing(place, device, here).wait_send()
        return total

    along_row = exchange(
        tile[...], tile_row, row, row_peers, [(row + away) % 4 for away in (1, 2, 3)], row_send, row_recv
    )
    totals[...] = exchange(
        along_row,
        tile_column,
        column,
        column_peers,
        [(column + away) % 8 for away in range(1, 8)],
        column_send,
        column_recv,
    )
    drain()


def reduce_scratch(widths, products, rows, depth):
    whole = lax.axis_size("dp")
    items, half = len(widths), rows // (2 * whole)
    scratch = [
        pltpu.VMEM((*lead, width), jnp.bfloat16)
        for width in widths
        for lead in ((2, rows), (8, half), (4, half), (4, half), (2, 4, half), (2, 2, 3, half))
    ]
    return scratch + [
        pltpu.SemaphoreType.DMA((2, items)),
        pltpu.SemaphoreType.DMA((2, 2)),
        pltpu.SemaphoreType.DMA((items, 2, 4)),
        pltpu.SemaphoreType.DMA((items, 2, 8)),
        pltpu.SemaphoreType.DMA((items, 3, 4)),
        pltpu.SemaphoreType.DMA((items, 2, 2, 3)),
        pltpu.SemaphoreType.DMA((items, 2, 2, 3)),
        pltpu.SemaphoreType.DMA((items, 4, products)),
        pltpu.SemaphoreType.REGULAR,
        pltpu.VMEM((2, 2, 4 * half, max(widths)), jnp.bfloat16),
        pltpu.VMEM((2, rows, max(widths)), jnp.bfloat16),
        pltpu.VMEM((4, depth, max(widths)), jnp.bfloat16),
    ]


def reduce_kernel(layout, lefts, rights, places, extra, facts, parts, gains_at, tag):
    anywhere = pl.BlockSpec(memory_space=pl.ANY)
    inside = pl.BlockSpec(memory_space=pltpu.VMEM)
    rows, depth = lefts[0].shape
    widths = [sum([product[2] for product in products]) for _, products in layout]
    shapes = [
        jax.ShapeDtypeStruct((rows // lax.axis_size("dp"), item[0].shape[1]), jnp.float32)
        for item in rights
    ]
    shapes.append(jax.ShapeDtypeStruct((8, 128), jnp.float32))
    found = pl.pallas_call(
        functools.partial(reduce_body, layout, parts, gains_at),
        name="reduce_grads",
        out_shape=shapes,
        in_specs=[anywhere] * 8 + [inside] * (3 + len(lefts)),
        out_specs=[inside] * 3,
        scratch_shapes=[
            pltpu.VMEM((8, 128), jnp.float32),
            pltpu.VMEM((4, 8, 128), jnp.float32),
            pltpu.VMEM((8, 8, 128), jnp.float32),
            pltpu.SemaphoreType.DMA((3,)),
            pltpu.SemaphoreType.DMA((4,)),
            pltpu.SemaphoreType.DMA((7,)),
            pltpu.SemaphoreType.DMA((8,)),
        ]
        + reduce_scratch(widths, 1, rows, depth),
        compiler_params=pltpu.CompilerParams(
            collective_id=tag, has_side_effects=True, vmem_limit_bytes=60 << 20
        ),
    )(*[item for quarters in rights for item in quarters], facts, places, extra, *lefts)
    return found[:-1], found[-1]


def update_body(sources, plans, *refs):
    count = len(plans)
    totals, fixes, grads = refs[0], refs[1], refs[2 : 2 + sources]
    refs = refs[2 + sources :]
    triples = [refs[3 * place : 3 * place + 3] for place in range(count)]
    outs = [refs[3 * (count + place) : 3 * (count + place) + 3] for place in range(count)]
    square, loss, real = totals[0:1, :], totals[1:2, :], totals[2:3, :]
    norm = jnp.sqrt(square) / real
    refs[6 * count][...] = jnp.concatenate([loss / real, norm] + [norm] * 6, axis=0)
    scale = (jnp.minimum(1.0, clip_at / norm) / real)[:, 0:1]
    over_one, over_two = fixes[0:1, 0:1], fixes[1:2, 0:1]

    def renew(place, grad, rows):
        source, turned, first, rate, decay = plans[place]
        weight, one, two = triples[place]
        clipped = grad * scale
        moment_one = beta_one * one[rows] + (1.0 - beta_one) * clipped
        moment_two = beta_two * two[rows] + (1.0 - beta_two) * clipped * clipped
        stepped = moment_one * over_one / (jnp.sqrt(moment_two * over_two) + adam_eps)
        outs[place][0][rows] = moment_one
        outs[place][1][rows] = moment_two
        outs[place][2][rows] = weight[rows] - rate * (stepped + decay * weight[rows])

    for place in range(count):
        source, turned, first, rate, decay = plans[place]
        rows, columns = triples[place][0].shape
        if turned and rows >= 128:
            for at in range(0, rows, 128):
                span = min(128, rows - at)
                block = grads[source][:, first + at : first + at + span].T
                renew(place, block, pl.ds(at, span))
        elif turned:
            start = first // 128 * 128
            block = grads[source][:, start : start + 128].T
            renew(place, block[first - start : first - start + rows], pl.ds(0, rows))
        else:
            for at in range(0, rows, 32):
                renew(place, grads[source][pl.ds(at, 32), first : first + columns], pl.ds(at, 32))


def update_kernel(totals, fixes, grads, plans, triples):
    inside = pl.BlockSpec(memory_space=pltpu.VMEM)
    flat = [item for triple in triples for item in triple]
    outs = [jax.ShapeDtypeStruct(item.shape, item.dtype) for item in flat] + [
        jax.ShapeDtypeStruct((8, 128), jnp.float32)
    ]
    found = pl.pallas_call(
        functools.partial(update_body, len(grads), plans),
        name="update_weights",
        out_shape=outs,
        in_specs=[inside] * (2 + len(grads) + len(flat)),
        out_specs=[inside] * len(outs),
        compiler_params=pltpu.CompilerParams(vmem_limit_bytes=60 << 20),
    )(totals, fixes, *grads, *flat)
    return found[:-1], found[-1]


def turn_halves(tile, cosine, sine):
    lane = lax.broadcasted_iota(jnp.int32, tile.shape, 1)
    other = jnp.where(lane % 64 < 32, pltpu.roll(tile, 96, 1), pltpu.roll(tile, 32, 1))
    return tile * cosine + other * sine


def attend_steps(normed, joints, cosine, sine, seg_row, seg_col, packed, lse, attended, between, leaving, heads_out, heads_in, send_sem, recv_sem, out_send, out_recv):
    device = neighbours()["c"]
    rows = normed.shape[0]

    def project(joint, put):
        found = jnp.dot(normed[...], joint[...], preferred_element_type=jnp.float32)
        for head in range(3):
            pair = turn_halves(found[:, 192 * head : 192 * head + 128], cosine[0:rows], sine[0:rows])
            value = found[:, 192 * head + 128 : 192 * head + 192]
            put(head, pair.astype(jnp.bfloat16), value.astype(jnp.bfloat16))

    def crossing(place):
        return pltpu.make_async_remote_copy(
            src_ref=leaving.at[place],
            dst_ref=packed.at[place, pl.ds(rows, rows)],
            send_sem=send_sem.at[place],
            recv_sem=recv_sem.at[place],
            device_id=device,
            device_id_type=MESH,
        )

    for side, joint in enumerate((joints[1], joints[3])):

        def put(head, pair, value):
            leaving[3 * side + head, :, 0:128] = pair
            leaving[3 * side + head, :, 128:192] = value
            crossing(3 * side + head).start()

        project(joint, put)
    for side, joint in enumerate((joints[0], joints[2])):

        def put(head, pair, value):
            packed[3 * side + head, pl.ds(0, rows), 0:128] = pair
            packed[3 * side + head, pl.ds(0, rows), 128:192] = value

        project(joint, put)

    def one_head(place):
        keys = packed[place, :, 0:128][:, 64:128]
        values_t = packed[place, :, 128:256][:, 0:64].astype(jnp.float32).T.astype(jnp.bfloat16)

        def block(turn, _):
            at = pl.ds(pl.multiple_of(turn * 256, 256), 256)
            query = packed[place, at, 0:128][:, 0:64] * jnp.bfloat16(HEAD_DIM ** (-0.5))
            scores = lax.dot_general(
                keys, query, (((1,), (1,)), ((), ())), preferred_element_type=jnp.float32
            )
            scores = jnp.where(seg_col[:, 0:1] == seg_row[0:1, at], scores, neg_fill)
            top = jnp.max(scores, axis=0, keepdims=True)
            expd = jnp.exp(scores - top)
            summed = jnp.sum(expd, axis=0, keepdims=True)
            probs = (expd * (1.0 / summed)).astype(jnp.bfloat16)
            found = jnp.dot(values_t, probs, preferred_element_type=jnp.float32)
            lse[pl.ds(place, 1), at] = top + jnp.log(summed)
            heads_out[place, at, 0:64] = found.T.astype(jnp.bfloat16)
            return 0

        lax.fori_loop(0, 2 * rows // 256, block, 0)

    between(0)
    for place in range(6):
        crossing(place).wait_recv()
    for place in range(6):
        one_head(place)
        between(1 + place)

    def returning(place):
        return pltpu.make_async_remote_copy(
            src_ref=heads_out.at[place, pl.ds(rows, rows)],
            dst_ref=heads_in.at[place],
            send_sem=out_send.at[place],
            recv_sem=out_recv.at[place],
            device_id=device,
            device_id_type=MESH,
        )

    for place in range(6):
        returning(place).start()
    for place in range(6):
        attended[:, 64 * place : 64 * place + 64] = heads_out[place, pl.ds(0, rows), 0:64]
    for place in range(6):
        returning(place).wait_recv()
        attended[:, 384 + 64 * place : 448 + 64 * place] = heads_in[place, :, 0:64]
    for place in range(6):
        crossing(place).wait_send()
        returning(place).wait_send()


def attend_back_body(layout, *refs):
    grad_out, packed, lse, attended, cosine, sine, seg_row, seg_col, left_up, left_down = refs[:10]
    ups, downs = refs[10:14], refs[14:18]
    r0, r1, r2, r3, summed, square_out = refs[18:24]
    grads, leaving, keys_t, probs, prob_grads, found, going, coming = refs[24:32]
    send_sem, recv_sem, out_send, out_recv = refs[32:36]
    span = ups[0].shape[1]
    outs = [summed.at[:, pl.ds(0, span)], summed.at[:, pl.ds(span, span)]]
    wide_refs = [[(ups, 0, span)], [(downs, 0, span)]]
    start_loads, begin, advance, turns, finish, drain = reduce_tools(
        layout, None, None, None, None, (left_up, left_down), wide_refs, outs, refs[36:]
    )
    start_loads()
    device = neighbours()["c"]
    rows = grad_out.shape[0]
    meet(lax.axis_index("dp") // 2, neighbours())

    def crossing(place):
        return pltpu.make_async_remote_copy(
            src_ref=leaving.at[place],
            dst_ref=grads.at[place, pl.ds(rows, rows)],
            send_sem=send_sem.at[place],
            recv_sem=recv_sem.at[place],
            device_id=device,
            device_id_type=MESH,
        )

    for place in range(6):
        leaving[place, :, 0:64] = grad_out[:, 384 + 64 * place : 448 + 64 * place]
        crossing(place).start()
        grads[place, pl.ds(0, rows), 0:64] = grad_out[:, 64 * place : 64 * place + 64]
    nothing = jnp.zeros((rows, 64), jnp.bfloat16)
    for order, right in enumerate((r0, r2, r1, r3)):
        right[:, 576:640] = nothing
        right[:, 640:832] = attended[:, 192 * order : 192 * order + 192]
        right[:, 832:896] = nothing
    begin()
    for place in range(6):
        crossing(place).wait_recv()

    def one_head(place):
        query = packed[place, :, 0:128][:, 0:64]
        scaled = query * jnp.bfloat16(HEAD_DIM ** (-0.5))
        wide_keys = packed[place, :, 0:128][:, 64:128].astype(jnp.float32)
        keys_t[...] = wide_keys.T.astype(jnp.bfloat16)
        grad = grads[place, :, 0:64]
        stat = lse[pl.ds(place, 1), :]

        def score(turn, inner):
            at = pl.ds(pl.multiple_of(turn * 256, 256), 256)
            keys = packed[place, at, 0:128][:, 64:128]
            values = packed[place, at, 128:256][:, 0:64]
            scores = lax.dot_general(
                keys, scaled, (((1,), (1,)), ((), ())), preferred_element_type=jnp.float32
            )
            scores = jnp.where(seg_col[at, 0:1] == seg_row[0:1, :], scores, neg_fill)
            prob = jnp.exp(scores - stat)
            prob_grad = lax.dot_general(
                values, grad, (((1,), (1,)), ((), ())), preferred_element_type=jnp.float32
            )
            probs[at] = prob
            prob_grads[at] = prob_grad
            value_grad = jnp.dot(prob.astype(jnp.bfloat16), grad, preferred_element_type=jnp.float32)
            found[place, at, 128:192] = value_grad
            return inner + jnp.sum(prob * prob_grad, axis=0, keepdims=True)

        inner = lax.fori_loop(0, 2 * rows // 256, score, jnp.zeros((1, 2 * rows), jnp.float32))

        def spread_back(turn, query_grad):
            at = pl.ds(pl.multiple_of(turn * 256, 256), 256)
            score_grad = (probs[at] * (prob_grads[at] - inner)).astype(jnp.bfloat16)
            key_grad = jnp.dot(score_grad, scaled, preferred_element_type=jnp.float32)
            found[place, at, 64:128] = key_grad
            return query_grad + jnp.dot(keys_t[:, at], score_grad, preferred_element_type=jnp.float32)

        query_grad = lax.fori_loop(
            0, 2 * rows // 256, spread_back, jnp.zeros((64, 2 * rows), jnp.float32)
        )
        found[place, :, 0:64] = query_grad.T * HEAD_DIM ** (-0.5)

    for place in range(6):
        advance(2 * place)
        if 2 * place + 1 < turns:
            advance(2 * place + 1)
        one_head(place)
    for turn in range(12, turns):
        advance(turn)

    def returning(side):
        return pltpu.make_async_remote_copy(
            src_ref=going.at[side],
            dst_ref=coming.at[side],
            send_sem=out_send.at[side],
            recv_sem=out_recv.at[side],
            device_id=device,
            device_id_type=MESH,
        )

    for half in (1, 0):
        at = pl.ds(half * rows, rows)
        for side in range(2):
            for head in range(3):
                place = 3 * side + head
                pair = turn_halves(found[place, at, 0:128], cosine[at], -sine[at]).astype(jnp.bfloat16)
                value = found[place, at, 128:192].astype(jnp.bfloat16)
                puts = [going.at[side]] if half else [(r0, r2)[side]]
                for put in puts:
                    put[:, 192 * head : 192 * head + 128] = pair
                    put[:, 192 * head + 128 : 192 * head + 192] = value
            if half:
                returning(side).start()
    square_out[...] = jnp.full(square_out.shape, finish(), jnp.float32)
    for side in range(2):
        returning(side).wait_recv()
        (r1, r3)[side][:, 0:576] = coming[side, :, 0:576]
    for place in range(6):
        crossing(place).wait_send()
    for side in range(2):
        returning(side).wait_send()
    drain()


def attend_back_kernel(layout, grad_out, packed, lse, attended, cosine, sine, seg_row, seg_col, lefts, ups, downs):
    rows = grad_out.shape[0]
    anywhere = pl.BlockSpec(memory_space=pl.ANY)
    width = ups[0].shape[1] + downs[0].shape[1]
    inside = pl.BlockSpec(memory_space=pltpu.VMEM)
    found = pl.pallas_call(
        functools.partial(attend_back_body, layout),
        name="attend_back",
        out_shape=[jax.ShapeDtypeStruct((rows, 896), jnp.bfloat16)] * 4
        + [
            jax.ShapeDtypeStruct((lefts[0].shape[0] // lax.axis_size("dp"), width), jnp.float32),
            jax.ShapeDtypeStruct((8, 128), jnp.float32),
        ],
        in_specs=[inside] * 10 + [anywhere] * 8,
        out_specs=[inside] * 6,
        scratch_shapes=[
            pltpu.VMEM((6, 2 * rows, 128), jnp.bfloat16),
            pltpu.VMEM((6, rows, 128), jnp.bfloat16),
            pltpu.VMEM((64, 2 * rows), jnp.bfloat16),
            pltpu.VMEM((2 * rows, 2 * rows), jnp.float32),
            pltpu.VMEM((2 * rows, 2 * rows), jnp.float32),
            pltpu.VMEM((6, 2 * rows, 256), jnp.float32),
            pltpu.VMEM((2, rows, 640), jnp.bfloat16),
            pltpu.VMEM((2, rows, 640), jnp.bfloat16),
            pltpu.SemaphoreType.DMA((6,)),
            pltpu.SemaphoreType.DMA((6,)),
            pltpu.SemaphoreType.DMA((2,)),
            pltpu.SemaphoreType.DMA((2,)),
        ]
        + reduce_scratch([width // 2] * 2, 1, *lefts[0].shape),
        compiler_params=pltpu.CompilerParams(
            collective_id=3, has_side_effects=True, vmem_limit_bytes=62 << 20
        ),
    )(grad_out, packed, lse, attended, cosine, sine, seg_row, seg_col, *lefts, *ups, *downs)
    return [item[:, :640] for item in found[:4]], found[:4], found[4], found[5]


def pieces_of(width):
    pieces, at = [], 0
    for span in (1024, 1024):
        pieces.append((at, span, span // 2 if span % 256 == 0 else span))
        at += span
    return pieces


def known_mesh():
    return lax.axis_size("dp") == 8 and lax.axis_size("tensor") == 4


def reduce_grads(layout, lefts, rights, places, extra, facts, parts, gains_at):
    if known_mesh():
        ordered = [[item[0], item[2], item[1], item[3]] for item in rights]
        return reduce_kernel(layout, lefts, ordered, places, extra, facts, parts, gains_at, 1)
    sums = []
    for item, (_, products) in enumerate(layout):
        quarters = []
        for quarter, mask in enumerate((0, 2, 1, 3)):
            right = rights[item][quarter]
            found = [mm(lefts[at], right[:, base : base + width]) for at, base, width, _ in products]
            if item == 0:
                spots = jnp.arange(right.shape[1], dtype=jnp.int32)[None, :]
                found[0] += mm(lefts[1], narrow(places[:, mask : mask + 1] == spots))
            if item == gains_at[0]:
                found[0] += extra
            quarters.append(narrow(jnp.concatenate(found, axis=1)))
        sums.append(reduce_all(quarters, True))
    square = sum(jnp.sum(item * item) for item in sums)
    repeated = sums[gains_at[0]][:, gains_at[1] : gains_at[1] + gains_at[2]]
    square = square - jnp.sum(repeated * repeated) * (1.0 - 1.0 / parts)
    tile = jnp.where(lax.broadcasted_iota(jnp.int32, (8, 128), 0) == 0, square, facts)
    return sums, everyone_sum(tile)


def wide(value):
    return value.astype(jnp.float32)


def narrow(value):
    return value.astype(jnp.bfloat16)


def fold(value, masks, last):
    rows = value.shape[0] // (len(masks) + 1)
    total = wide(value[:rows])
    for place, mask in enumerate(masks):
        total = total + wide(swap(value[(place + 1) * rows : (place + 2) * rows], "dp", mask))
    return total if last else narrow(total)


def reduce_all(quarters, x_first):
    groups = groups_of(lax.axis_size("dp"))
    own = narrow(wide(quarters[0]) + wide(swap(quarters[2], "tensor", 1)))
    other = narrow(wide(quarters[1]) + wide(swap(quarters[3], "tensor", 1)))
    if x_first:
        own = narrow(wide(own) + wide(swap(other, "tensor", 2)))
        own = fold(own, groups[0], len(groups) == 1)
    else:
        own = fold(own, groups[0], False)
        other = fold(other, groups[0], False)
        own = narrow(wide(own) + wide(swap(other, "tensor", 2)))
    for place in range(1, len(groups)):
        own = fold(own, groups[place], place == len(groups) - 1)
    return wide(own)


def everyone_sum(value):
    for masks in groups_of(lax.axis_size("dp")):
        value = sum([swap(value, "dp", mask) for mask in masks], value)
    for mask in (1, 2):
        value = value + swap(value, "tensor", mask)
    return value


def mm(left, right):
    return jnp.dot(left, right, preferred_element_type=jnp.float32)


def mm_nt(left, right):
    return lax.dot_general(left, right, (((1,), (1,)), ((), ())), preferred_element_type=jnp.float32)


def mm_tn(left, right):
    return lax.dot_general(left, right, (((0,), (0,)), ((), ())), preferred_element_type=jnp.float32)


def rotate_heads(values, cosine, sine):
    return rotate(values, cosine[:, None, :], sine[:, None, :])


def scores_of(query, key_rows, same_doc):
    scores = jnp.einsum(
        "qhe,khe->hqk", query, key_rows, preferred_element_type=jnp.float32
    ) * HEAD_DIM ** (-0.5)
    return jnp.where(same_doc[None], scores, neg_fill)


def split_heads(packed):
    packed = packed.reshape(packed.shape[0], -1, 3, HEAD_DIM)
    return packed[:, :, 0], packed[:, :, 1], packed[:, :, 2]


def attend(packed, same_doc):
    query, key_rows, value_rows = split_heads(packed)
    scores = scores_of(query, key_rows, same_doc)
    row_max = jnp.max(scores, axis=-1, keepdims=True)
    expd = jnp.exp(scores - row_max)
    summed = jnp.sum(expd, axis=-1, keepdims=True)
    probs = (expd / summed).astype(jnp.bfloat16)
    output = jnp.einsum("hqk,khe->qhe", probs, value_rows, preferred_element_type=jnp.float32)
    return (narrow(output).reshape(packed.shape[0], -1), (row_max + jnp.log(summed))[..., 0])


def attend_back(packed, same_doc, row_lse, grad_out, cosine, sine):
    query, key_rows, value_rows = split_heads(packed)
    grad_out = grad_out.reshape(packed.shape[0], -1, HEAD_DIM)
    scores = scores_of(query, key_rows, same_doc)
    probs = jnp.exp(scores - row_lse[..., None])
    value_grad = jnp.einsum(
        "hqk,qhe->khe", probs.astype(jnp.bfloat16), grad_out, preferred_element_type=jnp.float32
    )
    prob_grad = jnp.einsum("qhe,khe->hqk", grad_out, value_rows, preferred_element_type=jnp.float32)
    inner = jnp.sum(prob_grad * probs, axis=-1, keepdims=True)
    score_grad = (probs * (prob_grad - inner)).astype(jnp.bfloat16)
    query_grad = jnp.einsum(
        "hqk,khe->qhe", score_grad, key_rows, preferred_element_type=jnp.float32
    ) * HEAD_DIM ** (-0.5)
    key_grad = jnp.einsum(
        "hqk,qhe->khe", score_grad, query, preferred_element_type=jnp.float32
    ) * HEAD_DIM ** (-0.5)
    query_grad = rotate_heads(query_grad, cosine, -sine)
    key_grad = rotate_heads(key_grad, cosine, -sine)
    return narrow(jnp.stack([query_grad, key_grad, value_grad], axis=2).reshape(packed.shape))


def update_weights(totals, fixes, sums, plans, triples):
    if known_mesh():
        updated, results = update_kernel(totals, fixes, sums, plans, triples)
        return list(updated), results
    updated = []
    norm = jnp.sqrt(totals[0, 0]) / totals[2, 0]
    scale = jnp.minimum(1.0, clip_at / norm) / totals[2, 0]
    for (source, turned, first, rate, decay), (weight, one, two) in zip(plans, triples):
        columns = weight.shape[0] if turned else weight.shape[1]
        grad = sums[source][:, first : first + columns]
        clipped = (grad.T if turned else grad) * scale
        moment_one = beta_one * one + (1.0 - beta_one) * clipped
        moment_two = beta_two * two + (1.0 - beta_two) * clipped * clipped
        stepped = moment_one * fixes[0, 0] / (jnp.sqrt(moment_two * fixes[1, 0]) + adam_eps)
        updated.extend([moment_one, moment_two, weight - rate * (stepped + decay * weight)])
    return updated, jnp.stack([totals[1, 0] / totals[2, 0], norm])[:, None]


def per_device(
    tokens,
    lengths,
    timesteps,
    masks,
    step_count,
    table,
    joint_weight,
    output_weight,
    upward_weight,
    downward_weight,
    gains,
    momentum_table,
    momentum_joint,
    momentum_output,
    momentum_upward,
    momentum_downward,
    momentum_gains,
    variance_table,
    variance_joint,
    variance_output,
    variance_upward,
    variance_downward,
    variance_gains,
):
    place = lax.axis_index("tensor")
    parts = lax.axis_size("tensor")
    rows = tokens.shape[0] // parts
    vocab_part, head_part = table.shape[0], joint_weight.shape[1]
    out_part, ff_part = output_weight.shape[0], upward_weight.shape[1]

    gain_columns = jnp.pad(narrow(gains).T, ((0, 0), (0, 61)))
    shards = [
        narrow(table).T,
        jnp.concatenate([narrow(joint_weight), gain_columns], axis=1),
        narrow(upward_weight),
        narrow(downward_weight).T,
        narrow(output_weight).T,
    ]
    start = place * rows
    seq = start // SEQ_LEN
    mine = start - seq * SEQ_LEN
    cut = lambda array: lax.dynamic_slice(array, (start,), (rows,))
    targets = cut(tokens)
    corrupt = cut(masks) == 1
    inputs = jnp.where(corrupt, VOCAB - 1, targets)
    own_lengths = lax.dynamic_slice(lengths, (seq, 0), (1, DOCS))
    step_here = lax.dynamic_slice(timesteps, (seq,), (1,))
    theirs = mine ^ rows
    position = jnp.concatenate(
        [mine + jnp.arange(rows, dtype=jnp.int32), theirs + jnp.arange(rows, dtype=jnp.int32)]
    )
    doc_ends = jnp.cumsum(own_lengths[0])
    doc_starts = doc_ends - own_lengths[0]
    segment = jnp.sum((position[:, None] >= doc_ends[None, :]).astype(jnp.int32), axis=1)
    chosen = segment[:, None] == jnp.arange(DOCS, dtype=jnp.int32)[None, :]
    offset = position - jnp.sum(jnp.where(chosen, doc_starts[None, :], 0), axis=1)
    is_real = segment < DOCS - 1
    factor = jnp.where(step_here == 1, 1.0, T_DIFF / step_here.astype(jnp.float32))
    weights = jnp.where(corrupt & is_real[:rows], factor, 0.0)
    inverse_freq = 10000.0 ** (-jnp.arange(HEAD_DIM // 2, dtype=jnp.float32) / (HEAD_DIM // 2))
    angles = offset.astype(jnp.float32)[:, None] * inverse_freq
    cosine, sine = jnp.cos(angles), jnp.sin(angles)
    same_doc = segment[:, None] == segment[None, :]

    def hot(ids, piece):
        base = (place ^ (2 * (piece % 2) + piece // 2)) * vocab_part
        return (ids - base)[:, None] == jnp.arange(vocab_part, dtype=jnp.int32)[None, :]

    pieces = range(4)
    lane = jnp.arange(128, dtype=jnp.int32)[None, :]
    places = inputs[:, None] - (place ^ (lane % 4)) * vocab_part

    on_known = known_mesh()
    if on_known:
        cosines = jnp.concatenate([cosine] * 4, axis=1)
        sines = jnp.concatenate([-sine, sine] * 2, axis=1)
        seg_row = jnp.broadcast_to(segment[None, :], (8, 2 * rows))
        seg_col = jnp.broadcast_to(segment[:, None], (2 * rows, 128))
        groups, (embedded, normed_one, packed, attn_lse, attended_all) = start_kernel(
            shards, places, cosines, sines, seg_row, seg_col
        )
        groups = [[item[0], item[2], item[1], item[3]] for item in groups]
    else:
        groups = [gather_all(item, True) for item in shards]
    table_q, first_group, up_q, down_q, out_q = groups
    gain_full = wide(first_group[0][:, head_part : head_part + 3]).T
    out_all = jnp.concatenate(out_q, axis=1)
    if not on_known:
        joint_q = [item[:, :head_part] for item in first_group]
        looked = sum(mm_nt(narrow(hot(inputs, piece)), table_q[piece]) for piece in pieces)
        embedded = looked * D**0.5
        normed_one = narrow(norm_apply(embedded, gain_full[0]))

        def turned(projected):
            projected = projected.reshape(rows, -1, 3, HEAD_DIM)
            query = rotate_heads(projected[:, :, 0], cosine[:rows], sine[:rows])
            key_rows = rotate_heads(projected[:, :, 1], cosine[:rows], sine[:rows])
            stacked = jnp.stack([query, key_rows, projected[:, :, 2]], axis=2)
            return narrow(stacked.reshape(rows, -1))

        packed = [turned(mm(normed_one, item)) for item in joint_q]
        whole = [
            jnp.concatenate([packed[side], swap(packed[2 + side], "tensor", 1)], axis=0)
            for side in range(2)
        ]
        attended, attn_lse = zip(*[attend(item, same_doc) for item in whole])
        attended_all = jnp.concatenate(
            [item[:rows] for item in attended]
            + [swap(item[rows:], "tensor", 1) for item in attended],
            axis=1,
        )
    after_attn = embedded + mm_nt(attended_all, out_all)
    normed_two = narrow(norm_apply(after_attn, gain_full[1]))
    pre_gelu = [mm(normed_two, item) for item in up_q]
    below = [0.5 + 0.5 * lax.erf(item * 0.5**0.5) for item in pre_gelu]
    slopes = [
        part + item * jnp.exp(-0.5 * item * item) * (0.5 / jnp.pi) ** 0.5
        for part, item in zip(below, pre_gelu)
    ]
    activated = [narrow(item * part) for part, item in zip(below, pre_gelu)]
    after_mlp = after_attn + sum(mm_nt(activated[q], down_q[q]) for q in range(4))
    normed_out = narrow(norm_apply(after_mlp, gain_full[2]))
    logits = [mm(normed_out, item) for item in table_q]
    row_max = logits[0].max(axis=1)
    for item in logits[1:]:
        row_max = jnp.maximum(row_max, item.max(axis=1))
    row_sum = sum(jnp.sum(jnp.exp(item - row_max[:, None]), axis=1) for item in logits)
    target_hot = [hot(targets, piece) for piece in pieces]
    row_pick = sum(
        jnp.sum(jnp.where(target_hot[piece], logits[piece], 0.0), axis=1) for piece in pieces
    )
    row_lse = row_max + jnp.log(row_sum)
    loss_local = jnp.sum(weights * (row_lse - row_pick))
    count_local = jnp.sum(is_real[:rows].astype(jnp.float32))

    logit_grad = [
        narrow(
            weights[:, None]
            * (jnp.exp(logits[piece] - row_lse[:, None]) - target_hot[piece].astype(jnp.float32))
        )
        for piece in pieces
    ]
    out_grad = sum(mm_nt(logit_grad[piece], table_q[piece]) for piece in pieces)
    mlp_grad, gain_three = norm_back(after_mlp, gain_full[2], out_grad)
    mlp_branch = narrow(mlp_grad)
    up_input = [
        narrow(slopes[q] * mm(mlp_branch, down_q[q])) for q in range(4)
    ]
    normed_two_grad = sum(mm_nt(up_input[q], up_q[q]) for q in range(4))
    attn_in_grad, gain_two = norm_back(after_attn, gain_full[1], normed_two_grad)
    resid_one = mlp_grad + attn_in_grad
    attn_branch = narrow(resid_one)
    attended_grad = narrow(mm(attn_branch, out_all))
    if on_known:
        proj_grad, last_rights, middle_sum, middle_square = attend_back_kernel(
            ((None, ((0, 0, ff_part, ff_part // 2),)), (None, ((1, 0, ff_part, ff_part // 2),))),
            attended_grad,
            packed,
            attn_lse,
            attended_all,
            cosines,
            sines,
            seg_row,
            seg_col,
            [normed_two.T, mlp_branch.T],
            [up_input[q] for q in (0, 2, 1, 3)],
            [activated[q] for q in (0, 2, 1, 3)],
        )
        proj_grad = [proj_grad[q] for q in (0, 2, 1, 3)]
        last_rights = [last_rights[q] for q in (0, 2, 1, 3)]
        joint_back = first_group
    else:
        grad_parts = [attended_grad[:, q * out_part : (q + 1) * out_part] for q in range(4)]
        proj_whole = [
            attend_back(
                whole[side],
                same_doc,
                attn_lse[side],
                jnp.concatenate(
                    [grad_parts[side], swap(grad_parts[2 + side], "tensor", 1)], axis=0
                ),
                cosine,
                sine,
            )
            for side in range(2)
        ]
        proj_grad = [item[:rows] for item in proj_whole] + [
            swap(item[rows:], "tensor", 1) for item in proj_whole
        ]
        joint_back = joint_q
    normed_one_grad = sum(mm_nt(proj_grad[q], joint_back[q]) for q in range(4))
    embed_in, gain_one = norm_back(embedded, gain_full[0], normed_one_grad)
    embed_grad = resid_one + embed_in
    embed_scaled = narrow(embed_grad * D**0.5)
    sublane = lax.broadcasted_iota(jnp.int32, (8, 128), 0)
    facts = jnp.where(sublane == 1, loss_local, jnp.where(sublane == 2, count_local, 0.0))
    gains_end = (head_part + gains.shape[0] + 127) // 128 * 128
    out_fill = (out_part + 127) // 128 * 128
    fill = lambda array, columns: jnp.pad(array, ((0, 0), (0, columns - array.shape[1])))
    extra = jnp.pad(
        jnp.stack([gain_one, gain_two, gain_three]).T,
        ((0, 0), (head_part, gains_end - head_part - gains.shape[0])),
    )
    if not on_known:
        attended_q = [attended_all[:, q * out_part : (q + 1) * out_part] for q in range(4)]
        last_rights = [
            jnp.concatenate([fill(proj_grad[q], gains_end), fill(attended_q[q], out_fill)], axis=1)
            for q in range(4)
        ]
    lefts = [normed_out, embed_scaled, normed_one, attn_branch]
    rights = [logit_grad, last_rights]
    layout = (
        (None, ((2, 0, gains_end, gains_end), (3, gains_end, out_fill, out_fill))),
        *((at, ((0, 0, span, step),)) for at, span, step in pieces_of(vocab_part)),
    )
    gains_at = (0, head_part, gains_end - head_part)
    if on_known:
        facts = facts + jnp.where(sublane == 0, middle_square, 0.0)
    else:
        layout = (
            (0, ((0, 0, vocab_part, vocab_part),)),
            (None, ((2, 0, gains_end, gains_end), (3, gains_end, out_fill, out_fill))),
            (None, ((4, 0, ff_part, ff_part), (5, ff_part, ff_part, ff_part))),
        )
        gains_at = (1, head_part, gains_end - head_part)
        lefts = lefts + [normed_two, mlp_branch]
        rights = rights + [[jnp.concatenate([up_input[q], activated[q]], axis=1) for q in range(4)]]
    sums, totals = reduce_grads(
        layout, [item.T for item in lefts], rights, places, extra, facts, parts, gains_at
    )
    if on_known:
        sums = [*sums, middle_sum]
    step_float = step_count[0].astype(jnp.float32)
    fixes = jnp.where(
        sublane == 0,
        1.0 / (1.0 - jnp.power(beta_one, step_float)),
        1.0 / (1.0 - jnp.power(beta_two, step_float)),
    )
    plans = (
        (0, False, 0, rates[0], decays[0]),
        (1, False, 0, rates[1], decays[1]),
        (1, True, gains_end, rates[2], decays[2]),
        (2, False, 0, rates[3], decays[3]),
        (2, False, ff_part, rates[4], decays[4]),
        (1, True, head_part, rates[5], decays[5]),
    )
    triples = (
        (table.T, momentum_table.T, variance_table.T),
        (joint_weight, momentum_joint, variance_joint),
        (output_weight, momentum_output, variance_output),
        (upward_weight, momentum_upward, variance_upward),
        (downward_weight.T, momentum_downward.T, variance_downward.T),
        (gains, momentum_gains, variance_gains),
    )
    updated, results = update_weights(totals, fixes, sums, plans, triples)
    updated = [item.T if place // 3 in (0, 4) else item for place, item in enumerate(updated)]
    return tuple([results[0, 0], results[1, 0]] + updated)


def solution(mesh):
    placed = (
        P("dp"),
        P("dp", None),
        P("dp"),
        P("dp"),
        P(),
        P("tensor", "dp"),
        P("dp", "tensor"),
        P("tensor", "dp"),
        P("dp", "tensor"),
        P("tensor", "dp"),
        P(None, "dp"),
        P("tensor", "dp"),
        P("dp", "tensor"),
        P("tensor", "dp"),
        P("dp", "tensor"),
        P("tensor", "dp"),
        P(None, "dp"),
        P("tensor", "dp"),
        P("dp", "tensor"),
        P("tensor", "dp"),
        P("dp", "tensor"),
        P("tensor", "dp"),
        P(None, "dp"),
    )
    return jax.shard_map(
        per_device,
        mesh=mesh,
        in_specs=placed,
        out_specs=(
            P(),
            P(),
            P("tensor", "dp"),
            P("tensor", "dp"),
            P("tensor", "dp"),
            P("dp", "tensor"),
            P("dp", "tensor"),
            P("dp", "tensor"),
            P("tensor", "dp"),
            P("tensor", "dp"),
            P("tensor", "dp"),
            P("dp", "tensor"),
            P("dp", "tensor"),
            P("dp", "tensor"),
            P("tensor", "dp"),
            P("tensor", "dp"),
            P("tensor", "dp"),
            P(None, "dp"),
            P(None, "dp"),
            P(None, "dp"),
        ),
        check_vma=False,
    )
```
